32 devices in a mesh: dp: 4 (over z), expert: 8 (over y, x, core).
Axes of the slice: x: 2, y: 2, z: 4, core: 2. Of those that a mesh axis runs over, the one named last changes fastest.
Arguments:
- inputs: float32 [25216, 768], P(('dp', 'expert')), may hold values from -6 to 6
- gain_one: bfloat16 [768], P('dp'), may hold values from 0.5 to 1.5
- shift_one: bfloat16 [768], P('dp'), may hold values from -0.59765625 to 0.59765625
- qkv_weight: bfloat16 [768, 2304], P('dp'), may hold values from -0.21875 to 0.21875
- proj_weight: bfloat16 [768, 768], P('dp'), may hold values from -1.25 to 1.25
- gain_two: bfloat16 [768], P('dp'), may hold values from 0.5 to 1.5
- shift_two: bfloat16 [768], P('dp'), may hold values from -0.59765625 to 0.59765625
- router_weight: bfloat16 [768, 8], P('dp'), may hold values from -0.15625 to 0.15625
- expert_in: bfloat16 [8, 768, 3072], P('expert', None, 'dp'), may hold values from -0.21875 to 0.21875
- expert_bias: bfloat16 [8, 3072], P('expert', 'dp'), may hold values from -0.59765625 to 0.59765625
- expert_out: bfloat16 [8, 3072, 768], P('expert', 'dp'), may hold values from -0.875 to 0.875
- out_grad: float32 [25216, 768], P(('dp', 'expert')), may hold values from -6 to 6
- routes: int32 [25216, 2], P(('dp', 'expert')), may hold values from 0 to 7, all different within a row
- priority: int32 [128, 394], P(('dp', 'expert')), may hold values from 0 to 393, each once within a row
- capacity: int32 [128], P(('dp', 'expert')), may hold values from 45 to 62, as said below
Outputs:
- outputs: float32 [25216, 768], P(('dp', 'expert'))
- inputs_grad: float32 [25216, 768], P(('dp', 'expert'))
- gainone_grad: float32 [768], P('dp')
- shiftone_grad: float32 [768], P('dp')
- qkv_grad: float32 [768, 2304], P('dp')
- proj_grad: float32 [768, 768], P('dp')
- gaintwo_grad: float32 [768], P('dp')
- shifttwo_grad: float32 [768], P('dp')
- router_grad: float32 [768, 8], P('dp')
- expin_grad: float32 [8, 768, 3072], P('expert', None, 'dp')
- bias_grad: float32 [8, 3072], P('expert', 'dp')
- expout_grad: float32 [8, 3072, 768], P('expert', 'dp')
The draws below stay inside these ranges and needn't reach their ends.
Inputs may be any that keep to these rules, and one draw needn't show every extreme that they name: Each row of priority is a permutation; lower values fill first. `routes`: the two experts of a token differ. capacity[b] is at most 62 and equals 62 for some micro-batch in every draw.
All inputs are finite; a program needn't handle non-finite values.
Results may differ from the reference program's by a relative error of at most 0.022.
Values may be sent and summed in bfloat16 or wider, within the bound.
A program may use at most 152 MiB of HBM per device.

```python
import math
from functools import partial
import jax
import jax.numpy as jnp
from jax import lax

D = 768
HEADS = 12
HEAD = 64
FF = 3072
SEQ = 197
IMG_MB = 1
MB = 4
EXPERTS = 8
TMB = 197
TOKENS = 25216
NBLOCK = 128
CAP = 62


def draw_capacity(key, part):
    first_key, second_key = jax.random.split(jax.random.fold_in(key, 17))
    lowest = max(1, 3 * CAP // 4 - 1)
    drawn = jax.random.randint(first_key, (NBLOCK,), lowest, CAP + 1)
    chosen = jax.random.randint(second_key, (), 0, NBLOCK)
    return jnp.where(jnp.arange(NBLOCK) == chosen, CAP, drawn).astype(jnp.int32)


def block_scale(own_key, extent, cuts, least, high):
    def one(dim, blocks):
        heights = jax.random.uniform(jax.random.fold_in(jax.random.fold_in(own_key, 6), dim), (blocks,), jnp.float32, least / len(cuts), high / len(cuts))
        return jnp.repeat(jnp.exp(heights), extent[dim] // blocks).reshape((-1,) + (1,) * (len(extent) - dim - 1))

    level = one(*cuts[0])
    for cut in cuts[1:]:
        level = level * one(*cut)
    return level


def distinct(rng, rows, amount, top, lift):
    ranking = jax.random.permutation(jax.random.fold_in(rng, 1), amount)
    favour = ranking
    for power in range(3):
        favour = favour * favour // amount
    favour = favour * lift // amount
    chance = jax.random.randint(jax.random.fold_in(rng, 2), (rows, amount), 0, 4096) + favour
    holders = jax.random.permutation(jax.random.fold_in(rng, 3), rows)[jnp.arange(amount) % rows]
    chance = jnp.where(jnp.arange(rows)[:, None] == holders[None, :], 1 << 14, chance)
    score = chance * amount + jnp.arange(amount)
    return lax.top_k(score.astype(jnp.int32), top)[1].astype(jnp.int32)


def scatter_about(stream_key, dims, deviation, bound, cuts=(), dtype=jnp.bfloat16):
    loudness = block_scale(stream_key, dims, cuts, -0.22, 0.18) if cuts else 1.0
    result = jax.random.normal(stream_key, dims, jnp.float32) * deviation * loudness
    return jnp.minimum(jnp.maximum(result, -bound), bound).astype(dtype)


def setup_inputs(seed: int = 0) -> dict:
    seeds = jax.random.split(jax.random.key(seed), 16)
    return {
        "inputs": scatter_about(seeds[0], (TOKENS, D), 1.0, 6.0, ((0, 32),), jnp.float32),
        "gain_one": jnp.clip(1.0 + 0.1 * jax.random.normal(seeds[1], (D,), jnp.float32), 0.5, 1.5).astype(jnp.bfloat16),
        "shift_one": scatter_about(seeds[2], (D,), 0.1, 0.59765625, ((0, 4),)),
        "qkv_weight": scatter_about(seeds[3], (D, 3 * D), D ** -0.5, 0.21875, ((0, 4),)),
        "proj_weight": scatter_about(seeds[4], (D, D), (D / 32) ** -0.5, 1.25, ((0, 4),)),
        "gain_two": jnp.clip(1.0 + 0.1 * jax.random.normal(seeds[5], (D,), jnp.float32), 0.5, 1.5).astype(jnp.bfloat16),
        "shift_two": scatter_about(seeds[6], (D,), 0.1, 0.59765625, ((0, 4),)),
        "router_weight": scatter_about(seeds[7], (D, EXPERTS), (16 * D / 9) ** -0.5, 0.15625, ((0, 4),)),
        "expert_in": scatter_about(seeds[8], (EXPERTS, D, FF), D ** -0.5, 0.21875, ((0, 8), (2, 4))),
        "expert_bias": scatter_about(seeds[9], (EXPERTS, FF), 0.1, 0.59765625, ((0, 8), (1, 4))),
        "expert_out": scatter_about(seeds[10], (EXPERTS, FF, D), (FF / (EXPERTS * EXPERTS)) ** -0.5, 0.875, ((0, 8), (1, 4))),
        "out_grad": scatter_about(seeds[11], (TOKENS, D), 1.0, 6.0, ((0, 32),), jnp.float32),
        "routes": distinct(seeds[12], TOKENS, EXPERTS, 2, 2048),
        "priority": jax.vmap(lambda own: jax.random.permutation(own, 2 * TMB))(jax.random.split(seeds[13], NBLOCK)).reshape((NBLOCK, 2 * TMB)).astype(jnp.int32),
        "capacity": draw_capacity(jax.random.fold_in(seeds[15], 71), 0),
    }


EPS = 1e-06

@jax.custom_vjp
def low(v):
    return lax.optimization_barrier(v.astype(jnp.bfloat16)).astype(jnp.float32)

@jax.custom_vjp
def low_back(v):
    return v

def low_keep(v):
    return (low(v), None)

def low_pass(kept, grad):
    return (grad,)

def back_keep(v):
    return (v, None)

def back_low(kept, grad):
    return (low(grad),)
low.defvjp(low_keep, low_pass)
low_back.defvjp(back_keep, back_low)

def matmul(left, right):
    return jnp.dot(left, right, precision=lax.Precision.HIGHEST, preferred_element_type=jnp.float32)

def layer_norm(values, gain, shift):
    average = lax.optimization_barrier(jnp.mean(values, axis=-1, keepdims=True))
    centered = values - average
    spread = lax.optimization_barrier(jnp.mean(centered * centered, axis=-1, keepdims=True))
    return centered * lax.rsqrt(spread + EPS) * gain + shift

def attend(group):
    images = group.shape[0]
    split = group.reshape(images, SEQ, 3, HEADS, HEAD)
    query = split[:, :, 0]
    keys = split[:, :, 1]
    values = split[:, :, 2]
    raw = low_back(jnp.einsum('bqhd,bkhd->bhqk', query, keys, precision=lax.Precision.HIGHEST))
    probs = jax.nn.softmax(raw * (1.0 / math.sqrt(HEAD)), axis=-1)
    weights = low(probs)
    mixed = jnp.einsum('bhqk,bkhd->bqhd', weights, values, precision=lax.Precision.HIGHEST)
    return low(low_back(mixed.reshape(images, SEQ, HEADS * HEAD)))

def expert_apply(operands):
    rows, weight_in, bias, weight_out = operands
    pre = low_back(matmul(rows, weight_in) + bias)
    active = low(jax.nn.gelu(pre, approximate=False))
    return low(low_back(matmul(active, weight_out)))

def block_rank(operands):
    expert_row, order_row = operands
    same = expert_row[:, None] == expert_row[None, :]
    before = order_row[None, :] < order_row[:, None]
    return lax.optimization_barrier(jnp.sum(jnp.logical_and(same, before).astype(jnp.int32), axis=1))

def route_tables(routes, priority, capacity):
    pairs = routes.reshape(-1, 2 * TMB)
    blocks_count = pairs.shape[0]
    ranks = lax.map(block_rank, (pairs, priority))
    kept = ranks < capacity[:, None]
    blocks = lax.broadcasted_iota(jnp.int32, pairs.shape, 0)
    positions = lax.broadcasted_iota(jnp.int32, pairs.shape, 1)
    per_expert = blocks_count * CAP
    flat = pairs * per_expert + blocks * CAP + ranks
    total = EXPERTS * per_expert
    target = jnp.where(kept, flat, total).reshape(-1)
    token_ids = (blocks * TMB + positions // 2).reshape(-1)
    slot_token = jnp.zeros((total,), jnp.int32).at[target].set(token_ids, mode='drop')
    slot_valid = jnp.zeros((total,), jnp.float32).at[target].set(1.0, mode='drop')
    pair_slot = jnp.where(kept, flat, 0).reshape(-1)
    pair_kept = kept.astype(jnp.float32).reshape(-1, 2)
    return (slot_token.reshape(EXPERTS, per_expert), slot_valid.reshape(EXPERTS, per_expert), pair_slot, pair_kept)

def forward(tables, routes, inputs, gain_one, shift_one, qkv_weight, proj_weight, gain_two, shift_two, router_weight, expert_in, expert_bias, expert_out):
    slot_token, slot_valid, pair_slot, pair_kept = tables
    normed = low(layer_norm(inputs, gain_one, shift_one))
    qkv = low(low_back(matmul(normed, qkv_weight)))
    groups = qkv.reshape(-1, MB * IMG_MB, SEQ, 3 * D)
    mixed = lax.map(jax.checkpoint(attend), groups).reshape(-1, D)
    branch = low_back(matmul(mixed, proj_weight))
    hidden = inputs + branch
    second = low(layer_norm(hidden, gain_two, shift_two))
    logits = matmul(second, router_weight)
    router_probs = jax.nn.softmax(logits, axis=-1)
    gates = jnp.take_along_axis(router_probs, routes, axis=1)
    sent = low_back(second[slot_token] * slot_valid[:, :, None])
    returned = lax.map(jax.checkpoint(expert_apply), (sent, expert_in, expert_bias, expert_out))
    picked = returned.reshape(-1, D)[pair_slot].reshape(-1, 2, D)
    mixing = gates * pair_kept
    return hidden + lax.optimization_barrier(jnp.sum(picked * mixing[:, :, None], axis=1))

def reference(inputs, gain_one, shift_one, qkv_weight, proj_weight, gain_two, shift_two, router_weight, expert_in, expert_bias, expert_out, out_grad, routes, priority, capacity):
    tables = route_tables(routes, priority, capacity)
    primals = (inputs.astype(jnp.float32), gain_one.astype(jnp.float32), shift_one.astype(jnp.float32), qkv_weight.astype(jnp.float32), proj_weight.astype(jnp.float32), gain_two.astype(jnp.float32), shift_two.astype(jnp.float32), router_weight.astype(jnp.float32), expert_in.astype(jnp.float32), expert_bias.astype(jnp.float32), expert_out.astype(jnp.float32))
    outputs, pullback = jax.vjp(partial(forward, tables, routes), *primals)
    grads = pullback(out_grad.astype(jnp.float32))
    return (outputs, grads[0], grads[1], grads[2], grads[3], grads[4], grads[5], grads[6], grads[7], grads[8], grads[9], grads[10])
```

```python
import functools

import jax
import jax.numpy as jnp
from jax import lax
from jax.experimental import pallas as pl
from jax.experimental.pallas import tpu as pltpu
from jax.sharding import PartitionSpec as P

HEADS = 12
HEAD = 64
SEQ = 197
SEQ_PAD = 208
EPS = 1e-06
BF = jnp.bfloat16
F32 = jnp.float32
SMALL = 128
BIAS_ROWS = 16
NEG = -1e30
VMEM_LIMIT = 60 * 1024 * 1024


def ceil_to(value, step):
    return (value + step - 1) // step * step


def dot(a, b):
    return jnp.dot(a, b, preferred_element_type=F32)


def dot_nt(a, b):
    return lax.dot_general(a, b, (((1,), (1,)), ((), ())), preferred_element_type=F32)


def dot_tn(a, b):
    return lax.dot_general(a, b, (((0,), (0,)), ((), ())), preferred_element_type=F32)


def params(count=1):
    return pltpu.CompilerParams(
        dimension_semantics=("arbitrary",) * count, vmem_limit_bytes=VMEM_LIMIT
    )


def route_kernel(cap_pad, cols_ref, rows_ref, limit_ref, slot_rows_ref, slot_cols_ref):
    for b in range(cols_ref.shape[0]):
        limit = limit_ref[b]
        col = [cols_ref[b, :, k : k + 1] for k in range(4)]
        row = [rows_ref[b, k : k + 1, :] for k in range(4)]
        slot_rows_ref[b] = jnp.full(slot_rows_ref.shape[1:], -1, jnp.int32)
        slot_cols_ref[b] = jnp.full(slot_cols_ref.shape[1:], -1, jnp.int32)
        for j in range(2):
            rank_row = 0
            rank_col = 0
            for k in range(2):
                hit = (col[k] == row[j]) & (col[2 + k] < row[2 + j])
                rank_row = rank_row + jnp.sum(hit.astype(jnp.int32), axis=0, keepdims=True)
                hit = (row[k] == col[j]) & (row[2 + k] < col[2 + j])
                rank_col = rank_col + jnp.sum(hit.astype(jnp.int32), axis=1, keepdims=True)
            keep_row = (rank_row < limit) & (row[j] >= 0)
            keep_col = (rank_col < limit) & (col[j] >= 0)
            slot_rows_ref[b, j : j + 1, :] = jnp.where(keep_row, row[j] * cap_pad + rank_row, -1)
            slot_cols_ref[b, :, j : j + 1] = jnp.where(keep_col, col[j] * cap_pad + rank_col, -1)


def run_route(cols, rows, limits, cap_pad):
    batches = cols.shape[0]
    return pl.pallas_call(
        functools.partial(route_kernel, cap_pad),
        out_shape=(
            jax.ShapeDtypeStruct((batches, 8, SEQ_PAD), jnp.int32),
            jax.ShapeDtypeStruct((batches, SEQ_PAD, 8), jnp.int32),
        ),
        in_specs=[
            pl.BlockSpec(memory_space=pltpu.VMEM),
            pl.BlockSpec(memory_space=pltpu.VMEM),
            pl.BlockSpec(memory_space=pltpu.SMEM),
        ],
        out_specs=(
            pl.BlockSpec(memory_space=pltpu.VMEM),
            pl.BlockSpec(memory_space=pltpu.VMEM),
        ),
        compiler_params=pltpu.CompilerParams(vmem_limit_bytes=VMEM_LIMIT),
        cost_estimate=pl.CostEstimate(flops=4000000, bytes_accessed=1000000, transcendentals=0),
        name="route",
    )(cols, rows, limits)


def norm_stats(values):
    average = jnp.mean(values, axis=-1, keepdims=True)
    centered = values - average
    spread = jnp.mean(centered * centered, axis=-1, keepdims=True)
    inverse = lax.rsqrt(spread + EPS)
    return centered * inverse, inverse


def front_kernel(
    experts,
    x_ref,
    grad_ref,
    weight_ref,
    cols_ref,
    slot_rows_ref,
    send_ref,
    qkv_ref,
    mixed_ref,
    lse_ref,
    hidden_ref,
    one_ref,
    two_ref,
    probs_ref,
    small_ref,
):
    width = x_ref.shape[-1]
    rows = x_ref.shape[1]

    @pl.when(pl.program_id(0) == 0)
    def _():
        small_ref[...] = weight_ref[:, 4 * width :].astype(F32).T

    x = x_ref[0]
    hat, _ = norm_stats(x)
    one = (hat * small_ref[0:1, :] + small_ref[1:2, :]).astype(BF)
    one_ref[0] = one
    qkv_ref[0] = dot(one, weight_ref[:, : 3 * width]).astype(BF)
    lane = lax.broadcasted_iota(jnp.int32, (1, 128), 1)
    key_ok = lax.broadcasted_iota(jnp.int32, (1, rows), 1) < SEQ
    lse = jnp.zeros((rows, 128), F32)
    scale = HEAD ** (-0.5)
    for pair in range(HEADS // 2):
        low = pair * 128
        query = qkv_ref[0, :, low : low + 128]
        keys = qkv_ref[0, :, width + low : width + low + 128]
        values = qkv_ref[0, :, 2 * width + low : 2 * width + low + 128]
        total = None
        for side in range(2):
            mine = (lane // HEAD) == side
            scores = dot_nt(jnp.where(mine, query, jnp.zeros_like(query)), keys) * scale
            scores = jnp.where(key_ok, scores, NEG)
            highest = jnp.max(scores, axis=-1, keepdims=True)
            expo = jnp.exp(scores - highest)
            denom = jnp.sum(expo, axis=-1, keepdims=True)
            weights = (expo / denom).astype(BF)
            lse = jnp.where(lane == 2 * pair + side, highest + jnp.log(denom), lse)
            part = dot(weights, jnp.where(mine, values, jnp.zeros_like(values)))
            total = part if total is None else total + part
        mixed_ref[0, :, low : low + 128] = total.astype(BF)
    lse_ref[0] = lse
    hidden = x + dot(mixed_ref[0], weight_ref[:, 3 * width : 4 * width])
    hidden_ref[0] = hidden
    hat, _ = norm_stats(hidden)
    two = (hat * small_ref[2:3, :] + small_ref[3:4, :]).astype(BF)
    two_ref[0] = two
    logits = dot(two, weight_ref[:, 4 * width :])
    in_router = (lane >= 4) & (lane < 4 + experts)
    logits = jnp.where(in_router, logits, NEG)
    expo = jnp.exp(logits - jnp.max(logits, axis=-1, keepdims=True))
    probs = expo / jnp.sum(expo, axis=-1, keepdims=True)
    probs_ref[0] = probs
    out_grad = grad_ref[0]
    slots = send_ref.shape[0] * send_ref.shape[3]
    slot = lax.broadcasted_iota(jnp.int32, (slots, 1), 0)
    both = None
    grads = None
    for j in range(2):
        gate = jnp.sum(
            jnp.where(lane - 4 == cols_ref[0, :, j : j + 1], probs, 0.0), axis=-1, keepdims=True
        )
        pick = (slot == slot_rows_ref[0, j : j + 1, :]).astype(F32)
        both = pick if both is None else both + pick
        part = dot(pick.astype(BF), (gate * out_grad).astype(BF))
        grads = part if grads is None else grads + part
    sent = dot(both.astype(BF), two).astype(BF)
    send_ref[:, 0, 0] = sent.reshape(send_ref.shape[0], send_ref.shape[3], width)
    send_ref[:, 0, 1] = grads.astype(BF).reshape(send_ref.shape[0], send_ref.shape[3], width)


def run_front(x, grad, weight, cols, slot_rows, experts, cap_pad):
    batches, rows, width = x.shape
    total = weight.shape[1]

    def block(*shape):
        return pl.BlockSpec((1,) + shape, lambda i: (i,) + (0,) * len(shape))

    def out(shape, dtype):
        return jax.ShapeDtypeStruct((batches,) + shape, dtype)

    return pl.pallas_call(
        functools.partial(front_kernel, experts),
        grid=(batches,),
        out_shape=(
            jax.ShapeDtypeStruct((experts, batches, 2, cap_pad, width), BF),
            out((rows, 3 * width), BF),
            out((rows, width), BF),
            out((rows, 128), F32),
            out((rows, width), F32),
            out((rows, width), BF),
            out((rows, width), BF),
            out((rows, SMALL), F32),
        ),
        in_specs=[
            block(rows, width),
            block(rows, width),
            pl.BlockSpec((width, total), lambda i: (0, 0), pipeline_mode=pl.Buffered(1)),
            block(rows, 4),
            block(8, rows),
        ],
        out_specs=(
            pl.BlockSpec((experts, 1, 2, cap_pad, width), lambda i: (0, i, 0, 0, 0)),
            block(rows, 3 * width),
            block(rows, width),
            block(rows, 128),
            block(rows, width),
            block(rows, width),
            block(rows, width),
            block(rows, SMALL),
        ),
        scratch_shapes=[pltpu.VMEM((SMALL, width), F32)],
        compiler_params=params(),
        cost_estimate=pl.CostEstimate(
            flops=8000000000, bytes_accessed=40000000, transcendentals=3000000
        ),
        name="front",
    )(x, grad, weight, cols, slot_rows)


def expert_kernel(first, last, *refs):
    refs = list(refs)
    x_ref, grad_ref, win_ref, wout_ref = refs[:4]
    refs = refs[4:]
    if not first:
        y_in, dx_in = refs[:2]
        refs = refs[2:]
    back_refs = refs[:1] if last else refs[:2]
    refs = refs[len(back_refs) :]
    gin_ref, gout_ref, y_acc, dx_acc, gin_acc, gout_acc = refs
    shard = pl.program_id(0)
    block = pl.program_id(1)
    shards = pl.num_programs(0)
    blocks = pl.num_programs(1)
    width = x_ref.shape[-1]
    rows = x_ref.shape[0] * x_ref.shape[1] * x_ref.shape[3]
    x = x_ref[...].reshape(rows, width)
    grad = grad_ref[...].reshape(rows, width)
    win = win_ref[0, :width, :]
    wout = wout_ref[0]
    pre = dot(x, win) + win_ref[0, width : width + 1, :].astype(F32)
    cdf = 0.5 * lax.erf(pre * (0.5**0.5)) + 0.5
    active = (pre * cdf).astype(BF)
    slope = cdf + pre * (jnp.exp(-0.5 * pre * pre) * 0.3989422804014327)
    d_pre = dot_nt(grad, wout) * slope
    d_pre = d_pre.astype(BF)
    here = pl.ds(pl.multiple_of(block * rows, rows), rows)
    y_part = dot(active, wout)
    dx_part = dot_nt(d_pre, win)

    @pl.when(shard == 0)
    def _():
        if first:
            y_acc[here, :] = y_part
            dx_acc[here, :] = dx_part
        else:
            y_acc[here, :] = y_part + y_in[here, :]
            dx_acc[here, :] = dx_part + dx_in[here, :]

    @pl.when(shard > 0)
    def _():
        y_acc[here, :] += y_part
        dx_acc[here, :] += dx_part

    gout = dot_tn(active, grad)
    gin = dot_tn(x, d_pre)
    gbias = jnp.sum(d_pre.astype(F32), axis=0, keepdims=True)

    @pl.when(block == 0)
    def _():
        gout_acc[...] = gout
        gin_acc[:width, :] = gin
        gin_acc[width : width + 1, :] = gbias

    @pl.when(block > 0)
    def _():
        gout_acc[...] += gout
        gin_acc[:width, :] += gin
        gin_acc[width : width + 1, :] += gbias

    @pl.when(block == blocks - 1)
    def _():
        gout_ref[0] = gout_acc[...].astype(BF)
        gin_ref[0, :width, :] = gin_acc[:width, :].astype(BF)
        gin_ref[0, width:, :] = jnp.broadcast_to(
            gin_acc[width : width + 1, :].astype(BF), (BIAS_ROWS, gin_acc.shape[1])
        )

    @pl.when(shard == shards - 1)
    def _():
        if last:
            shape = (x_ref.shape[0], x_ref.shape[1], x_ref.shape[3], width)
            back_refs[0][:, :, 0] = y_acc[here, :].astype(BF).reshape(shape)
            back_refs[0][:, :, 1] = dx_acc[here, :].astype(BF).reshape(shape)
        else:
            back_refs[0][...] = y_acc[here, :]
            back_refs[1][...] = dx_acc[here, :]


def run_expert(received, win, wout, carried, last):
    sources, batches, _, cap_pad, width = received.shape
    shards, tall, span = win.shape
    group = max(1, 512 // (batches * cap_pad))
    while sources % group:
        group -= 1
    blocks = sources // group
    rows = group * batches * cap_pad
    total = sources * batches * cap_pad
    first = carried is None
    final = shards - 1

    def take(kind):
        return pl.BlockSpec((group, batches, 1, cap_pad, width), lambda s, r: (r, 0, kind, 0, 0))

    in_specs = [
        take(0),
        take(1),
        pl.BlockSpec((1, tall, span), lambda s, r: (s, 0, 0)),
        pl.BlockSpec((1, span, width), lambda s, r: (s, 0, 0)),
    ]
    operands = [received, received, win, wout]
    if not first:
        in_specs += [pl.BlockSpec((total, width), lambda s, r: (0, 0), pipeline_mode=pl.Buffered(1))] * 2
        operands += list(carried)
    if last:
        out_shape = [jax.ShapeDtypeStruct(received.shape, BF)]
        out_specs = [
            pl.BlockSpec(
                (group, batches, 2, cap_pad, width),
                lambda s, r: (jnp.where(s == final, r, 0), 0, 0, 0, 0),
            )
        ]
    else:
        out_shape = [jax.ShapeDtypeStruct((total, width), F32)] * 2
        out_specs = [pl.BlockSpec((rows, width), lambda s, r: (jnp.where(s == final, r, 0), 0))] * 2
    out_shape += [
        jax.ShapeDtypeStruct(win.shape, BF),
        jax.ShapeDtypeStruct(wout.shape, BF),
    ]
    out_specs += [
        pl.BlockSpec((1, tall, span), lambda s, r: (s, 0, 0)),
        pl.BlockSpec((1, span, width), lambda s, r: (s, 0, 0)),
    ]
    return pl.pallas_call(
        functools.partial(expert_kernel, first, last),
        grid=(shards, blocks),
        out_shape=tuple(out_shape),
        in_specs=in_specs,
        out_specs=tuple(out_specs),
        scratch_shapes=[
            pltpu.VMEM((total, width), F32),
            pltpu.VMEM((total, width), F32),
            pltpu.VMEM((tall, span), F32),
            pltpu.VMEM((span, width), F32),
        ],
        compiler_params=params(2),
        cost_estimate=pl.CostEstimate(
            flops=12 * total * width * span * shards,
            bytes_accessed=40000000,
            transcendentals=2 * total * span * shards,
        ),
        name="expert",
    )(*operands)


def tail_kernel(
    experts,
    x_ref,
    grad_ref,
    weight_ref,
    cols_ref,
    slot_cols_ref,
    back_ref,
    qkv_ref,
    mixed_ref,
    lse_ref,
    hidden_ref,
    one_ref,
    two_ref,
    probs_ref,
    out_ref,
    dx_ref,
    dense_ref,
    small_ref,
    sums_ref,
    d_qkv_ref,
    d_branch_ref,
    d_logits_ref,
    one_all,
    two_all,
    mixed_all,
):
    width = x_ref.shape[-1]
    rows = x_ref.shape[1]
    index = pl.program_id(0)

    @pl.when(index == 0)
    def _():
        small_ref[...] = weight_ref[:, 4 * width :].astype(F32).T
        sums_ref[...] = jnp.zeros_like(sums_ref)

    here = pl.ds(pl.multiple_of(index * rows, rows), rows)
    one_all[here, :] = one_ref[0]
    two_all[here, :] = two_ref[0]
    mixed_all[here, :] = mixed_ref[0]
    out_grad = grad_ref[0]
    hidden = hidden_ref[0]
    probs = probs_ref[0]
    lane = lax.broadcasted_iota(jnp.int32, (1, 128), 1)
    slots = back_ref.shape[0] * back_ref.shape[3]
    slot = lax.broadcasted_iota(jnp.int32, (1, slots), 1)
    answers = back_ref[:, 0, 0].reshape(slots, width)
    answer_grads = back_ref[:, 0, 1].reshape(slots, width)
    result = hidden
    d_probs = jnp.zeros_like(probs)
    both = None
    for j in range(2):
        pick = (slot == slot_cols_ref[0, :, j : j + 1]).astype(F32)
        both = pick if both is None else both + pick
        chosen = lane - 4 == cols_ref[0, :, j : j + 1]
        gate = jnp.sum(jnp.where(chosen, probs, 0.0), axis=-1, keepdims=True)
        picked = dot(pick.astype(BF), answers)
        result = result + gate * picked
        d_gate = jnp.sum(picked * out_grad, axis=-1, keepdims=True)
        d_probs = jnp.where(chosen, d_gate, d_probs)
    out_ref[0] = result
    d_logits = probs * (d_probs - jnp.sum(d_probs * probs, axis=-1, keepdims=True))
    d_logits = d_logits.astype(BF)
    d_logits_ref[here, :] = d_logits
    d_two = dot(both.astype(BF), answer_grads) + dot_nt(d_logits, weight_ref[:, 4 * width :])
    hat, inverse = norm_stats(hidden)
    sums_ref[2:3, :] += jnp.sum(d_two * hat, axis=0, keepdims=True)
    sums_ref[3:4, :] += jnp.sum(d_two, axis=0, keepdims=True)
    d_hat = d_two * small_ref[2:3, :]
    d_hidden = out_grad + inverse * (
        d_hat
        - jnp.mean(d_hat, axis=-1, keepdims=True)
        - hat * jnp.mean(d_hat * hat, axis=-1, keepdims=True)
    )
    d_branch = d_hidden.astype(BF)
    d_branch_ref[here, :] = d_branch
    d_mixed_all = dot_nt(d_branch, weight_ref[:, 3 * width : 4 * width]).astype(BF)
    key_ok = lax.broadcasted_iota(jnp.int32, (1, rows), 1) < SEQ
    scale = HEAD ** (-0.5)
    for pair in range(HEADS // 2):
        low = pair * 128
        query = qkv_ref[0, :, low : low + 128]
        keys = qkv_ref[0, :, width + low : width + low + 128]
        values = qkv_ref[0, :, 2 * width + low : 2 * width + low + 128]
        d_mixed = d_mixed_all[:, low : low + 128]
        d_query = d_keys = d_values = None
        for side in range(2):
            mine = (lane // HEAD) == side
            head = 2 * pair + side

            def own(array):
                return jnp.where(mine, array, jnp.zeros_like(array))

            my_query = own(query)
            my_keys = own(keys)
            my_d_mixed = own(d_mixed)
            scores = dot_nt(my_query, keys) * scale
            scores = jnp.where(key_ok, scores, NEG)
            probs_h = jnp.exp(scores - lse_ref[0, :, head : head + 1])
            d_weights = dot_nt(my_d_mixed, values)
            row_terms = jnp.sum(d_weights * probs_h, axis=-1, keepdims=True)
            d_scores = (probs_h * (d_weights - row_terms) * scale).astype(BF)
            parts = (
                dot(d_scores, my_keys),
                dot_tn(d_scores, my_query),
                dot_tn(probs_h.astype(BF), my_d_mixed),
            )
            if side == 0:
                d_query, d_keys, d_values = parts
            else:
                d_query, d_keys, d_values = (
                    d_query + parts[0],
                    d_keys + parts[1],
                    d_values + parts[2],
                )
        d_qkv_ref[here, low : low + 128] = d_query.astype(BF)
        d_qkv_ref[here, width + low : width + low + 128] = d_keys.astype(BF)
        d_qkv_ref[here, 2 * width + low : 2 * width + low + 128] = d_values.astype(BF)
    d_one = dot_nt(d_qkv_ref[here, :], weight_ref[:, : 3 * width])
    hat, inverse = norm_stats(x_ref[0])
    sums_ref[0:1, :] += jnp.sum(d_one * hat, axis=0, keepdims=True)
    sums_ref[1:2, :] += jnp.sum(d_one, axis=0, keepdims=True)
    d_hat = d_one * small_ref[0:1, :]
    dx_ref[0] = d_hidden + inverse * (
        d_hat
        - jnp.mean(d_hat, axis=-1, keepdims=True)
        - hat * jnp.mean(d_hat * hat, axis=-1, keepdims=True)
    )

    @pl.when(index == pl.num_programs(0) - 1)
    def _():
        dense_ref[:, 4 * width :] = (dot_tn(two_all[...], d_logits_ref[...]) + sums_ref[...].T).astype(BF)
        dense_ref[:, 3 * width : 4 * width] = dot_tn(mixed_all[...], d_branch_ref[...]).astype(BF)
        for part in range(3):
            cut = slice(part * width, (part + 1) * width)
            dense_ref[:, cut] = dot_tn(one_all[...], d_qkv_ref[:, cut]).astype(BF)


def run_tail(x, grad, weight, cols, slot_cols, back, saved, experts):
    batches, rows, width = x.shape
    total = weight.shape[1]
    cap_pad = back.shape[3]
    qkv, mixed, lse, hidden, one, two, probs = saved

    def block(*shape):
        return pl.BlockSpec((1,) + shape, lambda i: (i,) + (0,) * len(shape))

    return pl.pallas_call(
        functools.partial(tail_kernel, experts),
        grid=(batches,),
        out_shape=(
            jax.ShapeDtypeStruct(x.shape, F32),
            jax.ShapeDtypeStruct(x.shape, F32),
            jax.ShapeDtypeStruct((width, total), BF),
        ),
        in_specs=[
            block(rows, width),
            block(rows, width),
            pl.BlockSpec((width, total), lambda i: (0, 0), pipeline_mode=pl.Buffered(1)),
            block(rows, 4),
            block(rows, 8),
            pl.BlockSpec((experts, 1, 2, cap_pad, width), lambda i: (0, i, 0, 0, 0)),
            block(rows, 3 * width),
            block(rows, width),
            block(rows, 128),
            block(rows, width),
            block(rows, width),
            block(rows, width),
            block(rows, SMALL),
        ],
        out_specs=(
            block(rows, width),
            block(rows, width),
            pl.BlockSpec((width, total), lambda i: (0, 0), pipeline_mode=pl.Buffered(1)),
        ),
        scratch_shapes=[
            pltpu.VMEM((SMALL, width), F32),
            pltpu.VMEM((SMALL, width), F32),
            pltpu.VMEM((batches * rows, 3 * width), BF),
            pltpu.VMEM((batches * rows, width), BF),
            pltpu.VMEM((batches * rows, SMALL), BF),
            pltpu.VMEM((batches * rows, width), BF),
            pltpu.VMEM((batches * rows, width), BF),
            pltpu.VMEM((batches * rows, width), BF),
        ],
        compiler_params=params(),
        cost_estimate=pl.CostEstimate(
            flops=16000000000, bytes_accessed=50000000, transcendentals=2000000
        ),
        name="tail",
    )(x, grad, weight, cols, slot_cols, back, qkv, mixed, lse, hidden, one, two, probs)


def per_device(
    inputs,
    gain_one,
    shift_one,
    qkv_weight,
    proj_weight,
    gain_two,
    shift_two,
    router_weight,
    expert_in,
    expert_bias,
    expert_out,
    out_grad,
    routes,
    priority,
    capacity,
):
    batches = priority.shape[0]
    count = inputs.shape[0] // batches
    width = inputs.shape[1]
    experts = router_weight.shape[1]
    groups = lax.axis_size("expert")
    cap_pad = ceil_to(max(2, (5 * count + 2 * experts - 1) // (2 * experts)), 16)
    depth = qkv_weight.shape[0]
    both = ("dp", "expert")

    vectors = jnp.stack([gain_one, shift_one, gain_two, shift_two], axis=1)
    small = jnp.concatenate([vectors, router_weight], axis=1)
    small = jnp.pad(small, ((0, 0), (0, SMALL - small.shape[1])))
    pack = jnp.concatenate([qkv_weight, proj_weight, small], axis=1)
    slice_rows = depth // groups
    mine = lax.axis_index("expert")
    pack = lax.dynamic_slice_in_dim(pack, mine * slice_rows, slice_rows, axis=0)
    weight = lax.all_gather(pack, both, axis=0, tiled=True)

    hidden_units = expert_out.shape[1]
    cuts = 3
    span = hidden_units // cuts
    bias_rows = jnp.pad(expert_bias, ((0, BIAS_ROWS - 1), (0, 0)))
    tall_in = jnp.concatenate([expert_in[0], bias_rows], axis=0)
    gathered = []
    for cut in range(cuts):
        part_in = lax.all_gather(tall_in[:, cut * span : (cut + 1) * span], "dp", axis=0)
        part_out = lax.all_gather(expert_out[0, cut * span : (cut + 1) * span], "dp", axis=0)
        gathered.append((part_in, part_out))

    extra = SEQ_PAD - SEQ
    x = jnp.pad(inputs.reshape(batches, SEQ, width), ((0, 0), (0, extra), (0, 0)))
    grad = jnp.pad(out_grad.reshape(batches, SEQ, width), ((0, 0), (0, extra), (0, 0)))
    cols = jnp.concatenate(
        [routes.reshape(batches, SEQ, 2), priority.reshape(batches, SEQ, 2)], axis=2
    )
    cols = jnp.pad(cols, ((0, 0), (0, extra), (0, 0)), constant_values=-1)
    rows = jnp.swapaxes(cols, 1, 2)
    slot_rows, slot_cols = run_route(cols, rows, capacity, cap_pad)
    send, *saved = run_front(x, grad, weight, cols, slot_rows, experts, cap_pad)
    received = lax.all_to_all(send, "expert", split_axis=0, concat_axis=0, tiled=True)
    carried = None
    expert_sums = []
    for cut in range(cuts):
        last = cut == cuts - 1
        *carried, sum_in, sum_out = run_expert(received, *gathered[cut], carried, last)
        sum_in = lax.psum_scatter(sum_in, "dp", scatter_dimension=0, tiled=False)
        sum_out = lax.psum_scatter(sum_out, "dp", scatter_dimension=0, tiled=False)
        expert_sums.append((sum_in, sum_out))
    back = lax.all_to_all(carried[0], "expert", split_axis=0, concat_axis=0, tiled=True)
    outputs, inputs_grad, dense = run_tail(
        x, grad, weight, cols, slot_cols, back, saved, experts
    )
    dense = lax.psum_scatter(dense, both, scatter_dimension=0, tiled=True)
    dense = lax.all_gather(dense, "expert", axis=0, tiled=True).astype(F32)
    grad_in = jnp.concatenate([part[0] for part in expert_sums], axis=1).astype(F32)
    grad_out = jnp.concatenate([part[1] for part in expert_sums], axis=0).astype(F32)
    spot = 4 * width
    return (
        outputs[:, :SEQ].reshape(batches * SEQ, width),
        inputs_grad[:, :SEQ].reshape(batches * SEQ, width),
        dense[:, spot],
        dense[:, spot + 1],
        dense[:, : 3 * width],
        dense[:, 3 * width : spot],
        dense[:, spot + 2],
        dense[:, spot + 3],
        dense[:, spot + 4 : spot + 4 + experts],
        grad_in[None, :width],
        grad_in[None, width],
        grad_out[None],
    )


def solution(mesh):
    token = P(("dp", "expert"), None)
    vector = P("dp")
    matrix = P("dp", None)
    return jax.shard_map(
        per_device,
        mesh=mesh,
        in_specs=(
            token,
            vector,
            vector,
            matrix,
            matrix,
            vector,
            vector,
            matrix,
            P("expert", None, "dp"),
            P("expert", "dp"),
            P("expert", "dp", None),
            token,
            token,
            token,
            P(("dp", "expert")),
        ),
        out_specs=(
            token,
            token,
            vector,
            vector,
            matrix,
            matrix,
            vector,
            vector,
            matrix,
            P("expert", None, "dp"),
            P("expert", "dp"),
            P("expert", "dp", None),
        ),
        check_vma=False,
    )
```

```python
import functools

import jax
import jax.numpy as jnp
from jax import lax
from jax.experimental import pallas as pl
from jax.experimental.pallas import tpu as pltpu
from jax.sharding import PartitionSpec as P

HEADS = 12
HEAD = 64
SEQ = 197
SEQ_PAD = 208
EPS = 1e-06
BF = jnp.bfloat16
F32 = jnp.float32
SMALL = 128
MESH = pl.DeviceIdType.MESH
EARLY = 2
BIAS_ROWS = 16
NEG = -1e30
VMEM_LIMIT = 60 * 1024 * 1024
VMEM_MAX = 67043328


def ceil_to(value, step):
    return (value + step - 1) // step * step


def dot(a, b):
    return jnp.dot(a, b, preferred_element_type=F32)


def dot_nt(a, b):
    return lax.dot_general(a, b, (((1,), (1,)), ((), ())), preferred_element_type=F32)


def dot_tn(a, b):
    return lax.dot_general(a, b, (((0,), (0,)), ((), ())), preferred_element_type=F32)


def params(count=1):
    return pltpu.CompilerParams(
        dimension_semantics=("arbitrary",) * count, vmem_limit_bytes=VMEM_LIMIT
    )


class Line:
    def __init__(self, shards):
        self.shards = shards
        self.me = lax.axis_index("dp")
        self.has_below = self.me > 0
        self.has_above = self.me < shards - 1

    def greet(self, me, groups):
        barrier = pltpu.get_barrier_semaphore()
        for k in range(1, groups):
            pl.semaphore_signal(
                barrier, inc=1, device_id={"expert": lax.rem(me + k, groups)}, device_id_type=MESH
            )

        @pl.when(self.has_below)
        def _():
            pl.semaphore_signal(barrier, inc=1, device_id={"dp": self.me - 1}, device_id_type=MESH)

        @pl.when(self.has_above)
        def _():
            pl.semaphore_signal(barrier, inc=1, device_id={"dp": self.me + 1}, device_id_type=MESH)

        ends = self.has_below.astype(jnp.int32) + self.has_above.astype(jnp.int32)
        pl.semaphore_wait(barrier, groups - 1 + ends)

    def hop(self, way, round_id, source, target, send_sem, arrived):
        step = 1 - 2 * way
        slot = self.me - step * round_id
        copies = []
        for part in range(2):
            origin = source[part] if round_id == 0 else source[part].at[slot]
            copies.append(
                pltpu.make_async_remote_copy(
                    src_ref=origin,
                    dst_ref=target[part].at[slot],
                    send_sem=send_sem.at[way, round_id, part],
                    recv_sem=arrived.at[slot, part],
                    device_id={"dp": self.me + step},
                    device_id_type=MESH,
                )
            )
        return copies

    def sends(self, way, round_id):
        if way == 0:
            return (self.me >= round_id) & self.has_above
        return (self.me + round_id < self.shards) & self.has_below

    def push(self, round_id, own, spread, send_sem, arrived, source=None):
        source = own if round_id == 0 else (source or spread)
        for way in range(2):

            @pl.when(self.sends(way, round_id))
            def _():
                for copy in self.hop(way, round_id, source, spread, send_sem, arrived):
                    copy.start()

    def drain(self, round_id, own, spread, send_sem, arrived, source=None):
        source = own if round_id == 0 else (source or spread)
        for way in range(2):

            @pl.when(self.sends(way, round_id))
            def _():
                for copy in self.hop(way, round_id, source, spread, send_sem, arrived):
                    copy.wait_send()

    def receive(self, round_id, spread, arrived):
        far = round_id + 1

        @pl.when(self.me >= far)
        def _():
            self.wait_slot(self.me - far, spread, arrived)

        @pl.when(self.me + far < self.shards)
        def _():
            self.wait_slot(self.me + far, spread, arrived)

    def wait_slot(self, slot, spread, arrived):
        for part in range(2):
            view = spread[part].at[slot]
            pltpu.make_async_copy(view, view, arrived.at[slot, part]).wait()


def route_kernel(cap_pad, cols_ref, rows_ref, limit_ref, slot_rows_ref, slot_cols_ref):
    for b in range(cols_ref.shape[0]):
        limit = limit_ref[b]
        col = [cols_ref[b, :, k : k + 1] for k in range(4)]
        row = [rows_ref[b, k : k + 1, :] for k in range(4)]
        slot_rows_ref[b] = jnp.full(slot_rows_ref.shape[1:], -1, jnp.int32)
        slot_cols_ref[b] = jnp.full(slot_cols_ref.shape[1:], -1, jnp.int32)
        for j in range(2):
            rank_row = 0
            rank_col = 0
            for k in range(2):
                hit = (col[k] == row[j]) & (col[2 + k] < row[2 + j])
                rank_row = rank_row + jnp.sum(hit.astype(jnp.int32), axis=0, keepdims=True)
                hit = (row[k] == col[j]) & (row[2 + k] < col[2 + j])
                rank_col = rank_col + jnp.sum(hit.astype(jnp.int32), axis=1, keepdims=True)
            keep_row = (rank_row < limit) & (row[j] >= 0)
            keep_col = (rank_col < limit) & (col[j] >= 0)
            slot_rows_ref[b, j : j + 1, :] = jnp.where(keep_row, row[j] * cap_pad + rank_row, -1)
            slot_cols_ref[b, :, j : j + 1] = jnp.where(keep_col, col[j] * cap_pad + rank_col, -1)


def run_route(cols, rows, limits, cap_pad):
    batches = cols.shape[0]
    return pl.pallas_call(
        functools.partial(route_kernel, cap_pad),
        out_shape=(
            jax.ShapeDtypeStruct((batches, 8, SEQ_PAD), jnp.int32),
            jax.ShapeDtypeStruct((batches, SEQ_PAD, 8), jnp.int32),
        ),
        in_specs=[
            pl.BlockSpec(memory_space=pltpu.VMEM),
            pl.BlockSpec(memory_space=pltpu.VMEM),
            pl.BlockSpec(memory_space=pltpu.SMEM),
        ],
        out_specs=(
            pl.BlockSpec(memory_space=pltpu.VMEM),
            pl.BlockSpec(memory_space=pltpu.VMEM),
        ),
        compiler_params=pltpu.CompilerParams(vmem_limit_bytes=VMEM_LIMIT),
        cost_estimate=pl.CostEstimate(flops=4000000, bytes_accessed=1000000, transcendentals=0),
        name="route",
    )(cols, rows, limits)


def norm_stats(values):
    average = jnp.mean(values, axis=-1, keepdims=True)
    centered = values - average
    spread = jnp.mean(centered * centered, axis=-1, keepdims=True)
    inverse = lax.rsqrt(spread + EPS)
    return centered * inverse, inverse


def front_kernel(
    experts,
    shards,
    x_ref,
    grad_ref,
    weight_ref,
    cols_ref,
    slot_rows_ref,
    own_in_ref,
    own_out_ref,
    received_ref,
    qkv_ref,
    mixed_ref,
    lse_ref,
    hidden_ref,
    one_ref,
    two_ref,
    probs_ref,
    spread_in_ref,
    spread_out_ref,
    small_ref,
    send_ref,
    send_sem,
    arrived,
    rows_send,
    rows_recv,
):
    index = pl.program_id(0)
    me = lax.axis_index("expert")
    groups = received_ref.shape[0]
    width = x_ref.shape[-1]
    rows = x_ref.shape[1]
    line = Line(shards)
    own = (own_in_ref, own_out_ref)
    spread = (spread_in_ref, spread_out_ref)

    @pl.when(pl.program_id(0) == 0)
    def _():
        line.greet(me, groups)
        small_ref[...] = weight_ref[:, 4 * width :].astype(F32).T
        line.push(0, own, spread, send_sem, arrived)

    x = x_ref[0]
    hat, _ = norm_stats(x)
    one = (hat * small_ref[0:1, :] + small_ref[1:2, :]).astype(BF)
    one_ref[0] = one
    qkv_ref[0] = dot(one, weight_ref[:, : 3 * width]).astype(BF)
    lane = lax.broadcasted_iota(jnp.int32, (1, 128), 1)
    key_ok = lax.broadcasted_iota(jnp.int32, (1, rows), 1) < SEQ
    lse = jnp.zeros((rows, 128), F32)
    scale = HEAD ** (-0.5)
    for pair in range(HEADS // 2):
        low = pair * 128
        query = qkv_ref[0, :, low : low + 128]
        keys = qkv_ref[0, :, width + low : width + low + 128]
        values = qkv_ref[0, :, 2 * width + low : 2 * width + low + 128]
        total = None
        for side in range(2):
            mine = (lane // HEAD) == side
            scores = dot_nt(jnp.where(mine, query, jnp.zeros_like(query)), keys) * scale
            scores = jnp.where(key_ok, scores, NEG)
            highest = jnp.max(scores, axis=-1, keepdims=True)
            expo = jnp.exp(scores - highest)
            denom = jnp.sum(expo, axis=-1, keepdims=True)
            weights = (expo / denom).astype(BF)
            lse = jnp.where(lane == 2 * pair + side, highest + jnp.log(denom), lse)
            part = dot(weights, jnp.where(mine, values, jnp.zeros_like(values)))
            total = part if total is None else total + part
        mixed_ref[0, :, low : low + 128] = total.astype(BF)
    lse_ref[0] = lse
    hidden = x + dot(mixed_ref[0], weight_ref[:, 3 * width : 4 * width])
    hidden_ref[0] = hidden
    hat, _ = norm_stats(hidden)
    two = (hat * small_ref[2:3, :] + small_ref[3:4, :]).astype(BF)
    two_ref[0] = two
    logits = dot(two, weight_ref[:, 4 * width :])
    in_router = (lane >= 4) & (lane < 4 + experts)
    logits = jnp.where(in_router, logits, NEG)
    expo = jnp.exp(logits - jnp.max(logits, axis=-1, keepdims=True))
    probs = expo / jnp.sum(expo, axis=-1, keepdims=True)
    probs_ref[0] = probs
    out_grad = grad_ref[0]
    cap_pad = send_ref.shape[3]
    slot = lax.broadcasted_iota(jnp.int32, (groups * cap_pad, 1), 0)
    both = None
    grads = None
    for j in range(2):
        gate = jnp.sum(
            jnp.where(lane - 4 == cols_ref[0, :, j : j + 1], probs, 0.0), axis=-1, keepdims=True
        )
        pick = (slot == slot_rows_ref[0, j : j + 1, :]).astype(F32)
        both = pick if both is None else both + pick
        part = dot(pick.astype(BF), (gate * out_grad).astype(BF))
        grads = part if grads is None else grads + part
    sent = dot(both.astype(BF), two).astype(BF)
    send_ref[index, :, 0] = sent.reshape(groups, cap_pad, width)
    send_ref[index, :, 1] = grads.astype(BF).reshape(groups, cap_pad, width)

    def rows_copy(image, target):
        return pltpu.make_async_remote_copy(
            src_ref=send_ref.at[image, target],
            dst_ref=received_ref.at[me, image],
            send_sem=rows_send.at[image, target],
            recv_sem=rows_recv.at[me, image],
            device_id={"expert": target},
            device_id_type=MESH,
        )

    for k in range(1, groups):
        rows_copy(index, lax.rem(me + k, groups)).start()
    pltpu.make_async_copy(
        send_ref.at[index, me], received_ref.at[me, index], rows_recv.at[me, index]
    ).start()

    @pl.when(index == pl.num_programs(0) - 1)
    def _():
        rounds = min(EARLY, shards - 1)
        for round_id in range(1, rounds):
            line.receive(round_id - 1, spread, arrived)
            line.push(round_id, own, spread, send_sem, arrived)

        def finish(image, carry):
            for k in range(groups):
                source = lax.rem(me + k, groups)
                if k:
                    rows_copy(image, source).wait_send()
                view = received_ref.at[source, image]
                pltpu.make_async_copy(view, view, rows_recv.at[source, image]).wait()
            return carry

        lax.fori_loop(0, send_ref.shape[0], finish, 0)
        line.receive(rounds - 1, spread, arrived)
        for round_id in range(rounds):
            line.drain(round_id, own, spread, send_sem, arrived)


def run_front(x, grad, weight, cols, slot_rows, own_in, own_out, experts, cap_pad):
    batches, rows, width = x.shape
    shards = lax.axis_size("dp")
    total = weight.shape[1]

    def block(*shape):
        return pl.BlockSpec((1,) + shape, lambda i: (i,) + (0,) * len(shape))

    def out(shape, dtype):
        return jax.ShapeDtypeStruct((batches,) + shape, dtype)

    return pl.pallas_call(
        functools.partial(front_kernel, experts, shards),
        grid=(batches,),
        out_shape=(
            jax.ShapeDtypeStruct((experts, batches, 2, cap_pad, width), BF),
            out((rows, 3 * width), BF),
            out((rows, width), BF),
            out((rows, 128), F32),
            out((rows, width), F32),
            out((rows, width), BF),
            out((rows, width), BF),
            out((rows, SMALL), F32),
            jax.ShapeDtypeStruct((shards,) + own_in.shape, BF),
            jax.ShapeDtypeStruct((shards,) + own_out.shape, BF),
        ),
        in_specs=[
            block(rows, width),
            block(rows, width),
            pl.BlockSpec((width, total), lambda i: (0, 0), pipeline_mode=pl.Buffered(1)),
            block(rows, 4),
            block(8, rows),
            pl.BlockSpec(memory_space=pl.ANY),
            pl.BlockSpec(memory_space=pl.ANY),
        ],
        out_specs=(
            pl.BlockSpec(memory_space=pl.ANY),
            block(rows, 3 * width),
            block(rows, width),
            block(rows, 128),
            block(rows, width),
            block(rows, width),
            block(rows, width),
            block(rows, SMALL),
            pl.BlockSpec(memory_space=pl.ANY),
            pl.BlockSpec(memory_space=pl.ANY),
        ),
        scratch_shapes=[
            pltpu.VMEM((SMALL, width), F32),
            pltpu.VMEM((batches, experts, 2, cap_pad, width), BF),
            pltpu.SemaphoreType.DMA((2, EARLY, 2)),
            pltpu.SemaphoreType.DMA((shards, 2)),
            pltpu.SemaphoreType.DMA((batches, experts)),
            pltpu.SemaphoreType.DMA((experts, batches)),
        ],
        compiler_params=pltpu.CompilerParams(
            dimension_semantics=("arbitrary",),
            vmem_limit_bytes=VMEM_LIMIT,
            collective_id=1,
            has_side_effects=True,
        ),
        cost_estimate=pl.CostEstimate(
            flops=8000000000, bytes_accessed=40000000, transcendentals=3000000
        ),
        name="front",
    )(x, grad, weight, cols, slot_rows, own_in, own_out)


def pieces_of(tall, span):
    half = ceil_to(tall // 2, 16)
    mid = ceil_to(span // 2, 16)
    return ((0, 0, half), (0, half, tall - half), (1, 0, mid), (1, mid, span - mid))


def moe_kernel(
    shards,
    groups,
    x_hbm,
    own_in_ref,
    own_out_ref,
    spread_in_ref,
    spread_out_ref,
    back_ref,
    sum_in_ref,
    sum_out_ref,
    rows_ref,
    win_ref,
    wout_ref,
    y_acc,
    dx_acc,
    gin_acc,
    gout_acc,
    part_in_ref,
    part_out_ref,
    land_in_ref,
    land_out_ref,
    rows_sem,
    weight_send,
    arrived,
    sum_send,
    sum_recv,
    back_send,
    back_recv,
    final_sem,
):
    line = Line(shards)
    z = line.me
    me = lax.axis_index("expert")
    _, batches, _, cap_pad, width = rows_ref.shape
    tall, span = own_in_ref.shape
    group = max(1, 512 // (batches * cap_pad))
    while groups % group:
        group -= 1
    blocks = groups // group
    rows = group * batches * cap_pad
    early = min(EARLY, shards - 1)
    spread = (win_ref, wout_ref)
    early_spread = (spread_in_ref, spread_out_ref)
    own = (own_in_ref, own_out_ref)
    parts = (part_in_ref, part_out_ref)
    lands = (land_in_ref, land_out_ref)
    pieces = pieces_of(tall, span)

    for k in range(groups):
        source = lax.rem(me + k, groups)
        pltpu.make_async_copy(x_hbm.at[source], rows_ref.at[source], rows_sem.at[source]).start()
    for part in range(2):
        pltpu.make_async_copy(own[part], spread[part].at[z], arrived.at[z, part]).start()
    for far in range(1, early + 1):
        for sign in (-1, 1):
            slot = z + sign * far

            @pl.when((slot >= 0) & (slot < shards))
            def _():
                for part in range(2):
                    pltpu.make_async_copy(
                        early_spread[part].at[slot], spread[part].at[slot], arrived.at[slot, part]
                    ).start()

    line.greet(me, groups)
    if early < shards - 1:
        line.push(early, own, spread, weight_send, arrived, early_spread)

    table = []
    for at in range(shards):
        near = sorted(range(shards), key=lambda q: (abs(q - at), q))
        table.append(near[1:] + near[:1])

    def quarter(step):
        total = 0
        for at in range(shards):
            for s in range(shards):
                hit = jnp.where((z == at) & (step == s), table[at][s], 0)
                total = total + hit
        return total

    def sum_copy(way, q, piece):
        kind, low, size = pieces[piece]
        if way == 0:
            slot = q
            peer = z + 1
        else:
            slot = jnp.where(q == z - 1, shards, q)
            peer = z - 1
        cut = pl.ds(low, size)
        return pltpu.make_async_remote_copy(
            src_ref=parts[kind].at[q, cut],
            dst_ref=lands[kind].at[slot, cut],
            send_sem=sum_send.at[way, q, piece],
            recv_sem=sum_recv.at[slot, piece],
            device_id={"dp": peer},
            device_id_type=MESH,
        )

    def take_sum(slot, q, piece):
        kind, low, size = pieces[piece]
        cut = pl.ds(low, size)
        view = lands[kind].at[slot, cut]
        pltpu.make_async_copy(view, view, sum_recv.at[slot, piece]).wait()
        parts[kind][q, cut] = (
            parts[kind][q, cut].astype(F32) + lands[kind][slot, cut].astype(F32)
        ).astype(BF)

    def back_copy(source):
        return pltpu.make_async_remote_copy(
            src_ref=rows_ref.at[source],
            dst_ref=back_ref.at[me],
            send_sem=back_send.at[source],
            recv_sem=back_recv.at[me],
            device_id={"expert": source},
            device_id_type=MESH,
        )

    def back_start(first):
        for k in range(group):
            source = first + k

            @pl.when(source != me)
            def _():
                back_copy(source).start()

            @pl.when(source == me)
            def _():
                pltpu.make_async_copy(
                    rows_ref.at[source], back_ref.at[source], back_recv.at[source]
                ).start()

    def block_first(block):
        return lax.rem(me // group + 1 + block, blocks) * group

    def do_step(step, carry):
        q = quarter(step)
        line.wait_slot(q, spread, arrived)
        for round_id in range(early, shards - 2):
            for way in range(2):
                forward = 1 - 2 * way

                @pl.when((q == z - forward * (round_id + 1)) & line.sends(way, round_id + 1))
                def _():
                    for copy in line.hop(way, round_id + 1, spread, spread, weight_send, arrived):
                        copy.start()

        def do_block(block, inner):
            lead = block_first(block)
            low = pl.multiple_of(lead * (batches * cap_pad), rows)
            here = pl.ds(low, rows)
            mine = pl.ds(lead, group)

            @pl.when(step == 0)
            def _():
                for k in range(group):
                    view = rows_ref.at[lead + k]
                    pltpu.make_async_copy(view, view, rows_sem.at[lead + k]).wait()

            x = rows_ref[mine, :, 0].reshape(rows, width)
            grad = rows_ref[mine, :, 1].reshape(rows, width)
            win = win_ref[q, :width, :]
            wout = wout_ref[q]
            pre = dot(x, win) + win_ref[q, width : width + 1, :].astype(F32)
            cdf = 0.5 * lax.erf(pre * (0.5**0.5)) + 0.5
            active = (pre * cdf).astype(BF)
            slope = cdf + pre * (jnp.exp(-0.5 * pre * pre) * 0.3989422804014327)
            d_pre = (dot_nt(grad, wout) * slope).astype(BF)
            y_part = dot(active, wout)
            dx_part = dot_nt(d_pre, win)

            @pl.when(step == 0)
            def _():
                y_acc[here, :] = y_part
                dx_acc[here, :] = dx_part

            @pl.when(step > 0)
            def _():
                y_acc[here, :] += y_part
                dx_acc[here, :] += dx_part

            gout = dot_tn(active, grad)
            gin = dot_tn(x, d_pre)
            gbias = jnp.sum(d_pre.astype(F32), axis=0, keepdims=True)

            @pl.when(block == 0)
            def _():
                gout_acc[...] = gout
                gin_acc[:width, :] = gin
                gin_acc[width : width + 1, :] = gbias

            @pl.when(block > 0)
            def _():
                gout_acc[...] += gout
                gin_acc[:width, :] += gin
                gin_acc[width : width + 1, :] += gbias

            @pl.when(step == shards - 1)
            def _():
                shape = (group, batches, cap_pad, width)
                rows_ref[mine, :, 0] = y_acc[here, :].astype(BF).reshape(shape)
                rows_ref[mine, :, 1] = dx_acc[here, :].astype(BF).reshape(shape)

                @pl.when(block > 0)
                def _():
                    back_start(block_first(block - 1))

            return inner

        lax.fori_loop(0, blocks, do_block, 0)

        @pl.when(step == shards - 1)
        def _():
            back_start(block_first(blocks - 1))

        part_in_ref[q, :width, :] = gin_acc[:width, :].astype(BF)
        part_in_ref[q, width:, :] = jnp.broadcast_to(
            gin_acc[width : width + 1, :].astype(BF), (tall - width, span)
        )
        part_out_ref[q] = gout_acc[...].astype(BF)

        @pl.when((z == 0) & (q > z))
        def _():
            for piece in range(len(pieces)):
                sum_copy(0, q, piece).start()

        @pl.when((z == shards - 1) & (q < z))
        def _():
            for piece in range(len(pieces)):
                sum_copy(1, q, piece).start()

        return carry

    lax.fori_loop(0, shards, do_step, 0)

    def do_forward(turn, carry):
        up = turn
        down = shards - 1 - turn
        for piece in range(len(pieces)):

            @pl.when((up > z) & (z > 0))
            def _():
                take_sum(up, up, piece)
                sum_copy(0, up, piece).start()

            @pl.when((down < z) & (z < shards - 1))
            def _():
                take_sum(down, down, piece)
                sum_copy(1, down, piece).start()

        return carry

    lax.fori_loop(1, shards, do_forward, 0)
    for piece in range(len(pieces)):

        @pl.when(line.has_below)
        def _():
            take_sum(z, z, piece)

        @pl.when(line.has_above)
        def _():
            take_sum(shards, z, piece)

    finals = [
        pltpu.make_async_copy(part_in_ref.at[z], sum_in_ref, final_sem.at[0]),
        pltpu.make_async_copy(part_out_ref.at[z], sum_out_ref, final_sem.at[1]),
    ]
    for copy in finals:
        copy.start()

    def finish_sum(q, carry):
        @pl.when((q > z) & line.has_above)
        def _():
            for piece in range(len(pieces)):
                sum_copy(0, q, piece).wait_send()

        @pl.when((q < z) & line.has_below)
        def _():
            for piece in range(len(pieces)):
                sum_copy(1, q, piece).wait_send()

        return carry

    lax.fori_loop(0, shards, finish_sum, 0)
    for round_id in range(early, shards - 1):
        line.drain(round_id, own, spread, weight_send, arrived)
    for k in range(groups):
        source = lax.rem(me + k, groups)
        if k:
            back_copy(source).wait_send()
        view = back_ref.at[source]
        pltpu.make_async_copy(view, view, back_recv.at[source]).wait()
    for copy in finals:
        copy.wait()


def run_moe(received, own_in, own_out, spread_in, spread_out):
    groups, batches, _, cap_pad, width = received.shape
    shards, tall, span = spread_in.shape
    total = groups * batches * cap_pad
    count = len(pieces_of(tall, span))
    anywhere = pl.BlockSpec(memory_space=pl.ANY)
    return pl.pallas_call(
        functools.partial(moe_kernel, shards, groups),
        out_shape=(
            jax.ShapeDtypeStruct(received.shape, BF),
            jax.ShapeDtypeStruct((tall, span), BF),
            jax.ShapeDtypeStruct((span, width), BF),
        ),
        in_specs=[anywhere] * 5,
        out_specs=(anywhere,) * 3,
        scratch_shapes=[
            pltpu.VMEM(received.shape, BF),
            pltpu.VMEM((shards, tall, span), BF),
            pltpu.VMEM((shards, span, width), BF),
            pltpu.VMEM((total, width), F32),
            pltpu.VMEM((total, width), F32),
            pltpu.VMEM((ceil_to(width + 1, 8), span), F32),
            pltpu.VMEM((span, width), F32),
            pltpu.VMEM((shards, tall, span), BF),
            pltpu.VMEM((shards, span, width), BF),
            pltpu.VMEM((shards + 1, tall, span), BF),
            pltpu.VMEM((shards + 1, span, width), BF),
            pltpu.SemaphoreType.DMA((groups,)),
            pltpu.SemaphoreType.DMA((2, shards, 2)),
            pltpu.SemaphoreType.DMA((shards, 2)),
            pltpu.SemaphoreType.DMA((2, shards, count)),
            pltpu.SemaphoreType.DMA((shards + 1, count)),
            pltpu.SemaphoreType.DMA((groups,)),
            pltpu.SemaphoreType.DMA((groups,)),
            pltpu.SemaphoreType.DMA((2,)),
        ],
        compiler_params=pltpu.CompilerParams(
            vmem_limit_bytes=VMEM_MAX, collective_id=2, has_side_effects=True
        ),
        cost_estimate=pl.CostEstimate(
            flops=12 * total * width * span * shards,
            bytes_accessed=60000000,
            transcendentals=2 * total * span * shards,
        ),
        name="moe",
    )(received, own_in, own_out, spread_in, spread_out)


def tail_kernel(
    experts,
    x_ref,
    grad_ref,
    weight_ref,
    cols_ref,
    slot_cols_ref,
    back_ref,
    qkv_ref,
    mixed_ref,
    lse_ref,
    hidden_ref,
    one_ref,
    two_ref,
    probs_ref,
    out_ref,
    dx_ref,
    dense_ref,
    small_ref,
    sums_ref,
    d_qkv_ref,
    d_branch_ref,
    d_logits_ref,
    one_all,
    two_all,
    mixed_all,
):
    width = x_ref.shape[-1]
    rows = x_ref.shape[1]
    index = pl.program_id(0)

    @pl.when(index == 0)
    def _():
        small_ref[...] = weight_ref[:, 4 * width :].astype(F32).T
        sums_ref[...] = jnp.zeros_like(sums_ref)

    here = pl.ds(pl.multiple_of(index * rows, rows), rows)
    one_all[here, :] = one_ref[0]
    two_all[here, :] = two_ref[0]
    mixed_all[here, :] = mixed_ref[0]
    out_grad = grad_ref[0]
    hidden = hidden_ref[0]
    probs = probs_ref[0]
    lane = lax.broadcasted_iota(jnp.int32, (1, 128), 1)
    slots = back_ref.shape[0] * back_ref.shape[3]
    slot = lax.broadcasted_iota(jnp.int32, (1, slots), 1)
    answers = back_ref[:, 0, 0].reshape(slots, width)
    answer_grads = back_ref[:, 0, 1].reshape(slots, width)
    result = hidden
    d_probs = jnp.zeros_like(probs)
    both = None
    for j in range(2):
        pick = (slot == slot_cols_ref[0, :, j : j + 1]).astype(F32)
        both = pick if both is None else both + pick
        chosen = lane - 4 == cols_ref[0, :, j : j + 1]
        gate = jnp.sum(jnp.where(chosen, probs, 0.0), axis=-1, keepdims=True)
        picked = dot(pick.astype(BF), answers)
        result = result + gate * picked
        d_gate = jnp.sum(picked * out_grad, axis=-1, keepdims=True)
        d_probs = jnp.where(chosen, d_gate, d_probs)
    out_ref[0] = result
    d_logits = probs * (d_probs - jnp.sum(d_probs * probs, axis=-1, keepdims=True))
    d_logits = d_logits.astype(BF)
    d_logits_ref[here, :] = d_logits
    d_two = dot(both.astype(BF), answer_grads) + dot_nt(d_logits, weight_ref[:, 4 * width :])
    hat, inverse = norm_stats(hidden)
    sums_ref[2:3, :] += jnp.sum(d_two * hat, axis=0, keepdims=True)
    sums_ref[3:4, :] += jnp.sum(d_two, axis=0, keepdims=True)
    d_hat = d_two * small_ref[2:3, :]
    d_hidden = out_grad + inverse * (
        d_hat
        - jnp.mean(d_hat, axis=-1, keepdims=True)
        - hat * jnp.mean(d_hat * hat, axis=-1, keepdims=True)
    )
    d_branch = d_hidden.astype(BF)
    d_branch_ref[here, :] = d_branch
    d_mixed_all = dot_nt(d_branch, weight_ref[:, 3 * width : 4 * width]).astype(BF)
    key_ok = lax.broadcasted_iota(jnp.int32, (1, rows), 1) < SEQ
    scale = HEAD ** (-0.5)
    for pair in range(HEADS // 2):
        low = pair * 128
        query = qkv_ref[0, :, low : low + 128]
        keys = qkv_ref[0, :, width + low : width + low + 128]
        values = qkv_ref[0, :, 2 * width + low : 2 * width + low + 128]
        d_mixed = d_mixed_all[:, low : low + 128]
        d_query = d_keys = d_values = None
        for side in range(2):
            mine = (lane // HEAD) == side
            head = 2 * pair + side

            def own(array):
                return jnp.where(mine, array, jnp.zeros_like(array))

            my_query = own(query)
            my_keys = own(keys)
            my_d_mixed = own(d_mixed)
            scores = dot_nt(my_query, keys) * scale
            scores = jnp.where(key_ok, scores, NEG)
            probs_h = jnp.exp(scores - lse_ref[0, :, head : head + 1])
            d_weights = dot_nt(my_d_mixed, values)
            row_terms = jnp.sum(d_weights * probs_h, axis=-1, keepdims=True)
            d_scores = (probs_h * (d_weights - row_terms) * scale).astype(BF)
            parts = (
                dot(d_scores, my_keys),
                dot_tn(d_scores, my_query),
                dot_tn(probs_h.astype(BF), my_d_mixed),
            )
            if side == 0:
                d_query, d_keys, d_values = parts
            else:
                d_query, d_keys, d_values = (
                    d_query + parts[0],
                    d_keys + parts[1],
                    d_values + parts[2],
                )
        d_qkv_ref[here, low : low + 128] = d_query.astype(BF)
        d_qkv_ref[here, width + low : width + low + 128] = d_keys.astype(BF)
        d_qkv_ref[here, 2 * width + low : 2 * width + low + 128] = d_values.astype(BF)
    d_one = dot_nt(d_qkv_ref[here, :], weight_ref[:, : 3 * width])
    hat, inverse = norm_stats(x_ref[0])
    sums_ref[0:1, :] += jnp.sum(d_one * hat, axis=0, keepdims=True)
    sums_ref[1:2, :] += jnp.sum(d_one, axis=0, keepdims=True)
    d_hat = d_one * small_ref[0:1, :]
    dx_ref[0] = d_hidden + inverse * (
        d_hat
        - jnp.mean(d_hat, axis=-1, keepdims=True)
        - hat * jnp.mean(d_hat * hat, axis=-1, keepdims=True)
    )

    @pl.when(index == pl.num_programs(0) - 1)
    def _():
        dense_ref[:, 4 * width :] = (dot_tn(two_all[...], d_logits_ref[...]) + sums_ref[...].T).astype(BF)
        dense_ref[:, 3 * width : 4 * width] = dot_tn(mixed_all[...], d_branch_ref[...]).astype(BF)
        for part in range(3):
            cut = slice(part * width, (part + 1) * width)
            dense_ref[:, cut] = dot_tn(one_all[...], d_qkv_ref[:, cut]).astype(BF)


def run_tail(x, grad, weight, cols, slot_cols, back, saved, experts):
    batches, rows, width = x.shape
    total = weight.shape[1]
    cap_pad = back.shape[3]
    qkv, mixed, lse, hidden, one, two, probs = saved

    def block(*shape):
        return pl.BlockSpec((1,) + shape, lambda i: (i,) + (0,) * len(shape))

    return pl.pallas_call(
        functools.partial(tail_kernel, experts),
        grid=(batches,),
        out_shape=(
            jax.ShapeDtypeStruct(x.shape, F32),
            jax.ShapeDtypeStruct(x.shape, F32),
            jax.ShapeDtypeStruct((width, total), BF),
        ),
        in_specs=[
            block(rows, width),
            block(rows, width),
            pl.BlockSpec((width, total), lambda i: (0, 0), pipeline_mode=pl.Buffered(1)),
            block(rows, 4),
            block(rows, 8),
            pl.BlockSpec((experts, 1, 2, cap_pad, width), lambda i: (0, i, 0, 0, 0)),
            block(rows, 3 * width),
            block(rows, width),
            block(rows, 128),
            block(rows, width),
            block(rows, width),
            block(rows, width),
            block(rows, SMALL),
        ],
        out_specs=(
            block(rows, width),
            block(rows, width),
            pl.BlockSpec((width, total), lambda i: (0, 0), pipeline_mode=pl.Buffered(1)),
        ),
        scratch_shapes=[
            pltpu.VMEM((SMALL, width), F32),
            pltpu.VMEM((SMALL, width), F32),
            pltpu.VMEM((batches * rows, 3 * width), BF),
            pltpu.VMEM((batches * rows, width), BF),
            pltpu.VMEM((batches * rows, SMALL), BF),
            pltpu.VMEM((batches * rows, width), BF),
            pltpu.VMEM((batches * rows, width), BF),
            pltpu.VMEM((batches * rows, width), BF),
        ],
        compiler_params=params(),
        cost_estimate=pl.CostEstimate(
            flops=16000000000, bytes_accessed=50000000, transcendentals=2000000
        ),
        name="tail",
    )(x, grad, weight, cols, slot_cols, back, qkv, mixed, lse, hidden, one, two, probs)


def per_device(
    inputs,
    gain_one,
    shift_one,
    qkv_weight,
    proj_weight,
    gain_two,
    shift_two,
    router_weight,
    expert_in,
    expert_bias,
    expert_out,
    out_grad,
    routes,
    priority,
    capacity,
):
    batches = priority.shape[0]
    count = inputs.shape[0] // batches
    width = inputs.shape[1]
    experts = router_weight.shape[1]
    groups = lax.axis_size("expert")
    cap_pad = ceil_to(max(2, (5 * count + 2 * experts - 1) // (2 * experts)), 16)
    depth = qkv_weight.shape[0]
    both = ("dp", "expert")

    vectors = jnp.stack([gain_one, shift_one, gain_two, shift_two], axis=1)
    small = jnp.concatenate([vectors, router_weight], axis=1)
    small = jnp.pad(small, ((0, 0), (0, SMALL - small.shape[1])))
    pack = jnp.concatenate([qkv_weight, proj_weight, small], axis=1)
    slice_rows = depth // groups
    mine = lax.axis_index("expert")
    pack = lax.dynamic_slice_in_dim(pack, mine * slice_rows, slice_rows, axis=0)
    weight = lax.all_gather(pack, both, axis=0, tiled=True)

    bias_rows = jnp.pad(expert_bias, ((0, BIAS_ROWS - 1), (0, 0)))
    own_in = jnp.concatenate([expert_in[0], bias_rows], axis=0)
    own_out = expert_out[0]

    extra = SEQ_PAD - SEQ
    x = jnp.pad(inputs.reshape(batches, SEQ, width), ((0, 0), (0, extra), (0, 0)))
    grad = jnp.pad(out_grad.reshape(batches, SEQ, width), ((0, 0), (0, extra), (0, 0)))
    cols = jnp.concatenate(
        [routes.reshape(batches, SEQ, 2), priority.reshape(batches, SEQ, 2)], axis=2
    )
    cols = jnp.pad(cols, ((0, 0), (0, extra), (0, 0)), constant_values=-1)
    rows = jnp.swapaxes(cols, 1, 2)
    slot_rows, slot_cols = run_route(cols, rows, capacity, cap_pad)
    received, *saved, spread_in, spread_out = run_front(
        x, grad, weight, cols, slot_rows, own_in, own_out, experts, cap_pad
    )
    back, grad_in, grad_out = run_moe(received, own_in, own_out, spread_in, spread_out)
    outputs, inputs_grad, dense = run_tail(
        x, grad, weight, cols, slot_cols, back, saved, experts
    )
    dense = lax.psum_scatter(dense, both, scatter_dimension=0, tiled=True)
    dense = lax.all_gather(dense, "expert", axis=0, tiled=True).astype(F32)
    grad_in = grad_in.astype(F32)
    grad_out = grad_out.astype(F32)
    spot = 4 * width
    return (
        outputs[:, :SEQ].reshape(batches * SEQ, width),
        inputs_grad[:, :SEQ].reshape(batches * SEQ, width),
        dense[:, spot],
        dense[:, spot + 1],
        dense[:, : 3 * width],
        dense[:, 3 * width : spot],
        dense[:, spot + 2],
        dense[:, spot + 3],
        dense[:, spot + 4 : spot + 4 + experts],
        grad_in[None, :width],
        grad_in[None, width],
        grad_out[None],
    )


def solution(mesh):
    token = P(("dp", "expert"), None)
    vector = P("dp")
    matrix = P("dp", None)
    return jax.shard_map(
        per_device,
        mesh=mesh,
        in_specs=(
            token,
            vector,
            vector,
            matrix,
            matrix,
            vector,
            vector,
            matrix,
            P("expert", None, "dp"),
            P("expert", "dp"),
            P("expert", "dp", None),
            token,
            token,
            token,
            P(("dp", "expert")),
        ),
        out_specs=(
            token,
            token,
            vector,
            vector,
            matrix,
            matrix,
            vector,
            vector,
            matrix,
            P("expert", None, "dp"),
            P("expert", "dp"),
            P("expert", "dp", None),
        ),
        check_vma=False,
    )
```

```python
import functools

import jax
import jax.numpy as jnp
from jax import lax
from jax.experimental import pallas as pl
from jax.experimental.pallas import tpu as pltpu
from jax.sharding import PartitionSpec as P

HEADS = 12
HEAD = 64
SEQ = 197
SEQ_PAD = 208
EPS = 1e-06
BF = jnp.bfloat16
F32 = jnp.float32
SMALL = 128
MESH = pl.DeviceIdType.MESH
EARLY = 2
BIAS_ROWS = 16
NEG = -1e30
VMEM_LIMIT = 60 * 1024 * 1024
VMEM_MAX = 67043328


def ceil_to(value, step):
    return (value + step - 1) // step * step


def dot(a, b):
    return jnp.dot(a, b, preferred_element_type=F32)


def dot_nt(a, b):
    return lax.dot_general(a, b, (((1,), (1,)), ((), ())), preferred_element_type=F32)


def dot_tn(a, b):
    return lax.dot_general(a, b, (((0,), (0,)), ((), ())), preferred_element_type=F32)


def params(count=1):
    return pltpu.CompilerParams(
        dimension_semantics=("arbitrary",) * count, vmem_limit_bytes=VMEM_LIMIT
    )


class Line:
    def __init__(self, shards):
        self.shards = shards
        self.me = lax.axis_index("dp")
        self.has_below = self.me > 0
        self.has_above = self.me < shards - 1

    def greet(self, me, groups):
        barrier = pltpu.get_barrier_semaphore()
        for k in range(1, groups):
            pl.semaphore_signal(
                barrier, inc=1, device_id={"expert": lax.rem(me + k, groups)}, device_id_type=MESH
            )

        @pl.when(self.has_below)
        def _():
            pl.semaphore_signal(barrier, inc=1, device_id={"dp": self.me - 1}, device_id_type=MESH)

        @pl.when(self.has_above)
        def _():
            pl.semaphore_signal(barrier, inc=1, device_id={"dp": self.me + 1}, device_id_type=MESH)

        ends = self.has_below.astype(jnp.int32) + self.has_above.astype(jnp.int32)
        pl.semaphore_wait(barrier, groups - 1 + ends)

    def hop(self, way, round_id, source, target, send_sem, arrived):
        step = 1 - 2 * way
        slot = self.me - step * round_id
        copies = []
        for part in range(2):
            origin = source[part] if round_id == 0 else source[part].at[slot]
            copies.append(
                pltpu.make_async_remote_copy(
                    src_ref=origin,
                    dst_ref=target[part].at[slot],
                    send_sem=send_sem.at[way, round_id, part],
                    recv_sem=arrived.at[slot, part],
                    device_id={"dp": self.me + step},
                    device_id_type=MESH,
                )
            )
        return copies

    def sends(self, way, round_id):
        if way == 0:
            return (self.me >= round_id) & self.has_above
        return (self.me + round_id < self.shards) & self.has_below

    def push(self, round_id, own, spread, send_sem, arrived, source=None):
        source = own if round_id == 0 else (source or spread)
        for way in range(2):

            @pl.when(self.sends(way, round_id))
            def _():
                for copy in self.hop(way, round_id, source, spread, send_sem, arrived):
                    copy.start()

    def drain(self, round_id, own, spread, send_sem, arrived, source=None):
        source = own if round_id == 0 else (source or spread)
        for way in range(2):

            @pl.when(self.sends(way, round_id))
            def _():
                for copy in self.hop(way, round_id, source, spread, send_sem, arrived):
                    copy.wait_send()

    def receive(self, round_id, spread, arrived):
        far = round_id + 1

        @pl.when(self.me >= far)
        def _():
            self.wait_slot(self.me - far, spread, arrived)

        @pl.when(self.me + far < self.shards)
        def _():
            self.wait_slot(self.me + far, spread, arrived)

    def wait_slot(self, slot, spread, arrived):
        for part in range(2):
            view = spread[part].at[slot]
            pltpu.make_async_copy(view, view, arrived.at[slot, part]).wait()


def route_kernel(cap_pad, cols_ref, rows_ref, limit_ref, slot_rows_ref, slot_cols_ref):
    for b in range(cols_ref.shape[0]):
        limit = limit_ref[b]
        col = [cols_ref[b, :, k : k + 1] for k in range(4)]
        row = [rows_ref[b, k : k + 1, :] for k in range(4)]
        slot_rows_ref[b] = jnp.full(slot_rows_ref.shape[1:], -1, jnp.int32)
        slot_cols_ref[b] = jnp.full(slot_cols_ref.shape[1:], -1, jnp.int32)
        for j in range(2):
            rank_row = 0
            rank_col = 0
            for k in range(2):
                hit = (col[k] == row[j]) & (col[2 + k] < row[2 + j])
                rank_row = rank_row + jnp.sum(hit.astype(jnp.int32), axis=0, keepdims=True)
                hit = (row[k] == col[j]) & (row[2 + k] < col[2 + j])
                rank_col = rank_col + jnp.sum(hit.astype(jnp.int32), axis=1, keepdims=True)
            keep_row = (rank_row < limit) & (row[j] >= 0)
            keep_col = (rank_col < limit) & (col[j] >= 0)
            slot_rows_ref[b, j : j + 1, :] = jnp.where(keep_row, row[j] * cap_pad + rank_row, -1)
            slot_cols_ref[b, :, j : j + 1] = jnp.where(keep_col, col[j] * cap_pad + rank_col, -1)


def run_route(cols, rows, limits, cap_pad):
    batches = cols.shape[0]
    return pl.pallas_call(
        functools.partial(route_kernel, cap_pad),
        out_shape=(
            jax.ShapeDtypeStruct((batches, 8, SEQ_PAD), jnp.int32),
            jax.ShapeDtypeStruct((batches, SEQ_PAD, 8), jnp.int32),
        ),
        in_specs=[
            pl.BlockSpec(memory_space=pltpu.VMEM),
            pl.BlockSpec(memory_space=pltpu.VMEM),
            pl.BlockSpec(memory_space=pltpu.SMEM),
        ],
        out_specs=(
            pl.BlockSpec(memory_space=pltpu.VMEM),
            pl.BlockSpec(memory_space=pltpu.VMEM),
        ),
        compiler_params=pltpu.CompilerParams(vmem_limit_bytes=VMEM_LIMIT),
        cost_estimate=pl.CostEstimate(flops=4000000, bytes_accessed=1000000, transcendentals=0),
        name="route",
    )(cols, rows, limits)


def norm_stats(values):
    average = jnp.mean(values, axis=-1, keepdims=True)
    centered = values - average
    spread = jnp.mean(centered * centered, axis=-1, keepdims=True)
    inverse = lax.rsqrt(spread + EPS)
    return centered * inverse, inverse


def front_kernel(
    experts,
    shards,
    x_ref,
    grad_ref,
    weight_ref,
    cols_ref,
    slot_rows_ref,
    own_in_ref,
    own_out_ref,
    received_ref,
    qkv_ref,
    mixed_ref,
    lse_ref,
    hidden_ref,
    one_ref,
    two_ref,
    probs_ref,
    spread_in_ref,
    spread_out_ref,
    small_ref,
    send_ref,
    send_sem,
    arrived,
    rows_send,
    rows_recv,
):
    index = pl.program_id(0)
    me = lax.axis_index("expert")
    groups = received_ref.shape[0]
    width = x_ref.shape[-1]
    rows = x_ref.shape[1]
    line = Line(shards)
    own = (own_in_ref, own_out_ref)
    spread = (spread_in_ref, spread_out_ref)

    @pl.when(pl.program_id(0) == 0)
    def _():
        line.greet(me, groups)
        small_ref[...] = weight_ref[:, 4 * width :].astype(F32).T
        line.push(0, own, spread, send_sem, arrived)

    x = x_ref[0]
    hat, _ = norm_stats(x)
    one = (hat * small_ref[0:1, :] + small_ref[1:2, :]).astype(BF)
    one_ref[0] = one
    qkv_ref[0] = dot(one, weight_ref[:, : 3 * width]).astype(BF)
    lane = lax.broadcasted_iota(jnp.int32, (1, 128), 1)
    key_ok = lax.broadcasted_iota(jnp.int32, (1, rows), 1) < SEQ
    lse = jnp.zeros((rows, 128), F32)
    scale = HEAD ** (-0.5)
    for pair in range(HEADS // 2):
        low = pair * 128
        query = qkv_ref[0, :, low : low + 128]
        keys = qkv_ref[0, :, width + low : width + low + 128]
        values = qkv_ref[0, :, 2 * width + low : 2 * width + low + 128]
        total = None
        for side in range(2):
            mine = (lane // HEAD) == side
            scores = dot_nt(jnp.where(mine, query, jnp.zeros_like(query)), keys) * scale
            scores = jnp.where(key_ok, scores, NEG)
            highest = jnp.max(scores, axis=-1, keepdims=True)
            expo = jnp.exp(scores - highest)
            denom = jnp.sum(expo, axis=-1, keepdims=True)
            weights = (expo / denom).astype(BF)
            lse = jnp.where(lane == 2 * pair + side, highest + jnp.log(denom), lse)
            part = dot(weights, jnp.where(mine, values, jnp.zeros_like(values)))
            total = part if total is None else total + part
        mixed_ref[0, :, low : low + 128] = total.astype(BF)
    lse_ref[0] = lse
    hidden = x + dot(mixed_ref[0], weight_ref[:, 3 * width : 4 * width])
    hidden_ref[0] = hidden
    hat, _ = norm_stats(hidden)
    two = (hat * small_ref[2:3, :] + small_ref[3:4, :]).astype(BF)
    two_ref[0] = two
    logits = dot(two, weight_ref[:, 4 * width :])
    in_router = (lane >= 4) & (lane < 4 + experts)
    logits = jnp.where(in_router, logits, NEG)
    expo = jnp.exp(logits - jnp.max(logits, axis=-1, keepdims=True))
    probs = expo / jnp.sum(expo, axis=-1, keepdims=True)
    probs_ref[0] = probs
    out_grad = grad_ref[0]
    cap_pad = send_ref.shape[3]
    slot = lax.broadcasted_iota(jnp.int32, (groups * cap_pad, 1), 0)
    both = None
    grads = None
    for j in range(2):
        gate = jnp.sum(
            jnp.where(lane - 4 == cols_ref[0, :, j : j + 1], probs, 0.0), axis=-1, keepdims=True
        )
        pick = (slot == slot_rows_ref[0, j : j + 1, :]).astype(F32)
        both = pick if both is None else both + pick
        part = dot(pick.astype(BF), (gate * out_grad).astype(BF))
        grads = part if grads is None else grads + part
    sent = dot(both.astype(BF), two).astype(BF)
    send_ref[index, :, 0] = sent.reshape(groups, cap_pad, width)
    send_ref[index, :, 1] = grads.astype(BF).reshape(groups, cap_pad, width)

    def rows_copy(image, target):
        return pltpu.make_async_remote_copy(
            src_ref=send_ref.at[image, target],
            dst_ref=received_ref.at[me, image],
            send_sem=rows_send.at[image, target],
            recv_sem=rows_recv.at[me, image],
            device_id={"expert": target},
            device_id_type=MESH,
        )

    for k in range(1, groups):
        rows_copy(index, lax.rem(me + k, groups)).start()
    pltpu.make_async_copy(
        send_ref.at[index, me], received_ref.at[me, index], rows_recv.at[me, index]
    ).start()

    @pl.when(index == pl.num_programs(0) - 1)
    def _():
        rounds = min(EARLY, shards - 1)
        for round_id in range(1, rounds):
            line.receive(round_id - 1, spread, arrived)
            line.push(round_id, own, spread, send_sem, arrived)

        def finish(image, carry):
            for k in range(groups):
                source = lax.rem(me + k, groups)
                if k:
                    rows_copy(image, source).wait_send()
                view = received_ref.at[source, image]
                pltpu.make_async_copy(view, view, rows_recv.at[source, image]).wait()
            return carry

        lax.fori_loop(0, send_ref.shape[0], finish, 0)
        line.receive(rounds - 1, spread, arrived)
        for round_id in range(rounds):
            line.drain(round_id, own, spread, send_sem, arrived)


def run_front(x, grad, weight, cols, slot_rows, own_in, own_out, experts, cap_pad):
    batches, rows, width = x.shape
    shards = lax.axis_size("dp")
    total = weight.shape[1]

    def block(*shape):
        return pl.BlockSpec((1,) + shape, lambda i: (i,) + (0,) * len(shape))

    def out(shape, dtype):
        return jax.ShapeDtypeStruct((batches,) + shape, dtype)

    return pl.pallas_call(
        functools.partial(front_kernel, experts, shards),
        grid=(batches,),
        out_shape=(
            jax.ShapeDtypeStruct((experts, batches, 2, cap_pad, width), BF),
            out((rows, 3 * width), BF),
            out((rows, width), BF),
            out((rows, 128), F32),
            out((rows, width), F32),
            out((rows, width), BF),
            out((rows, width), BF),
            out((rows, SMALL), F32),
            jax.ShapeDtypeStruct((shards,) + own_in.shape, BF),
            jax.ShapeDtypeStruct((shards,) + own_out.shape, BF),
        ),
        in_specs=[
            block(rows, width),
            block(rows, width),
            pl.BlockSpec((width, total), lambda i: (0, 0), pipeline_mode=pl.Buffered(1)),
            block(rows, 4),
            block(8, rows),
            pl.BlockSpec(memory_space=pl.ANY),
            pl.BlockSpec(memory_space=pl.ANY),
        ],
        out_specs=(
            pl.BlockSpec(memory_space=pl.ANY),
            block(rows, 3 * width),
            block(rows, width),
            block(rows, 128),
            block(rows, width),
            block(rows, width),
            block(rows, width),
            block(rows, SMALL),
            pl.BlockSpec(memory_space=pl.ANY),
            pl.BlockSpec(memory_space=pl.ANY),
        ),
        scratch_shapes=[
            pltpu.VMEM((SMALL, width), F32),
            pltpu.VMEM((batches, experts, 2, cap_pad, width), BF),
            pltpu.SemaphoreType.DMA((2, EARLY, 2)),
            pltpu.SemaphoreType.DMA((shards, 2)),
            pltpu.SemaphoreType.DMA((batches, experts)),
            pltpu.SemaphoreType.DMA((experts, batches)),
        ],
        compiler_params=pltpu.CompilerParams(
            dimension_semantics=("arbitrary",),
            vmem_limit_bytes=VMEM_LIMIT,
            collective_id=1,
            has_side_effects=True,
        ),
        cost_estimate=pl.CostEstimate(
            flops=8000000000, bytes_accessed=40000000, transcendentals=3000000
        ),
        name="front",
    )(x, grad, weight, cols, slot_rows, own_in, own_out)


def pieces_of(tall, span):
    half = ceil_to(tall // 2, 16)
    mid = ceil_to(span // 2, 16)
    return ((0, 0, half), (0, half, tall - half), (1, 0, mid), (1, mid, span - mid))


def moe_kernel(
    shards,
    groups,
    x_hbm,
    own_in_ref,
    own_out_ref,
    spread_in_ref,
    spread_out_ref,
    back_ref,
    sum_in_ref,
    sum_out_ref,
    rows_ref,
    win_ref,
    wout_ref,
    y_acc,
    dx_acc,
    gin_acc,
    gout_acc,
    part_in_ref,
    part_out_ref,
    land_in_ref,
    land_out_ref,
    rows_sem,
    weight_send,
    arrived,
    sum_send,
    sum_recv,
    back_send,
    back_recv,
    final_sem,
):
    line = Line(shards)
    z = line.me
    me = lax.axis_index("expert")
    _, batches, _, cap_pad, width = rows_ref.shape
    tall, span = own_in_ref.shape
    group = max(1, 512 // (batches * cap_pad))
    while groups % group:
        group -= 1
    blocks = groups // group
    rows = group * batches * cap_pad
    early = min(EARLY, shards - 1)
    spread = (win_ref, wout_ref)
    early_spread = (spread_in_ref, spread_out_ref)
    own = (own_in_ref, own_out_ref)
    parts = (part_in_ref, part_out_ref)
    lands = (land_in_ref, land_out_ref)
    pieces = pieces_of(tall, span)

    for k in range(groups):
        source = lax.rem(me + k, groups)
        pltpu.make_async_copy(x_hbm.at[source], rows_ref.at[source], rows_sem.at[source]).start()
    for part in range(2):
        pltpu.make_async_copy(own[part], spread[part].at[z], arrived.at[z, part]).start()
    for far in range(1, early + 1):
        for sign in (-1, 1):
            slot = z + sign * far

            @pl.when((slot >= 0) & (slot < shards))
            def _():
                for part in range(2):
                    pltpu.make_async_copy(
                        early_spread[part].at[slot], spread[part].at[slot], arrived.at[slot, part]
                    ).start()

    line.greet(me, groups)
    if early < shards - 1:
        line.push(early, own, spread, weight_send, arrived, early_spread)

    table = []
    for at in range(shards):
        near = sorted(range(shards), key=lambda q: (abs(q - at), q))
        table.append(near[1:] + near[:1])

    def quarter(step):
        total = 0
        for at in range(shards):
            for s in range(shards):
                hit = jnp.where((z == at) & (step == s), table[at][s], 0)
                total = total + hit
        return total

    def sum_copy(way, q, piece):
        kind, low, size = pieces[piece]
        if way == 0:
            slot = q
            peer = z + 1
        else:
            slot = jnp.where(q == z - 1, shards, q)
            peer = z - 1
        cut = pl.ds(low, size)
        return pltpu.make_async_remote_copy(
            src_ref=parts[kind].at[q, cut],
            dst_ref=lands[kind].at[slot, cut],
            send_sem=sum_send.at[way, q, piece],
            recv_sem=sum_recv.at[slot, piece],
            device_id={"dp": peer},
            device_id_type=MESH,
        )

    def take_sum(slot, q, piece):
        kind, low, size = pieces[piece]
        cut = pl.ds(low, size)
        view = lands[kind].at[slot, cut]
        pltpu.make_async_copy(view, view, sum_recv.at[slot, piece]).wait()
        parts[kind][q, cut] = (
            parts[kind][q, cut].astype(F32) + lands[kind][slot, cut].astype(F32)
        ).astype(BF)

    def back_copy(source):
        return pltpu.make_async_remote_copy(
            src_ref=rows_ref.at[source],
            dst_ref=back_ref.at[me],
            send_sem=back_send.at[source],
            recv_sem=back_recv.at[me],
            device_id={"expert": source},
            device_id_type=MESH,
        )

    def back_start(first):
        for k in range(group):
            source = first + k

            @pl.when(source != me)
            def _():
                back_copy(source).start()

            @pl.when(source == me)
            def _():
                pltpu.make_async_copy(
                    rows_ref.at[source], back_ref.at[source], back_recv.at[source]
                ).start()

    def block_first(block):
        return lax.rem(me // group + 1 + block, blocks) * group

    def do_step(step, carry):
        q = quarter(step)
        line.wait_slot(q, spread, arrived)
        for round_id in range(early, shards - 2):
            for way in range(2):
                forward = 1 - 2 * way

                @pl.when((q == z - forward * (round_id + 1)) & line.sends(way, round_id + 1))
                def _():
                    for copy in line.hop(way, round_id + 1, spread, spread, weight_send, arrived):
                        copy.start()

        def do_block(block, inner):
            lead = block_first(block)
            low = pl.multiple_of(lead * (batches * cap_pad), rows)
            here = pl.ds(low, rows)
            mine = pl.ds(lead, group)

            @pl.when(step == 0)
            def _():
                for k in range(group):
                    view = rows_ref.at[lead + k]
                    pltpu.make_async_copy(view, view, rows_sem.at[lead + k]).wait()

            x = rows_ref[mine, :, 0].reshape(rows, width)
            grad = rows_ref[mine, :, 1].reshape(rows, width)
            win = win_ref[q, :width, :]
            wout = wout_ref[q]
            pre = dot(x, win) + win_ref[q, width : width + 1, :].astype(F32)
            cdf = 0.5 * lax.erf(pre * (0.5**0.5)) + 0.5
            active = (pre * cdf).astype(BF)
            slope = cdf + pre * (jnp.exp(-0.5 * pre * pre) * 0.3989422804014327)
            d_pre = (dot_nt(grad, wout) * slope).astype(BF)
            y_part = dot(active, wout)
            dx_part = dot_nt(d_pre, win)

            @pl.when(step == 0)
            def _():
                y_acc[here, :] = y_part
                dx_acc[here, :] = dx_part

            @pl.when(step > 0)
            def _():
                y_acc[here, :] += y_part
                dx_acc[here, :] += dx_part

            gout = dot_tn(active, grad)
            gin = dot_tn(x, d_pre)
            gbias = jnp.sum(d_pre.astype(F32), axis=0, keepdims=True)

            @pl.when(block == 0)
            def _():
                gout_acc[...] = gout
                gin_acc[:width, :] = gin
                gin_acc[width : width + 1, :] = gbias

            @pl.when(block > 0)
            def _():
                gout_acc[...] += gout
                gin_acc[:width, :] += gin
                gin_acc[width : width + 1, :] += gbias

            @pl.when(step == shards - 1)
            def _():
                shape = (group, batches, cap_pad, width)
                rows_ref[mine, :, 0] = y_acc[here, :].astype(BF).reshape(shape)
                rows_ref[mine, :, 1] = dx_acc[here, :].astype(BF).reshape(shape)

                @pl.when(block > 0)
                def _():
                    back_start(block_first(block - 1))

            return inner

        lax.fori_loop(0, blocks, do_block, 0)

        @pl.when(step == shards - 1)
        def _():
            back_start(block_first(blocks - 1))

        part_in_ref[q, :width, :] = gin_acc[:width, :].astype(BF)
        part_in_ref[q, width:, :] = jnp.broadcast_to(
            gin_acc[width : width + 1, :].astype(BF), (tall - width, span)
        )
        part_out_ref[q] = gout_acc[...].astype(BF)

        @pl.when((z == 0) & (q > z))
        def _():
            for piece in range(len(pieces)):
                sum_copy(0, q, piece).start()

        @pl.when((z == shards - 1) & (q < z))
        def _():
            for piece in range(len(pieces)):
                sum_copy(1, q, piece).start()

        return carry

    lax.fori_loop(0, shards, do_step, 0)

    def do_forward(turn, carry):
        up = turn
        down = shards - 1 - turn
        for piece in range(len(pieces)):

            @pl.when((up > z) & (z > 0))
            def _():
                take_sum(up, up, piece)
                sum_copy(0, up, piece).start()

            @pl.when((down < z) & (z < shards - 1))
            def _():
                take_sum(down, down, piece)
                sum_copy(1, down, piece).start()

        return carry

    lax.fori_loop(1, shards, do_forward, 0)
    for piece in range(len(pieces)):

        @pl.when(line.has_below)
        def _():
            take_sum(z, z, piece)

        @pl.when(line.has_above)
        def _():
            take_sum(shards, z, piece)

    finals = [
        pltpu.make_async_copy(part_in_ref.at[z], sum_in_ref, final_sem.at[0]),
        pltpu.make_async_copy(part_out_ref.at[z], sum_out_ref, final_sem.at[1]),
    ]
    for copy in finals:
        copy.start()

    def finish_sum(q, carry):
        @pl.when((q > z) & line.has_above)
        def _():
            for piece in range(len(pieces)):
                sum_copy(0, q, piece).wait_send()

        @pl.when((q < z) & line.has_below)
        def _():
            for piece in range(len(pieces)):
                sum_copy(1, q, piece).wait_send()

        return carry

    lax.fori_loop(0, shards, finish_sum, 0)
    for round_id in range(early, shards - 1):
        line.drain(round_id, own, spread, weight_send, arrived)
    for k in range(groups):
        source = lax.rem(me + k, groups)
        if k:
            back_copy(source).wait_send()
        view = back_ref.at[source]
        pltpu.make_async_copy(view, view, back_recv.at[source]).wait()
    for copy in finals:
        copy.wait()


def run_moe(received, own_in, own_out, spread_in, spread_out):
    groups, batches, _, cap_pad, width = received.shape
    shards, tall, span = spread_in.shape
    total = groups * batches * cap_pad
    count = len(pieces_of(tall, span))
    anywhere = pl.BlockSpec(memory_space=pl.ANY)
    return pl.pallas_call(
        functools.partial(moe_kernel, shards, groups),
        out_shape=(
            jax.ShapeDtypeStruct(received.shape, BF),
            jax.ShapeDtypeStruct((tall, span), BF),
            jax.ShapeDtypeStruct((span, width), BF),
        ),
        in_specs=[anywhere] * 5,
        out_specs=(anywhere,) * 3,
        scratch_shapes=[
            pltpu.VMEM(received.shape, BF),
            pltpu.VMEM((shards, tall, span), BF),
            pltpu.VMEM((shards, span, width), BF),
            pltpu.VMEM((total, width), F32),
            pltpu.VMEM((total, width), F32),
            pltpu.VMEM((ceil_to(width + 1, 8), span), F32),
            pltpu.VMEM((span, width), F32),
            pltpu.VMEM((shards, tall, span), BF),
            pltpu.VMEM((shards, span, width), BF),
            pltpu.VMEM((shards + 1, tall, span), BF),
            pltpu.VMEM((shards + 1, span, width), BF),
            pltpu.SemaphoreType.DMA((groups,)),
            pltpu.SemaphoreType.DMA((2, shards, 2)),
            pltpu.SemaphoreType.DMA((shards, 2)),
            pltpu.SemaphoreType.DMA((2, shards, count)),
            pltpu.SemaphoreType.DMA((shards + 1, count)),
            pltpu.SemaphoreType.DMA((groups,)),
            pltpu.SemaphoreType.DMA((groups,)),
            pltpu.SemaphoreType.DMA((2,)),
        ],
        compiler_params=pltpu.CompilerParams(
            vmem_limit_bytes=VMEM_MAX, collective_id=2, has_side_effects=True
        ),
        cost_estimate=pl.CostEstimate(
            flops=12 * total * width * span * shards,
            bytes_accessed=60000000,
            transcendentals=2 * total * span * shards,
        ),
        name="moe",
    )(received, own_in, own_out, spread_in, spread_out)


def tail_kernel(
    experts,
    x_ref,
    grad_ref,
    weight_ref,
    cols_ref,
    slot_cols_ref,
    back_ref,
    qkv_ref,
    mixed_ref,
    lse_ref,
    hidden_ref,
    one_ref,
    two_ref,
    probs_ref,
    out_ref,
    dx_ref,
    dense_ref,
    small_ref,
    sums_ref,
    d_qkv_ref,
    d_branch_ref,
    d_logits_ref,
    one_all,
    two_all,
    mixed_all,
):
    width = x_ref.shape[-1]
    rows = x_ref.shape[1]
    index = pl.program_id(0)

    @pl.when(index == 0)
    def _():
        small_ref[...] = weight_ref[:, 4 * width :].astype(F32).T
        sums_ref[...] = jnp.zeros_like(sums_ref)

    here = pl.ds(pl.multiple_of(index * rows, rows), rows)
    one_all[here, :] = one_ref[0]
    two_all[here, :] = two_ref[0]
    mixed_all[here, :] = mixed_ref[0]
    out_grad = grad_ref[0]
    hidden = hidden_ref[0]
    probs = probs_ref[0]
    lane = lax.broadcasted_iota(jnp.int32, (1, 128), 1)
    slots = back_ref.shape[0] * back_ref.shape[3]
    slot = lax.broadcasted_iota(jnp.int32, (1, slots), 1)
    answers = back_ref[:, 0, 0].reshape(slots, width)
    answer_grads = back_ref[:, 0, 1].reshape(slots, width)
    result = hidden
    d_probs = jnp.zeros_like(probs)
    both = None
    for j in range(2):
        pick = (slot == slot_cols_ref[0, :, j : j + 1]).astype(F32)
        both = pick if both is None else both + pick
        chosen = lane - 4 == cols_ref[0, :, j : j + 1]
        gate = jnp.sum(jnp.where(chosen, probs, 0.0), axis=-1, keepdims=True)
        picked = dot(pick.astype(BF), answers)
        result = result + gate * picked
        d_gate = jnp.sum(picked * out_grad, axis=-1, keepdims=True)
        d_probs = jnp.where(chosen, d_gate, d_probs)
    out_ref[0] = result
    d_logits = probs * (d_probs - jnp.sum(d_probs * probs, axis=-1, keepdims=True))
    d_logits = d_logits.astype(BF)
    d_logits_ref[here, :] = d_logits
    d_two = dot(both.astype(BF), answer_grads) + dot_nt(d_logits, weight_ref[:, 4 * width :])
    hat, inverse = norm_stats(hidden)
    sums_ref[2:3, :] += jnp.sum(d_two * hat, axis=0, keepdims=True)
    sums_ref[3:4, :] += jnp.sum(d_two, axis=0, keepdims=True)
    d_hat = d_two * small_ref[2:3, :]
    d_hidden = out_grad + inverse * (
        d_hat
        - jnp.mean(d_hat, axis=-1, keepdims=True)
        - hat * jnp.mean(d_hat * hat, axis=-1, keepdims=True)
    )
    d_branch = d_hidden.astype(BF)
    d_branch_ref[here, :] = d_branch
    d_mixed_all = dot_nt(d_branch, weight_ref[:, 3 * width : 4 * width]).astype(BF)
    key_ok = lax.broadcasted_iota(jnp.int32, (1, rows), 1) < SEQ
    scale = HEAD ** (-0.5)
    for pair in range(HEADS // 2):
        low = pair * 128
        query = qkv_ref[0, :, low : low + 128]
        keys = qkv_ref[0, :, width + low : width + low + 128]
        values = qkv_ref[0, :, 2 * width + low : 2 * width + low + 128]
        d_mixed = d_mixed_all[:, low : low + 128]
        d_query = d_keys = d_values = None
        for side in range(2):
            mine = (lane // HEAD) == side
            head = 2 * pair + side

            def own(array):
                return jnp.where(mine, array, jnp.zeros_like(array))

            my_query = own(query)
            my_keys = own(keys)
            my_d_mixed = own(d_mixed)
            scores = dot_nt(my_query, keys) * scale
            scores = jnp.where(key_ok, scores, NEG)
            probs_h = jnp.exp(scores - lse_ref[0, :, head : head + 1])
            d_weights = dot_nt(my_d_mixed, values)
            row_terms = jnp.sum(d_weights * probs_h, axis=-1, keepdims=True)
            d_scores = (probs_h * (d_weights - row_terms) * scale).astype(BF)
            parts = (
                dot(d_scores, my_keys),
                dot_tn(d_scores, my_query),
                dot_tn(probs_h.astype(BF), my_d_mixed),
            )
            if side == 0:
                d_query, d_keys, d_values = parts
            else:
                d_query, d_keys, d_values = (
                    d_query + parts[0],
                    d_keys + parts[1],
                    d_values + parts[2],
                )
        d_qkv_ref[here, low : low + 128] = d_query.astype(BF)
        d_qkv_ref[here, width + low : width + low + 128] = d_keys.astype(BF)
        d_qkv_ref[here, 2 * width + low : 2 * width + low + 128] = d_values.astype(BF)
    d_one = dot_nt(d_qkv_ref[here, :], weight_ref[:, : 3 * width])
    hat, inverse = norm_stats(x_ref[0])
    sums_ref[0:1, :] += jnp.sum(d_one * hat, axis=0, keepdims=True)
    sums_ref[1:2, :] += jnp.sum(d_one, axis=0, keepdims=True)
    d_hat = d_one * small_ref[0:1, :]
    dx_ref[0] = d_hidden + inverse * (
        d_hat
        - jnp.mean(d_hat, axis=-1, keepdims=True)
        - hat * jnp.mean(d_hat * hat, axis=-1, keepdims=True)
    )

    @pl.when(index == pl.num_programs(0) - 1)
    def _():
        dense_ref[:, 4 * width :] = (dot_tn(two_all[...], d_logits_ref[...]) + sums_ref[...].T).astype(BF)
        dense_ref[:, 3 * width : 4 * width] = dot_tn(mixed_all[...], d_branch_ref[...]).astype(BF)
        for part in range(3):
            cut = slice(part * width, (part + 1) * width)
            dense_ref[:, cut] = dot_tn(one_all[...], d_qkv_ref[:, cut]).astype(BF)


def run_tail(x, grad, weight, cols, slot_cols, back, saved, experts):
    batches, rows, width = x.shape
    total = weight.shape[1]
    cap_pad = back.shape[3]
    qkv, mixed, lse, hidden, one, two, probs = saved

    def block(*shape):
        return pl.BlockSpec((1,) + shape, lambda i: (i,) + (0,) * len(shape))

    return pl.pallas_call(
        functools.partial(tail_kernel, experts),
        grid=(batches,),
        out_shape=(
            jax.ShapeDtypeStruct(x.shape, F32),
            jax.ShapeDtypeStruct(x.shape, F32),
            jax.ShapeDtypeStruct((width, total), BF),
        ),
        in_specs=[
            block(rows, width),
            block(rows, width),
            pl.BlockSpec((width, total), lambda i: (0, 0), pipeline_mode=pl.Buffered(1)),
            block(rows, 4),
            block(rows, 8),
            pl.BlockSpec((experts, 1, 2, cap_pad, width), lambda i: (0, i, 0, 0, 0)),
            block(rows, 3 * width),
            block(rows, width),
            block(rows, 128),
            block(rows, width),
            block(rows, width),
            block(rows, width),
            block(rows, SMALL),
        ],
        out_specs=(
            block(rows, width),
            block(rows, width),
            pl.BlockSpec((width, total), lambda i: (0, 0), pipeline_mode=pl.Buffered(1)),
        ),
        scratch_shapes=[
            pltpu.VMEM((SMALL, width), F32),
            pltpu.VMEM((SMALL, width), F32),
            pltpu.VMEM((batches * rows, 3 * width), BF),
            pltpu.VMEM((batches * rows, width), BF),
            pltpu.VMEM((batches * rows, SMALL), BF),
            pltpu.VMEM((batches * rows, width), BF),
            pltpu.VMEM((batches * rows, width), BF),
            pltpu.VMEM((batches * rows, width), BF),
        ],
        compiler_params=params(),
        cost_estimate=pl.CostEstimate(
            flops=16000000000, bytes_accessed=50000000, transcendentals=2000000
        ),
        name="tail",
    )(x, grad, weight, cols, slot_cols, back, qkv, mixed, lse, hidden, one, two, probs)


TILE = 128
PLANE = 8


def reduce_kernel(
    experts,
    shards,
    cols_ref,
    slot_cols_ref,
    lse_ref,
    probs_ref,
    x_hbm,
    grad_hbm,
    weight_hbm,
    back_hbm,
    qkv_hbm,
    mixed_hbm,
    hidden_hbm,
    one_hbm,
    two_hbm,
    out_hbm,
    dx_hbm,
    qkv_grad_ref,
    proj_grad_ref,
    small_grad_ref,
    x_ref,
    grad_ref,
    weight_ref,
    back_ref,
    qkv_ref,
    mixed_ref,
    hidden_ref,
    one_ref,
    two_ref,
    small_ref,
    sums_ref,
    one_flip,
    d_qkv_ref,
    d_branch_ref,
    d_mixed_ref,
    d_logits_ref,
    tiles_ref,
    near_ref,
    plane_land,
    plane_ref,
    line_land,
    final_ref,
    small_land,
    small_far,
    load_sem,
    store_sem,
    near_send,
    near_recv,
    plane_send,
    plane_recv,
    line_send,
    line_recv,
    final_send,
    final_recv,
    small_send,
    small_recv,
):
    batches, rows, width = x_ref.shape
    z = lax.axis_index("dp")
    me = lax.axis_index("expert")
    core = lax.rem(me, 2)
    sibling = me + 1 - 2 * core
    chip = me // 2
    chips = PLANE // 2
    pairs = HEADS // 2
    depth = width // shards
    head_tiles = width // TILE
    own_tiles = (4 * width // TILE) // PLANE

    def loads(kind, image):
        pair = {
            0: (back_hbm.at[:, image], back_ref.at[:, image]),
            1: (hidden_hbm.at[image], hidden_ref.at[image]),
            2: (grad_hbm.at[image], grad_ref.at[image]),
            3: (mixed_hbm.at[image], mixed_ref.at[pl.ds(image * rows, rows)]),
            4: (two_hbm.at[image], two_ref.at[pl.ds(image * rows, rows)]),
            5: (one_hbm.at[image], one_ref.at[pl.ds(image * rows, rows)]),
            6: (qkv_hbm.at[image], qkv_ref.at[image]),
            7: (x_hbm.at[image], x_ref.at[image]),
        }[kind]
        return pltpu.make_async_copy(pair[0], pair[1], load_sem.at[kind, image])

    weight_load = pltpu.make_async_copy(weight_hbm, weight_ref, load_sem.at[8, 0])
    for kind in range(3):
        loads(kind, 0).start()
    weight_load.start()
    for image in range(1, batches):
        for kind in range(3):
            loads(kind, image).start()
    for kind in range(3, 8):
        for image in range(batches):
            loads(kind, image).start()

    barrier = pltpu.get_barrier_semaphore()
    for k in range(1, PLANE):
        pl.semaphore_signal(
            barrier, inc=1, device_id={"expert": lax.rem(me + k, PLANE)}, device_id_type=MESH
        )
    for k in range(1, shards):
        pl.semaphore_signal(
            barrier, inc=1, device_id={"dp": lax.rem(z + k, shards)}, device_id_type=MESH
        )
    pl.semaphore_wait(barrier, PLANE - 1 + shards - 1)

    def remote(source, target, send_sem, recv_sem, peer):
        return pltpu.make_async_remote_copy(
            src_ref=source,
            dst_ref=target,
            send_sem=send_sem,
            recv_sem=recv_sem,
            device_id=peer,
            device_id_type=MESH,
        )

    def landed(view, sem):
        pltpu.make_async_copy(view, view, sem).wait()

    def near_copy(tile):
        return remote(
            tiles_ref.at[tile],
            near_ref.at[tile],
            near_send.at[tile],
            near_recv.at[tile],
            {"expert": sibling},
        )

    def plane_copy(tile):
        return remote(
            tiles_ref.at[tile],
            plane_land.at[tile // PLANE, chip],
            plane_send.at[tile],
            plane_recv.at[tile // PLANE, chip],
            {"expert": lax.rem(tile, PLANE)},
        )

    def line_copy(k, far):
        return remote(
            plane_ref.at[k, pl.ds(pl.multiple_of(far * depth, depth), depth)],
            line_land.at[k, z],
            line_send.at[k, far],
            line_recv.at[k, z],
            {"dp": far},
        )

    def final_copy(k, peer):
        tile = me + PLANE * k
        return remote(
            final_ref.at[tile],
            final_ref.at[tile],
            final_send.at[k, peer],
            final_recv.at[tile],
            {"expert": peer},
        )

    def leave(tile):
        @pl.when(lax.rem(tile, 2) != core)
        def _():
            near_copy(tile).start()

    def combine(tile):
        @pl.when(lax.rem(tile, 2) == core)
        def _():
            landed(near_ref.at[tile], near_recv.at[tile])
            tiles_ref[tile] = (
                tiles_ref[tile].astype(F32) + near_ref[tile].astype(F32)
            ).astype(BF)

            @pl.when(lax.rem(tile, PLANE) != me)
            def _():
                plane_copy(tile).start()

    def plane_sum(k):
        total = tiles_ref[me + PLANE * k].astype(F32)
        for j in range(1, chips):
            far = lax.rem(chip + j, chips)
            landed(plane_land.at[k, far], plane_recv.at[k, far])
            total = total + plane_land[k, far].astype(F32)
        plane_ref[k] = total.astype(BF)
        for j in range(1, shards):
            line_copy(k, lax.rem(z + j, shards)).start()

    def line_sum(k):
        mine = pl.ds(pl.multiple_of(z * depth, depth), depth)
        total = plane_ref[k, mine].astype(F32)
        for j in range(1, shards):
            far = lax.rem(z + j, shards)
            landed(line_land.at[k, far], line_recv.at[k, far])
            total = total + line_land[k, far].astype(F32)
        final_ref[me + PLANE * k] = total.astype(BF)
        for j in range(1, PLANE):
            final_copy(k, lax.rem(me + j, PLANE)).start()

    lane = lax.broadcasted_iota(jnp.int32, (1, 128), 1)
    groups, _, _, cap_pad, _ = back_ref.shape
    slots = groups * cap_pad
    slot = lax.broadcasted_iota(jnp.int32, (1, slots), 1)
    sums_ref[...] = jnp.zeros_like(sums_ref)

    def phase_one(image, carry):
        here = pl.ds(pl.multiple_of(image * rows, rows), rows)
        for kind in range(3):
            view = (back_ref.at[:, image], hidden_ref.at[image], grad_ref.at[image])[kind]
            landed(view, load_sem.at[kind, image])

        @pl.when(image == 0)
        def _():
            weight_load.wait()
            small_ref[...] = weight_ref[:, 4 * width :].astype(F32).T

        out_grad = grad_ref[image]
        hidden = hidden_ref[image]
        probs = probs_ref[image]
        answers = back_ref[:, image, 0].reshape(slots, width)
        answer_grads = back_ref[:, image, 1].reshape(slots, width)
        result = hidden
        d_probs = jnp.zeros_like(probs)
        both = None
        for j in range(2):
            pick = (slot == slot_cols_ref[image, :, j : j + 1]).astype(F32)
            both = pick if both is None else both + pick
            chosen = lane - 4 == cols_ref[image, :, j : j + 1]
            gate = jnp.sum(jnp.where(chosen, probs, 0.0), axis=-1, keepdims=True)
            picked = dot(pick.astype(BF), answers)
            result = result + gate * picked
            d_gate = jnp.sum(picked * out_grad, axis=-1, keepdims=True)
            d_probs = jnp.where(chosen, d_gate, d_probs)
        d_logits = probs * (d_probs - jnp.sum(d_probs * probs, axis=-1, keepdims=True))
        d_logits = d_logits.astype(BF)
        d_logits_ref[here, :] = d_logits
        d_two = dot(both.astype(BF), answer_grads) + dot_nt(d_logits, weight_ref[:, 4 * width :])
        hat, inverse = norm_stats(hidden)
        sums_ref[2:3, :] += jnp.sum(d_two * hat, axis=0, keepdims=True)
        sums_ref[3:4, :] += jnp.sum(d_two, axis=0, keepdims=True)
        d_hat = d_two * small_ref[2:3, :]
        d_hidden = out_grad + inverse * (
            d_hat
            - jnp.mean(d_hat, axis=-1, keepdims=True)
            - hat * jnp.mean(d_hat * hat, axis=-1, keepdims=True)
        )
        d_branch = d_hidden.astype(BF)
        d_branch_ref[here, :] = d_branch
        d_mixed_ref[here, :] = dot_nt(d_branch, weight_ref[:, 3 * width : 4 * width]).astype(BF)
        grad_ref[image] = d_hidden
        hidden_ref[image] = result
        pltpu.make_async_copy(hidden_ref.at[image], out_hbm.at[image], store_sem.at[0, image]).start()
        return carry

    lax.fori_loop(0, batches, phase_one, 0)
    for kind, view in ((3, mixed_ref), (4, two_ref), (5, one_ref)):
        for image in range(batches):
            landed(view.at[pl.ds(image * rows, rows)], load_sem.at[kind, image])
    proj = dot_tn(mixed_ref[...], d_branch_ref[...]).astype(BF)
    for tile in range(head_tiles):
        tiles_ref[tile] = proj[:, tile * TILE : (tile + 1) * TILE]
    for tile in range(head_tiles):
        leave(tile)
    one_flip[...] = one_ref[...].T
    flipped = dot_tn(d_logits_ref[...], two_ref[...])
    for image in range(batches):
        landed(qkv_ref.at[image], load_sem.at[6, image])

    key_ok = lax.broadcasted_iota(jnp.int32, (1, rows), 1) < SEQ
    scale = HEAD ** (-0.5)

    def phase_two(pair, carry):
        low = pl.multiple_of(pair * TILE, TILE)
        spots = [pl.ds(pl.multiple_of(part * width + low, TILE), TILE) for part in range(3)]
        for image in range(batches):
            here = pl.ds(image * rows, rows)
            query, keys, values = (qkv_ref[image, :, spot] for spot in spots)
            d_mixed = d_mixed_ref[here, pl.ds(low, TILE)]
            total = [None, None, None]
            for side in range(2):
                mine = (lane // HEAD) == side

                def own(array):
                    return jnp.where(mine, array, jnp.zeros_like(array))

                my_query = own(query)
                my_d_mixed = own(d_mixed)
                scores = dot_nt(my_query, keys) * scale
                scores = jnp.where(key_ok, scores, NEG)
                log_total = jnp.sum(
                    jnp.where(lane == 2 * pair + side, lse_ref[image], 0.0), axis=-1, keepdims=True
                )
                probs_h = jnp.exp(scores - log_total)
                d_weights = dot_nt(my_d_mixed, values)
                row_terms = jnp.sum(d_weights * probs_h, axis=-1, keepdims=True)
                d_scores = (probs_h * (d_weights - row_terms) * scale).astype(BF)
                fresh = (
                    dot(d_scores, own(keys)),
                    dot_tn(d_scores, my_query),
                    dot_tn(probs_h.astype(BF), my_d_mixed),
                )
                total = [new if old is None else old + new for old, new in zip(total, fresh)]
            for part in range(3):
                d_qkv_ref[here, spots[part]] = total[part].astype(BF)
        first = head_tiles + 3 * pair
        for part in range(3):
            tiles_ref[first + part] = dot(one_flip[...], d_qkv_ref[:, spots[part]]).astype(BF)
        for part in range(3):
            leave(first + part)

        @pl.when(pair == 0)
        def _():
            for tile in range(head_tiles):
                combine(tile)

        @pl.when(pair > 0)
        def _():
            for part in range(3):
                combine(first - 3 + part)

        @pl.when(pair == pairs - 3)
        def _():
            plane_sum(0)

        @pl.when(pair == pairs - 1)
        def _():
            line_sum(0)
            plane_sum(1)

        return carry

    lax.fori_loop(0, pairs, phase_two, 0)
    for part in range(3):
        combine(head_tiles + 3 * (pairs - 1) + part)

    for image in range(batches):
        landed(x_ref.at[image], load_sem.at[7, image])

    def phase_three(image, carry):
        here = pl.ds(pl.multiple_of(image * rows, rows), rows)
        d_one = dot_nt(d_qkv_ref[here, :], weight_ref[:, : 3 * width])
        hat, inverse = norm_stats(x_ref[image])
        sums_ref[0:1, :] += jnp.sum(d_one * hat, axis=0, keepdims=True)
        sums_ref[1:2, :] += jnp.sum(d_one, axis=0, keepdims=True)
        d_hat = d_one * small_ref[0:1, :]
        x_ref[image] = grad_ref[image] + inverse * (
            d_hat
            - jnp.mean(d_hat, axis=-1, keepdims=True)
            - hat * jnp.mean(d_hat * hat, axis=-1, keepdims=True)
        )
        pltpu.make_async_copy(x_ref.at[image], dx_hbm.at[image], store_sem.at[1, image]).start()

        @pl.when(image == batches // 2 - 1)
        def _():
            line_sum(1)
            plane_sum(2)

        return carry

    lax.fori_loop(0, batches, phase_three, 0)

    def small_copy(k):
        peer = lax.rem(me + k, PLANE)
        return remote(
            sums_ref, small_land.at[me], small_send.at[peer], small_recv.at[me], {"expert": peer}
        )

    def small_far_copy(k):
        peer = lax.rem(z + k, shards)
        return remote(
            small_land.at[me],
            small_far.at[z],
            small_send.at[PLANE + peer],
            small_recv.at[PLANE + z],
            {"dp": peer},
        )

    sums_ref[...] += flipped[: sums_ref.shape[0]]
    for k in range(1, PLANE):
        small_copy(k).start()
    line_sum(2)
    total = sums_ref[...]
    for k in range(1, PLANE):
        peer = lax.rem(me + k, PLANE)
        landed(small_land.at[peer], small_recv.at[peer])
        total = total + small_land[peer]
    small_land[me] = total
    for k in range(1, shards):
        small_far_copy(k).start()
    for k in range(1, shards):
        peer = lax.rem(z + k, shards)
        landed(small_far.at[peer], small_recv.at[PLANE + peer])
        total = total + small_far[peer]
    small_grad_ref[...] = total

    def finish(tile, carry):
        @pl.when(lax.rem(tile, PLANE) != me)
        def _():
            landed(final_ref.at[tile], final_recv.at[tile])

        @pl.when(lax.rem(tile, 2) != core)
        def _():
            near_copy(tile).wait_send()

        @pl.when((lax.rem(tile, 2) == core) & (lax.rem(tile, PLANE) != me))
        def _():
            plane_copy(tile).wait_send()

        return carry

    lax.fori_loop(0, 4 * head_tiles, finish, 0)
    for tile in range(head_tiles):
        proj_grad_ref[:, tile * TILE : (tile + 1) * TILE] = final_ref[tile].astype(F32)
    for pair in range(pairs):
        for part in range(3):
            low = part * width + pair * TILE
            qkv_grad_ref[:, low : low + TILE] = final_ref[head_tiles + 3 * pair + part].astype(F32)
    for k in range(own_tiles):
        for j in range(1, shards):
            line_copy(k, lax.rem(z + j, shards)).wait_send()
        for j in range(1, PLANE):
            final_copy(k, lax.rem(me + j, PLANE)).wait_send()
    for k in range(1, PLANE):
        small_copy(k).wait_send()
    for k in range(1, shards):
        small_far_copy(k).wait_send()
    for image in range(batches):
        pltpu.make_async_copy(hidden_ref.at[image], out_hbm.at[image], store_sem.at[0, image]).wait()
        pltpu.make_async_copy(x_ref.at[image], dx_hbm.at[image], store_sem.at[1, image]).wait()


def run_reduce(x, grad, weight, cols, slot_cols, back, saved, experts):
    batches, rows, width = x.shape
    total = weight.shape[1]
    shards = lax.axis_size("dp")
    qkv, mixed, lse, hidden, one, two, probs = saved
    depth = width // shards
    tiles = 4 * width // TILE
    own_tiles = tiles // PLANE
    small_rows = ceil_to(4 + experts, 8)
    anywhere = pl.BlockSpec(memory_space=pl.ANY)
    inside = pl.BlockSpec(memory_space=pltpu.VMEM)
    dma = pltpu.SemaphoreType.DMA
    return pl.pallas_call(
        functools.partial(reduce_kernel, experts, shards),
        out_shape=(
            jax.ShapeDtypeStruct(x.shape, F32),
            jax.ShapeDtypeStruct(x.shape, F32),
            jax.ShapeDtypeStruct((depth, 3 * width), F32),
            jax.ShapeDtypeStruct((depth, width), F32),
            jax.ShapeDtypeStruct((small_rows, width), F32),
        ),
        in_specs=[inside] * 4 + [anywhere] * 9,
        out_specs=(anywhere, anywhere, inside, inside, inside),
        scratch_shapes=[
            pltpu.VMEM(x.shape, F32),
            pltpu.VMEM(x.shape, F32),
            pltpu.VMEM(weight.shape, BF),
            pltpu.VMEM(back.shape, BF),
            pltpu.VMEM(qkv.shape, BF),
            pltpu.VMEM((batches * rows, width), BF),
            pltpu.VMEM(x.shape, F32),
            pltpu.VMEM((batches * rows, width), BF),
            pltpu.VMEM((batches * rows, width), BF),
            pltpu.VMEM((SMALL, width), F32),
            pltpu.VMEM((small_rows, width), F32),
            pltpu.VMEM((width, batches * rows), BF),
            pltpu.VMEM((batches * rows, 3 * width), BF),
            pltpu.VMEM((batches * rows, width), BF),
            pltpu.VMEM((batches * rows, width), BF),
            pltpu.VMEM((batches * rows, SMALL), BF),
            pltpu.VMEM((tiles, width, TILE), BF),
            pltpu.VMEM((tiles, width, TILE), BF),
            pltpu.VMEM((own_tiles, PLANE // 2, width, TILE), BF),
            pltpu.VMEM((own_tiles, width, TILE), BF),
            pltpu.VMEM((own_tiles, shards, depth, TILE), BF),
            pltpu.VMEM((tiles, depth, TILE), BF),
            pltpu.VMEM((PLANE, small_rows, width), F32),
            pltpu.VMEM((shards, small_rows, width), F32),
            dma((9, batches)),
            dma((2, batches)),
            dma((tiles,)),
            dma((tiles,)),
            dma((tiles,)),
            dma((own_tiles, PLANE // 2)),
            dma((own_tiles, shards)),
            dma((own_tiles, shards)),
            dma((own_tiles, PLANE)),
            dma((tiles,)),
            dma((PLANE + shards,)),
            dma((PLANE + shards,)),
        ],
        compiler_params=pltpu.CompilerParams(
            vmem_limit_bytes=VMEM_MAX, collective_id=3, has_side_effects=True
        ),
        cost_estimate=pl.CostEstimate(
            flops=16000000000, bytes_accessed=50000000, transcendentals=2000000
        ),
        name="tail",
    )(cols, slot_cols, lse, probs, x, grad, weight, back, qkv, mixed, hidden, one, two)


def per_device(
    inputs,
    gain_one,
    shift_one,
    qkv_weight,
    proj_weight,
    gain_two,
    shift_two,
    router_weight,
    expert_in,
    expert_bias,
    expert_out,
    out_grad,
    routes,
    priority,
    capacity,
):
    batches = priority.shape[0]
    count = inputs.shape[0] // batches
    width = inputs.shape[1]
    experts = router_weight.shape[1]
    groups = lax.axis_size("expert")
    cap_pad = ceil_to(max(2, (5 * count + 2 * experts - 1) // (2 * experts)), 16)
    depth = qkv_weight.shape[0]
    both = ("dp", "expert")

    vectors = jnp.stack([gain_one, shift_one, gain_two, shift_two], axis=1)
    small = jnp.concatenate([vectors, router_weight], axis=1)
    small = jnp.pad(small, ((0, 0), (0, SMALL - small.shape[1])))
    pack = jnp.concatenate([qkv_weight, proj_weight, small], axis=1)
    slice_rows = depth // groups
    mine = lax.axis_index("expert")
    pack = lax.dynamic_slice_in_dim(pack, mine * slice_rows, slice_rows, axis=0)
    weight = lax.all_gather(pack, both, axis=0, tiled=True)

    bias_rows = jnp.pad(expert_bias, ((0, BIAS_ROWS - 1), (0, 0)))
    own_in = jnp.concatenate([expert_in[0], bias_rows], axis=0)
    own_out = expert_out[0]

    extra = SEQ_PAD - SEQ
    x = jnp.pad(inputs.reshape(batches, SEQ, width), ((0, 0), (0, extra), (0, 0)))
    grad = jnp.pad(out_grad.reshape(batches, SEQ, width), ((0, 0), (0, extra), (0, 0)))
    cols = jnp.concatenate(
        [routes.reshape(batches, SEQ, 2), priority.reshape(batches, SEQ, 2)], axis=2
    )
    cols = jnp.pad(cols, ((0, 0), (0, extra), (0, 0)), constant_values=-1)
    rows = jnp.swapaxes(cols, 1, 2)
    slot_rows, slot_cols = run_route(cols, rows, capacity, cap_pad)
    received, *saved, spread_in, spread_out = run_front(
        x, grad, weight, cols, slot_rows, own_in, own_out, experts, cap_pad
    )
    back, grad_in, grad_out = run_moe(received, own_in, own_out, spread_in, spread_out)
    spot = 4 * width
    if groups == PLANE:
        outputs, inputs_grad, qkv_grad, proj_grad, small_grad = run_reduce(
            x, grad, weight, cols, slot_cols, back, saved, experts
        )
        small_grad = lax.dynamic_slice_in_dim(
            small_grad, lax.axis_index("dp") * depth, depth, axis=1
        )
        vectors = [small_grad[k] for k in range(4)]
        router_grad = small_grad[4 : 4 + experts].T
    else:
        outputs, inputs_grad, dense = run_tail(
            x, grad, weight, cols, slot_cols, back, saved, experts
        )
        dense = lax.psum_scatter(dense, both, scatter_dimension=0, tiled=True)
        dense = lax.all_gather(dense, "expert", axis=0, tiled=True).astype(F32)
        qkv_grad = dense[:, : 3 * width]
        proj_grad = dense[:, 3 * width : spot]
        vectors = [dense[:, spot + k] for k in range(4)]
        router_grad = dense[:, spot + 4 : spot + 4 + experts]
    grad_in = grad_in.astype(F32)
    grad_out = grad_out.astype(F32)
    return (
        outputs[:, :SEQ].reshape(batches * SEQ, width),
        inputs_grad[:, :SEQ].reshape(batches * SEQ, width),
        vectors[0],
        vectors[1],
        qkv_grad,
        proj_grad,
        vectors[2],
        vectors[3],
        router_grad,
        grad_in[None, :width],
        grad_in[None, width],
        grad_out[None],
    )


def solution(mesh):
    token = P(("dp", "expert"), None)
    vector = P("dp")
    matrix = P("dp", None)
    return jax.shard_map(
        per_device,
        mesh=mesh,
        in_specs=(
            token,
            vector,
            vector,
            matrix,
            matrix,
            vector,
            vector,
            matrix,
            P("expert", None, "dp"),
            P("expert", "dp"),
            P("expert", "dp", None),
            token,
            token,
            token,
            P(("dp", "expert")),
        ),
        out_specs=(
            token,
            token,
            vector,
            vector,
            matrix,
            matrix,
            vector,
            vector,
            matrix,
            P("expert", None, "dp"),
            P("expert", "dp"),
            P("expert", "dp", None),
        ),
        check_vma=False,
    )
```

```python
import functools

import jax
import jax.numpy as jnp
from jax import lax
from jax.experimental import pallas as pl
from jax.experimental.pallas import tpu as pltpu
from jax.sharding import PartitionSpec as P

HEADS = 12
HEAD = 64
SEQ = 197
SEQ_PAD = 208
EPS = 1e-06
BF = jnp.bfloat16
F32 = jnp.float32
SMALL = 128
MESH = pl.DeviceIdType.MESH
EARLY = 2
TILE = 128
PLANE = 8
BIAS_ROWS = 16
NEG = -1e30
VMEM_LIMIT = 60 * 1024 * 1024
VMEM_MAX = 67043328


def ceil_to(value, step):
    return (value + step - 1) // step * step


def dot(a, b):
    return jnp.dot(a, b, preferred_element_type=F32)


def dot_nt(a, b):
    return lax.dot_general(a, b, (((1,), (1,)), ((), ())), preferred_element_type=F32)


def dot_tn(a, b):
    return lax.dot_general(a, b, (((0,), (0,)), ((), ())), preferred_element_type=F32)


def params(count=1):
    return pltpu.CompilerParams(
        dimension_semantics=("arbitrary",) * count, vmem_limit_bytes=VMEM_LIMIT
    )


class Line:
    def __init__(self, shards):
        self.shards = shards
        self.me = lax.axis_index("dp")
        self.has_below = self.me > 0
        self.has_above = self.me < shards - 1

    def greet(self, me, groups):
        barrier = pltpu.get_barrier_semaphore()
        for k in range(1, groups):
            pl.semaphore_signal(
                barrier, inc=1, device_id={"expert": lax.rem(me + k, groups)}, device_id_type=MESH
            )
        for k in range(1, self.shards):
            pl.semaphore_signal(
                barrier,
                inc=1,
                device_id={"dp": lax.rem(self.me + k, self.shards)},
                device_id_type=MESH,
            )
        pl.semaphore_wait(barrier, groups - 1 + self.shards - 1)

    def hop(self, way, round_id, source, target, send_sem, arrived):
        step = 1 - 2 * way
        slot = self.me - step * round_id
        if round_id == 0:
            body, bias, out = source
            tall = body.shape[0]
            moves = [
                (body, target[0].at[slot, pl.ds(0, tall)], 0),
                (bias, target[0].at[slot, pl.ds(tall, bias.shape[0])], 0),
                (out, target[1].at[slot], 1),
            ]
        else:
            moves = [(source[part].at[slot], target[part].at[slot], part) for part in range(2)]
        return [
            pltpu.make_async_remote_copy(
                src_ref=origin,
                dst_ref=place,
                send_sem=send_sem.at[way, round_id, k],
                recv_sem=arrived.at[slot, part],
                device_id={"dp": self.me + step},
                device_id_type=MESH,
            )
            for k, (origin, place, part) in enumerate(moves)
        ]

    def sends(self, way, round_id):
        if way == 0:
            return (self.me >= round_id) & self.has_above
        return (self.me + round_id < self.shards) & self.has_below

    def push(self, round_id, own, spread, send_sem, arrived, source=None):
        source = own if round_id == 0 else (source or spread)
        for way in range(2):

            @pl.when(self.sends(way, round_id))
            def _():
                for copy in self.hop(way, round_id, source, spread, send_sem, arrived):
                    copy.start()

    def drain(self, round_id, own, spread, send_sem, arrived, source=None):
        source = own if round_id == 0 else (source or spread)
        for way in range(2):

            @pl.when(self.sends(way, round_id))
            def _():
                for copy in self.hop(way, round_id, source, spread, send_sem, arrived):
                    copy.wait_send()

    def receive(self, round_id, spread, arrived):
        far = round_id + 1

        @pl.when(self.me >= far)
        def _():
            self.wait_slot(self.me - far, spread, arrived)

        @pl.when(self.me + far < self.shards)
        def _():
            self.wait_slot(self.me + far, spread, arrived)

    def wait_slot(self, slot, spread, arrived):
        for part in range(2):
            view = spread[part].at[slot]
            pltpu.make_async_copy(view, view, arrived.at[slot, part]).wait()


def route(cap_pad, cols_ref, rows_ref, limit_ref, slot_rows_ref, slot_cols_ref):
    for b in range(cols_ref.shape[0]):
        limit = limit_ref[b]
        col = [cols_ref[b, :, k : k + 1] for k in range(4)]
        row = [rows_ref[b, k : k + 1, :] for k in range(4)]
        for j in range(2):
            rank_row = 0
            rank_col = 0
            for k in range(2):
                hit = (col[k] == row[j]) & (col[2 + k] < row[2 + j])
                rank_row = rank_row + jnp.sum(hit.astype(jnp.int32), axis=0, keepdims=True)
                hit = (row[k] == col[j]) & (row[2 + k] < col[2 + j])
                rank_col = rank_col + jnp.sum(hit.astype(jnp.int32), axis=1, keepdims=True)
            keep_row = (rank_row < limit) & (row[j] >= 0)
            keep_col = (rank_col < limit) & (col[j] >= 0)
            slot_rows_ref[b, j : j + 1, :] = jnp.where(keep_row, row[j] * cap_pad + rank_row, -1)
            slot_cols_ref[b, :, j : j + 1] = jnp.where(keep_col, col[j] * cap_pad + rank_col, -1)


def norm_stats(values):
    average = jnp.mean(values, axis=-1, keepdims=True)
    centered = values - average
    spread = jnp.mean(centered * centered, axis=-1, keepdims=True)
    inverse = lax.rsqrt(spread + EPS)
    return centered * inverse, inverse


def front_kernel(
    experts,
    shards,
    limit_ref,
    cols_ref,
    rows_ref,
    raw_hbm,
    raw_grad_hbm,
    qkv_own,
    proj_own,
    small_own,
    own_body,
    own_bias,
    own_out,
    received_ref,
    x_hbm,
    grad_hbm,
    weight_hbm,
    qkv_hbm,
    mixed_hbm,
    hidden_hbm,
    one_hbm,
    two_hbm,
    lse_ref,
    probs_ref,
    slot_cols_ref,
    spread_in_ref,
    spread_out_ref,
    raw_ref,
    raw_grad_ref,
    x_ref,
    grad_ref,
    weight_ref,
    qkv_ref,
    mixed_ref,
    hidden_ref,
    one_ref,
    two_ref,
    small_ref,
    slot_rows_ref,
    send_ref,
    load_sem,
    store_sem,
    send_sem,
    arrived,
    rows_send,
    rows_recv,
    small_send,
    small_recv,
    line_send,
    piece_recv,
    plane_send,
    near_send,
):
    batches, rows, width = x_ref.shape
    groups = received_ref.shape[0]
    cap_pad = received_ref.shape[3]
    me = lax.axis_index("expert")
    line = Line(shards)
    z = line.me
    own = (own_body, own_bias, own_out)
    spread = (spread_in_ref, spread_out_ref)
    depth = width // shards
    piece_width = 4 * width // PLANE
    base = me // PLANE * PLANE
    spot = me - base
    core = lax.rem(me, 2)
    sibling = me + 1 - 2 * core
    chip = spot // 2
    chips = PLANE // 2
    cut = 3 * width // piece_width

    def remote(source, target, send, recv, peer):
        return pltpu.make_async_remote_copy(
            src_ref=source,
            dst_ref=target,
            send_sem=send,
            recv_sem=recv,
            device_id=peer,
            device_id_type=MESH,
        )

    def landed(view, sem):
        pltpu.make_async_copy(view, view, sem).wait()

    def rows_of(shard):
        return pl.ds(pl.multiple_of(shard * depth, depth), depth)

    def piece(shard, index):
        low = pl.multiple_of(index * piece_width, piece_width)
        return weight_ref.at[rows_of(shard), pl.ds(low, piece_width)]

    small_cols = pl.ds(4 * width, SMALL)

    raws = [
        pltpu.make_async_copy(raw_hbm, raw_ref, load_sem.at[0]),
        pltpu.make_async_copy(raw_grad_hbm, raw_grad_ref, load_sem.at[1]),
    ]
    mine = [
        pltpu.make_async_copy(
            qkv_own, weight_ref.at[rows_of(z), pl.ds(0, 3 * width)], load_sem.at[2]
        ),
        pltpu.make_async_copy(
            proj_own, weight_ref.at[rows_of(z), pl.ds(3 * width, width)], load_sem.at[3]
        ),
        pltpu.make_async_copy(small_own, weight_ref.at[rows_of(z), small_cols], load_sem.at[4]),
    ]
    for copy in mine:
        copy.start()
    for copy in raws:
        copy.start()
    line.greet(me, groups)
    for copy in mine:
        copy.wait()

    def small_copy(far):
        view = weight_ref.at[rows_of(z), small_cols]
        return remote(view, view, small_send.at[far], small_recv.at[z], {"dp": far})

    def line_copy(far):
        view = piece(z, spot)
        return remote(view, view, line_send.at[far], piece_recv.at[z, spot], {"dp": far})

    def plane_copy(shard, other):
        view = piece(shard, spot)
        peer = base + 2 * other + core
        return remote(
            view, view, plane_send.at[shard, other], piece_recv.at[shard, spot], {"expert": peer}
        )

    def near_copy(shard, other):
        index = 2 * other + core
        view = piece(shard, index)
        return remote(
            view, view, near_send.at[shard, other], piece_recv.at[shard, index], {"expert": sibling}
        )

    peers = [lax.rem(z + k, shards) for k in range(1, shards)]
    others = [lax.rem(chip + k, chips) for k in range(1, chips)]
    for far in peers:
        line_copy(far).start()
    for far in peers:
        small_copy(far).start()
    zero_rows = jnp.zeros((rows - SEQ, width), F32)

    def pad_image(image):
        x_ref[image, :SEQ] = raw_ref[image * SEQ : (image + 1) * SEQ]
        x_ref[image, SEQ:] = zero_rows
        pltpu.make_async_copy(x_ref.at[image], x_hbm.at[image], store_sem.at[0, image]).start()
        grad_ref[image, :SEQ] = raw_grad_ref[image * SEQ : (image + 1) * SEQ]
        grad_ref[image, SEQ:] = zero_rows
        pltpu.make_async_copy(
            grad_ref.at[image], grad_hbm.at[image], store_sem.at[1, image]
        ).start()

    for copy in raws:
        copy.wait()
    pad_image(0)
    for far in peers:
        landed(piece(far, spot), piece_recv.at[far, spot])
        for other in others:
            plane_copy(far, other).start()
        near_copy(far, chip).start()
    line.push(0, own, spread, send_sem, arrived)
    for image in range(1, batches):
        pad_image(image)
    slot_rows_ref[...] = jnp.full(slot_rows_ref.shape, -1, jnp.int32)
    slot_cols_ref[...] = jnp.full(slot_cols_ref.shape, -1, jnp.int32)
    route(cap_pad, cols_ref, rows_ref, limit_ref, slot_rows_ref, slot_cols_ref)
    for far in peers:
        for other in others:
            index = 2 * other + core
            landed(piece(far, index), piece_recv.at[far, index])
            near_copy(far, other).start()
    for far in peers:
        landed(weight_ref.at[rows_of(far), small_cols], small_recv.at[far])
        for k in range(chips):
            index = 2 * k + 1 - core
            landed(piece(far, index), piece_recv.at[far, index])
    weight_store = pltpu.make_async_copy(weight_ref, weight_hbm, load_sem.at[5])
    weight_store.start()
    small_ref[...] = weight_ref[:, 4 * width :].astype(F32).T

    def rows_copy(image, target):
        return remote(
            send_ref.at[image, target],
            received_ref.at[me, image],
            rows_send.at[image, target],
            rows_recv.at[me, image],
            {"expert": target},
        )

    saves = (
        (qkv_ref, qkv_hbm),
        (mixed_ref, mixed_hbm),
        (hidden_ref, hidden_hbm),
        (one_ref, one_hbm),
        (two_ref, two_hbm),
    )
    lane = lax.broadcasted_iota(jnp.int32, (1, 128), 1)
    key_ok = lax.broadcasted_iota(jnp.int32, (1, rows), 1) < SEQ
    slot = lax.broadcasted_iota(jnp.int32, (groups * cap_pad, 1), 0)
    scale = HEAD ** (-0.5)

    def do_image(index, carry):
        x = x_ref[index]
        hat, _ = norm_stats(x)
        one = (hat * small_ref[0:1, :] + small_ref[1:2, :]).astype(BF)
        one_ref[index] = one
        qkv_ref[index] = dot(one, weight_ref[:, : 3 * width]).astype(BF)
        lse = jnp.zeros((rows, 128), F32)
        for pair in range(HEADS // 2):
            low = pair * 128
            query = qkv_ref[index, :, low : low + 128]
            keys = qkv_ref[index, :, width + low : width + low + 128]
            values = qkv_ref[index, :, 2 * width + low : 2 * width + low + 128]
            total = None
            for side in range(2):
                part_of = (lane // HEAD) == side
                scores = dot_nt(jnp.where(part_of, query, jnp.zeros_like(query)), keys) * scale
                scores = jnp.where(key_ok, scores, NEG)
                highest = jnp.max(scores, axis=-1, keepdims=True)
                expo = jnp.exp(scores - highest)
                denom = jnp.sum(expo, axis=-1, keepdims=True)
                weights = (expo / denom).astype(BF)
                lse = jnp.where(lane == 2 * pair + side, highest + jnp.log(denom), lse)
                part = dot(weights, jnp.where(part_of, values, jnp.zeros_like(values)))
                total = part if total is None else total + part
            mixed_ref[index, :, low : low + 128] = total.astype(BF)
        lse_ref[index] = lse
        hidden = x + dot(mixed_ref[index], weight_ref[:, 3 * width : 4 * width])
        hidden_ref[index] = hidden
        hat, _ = norm_stats(hidden)
        two = (hat * small_ref[2:3, :] + small_ref[3:4, :]).astype(BF)
        two_ref[index] = two
        logits = dot(two, weight_ref[:, 4 * width :])
        in_router = (lane >= 4) & (lane < 4 + experts)
        logits = jnp.where(in_router, logits, NEG)
        expo = jnp.exp(logits - jnp.max(logits, axis=-1, keepdims=True))
        probs = expo / jnp.sum(expo, axis=-1, keepdims=True)
        probs_ref[index] = probs
        out_grad = grad_ref[index]
        both = None
        grads = None
        for j in range(2):
            gate = jnp.sum(
                jnp.where(lane - 4 == cols_ref[index, :, j : j + 1], probs, 0.0),
                axis=-1,
                keepdims=True,
            )
            pick = (slot == slot_rows_ref[index, j : j + 1, :]).astype(F32)
            both = pick if both is None else both + pick
            part = dot(pick.astype(BF), (gate * out_grad).astype(BF))
            grads = part if grads is None else grads + part
        sent = dot(both.astype(BF), two).astype(BF)
        send_ref[index, :, 0] = sent.reshape(groups, cap_pad, width)
        send_ref[index, :, 1] = grads.astype(BF).reshape(groups, cap_pad, width)
        for k in range(1, groups):
            rows_copy(index, lax.rem(me + k, groups)).start()
        pltpu.make_async_copy(
            send_ref.at[index, me], received_ref.at[me, index], rows_recv.at[me, index]
        ).start()
        for k, (here, there) in enumerate(saves):
            pltpu.make_async_copy(here.at[index], there.at[index], store_sem.at[2 + k, index]).start()
        return carry

    lax.fori_loop(0, batches, do_image, 0)

    rounds = min(EARLY, shards - 1)
    for round_id in range(1, rounds):
        line.receive(round_id - 1, spread, arrived)
        line.push(round_id, own, spread, send_sem, arrived)

    def finish(image, carry):
        for k in range(groups):
            source = lax.rem(me + k, groups)
            if k:
                rows_copy(image, source).wait_send()
            landed(received_ref.at[source, image], rows_recv.at[source, image])
        pltpu.make_async_copy(x_ref.at[image], x_hbm.at[image], store_sem.at[0, image]).wait()
        pltpu.make_async_copy(grad_ref.at[image], grad_hbm.at[image], store_sem.at[1, image]).wait()
        for k, (here, there) in enumerate(saves):
            pltpu.make_async_copy(here.at[image], there.at[image], store_sem.at[2 + k, image]).wait()
        return carry

    lax.fori_loop(0, batches, finish, 0)
    weight_store.wait()
    for far in peers:
        line_copy(far).wait_send()
        small_copy(far).wait_send()
        for other in others:
            plane_copy(far, other).wait_send()
        for k in range(chips):
            near_copy(far, k).wait_send()
    line.receive(rounds - 1, spread, arrived)
    for round_id in range(rounds):
        line.drain(round_id, own, spread, send_sem, arrived)


def run_front(raw, raw_grad, dense, own, cols, rows_first, limits, experts, cap_pad):
    batches, rows = cols.shape[:2]
    width = raw.shape[1]
    shards = lax.axis_size("dp")
    groups = lax.axis_size("expert")
    body, bias, out = own
    tall = body.shape[0] + bias.shape[0]
    anywhere = pl.BlockSpec(memory_space=pl.ANY)
    inside = pl.BlockSpec(memory_space=pltpu.VMEM)
    dma = pltpu.SemaphoreType.DMA
    chips = PLANE // 2

    def shape(*dims, dtype=BF):
        return jax.ShapeDtypeStruct((batches, rows) + dims, dtype)

    return pl.pallas_call(
        functools.partial(front_kernel, experts, shards),
        out_shape=(
            jax.ShapeDtypeStruct((groups, batches, 2, cap_pad, width), BF),
            shape(width, dtype=F32),
            shape(width, dtype=F32),
            jax.ShapeDtypeStruct((width, 4 * width + SMALL), BF),
            shape(3 * width),
            shape(width),
            shape(width, dtype=F32),
            shape(width),
            shape(width),
            shape(128, dtype=F32),
            shape(SMALL, dtype=F32),
            shape(8, dtype=jnp.int32),
            jax.ShapeDtypeStruct((shards, tall, body.shape[1]), BF),
            jax.ShapeDtypeStruct((shards,) + out.shape, BF),
        ),
        in_specs=[pl.BlockSpec(memory_space=pltpu.SMEM), inside, inside] + [anywhere] * 8,
        out_specs=(anywhere,) * 9 + (inside,) * 3 + (anywhere,) * 2,
        scratch_shapes=[
            pltpu.VMEM(raw.shape, F32),
            pltpu.VMEM(raw.shape, F32),
            pltpu.VMEM((batches, rows, width), F32),
            pltpu.VMEM((batches, rows, width), F32),
            pltpu.VMEM((width, 4 * width + SMALL), BF),
            pltpu.VMEM((batches, rows, 3 * width), BF),
            pltpu.VMEM((batches, rows, width), BF),
            pltpu.VMEM((batches, rows, width), F32),
            pltpu.VMEM((batches, rows, width), BF),
            pltpu.VMEM((batches, rows, width), BF),
            pltpu.VMEM((SMALL, width), F32),
            pltpu.VMEM((batches, 8, rows), jnp.int32),
            pltpu.VMEM((batches, groups, 2, cap_pad, width), BF),
            dma((6,)),
            dma((7, batches)),
            dma((2, EARLY, 3)),
            dma((shards, 2)),
            dma((batches, groups)),
            dma((groups, batches)),
            dma((shards,)),
            dma((shards,)),
            dma((shards,)),
            dma((shards, PLANE)),
            dma((shards, chips)),
            dma((shards, chips)),
        ],
        compiler_params=pltpu.CompilerParams(
            vmem_limit_bytes=VMEM_LIMIT, collective_id=1, has_side_effects=True
        ),
        cost_estimate=pl.CostEstimate(
            flops=8000000000, bytes_accessed=40000000, transcendentals=3000000
        ),
        name="front",
    )(limits, cols, rows_first, raw, raw_grad, *dense, *own)


def pieces_of(tall, span):
    half = ceil_to(tall // 2, 16)
    mid = ceil_to(span // 2, 16)
    return ((0, 0, half), (0, half, tall - half), (1, 0, mid), (1, mid, span - mid))


def moe_kernel(
    shards,
    groups,
    x_hbm,
    own_body,
    own_bias,
    own_out,
    spread_in_ref,
    spread_out_ref,
    back_ref,
    sum_in_ref,
    sum_out_ref,
    rows_ref,
    win_ref,
    wout_ref,
    y_acc,
    dx_acc,
    gin_acc,
    gout_acc,
    part_in_ref,
    part_out_ref,
    land_in_ref,
    land_out_ref,
    rows_sem,
    weight_send,
    arrived,
    sum_send,
    sum_recv,
    back_send,
    back_recv,
    final_sem,
):
    line = Line(shards)
    z = line.me
    me = lax.axis_index("expert")
    _, batches, _, cap_pad, width = rows_ref.shape
    _, tall, span = spread_in_ref.shape
    group = max(1, 512 // (batches * cap_pad))
    while groups % group:
        group -= 1
    blocks = groups // group
    rows = group * batches * cap_pad
    early = min(EARLY, shards - 1)
    spread = (win_ref, wout_ref)
    early_spread = (spread_in_ref, spread_out_ref)
    own = (own_body, own_bias, own_out)
    parts = (part_in_ref, part_out_ref)
    lands = (land_in_ref, land_out_ref)
    pieces = pieces_of(tall, span)

    for k in range(groups):
        source = lax.rem(me + k, groups)
        pltpu.make_async_copy(x_hbm.at[source], rows_ref.at[source], rows_sem.at[source]).start()
    mine = (
        (own_body, win_ref.at[z, pl.ds(0, width)], 0),
        (own_bias, win_ref.at[z, pl.ds(width, tall - width)], 0),
        (own_out, wout_ref.at[z], 1),
    )
    for here, there, part in mine:
        pltpu.make_async_copy(here, there, arrived.at[z, part]).start()
    for far in range(1, early + 1):
        for sign in (-1, 1):
            slot = z + sign * far

            @pl.when((slot >= 0) & (slot < shards))
            def _():
                for part in range(2):
                    pltpu.make_async_copy(
                        early_spread[part].at[slot], spread[part].at[slot], arrived.at[slot, part]
                    ).start()

    line.greet(me, groups)
    if early < shards - 1:
        line.push(early, own, spread, weight_send, arrived, early_spread)

    table = []
    for at in range(shards):
        near = sorted(range(shards), key=lambda q: (abs(q - at), q))
        table.append(near[1:] + near[:1])

    def quarter(step):
        total = 0
        for at in range(shards):
            for s in range(shards):
                hit = jnp.where((z == at) & (step == s), table[at][s], 0)
                total = total + hit
        return total

    def sum_copy(way, q, piece):
        kind, low, size = pieces[piece]
        if way == 0:
            slot = q
            peer = z + 1
        else:
            slot = jnp.where(q == z - 1, shards, q)
            peer = z - 1
        cut = pl.ds(low, size)
        return pltpu.make_async_remote_copy(
            src_ref=parts[kind].at[q, cut],
            dst_ref=lands[kind].at[slot, cut],
            send_sem=sum_send.at[way, q, piece],
            recv_sem=sum_recv.at[slot, piece],
            device_id={"dp": peer},
            device_id_type=MESH,
        )

    def take_sum(slot, q, piece):
        kind, low, size = pieces[piece]
        cut = pl.ds(low, size)
        view = lands[kind].at[slot, cut]
        pltpu.make_async_copy(view, view, sum_recv.at[slot, piece]).wait()
        parts[kind][q, cut] = (
            parts[kind][q, cut].astype(F32) + lands[kind][slot, cut].astype(F32)
        ).astype(BF)

    def back_copy(source):
        return pltpu.make_async_remote_copy(
            src_ref=rows_ref.at[source],
            dst_ref=back_ref.at[me],
            send_sem=back_send.at[source],
            recv_sem=back_recv.at[me],
            device_id={"expert": source},
            device_id_type=MESH,
        )

    def back_start(first):
        for k in range(group):
            source = first + k

            @pl.when(source != me)
            def _():
                back_copy(source).start()

            @pl.when(source == me)
            def _():
                pltpu.make_async_copy(
                    rows_ref.at[source], back_ref.at[source], back_recv.at[source]
                ).start()

    def block_first(block):
        return lax.rem(me // group + 1 + block, blocks) * group

    def do_step(step, carry):
        q = quarter(step)
        line.wait_slot(q, spread, arrived)
        for round_id in range(early, shards - 2):
            for way in range(2):
                forward = 1 - 2 * way

                @pl.when((q == z - forward * (round_id + 1)) & line.sends(way, round_id + 1))
                def _():
                    for copy in line.hop(way, round_id + 1, spread, spread, weight_send, arrived):
                        copy.start()

        def do_block(block, inner):
            lead = block_first(block)
            low = pl.multiple_of(lead * (batches * cap_pad), rows)
            here = pl.ds(low, rows)
            mine = pl.ds(lead, group)

            @pl.when(step == 0)
            def _():
                for k in range(group):
                    view = rows_ref.at[lead + k]
                    pltpu.make_async_copy(view, view, rows_sem.at[lead + k]).wait()

            x = rows_ref[mine, :, 0].reshape(rows, width)
            grad = rows_ref[mine, :, 1].reshape(rows, width)
            win = win_ref[q, :width, :]
            wout = wout_ref[q]
            pre = dot(x, win) + win_ref[q, width : width + 1, :].astype(F32)
            cdf = 0.5 * lax.erf(pre * (0.5**0.5)) + 0.5
            active = (pre * cdf).astype(BF)
            slope = cdf + pre * (jnp.exp(-0.5 * pre * pre) * 0.3989422804014327)
            d_pre = (dot_nt(grad, wout) * slope).astype(BF)
            y_part = dot(active, wout)
            dx_part = dot_nt(d_pre, win)

            @pl.when(step == 0)
            def _():
                y_acc[here, :] = y_part
                dx_acc[here, :] = dx_part

            @pl.when(step > 0)
            def _():
                y_acc[here, :] += y_part
                dx_acc[here, :] += dx_part

            gout = dot_tn(active, grad)
            gin = dot_tn(x, d_pre)
            gbias = jnp.sum(d_pre.astype(F32), axis=0, keepdims=True)

            @pl.when(block == 0)
            def _():
                gout_acc[...] = gout
                gin_acc[:width, :] = gin
                gin_acc[width : width + 1, :] = gbias

            @pl.when(block > 0)
            def _():
                gout_acc[...] += gout
                gin_acc[:width, :] += gin
                gin_acc[width : width + 1, :] += gbias

            @pl.when(step == shards - 1)
            def _():
                shape = (group, batches, cap_pad, width)
                rows_ref[mine, :, 0] = y_acc[here, :].astype(BF).reshape(shape)
                rows_ref[mine, :, 1] = dx_acc[here, :].astype(BF).reshape(shape)

                @pl.when(block > 0)
                def _():
                    back_start(block_first(block - 1))

            return inner

        lax.fori_loop(0, blocks, do_block, 0)

        @pl.when(step == shards - 1)
        def _():
            back_start(block_first(blocks - 1))

        part_in_ref[q, :width, :] = gin_acc[:width, :].astype(BF)
        part_in_ref[q, width:, :] = jnp.broadcast_to(
            gin_acc[width : width + 1, :].astype(BF), (tall - width, span)
        )
        part_out_ref[q] = gout_acc[...].astype(BF)

        @pl.when((z == 0) & (q > z))
        def _():
            for piece in range(len(pieces)):
                sum_copy(0, q, piece).start()

        @pl.when((z == shards - 1) & (q < z))
        def _():
            for piece in range(len(pieces)):
                sum_copy(1, q, piece).start()

        return carry

    lax.fori_loop(0, shards, do_step, 0)

    def do_forward(turn, carry):
        up = turn
        down = shards - 1 - turn
        for piece in range(len(pieces)):

            @pl.when((up > z) & (z > 0))
            def _():
                take_sum(up, up, piece)
                sum_copy(0, up, piece).start()

            @pl.when((down < z) & (z < shards - 1))
            def _():
                take_sum(down, down, piece)
                sum_copy(1, down, piece).start()

        return carry

    lax.fori_loop(1, shards, do_forward, 0)
    for piece in range(len(pieces)):

        @pl.when(line.has_below)
        def _():
            take_sum(z, z, piece)

        @pl.when(line.has_above)
        def _():
            take_sum(shards, z, piece)

    finals = [
        pltpu.make_async_copy(part_in_ref.at[z], sum_in_ref, final_sem.at[0]),
        pltpu.make_async_copy(part_out_ref.at[z], sum_out_ref, final_sem.at[1]),
    ]
    for copy in finals:
        copy.start()

    def finish_sum(q, carry):
        @pl.when((q > z) & line.has_above)
        def _():
            for piece in range(len(pieces)):
                sum_copy(0, q, piece).wait_send()

        @pl.when((q < z) & line.has_below)
        def _():
            for piece in range(len(pieces)):
                sum_copy(1, q, piece).wait_send()

        return carry

    lax.fori_loop(0, shards, finish_sum, 0)
    for round_id in range(early, shards - 1):
        line.drain(round_id, own, spread, weight_send, arrived)
    for k in range(groups):
        source = lax.rem(me + k, groups)
        if k:
            back_copy(source).wait_send()
        view = back_ref.at[source]
        pltpu.make_async_copy(view, view, back_recv.at[source]).wait()
    for copy in finals:
        copy.wait()


def run_moe(received, own, spread_in, spread_out):
    groups, batches, _, cap_pad, width = received.shape
    shards, tall, span = spread_in.shape
    total = groups * batches * cap_pad
    count = len(pieces_of(tall, span))
    anywhere = pl.BlockSpec(memory_space=pl.ANY)
    return pl.pallas_call(
        functools.partial(moe_kernel, shards, groups),
        out_shape=(
            jax.ShapeDtypeStruct(received.shape, BF),
            jax.ShapeDtypeStruct((tall, span), BF),
            jax.ShapeDtypeStruct((span, width), BF),
        ),
        in_specs=[anywhere] * 6,
        out_specs=(anywhere,) * 3,
        scratch_shapes=[
            pltpu.VMEM(received.shape, BF),
            pltpu.VMEM((shards, tall, span), BF),
            pltpu.VMEM((shards, span, width), BF),
            pltpu.VMEM((total, width), F32),
            pltpu.VMEM((total, width), F32),
            pltpu.VMEM((ceil_to(width + 1, 8), span), F32),
            pltpu.VMEM((span, width), F32),
            pltpu.VMEM((shards, tall, span), BF),
            pltpu.VMEM((shards, span, width), BF),
            pltpu.VMEM((shards + 1, tall, span), BF),
            pltpu.VMEM((shards + 1, span, width), BF),
            pltpu.SemaphoreType.DMA((groups,)),
            pltpu.SemaphoreType.DMA((2, shards, 2)),
            pltpu.SemaphoreType.DMA((shards, 2)),
            pltpu.SemaphoreType.DMA((2, shards, count)),
            pltpu.SemaphoreType.DMA((shards + 1, count)),
            pltpu.SemaphoreType.DMA((groups,)),
            pltpu.SemaphoreType.DMA((groups,)),
            pltpu.SemaphoreType.DMA((2,)),
        ],
        compiler_params=pltpu.CompilerParams(
            vmem_limit_bytes=VMEM_MAX, collective_id=2, has_side_effects=True
        ),
        cost_estimate=pl.CostEstimate(
            flops=12 * total * width * span * shards,
            bytes_accessed=60000000,
            transcendentals=2 * total * span * shards,
        ),
        name="moe",
    )(received, *own, spread_in, spread_out)


def tail_kernel(
    experts,
    x_ref,
    grad_ref,
    weight_ref,
    cols_ref,
    slot_cols_ref,
    back_ref,
    qkv_ref,
    mixed_ref,
    lse_ref,
    hidden_ref,
    one_ref,
    two_ref,
    probs_ref,
    out_ref,
    dx_ref,
    dense_ref,
    small_ref,
    sums_ref,
    d_qkv_ref,
    d_branch_ref,
    d_logits_ref,
    one_all,
    two_all,
    mixed_all,
):
    width = x_ref.shape[-1]
    rows = x_ref.shape[1]
    index = pl.program_id(0)

    @pl.when(index == 0)
    def _():
        small_ref[...] = weight_ref[:, 4 * width :].astype(F32).T
        sums_ref[...] = jnp.zeros_like(sums_ref)

    here = pl.ds(pl.multiple_of(index * rows, rows), rows)
    one_all[here, :] = one_ref[0]
    two_all[here, :] = two_ref[0]
    mixed_all[here, :] = mixed_ref[0]
    out_grad = grad_ref[0]
    hidden = hidden_ref[0]
    probs = probs_ref[0]
    lane = lax.broadcasted_iota(jnp.int32, (1, 128), 1)
    slots = back_ref.shape[0] * back_ref.shape[3]
    slot = lax.broadcasted_iota(jnp.int32, (1, slots), 1)
    answers = back_ref[:, 0, 0].reshape(slots, width)
    answer_grads = back_ref[:, 0, 1].reshape(slots, width)
    result = hidden
    d_probs = jnp.zeros_like(probs)
    both = None
    for j in range(2):
        pick = (slot == slot_cols_ref[0, :, j : j + 1]).astype(F32)
        both = pick if both is None else both + pick
        chosen = lane - 4 == cols_ref[0, :, j : j + 1]
        gate = jnp.sum(jnp.where(chosen, probs, 0.0), axis=-1, keepdims=True)
        picked = dot(pick.astype(BF), answers)
        result = result + gate * picked
        d_gate = jnp.sum(picked * out_grad, axis=-1, keepdims=True)
        d_probs = jnp.where(chosen, d_gate, d_probs)
    out_ref[0] = result
    d_logits = probs * (d_probs - jnp.sum(d_probs * probs, axis=-1, keepdims=True))
    d_logits = d_logits.astype(BF)
    d_logits_ref[here, :] = d_logits
    d_two = dot(both.astype(BF), answer_grads) + dot_nt(d_logits, weight_ref[:, 4 * width :])
    hat, inverse = norm_stats(hidden)
    sums_ref[2:3, :] += jnp.sum(d_two * hat, axis=0, keepdims=True)
    sums_ref[3:4, :] += jnp.sum(d_two, axis=0, keepdims=True)
    d_hat = d_two * small_ref[2:3, :]
    d_hidden = out_grad + inverse * (
        d_hat
        - jnp.mean(d_hat, axis=-1, keepdims=True)
        - hat * jnp.mean(d_hat * hat, axis=-1, keepdims=True)
    )
    d_branch = d_hidden.astype(BF)
    d_branch_ref[here, :] = d_branch
    d_mixed_all = dot_nt(d_branch, weight_ref[:, 3 * width : 4 * width]).astype(BF)
    key_ok = lax.broadcasted_iota(jnp.int32, (1, rows), 1) < SEQ
    scale = HEAD ** (-0.5)
    for pair in range(HEADS // 2):
        low = pair * 128
        query = qkv_ref[0, :, low : low + 128]
        keys = qkv_ref[0, :, width + low : width + low + 128]
        values = qkv_ref[0, :, 2 * width + low : 2 * width + low + 128]
        d_mixed = d_mixed_all[:, low : low + 128]
        d_query = d_keys = d_values = None
        for side in range(2):
            mine = (lane // HEAD) == side
            head = 2 * pair + side

            def own(array):
                return jnp.where(mine, array, jnp.zeros_like(array))

            my_query = own(query)
            my_keys = own(keys)
            my_d_mixed = own(d_mixed)
            scores = dot_nt(my_query, keys) * scale
            scores = jnp.where(key_ok, scores, NEG)
            probs_h = jnp.exp(scores - lse_ref[0, :, head : head + 1])
            d_weights = dot_nt(my_d_mixed, values)
            row_terms = jnp.sum(d_weights * probs_h, axis=-1, keepdims=True)
            d_scores = (probs_h * (d_weights - row_terms) * scale).astype(BF)
            parts = (
                dot(d_scores, my_keys),
                dot_tn(d_scores, my_query),
                dot_tn(probs_h.astype(BF), my_d_mixed),
            )
            if side == 0:
                d_query, d_keys, d_values = parts
            else:
                d_query, d_keys, d_values = (
                    d_query + parts[0],
                    d_keys + parts[1],
                    d_values + parts[2],
                )
        d_qkv_ref[here, low : low + 128] = d_query.astype(BF)
        d_qkv_ref[here, width + low : width + low + 128] = d_keys.astype(BF)
        d_qkv_ref[here, 2 * width + low : 2 * width + low + 128] = d_values.astype(BF)
    d_one = dot_nt(d_qkv_ref[here, :], weight_ref[:, : 3 * width])
    hat, inverse = norm_stats(x_ref[0])
    sums_ref[0:1, :] += jnp.sum(d_one * hat, axis=0, keepdims=True)
    sums_ref[1:2, :] += jnp.sum(d_one, axis=0, keepdims=True)
    d_hat = d_one * small_ref[0:1, :]
    dx_ref[0] = d_hidden + inverse * (
        d_hat
        - jnp.mean(d_hat, axis=-1, keepdims=True)
        - hat * jnp.mean(d_hat * hat, axis=-1, keepdims=True)
    )

    @pl.when(index == pl.num_programs(0) - 1)
    def _():
        dense_ref[:, 4 * width :] = (dot_tn(two_all[...], d_logits_ref[...]) + sums_ref[...].T).astype(BF)
        dense_ref[:, 3 * width : 4 * width] = dot_tn(mixed_all[...], d_branch_ref[...]).astype(BF)
        for part in range(3):
            cut = slice(part * width, (part + 1) * width)
            dense_ref[:, cut] = dot_tn(one_all[...], d_qkv_ref[:, cut]).astype(BF)


def run_tail(x, grad, weight, cols, slot_cols, back, saved, experts):
    batches, rows, width = x.shape
    total = weight.shape[1]
    cap_pad = back.shape[3]
    qkv, mixed, lse, hidden, one, two, probs = saved

    def block(*shape):
        return pl.BlockSpec((1,) + shape, lambda i: (i,) + (0,) * len(shape))

    return pl.pallas_call(
        functools.partial(tail_kernel, experts),
        grid=(batches,),
        out_shape=(
            jax.ShapeDtypeStruct(x.shape, F32),
            jax.ShapeDtypeStruct(x.shape, F32),
            jax.ShapeDtypeStruct((width, total), BF),
        ),
        in_specs=[
            block(rows, width),
            block(rows, width),
            pl.BlockSpec((width, total), lambda i: (0, 0), pipeline_mode=pl.Buffered(1)),
            block(rows, 4),
            block(rows, 8),
            pl.BlockSpec((experts, 1, 2, cap_pad, width), lambda i: (0, i, 0, 0, 0)),
            block(rows, 3 * width),
            block(rows, width),
            block(rows, 128),
            block(rows, width),
            block(rows, width),
            block(rows, width),
            block(rows, SMALL),
        ],
        out_specs=(
            block(rows, width),
            block(rows, width),
            pl.BlockSpec((width, total), lambda i: (0, 0), pipeline_mode=pl.Buffered(1)),
        ),
        scratch_shapes=[
            pltpu.VMEM((SMALL, width), F32),
            pltpu.VMEM((SMALL, width), F32),
            pltpu.VMEM((batches * rows, 3 * width), BF),
            pltpu.VMEM((batches * rows, width), BF),
            pltpu.VMEM((batches * rows, SMALL), BF),
            pltpu.VMEM((batches * rows, width), BF),
            pltpu.VMEM((batches * rows, width), BF),
            pltpu.VMEM((batches * rows, width), BF),
        ],
        compiler_params=params(),
        cost_estimate=pl.CostEstimate(
            flops=16000000000, bytes_accessed=50000000, transcendentals=2000000
        ),
        name="tail",
    )(x, grad, weight, cols, slot_cols, back, qkv, mixed, lse, hidden, one, two, probs)


def reduce_kernel(
    experts,
    shards,
    cols_ref,
    slot_cols_ref,
    lse_ref,
    probs_ref,
    x_hbm,
    grad_hbm,
    weight_hbm,
    back_hbm,
    qkv_hbm,
    mixed_hbm,
    hidden_hbm,
    one_hbm,
    two_hbm,
    out_hbm,
    dx_hbm,
    qkv_grad_ref,
    proj_grad_ref,
    small_grad_ref,
    x_ref,
    grad_ref,
    weight_ref,
    back_ref,
    qkv_ref,
    mixed_ref,
    hidden_ref,
    one_ref,
    two_ref,
    small_ref,
    sums_ref,
    one_flip,
    d_qkv_ref,
    d_branch_ref,
    d_mixed_ref,
    d_logits_ref,
    tiles_ref,
    near_ref,
    plane_land,
    plane_ref,
    line_land,
    final_ref,
    small_land,
    small_far,
    load_sem,
    store_sem,
    near_send,
    near_recv,
    plane_send,
    plane_recv,
    line_send,
    line_recv,
    final_send,
    final_recv,
    small_send,
    small_recv,
):
    batches, rows, width = x_ref.shape
    z = lax.axis_index("dp")
    me = lax.axis_index("expert")
    core = lax.rem(me, 2)
    sibling = me + 1 - 2 * core
    chip = me // 2
    chips = PLANE // 2
    pairs = HEADS // 2
    depth = width // shards
    head_tiles = width // TILE
    own_tiles = (4 * width // TILE) // PLANE

    def loads(kind, image):
        pair = {
            0: (back_hbm.at[:, image], back_ref.at[:, image]),
            1: (hidden_hbm.at[image], hidden_ref.at[image]),
            2: (grad_hbm.at[image], grad_ref.at[image]),
            3: (mixed_hbm.at[image], mixed_ref.at[pl.ds(image * rows, rows)]),
            4: (two_hbm.at[image], two_ref.at[pl.ds(image * rows, rows)]),
            5: (one_hbm.at[image], one_ref.at[pl.ds(image * rows, rows)]),
            6: (qkv_hbm.at[image], qkv_ref.at[image]),
            7: (x_hbm.at[image], x_ref.at[image]),
        }[kind]
        return pltpu.make_async_copy(pair[0], pair[1], load_sem.at[kind, image])

    weight_load = pltpu.make_async_copy(weight_hbm, weight_ref, load_sem.at[8, 0])
    for kind in range(3):
        loads(kind, 0).start()
    weight_load.start()
    for image in range(1, batches):
        for kind in range(3):
            loads(kind, image).start()
    for kind in range(3, 8):
        for image in range(batches):
            loads(kind, image).start()

    barrier = pltpu.get_barrier_semaphore()
    for k in range(1, PLANE):
        pl.semaphore_signal(
            barrier, inc=1, device_id={"expert": lax.rem(me + k, PLANE)}, device_id_type=MESH
        )
    for k in range(1, shards):
        pl.semaphore_signal(
            barrier, inc=1, device_id={"dp": lax.rem(z + k, shards)}, device_id_type=MESH
        )
    pl.semaphore_wait(barrier, PLANE - 1 + shards - 1)

    def remote(source, target, send_sem, recv_sem, peer):
        return pltpu.make_async_remote_copy(
            src_ref=source,
            dst_ref=target,
            send_sem=send_sem,
            recv_sem=recv_sem,
            device_id=peer,
            device_id_type=MESH,
        )

    def landed(view, sem):
        pltpu.make_async_copy(view, view, sem).wait()

    def near_copy(tile):
        return remote(
            tiles_ref.at[tile],
            near_ref.at[tile],
            near_send.at[tile],
            near_recv.at[tile],
            {"expert": sibling},
        )

    def plane_copy(tile):
        return remote(
            tiles_ref.at[tile],
            plane_land.at[tile // PLANE, chip],
            plane_send.at[tile],
            plane_recv.at[tile // PLANE, chip],
            {"expert": lax.rem(tile, PLANE)},
        )

    def line_copy(k, far):
        return remote(
            plane_ref.at[k, pl.ds(pl.multiple_of(far * depth, depth), depth)],
            line_land.at[k, z],
            line_send.at[k, far],
            line_recv.at[k, z],
            {"dp": far},
        )

    def final_copy(k, peer):
        tile = me + PLANE * k
        return remote(
            final_ref.at[tile],
            final_ref.at[tile],
            final_send.at[k, peer],
            final_recv.at[tile],
            {"expert": peer},
        )

    def leave(tile):
        @pl.when(lax.rem(tile, 2) != core)
        def _():
            near_copy(tile).start()

    def combine(tile):
        @pl.when(lax.rem(tile, 2) == core)
        def _():
            landed(near_ref.at[tile], near_recv.at[tile])
            tiles_ref[tile] = (
                tiles_ref[tile].astype(F32) + near_ref[tile].astype(F32)
            ).astype(BF)

            @pl.when(lax.rem(tile, PLANE) != me)
            def _():
                plane_copy(tile).start()

    def plane_sum(k):
        total = tiles_ref[me + PLANE * k].astype(F32)
        for j in range(1, chips):
            far = lax.rem(chip + j, chips)
            landed(plane_land.at[k, far], plane_recv.at[k, far])
            total = total + plane_land[k, far].astype(F32)
        plane_ref[k] = total.astype(BF)
        for j in range(1, shards):
            line_copy(k, lax.rem(z + j, shards)).start()

    def line_sum(k):
        mine = pl.ds(pl.multiple_of(z * depth, depth), depth)
        total = plane_ref[k, mine].astype(F32)
        for j in range(1, shards):
            far = lax.rem(z + j, shards)
            landed(line_land.at[k, far], line_recv.at[k, far])
            total = total + line_land[k, far].astype(F32)
        final_ref[me + PLANE * k] = total.astype(BF)
        for j in range(1, PLANE):
            final_copy(k, lax.rem(me + j, PLANE)).start()

    lane = lax.broadcasted_iota(jnp.int32, (1, 128), 1)
    groups, _, _, cap_pad, _ = back_ref.shape
    slots = groups * cap_pad
    slot = lax.broadcasted_iota(jnp.int32, (1, slots), 1)
    sums_ref[...] = jnp.zeros_like(sums_ref)

    def phase_one(image, carry):
        here = pl.ds(pl.multiple_of(image * rows, rows), rows)
        for kind in range(3):
            view = (back_ref.at[:, image], hidden_ref.at[image], grad_ref.at[image])[kind]
            landed(view, load_sem.at[kind, image])

        @pl.when(image == 0)
        def _():
            weight_load.wait()
            small_ref[...] = weight_ref[:, 4 * width :].astype(F32).T

        out_grad = grad_ref[image]
        hidden = hidden_ref[image]
        probs = probs_ref[image]
        answers = back_ref[:, image, 0].reshape(slots, width)
        answer_grads = back_ref[:, image, 1].reshape(slots, width)
        result = hidden
        d_probs = jnp.zeros_like(probs)
        both = None
        for j in range(2):
            pick = (slot == slot_cols_ref[image, :, j : j + 1]).astype(F32)
            both = pick if both is None else both + pick
            chosen = lane - 4 == cols_ref[image, :, j : j + 1]
            gate = jnp.sum(jnp.where(chosen, probs, 0.0), axis=-1, keepdims=True)
            picked = dot(pick.astype(BF), answers)
            result = result + gate * picked
            d_gate = jnp.sum(picked * out_grad, axis=-1, keepdims=True)
            d_probs = jnp.where(chosen, d_gate, d_probs)
        d_logits = probs * (d_probs - jnp.sum(d_probs * probs, axis=-1, keepdims=True))
        d_logits = d_logits.astype(BF)
        d_logits_ref[here, :] = d_logits
        d_two = dot(both.astype(BF), answer_grads) + dot_nt(d_logits, weight_ref[:, 4 * width :])
        hat, inverse = norm_stats(hidden)
        sums_ref[2:3, :] += jnp.sum(d_two * hat, axis=0, keepdims=True)
        sums_ref[3:4, :] += jnp.sum(d_two, axis=0, keepdims=True)
        d_hat = d_two * small_ref[2:3, :]
        d_hidden = out_grad + inverse * (
            d_hat
            - jnp.mean(d_hat, axis=-1, keepdims=True)
            - hat * jnp.mean(d_hat * hat, axis=-1, keepdims=True)
        )
        d_branch = d_hidden.astype(BF)
        d_branch_ref[here, :] = d_branch
        d_mixed_ref[here, :] = dot_nt(d_branch, weight_ref[:, 3 * width : 4 * width]).astype(BF)
        grad_ref[image] = d_hidden
        hidden_ref[image] = result
        pltpu.make_async_copy(hidden_ref.at[image], out_hbm.at[image], store_sem.at[0, image]).start()
        return carry

    lax.fori_loop(0, batches, phase_one, 0)
    for kind, view in ((3, mixed_ref), (4, two_ref), (5, one_ref)):
        for image in range(batches):
            landed(view.at[pl.ds(image * rows, rows)], load_sem.at[kind, image])
    proj = dot_tn(mixed_ref[...], d_branch_ref[...]).astype(BF)
    for tile in range(head_tiles):
        tiles_ref[tile] = proj[:, tile * TILE : (tile + 1) * TILE]
    for tile in range(head_tiles):
        leave(tile)
    one_flip[...] = one_ref[...].T
    flipped = dot_tn(d_logits_ref[...], two_ref[...])
    for image in range(batches):
        landed(qkv_ref.at[image], load_sem.at[6, image])

    key_ok = lax.broadcasted_iota(jnp.int32, (1, rows), 1) < SEQ
    scale = HEAD ** (-0.5)

    def phase_two(pair, carry):
        low = pl.multiple_of(pair * TILE, TILE)
        spots = [pl.ds(pl.multiple_of(part * width + low, TILE), TILE) for part in range(3)]
        for image in range(batches):
            here = pl.ds(image * rows, rows)
            query, keys, values = (qkv_ref[image, :, spot] for spot in spots)
            d_mixed = d_mixed_ref[here, pl.ds(low, TILE)]
            total = [None, None, None]
            for side in range(2):
                mine = (lane // HEAD) == side

                def own(array):
                    return jnp.where(mine, array, jnp.zeros_like(array))

                my_query = own(query)
                my_d_mixed = own(d_mixed)
                scores = dot_nt(my_query, keys) * scale
                scores = jnp.where(key_ok, scores, NEG)
                log_total = jnp.sum(
                    jnp.where(lane == 2 * pair + side, lse_ref[image], 0.0), axis=-1, keepdims=True
                )
                probs_h = jnp.exp(scores - log_total)
                d_weights = dot_nt(my_d_mixed, values)
                row_terms = jnp.sum(d_weights * probs_h, axis=-1, keepdims=True)
                d_scores = (probs_h * (d_weights - row_terms) * scale).astype(BF)
                fresh = (
                    dot(d_scores, own(keys)),
                    dot_tn(d_scores, my_query),
                    dot_tn(probs_h.astype(BF), my_d_mixed),
                )
                total = [new if old is None else old + new for old, new in zip(total, fresh)]
            for part in range(3):
                d_qkv_ref[here, spots[part]] = total[part].astype(BF)
        first = head_tiles + 3 * pair
        for part in range(3):
            tiles_ref[first + part] = dot(one_flip[...], d_qkv_ref[:, spots[part]]).astype(BF)
        for part in range(3):
            leave(first + part)

        @pl.when(pair == 0)
        def _():
            for tile in range(head_tiles):
                combine(tile)

        @pl.when(pair > 0)
        def _():
            for part in range(3):
                combine(first - 3 + part)

        @pl.when(pair == pairs - 3)
        def _():
            plane_sum(0)

        @pl.when(pair == pairs - 1)
        def _():
            line_sum(0)
            plane_sum(1)

        return carry

    lax.fori_loop(0, pairs, phase_two, 0)
    for part in range(3):
        combine(head_tiles + 3 * (pairs - 1) + part)

    for image in range(batches):
        landed(x_ref.at[image], load_sem.at[7, image])

    def phase_three(image, carry):
        here = pl.ds(pl.multiple_of(image * rows, rows), rows)
        d_one = dot_nt(d_qkv_ref[here, :], weight_ref[:, : 3 * width])
        hat, inverse = norm_stats(x_ref[image])
        sums_ref[0:1, :] += jnp.sum(d_one * hat, axis=0, keepdims=True)
        sums_ref[1:2, :] += jnp.sum(d_one, axis=0, keepdims=True)
        d_hat = d_one * small_ref[0:1, :]
        x_ref[image] = grad_ref[image] + inverse * (
            d_hat
            - jnp.mean(d_hat, axis=-1, keepdims=True)
            - hat * jnp.mean(d_hat * hat, axis=-1, keepdims=True)
        )
        pltpu.make_async_copy(x_ref.at[image], dx_hbm.at[image], store_sem.at[1, image]).start()

        @pl.when(image == batches // 2 - 1)
        def _():
            line_sum(1)
            plane_sum(2)

        return carry

    lax.fori_loop(0, batches, phase_three, 0)

    def small_copy(k):
        peer = lax.rem(me + k, PLANE)
        return remote(
            sums_ref, small_land.at[me], small_send.at[peer], small_recv.at[me], {"expert": peer}
        )

    def small_far_copy(k):
        peer = lax.rem(z + k, shards)
        return remote(
            small_land.at[me],
            small_far.at[z],
            small_send.at[PLANE + peer],
            small_recv.at[PLANE + z],
            {"dp": peer},
        )

    sums_ref[...] += flipped[: sums_ref.shape[0]]
    for k in range(1, PLANE):
        small_copy(k).start()
    line_sum(2)
    total = sums_ref[...]
    for k in range(1, PLANE):
        peer = lax.rem(me + k, PLANE)
        landed(small_land.at[peer], small_recv.at[peer])
        total = total + small_land[peer]
    small_land[me] = total
    for k in range(1, shards):
        small_far_copy(k).start()
    for k in range(1, shards):
        peer = lax.rem(z + k, shards)
        landed(small_far.at[peer], small_recv.at[PLANE + peer])
        total = total + small_far[peer]
    small_grad_ref[...] = total

    def finish(tile, carry):
        @pl.when(lax.rem(tile, PLANE) != me)
        def _():
            landed(final_ref.at[tile], final_recv.at[tile])

        @pl.when(lax.rem(tile, 2) != core)
        def _():
            near_copy(tile).wait_send()

        @pl.when((lax.rem(tile, 2) == core) & (lax.rem(tile, PLANE) != me))
        def _():
            plane_copy(tile).wait_send()

        return carry

    lax.fori_loop(0, 4 * head_tiles, finish, 0)
    for tile in range(head_tiles):
        proj_grad_ref[:, tile * TILE : (tile + 1) * TILE] = final_ref[tile].astype(F32)
    for pair in range(pairs):
        for part in range(3):
            low = part * width + pair * TILE
            qkv_grad_ref[:, low : low + TILE] = final_ref[head_tiles + 3 * pair + part].astype(F32)
    for k in range(own_tiles):
        for j in range(1, shards):
            line_copy(k, lax.rem(z + j, shards)).wait_send()
        for j in range(1, PLANE):
            final_copy(k, lax.rem(me + j, PLANE)).wait_send()
    for k in range(1, PLANE):
        small_copy(k).wait_send()
    for k in range(1, shards):
        small_far_copy(k).wait_send()
    for image in range(batches):
        pltpu.make_async_copy(hidden_ref.at[image], out_hbm.at[image], store_sem.at[0, image]).wait()
        pltpu.make_async_copy(x_ref.at[image], dx_hbm.at[image], store_sem.at[1, image]).wait()


def run_reduce(x, grad, weight, cols, slot_cols, back, saved, experts):
    batches, rows, width = x.shape
    total = weight.shape[1]
    shards = lax.axis_size("dp")
    qkv, mixed, lse, hidden, one, two, probs = saved
    depth = width // shards
    tiles = 4 * width // TILE
    own_tiles = tiles // PLANE
    small_rows = ceil_to(4 + experts, 8)
    anywhere = pl.BlockSpec(memory_space=pl.ANY)
    inside = pl.BlockSpec(memory_space=pltpu.VMEM)
    dma = pltpu.SemaphoreType.DMA
    return pl.pallas_call(
        functools.partial(reduce_kernel, experts, shards),
        out_shape=(
            jax.ShapeDtypeStruct(x.shape, F32),
            jax.ShapeDtypeStruct(x.shape, F32),
            jax.ShapeDtypeStruct((depth, 3 * width), F32),
            jax.ShapeDtypeStruct((depth, width), F32),
            jax.ShapeDtypeStruct((small_rows, width), F32),
        ),
        in_specs=[inside] * 4 + [anywhere] * 9,
        out_specs=(anywhere, anywhere, inside, inside, inside),
        scratch_shapes=[
            pltpu.VMEM(x.shape, F32),
            pltpu.VMEM(x.shape, F32),
            pltpu.VMEM(weight.shape, BF),
            pltpu.VMEM(back.shape, BF),
            pltpu.VMEM(qkv.shape, BF),
            pltpu.VMEM((batches * rows, width), BF),
            pltpu.VMEM(x.shape, F32),
            pltpu.VMEM((batches * rows, width), BF),
            pltpu.VMEM((batches * rows, width), BF),
            pltpu.VMEM((SMALL, width), F32),
            pltpu.VMEM((small_rows, width), F32),
            pltpu.VMEM((width, batches * rows), BF),
            pltpu.VMEM((batches * rows, 3 * width), BF),
            pltpu.VMEM((batches * rows, width), BF),
            pltpu.VMEM((batches * rows, width), BF),
            pltpu.VMEM((batches * rows, SMALL), BF),
            pltpu.VMEM((tiles, width, TILE), BF),
            pltpu.VMEM((tiles, width, TILE), BF),
            pltpu.VMEM((own_tiles, PLANE // 2, width, TILE), BF),
            pltpu.VMEM((own_tiles, width, TILE), BF),
            pltpu.VMEM((own_tiles, shards, depth, TILE), BF),
            pltpu.VMEM((tiles, depth, TILE), BF),
            pltpu.VMEM((PLANE, small_rows, width), F32),
            pltpu.VMEM((shards, small_rows, width), F32),
            dma((9, batches)),
            dma((2, batches)),
            dma((tiles,)),
            dma((tiles,)),
            dma((tiles,)),
            dma((own_tiles, PLANE // 2)),
            dma((own_tiles, shards)),
            dma((own_tiles, shards)),
            dma((own_tiles, PLANE)),
            dma((tiles,)),
            dma((PLANE + shards,)),
            dma((PLANE + shards,)),
        ],
        compiler_params=pltpu.CompilerParams(
            vmem_limit_bytes=VMEM_MAX, collective_id=3, has_side_effects=True
        ),
        cost_estimate=pl.CostEstimate(
            flops=16000000000, bytes_accessed=50000000, transcendentals=2000000
        ),
        name="tail",
    )(cols, slot_cols, lse, probs, x, grad, weight, back, qkv, mixed, hidden, one, two)


def per_device(
    inputs,
    gain_one,
    shift_one,
    qkv_weight,
    proj_weight,
    gain_two,
    shift_two,
    router_weight,
    expert_in,
    expert_bias,
    expert_out,
    out_grad,
    routes,
    priority,
    capacity,
):
    batches = priority.shape[0]
    count = inputs.shape[0] // batches
    width = inputs.shape[1]
    experts = router_weight.shape[1]
    groups = lax.axis_size("expert")
    cap_pad = ceil_to(max(2, (5 * count + 2 * experts - 1) // (2 * experts)), 16)
    depth = qkv_weight.shape[0]
    both = ("dp", "expert")

    vectors = jnp.stack([gain_one, shift_one, gain_two, shift_two], axis=1)
    small = jnp.concatenate([vectors, router_weight], axis=1)
    small = jnp.pad(small, ((0, 0), (0, SMALL - small.shape[1])))
    dense = (qkv_weight, proj_weight, small)
    own = (expert_in[0], jnp.pad(expert_bias, ((0, BIAS_ROWS - 1), (0, 0))), expert_out[0])
    cols = jnp.concatenate([routes, priority.reshape(batches * SEQ, 2)], axis=1)
    cols = cols.reshape(batches, SEQ, 4)
    cols = jnp.pad(cols, ((0, 0), (0, SEQ_PAD - SEQ), (0, 0)), constant_values=-1)
    rows_first = jnp.swapaxes(cols, 1, 2)
    received, x, grad, weight, qkv, mixed, hidden, one, two, lse, probs, slot_cols, *spread = run_front(
        inputs, out_grad, dense, own, cols, rows_first, capacity, experts, cap_pad
    )
    saved = (qkv, mixed, lse, hidden, one, two, probs)
    back, grad_in, grad_out = run_moe(received, own, *spread)
    spot = 4 * width
    if groups == PLANE:
        outputs, inputs_grad, qkv_grad, proj_grad, small_grad = run_reduce(
            x, grad, weight, cols, slot_cols, back, saved, experts
        )
        small_grad = lax.dynamic_slice_in_dim(
            small_grad, lax.axis_index("dp") * depth, depth, axis=1
        )
        vectors = [small_grad[k] for k in range(4)]
        router_grad = small_grad[4 : 4 + experts].T
    else:
        outputs, inputs_grad, dense = run_tail(
            x, grad, weight, cols, slot_cols, back, saved, experts
        )
        dense = lax.psum_scatter(dense, both, scatter_dimension=0, tiled=True)
        dense = lax.all_gather(dense, "expert", axis=0, tiled=True).astype(F32)
        qkv_grad = dense[:, : 3 * width]
        proj_grad = dense[:, 3 * width : spot]
        vectors = [dense[:, spot + k] for k in range(4)]
        router_grad = dense[:, spot + 4 : spot + 4 + experts]
    grad_in = grad_in.astype(F32)
    grad_out = grad_out.astype(F32)
    return (
        outputs[:, :SEQ].reshape(batches * SEQ, width),
        inputs_grad[:, :SEQ].reshape(batches * SEQ, width),
        vectors[0],
        vectors[1],
        qkv_grad,
        proj_grad,
        vectors[2],
        vectors[3],
        router_grad,
        grad_in[None, :width],
        grad_in[None, width],
        grad_out[None],
    )


def solution(mesh):
    token = P(("dp", "expert"), None)
    vector = P("dp")
    matrix = P("dp", None)
    return jax.shard_map(
        per_device,
        mesh=mesh,
        in_specs=(
            token,
            vector,
            vector,
            matrix,
            matrix,
            vector,
            vector,
            matrix,
            P("expert", None, "dp"),
            P("expert", "dp"),
            P("expert", "dp", None),
            token,
            token,
            token,
            P(("dp", "expert")),
        ),
        out_specs=(
            token,
            token,
            vector,
            vector,
            matrix,
            matrix,
            vector,
            vector,
            matrix,
            P("expert", None, "dp"),
            P("expert", "dp"),
            P("expert", "dp", None),
        ),
        check_vma=False,
    )
```

```python
import functools

import jax
import jax.numpy as jnp
from jax import lax
from jax.experimental import pallas as pl
from jax.experimental.pallas import tpu as pltpu
from jax.sharding import PartitionSpec as P

HEADS = 12
HEAD = 64
SEQ = 197
SEQ_PAD = 208
EPS = 1e-06
BF = jnp.bfloat16
F32 = jnp.float32
SMALL = 128
MESH = pl.DeviceIdType.MESH
EARLY = 2
FAR_CUTS = 4
FAR_TURNS = (
    (0, True, 1),
    (0, True, 2),
    (1, True, 3),
    (1, False, 0),
    (2, True, 4),
    (2, False, 1),
    (3, False, 2),
    (4, True, 5),
    (4, False, 3),
    (5, True, 6),
    (5, False, 4),
)
TILE = 128
PLANE = 8
BIAS_ROWS = 16
NEG = -1e30
VMEM_LIMIT = 60 * 1024 * 1024
VMEM_MAX = 67043328


def ceil_to(value, step):
    return (value + step - 1) // step * step


def dot(a, b):
    return jnp.dot(a, b, preferred_element_type=F32)


def dot_nt(a, b):
    return lax.dot_general(a, b, (((1,), (1,)), ((), ())), preferred_element_type=F32)


def dot_tn(a, b):
    return lax.dot_general(a, b, (((0,), (0,)), ((), ())), preferred_element_type=F32)


def params(count=1):
    return pltpu.CompilerParams(
        dimension_semantics=("arbitrary",) * count, vmem_limit_bytes=VMEM_LIMIT
    )


class Line:
    def __init__(self, shards):
        self.shards = shards
        self.me = lax.axis_index("dp")
        self.has_below = self.me > 0
        self.has_above = self.me < shards - 1

    def greet(self, me, groups):
        barrier = pltpu.get_barrier_semaphore()
        for k in range(1, groups):
            pl.semaphore_signal(
                barrier, inc=1, device_id={"expert": lax.rem(me + k, groups)}, device_id_type=MESH
            )
        for k in range(1, self.shards):
            pl.semaphore_signal(
                barrier,
                inc=1,
                device_id={"dp": lax.rem(self.me + k, self.shards)},
                device_id_type=MESH,
            )
        pl.semaphore_wait(barrier, groups - 1 + self.shards - 1)

    def hop(self, way, round_id, source, target, send_sem, arrived):
        step = 1 - 2 * way
        slot = self.me - step * round_id
        if round_id == 0:
            body, bias, out = source
            tall = body.shape[0]
            moves = [
                (body, target[0].at[slot, pl.ds(0, tall)], 0),
                (bias, target[0].at[slot, pl.ds(tall, bias.shape[0])], 0),
                (out, target[1].at[slot], 1),
            ]
        else:
            moves = [(source[part].at[slot], target[part].at[slot], part) for part in range(2)]
        return [
            pltpu.make_async_remote_copy(
                src_ref=origin,
                dst_ref=place,
                send_sem=send_sem.at[way, round_id, k],
                recv_sem=arrived.at[slot, part],
                device_id={"dp": self.me + step},
                device_id_type=MESH,
            )
            for k, (origin, place, part) in enumerate(moves)
        ]

    def sends(self, way, round_id):
        if way == 0:
            return (self.me >= round_id) & self.has_above
        return (self.me + round_id < self.shards) & self.has_below

    def push(self, round_id, own, spread, send_sem, arrived, source=None):
        source = own if round_id == 0 else (source or spread)
        for way in range(2):

            @pl.when(self.sends(way, round_id))
            def _():
                for copy in self.hop(way, round_id, source, spread, send_sem, arrived):
                    copy.start()

    def drain(self, round_id, own, spread, send_sem, arrived, source=None):
        source = own if round_id == 0 else (source or spread)
        for way in range(2):

            @pl.when(self.sends(way, round_id))
            def _():
                for copy in self.hop(way, round_id, source, spread, send_sem, arrived):
                    copy.wait_send()

    def receive(self, round_id, spread, arrived):
        far = round_id + 1

        @pl.when(self.me >= far)
        def _():
            self.wait_slot(self.me - far, spread, arrived)

        @pl.when(self.me + far < self.shards)
        def _():
            self.wait_slot(self.me + far, spread, arrived)

    def wait_slot(self, slot, spread, arrived):
        for part in range(2):
            view = spread[part].at[slot]
            pltpu.make_async_copy(view, view, arrived.at[slot, part]).wait()


def route(cap_pad, cols_ref, rows_ref, limit_ref, slot_rows_ref, slot_cols_ref):
    for b in range(cols_ref.shape[0]):
        limit = limit_ref[b]
        col = [cols_ref[b, :, k : k + 1] for k in range(4)]
        row = [rows_ref[b, k : k + 1, :] for k in range(4)]
        for j in range(2):
            rank_row = 0
            rank_col = 0
            for k in range(2):
                hit = (col[k] == row[j]) & (col[2 + k] < row[2 + j])
                rank_row = rank_row + jnp.sum(hit.astype(jnp.int32), axis=0, keepdims=True)
                hit = (row[k] == col[j]) & (row[2 + k] < col[2 + j])
                rank_col = rank_col + jnp.sum(hit.astype(jnp.int32), axis=1, keepdims=True)
            keep_row = (rank_row < limit) & (row[j] >= 0)
            keep_col = (rank_col < limit) & (col[j] >= 0)
            slot_rows_ref[b, j : j + 1, :] = jnp.where(keep_row, row[j] * cap_pad + rank_row, -1)
            slot_cols_ref[b, :, j : j + 1] = jnp.where(keep_col, col[j] * cap_pad + rank_col, -1)


def norm_stats(values):
    average = jnp.mean(values, axis=-1, keepdims=True)
    centered = values - average
    spread = jnp.mean(centered * centered, axis=-1, keepdims=True)
    inverse = lax.rsqrt(spread + EPS)
    return centered * inverse, inverse


def front_kernel(
    experts,
    shards,
    limit_ref,
    cols_ref,
    rows_ref,
    raw_hbm,
    raw_grad_hbm,
    qkv_own,
    proj_own,
    small_own,
    own_body,
    own_bias,
    own_out,
    received_ref,
    x_hbm,
    grad_hbm,
    weight_hbm,
    qkv_hbm,
    mixed_hbm,
    hidden_hbm,
    one_hbm,
    two_hbm,
    lse_ref,
    probs_ref,
    slot_cols_ref,
    spread_in_ref,
    spread_out_ref,
    raw_ref,
    raw_grad_ref,
    x_ref,
    grad_ref,
    weight_ref,
    qkv_ref,
    mixed_ref,
    hidden_ref,
    one_ref,
    two_ref,
    small_ref,
    slot_rows_ref,
    send_ref,
    load_sem,
    store_sem,
    send_sem,
    arrived,
    rows_send,
    rows_recv,
    small_send,
    small_recv,
    line_send,
    piece_recv,
    plane_send,
    near_send,
):
    batches, rows, width = x_ref.shape
    groups = received_ref.shape[0]
    cap_pad = received_ref.shape[3]
    me = lax.axis_index("expert")
    line = Line(shards)
    z = line.me
    own = (own_body, own_bias, own_out)
    spread = (spread_in_ref, spread_out_ref)
    depth = width // shards
    piece_width = 4 * width // PLANE
    base = me // PLANE * PLANE
    spot = me - base
    core = lax.rem(me, 2)
    sibling = me + 1 - 2 * core
    chip = spot // 2
    chips = PLANE // 2
    cut = 3 * width // piece_width

    def remote(source, target, send, recv, peer):
        return pltpu.make_async_remote_copy(
            src_ref=source,
            dst_ref=target,
            send_sem=send,
            recv_sem=recv,
            device_id=peer,
            device_id_type=MESH,
        )

    def landed(view, sem):
        pltpu.make_async_copy(view, view, sem).wait()

    def rows_of(shard):
        return pl.ds(pl.multiple_of(shard * depth, depth), depth)

    def piece(shard, index):
        low = pl.multiple_of(index * piece_width, piece_width)
        return weight_ref.at[rows_of(shard), pl.ds(low, piece_width)]

    small_cols = pl.ds(4 * width, SMALL)

    raws = [
        pltpu.make_async_copy(raw_hbm, raw_ref, load_sem.at[0]),
        pltpu.make_async_copy(raw_grad_hbm, raw_grad_ref, load_sem.at[1]),
    ]
    mine = [
        pltpu.make_async_copy(
            qkv_own, weight_ref.at[rows_of(z), pl.ds(0, 3 * width)], load_sem.at[2]
        ),
        pltpu.make_async_copy(
            proj_own, weight_ref.at[rows_of(z), pl.ds(3 * width, width)], load_sem.at[3]
        ),
        pltpu.make_async_copy(small_own, weight_ref.at[rows_of(z), small_cols], load_sem.at[4]),
    ]
    for copy in mine:
        copy.start()
    for copy in raws:
        copy.start()
    line.greet(me, groups)
    for copy in mine:
        copy.wait()

    def small_copy(far):
        view = weight_ref.at[rows_of(z), small_cols]
        return remote(view, view, small_send.at[far], small_recv.at[z], {"dp": far})

    def line_copy(far):
        view = piece(z, spot)
        return remote(view, view, line_send.at[far], piece_recv.at[z, spot], {"dp": far})

    def plane_copy(shard, other):
        view = piece(shard, spot)
        peer = base + 2 * other + core
        return remote(
            view, view, plane_send.at[shard, other], piece_recv.at[shard, spot], {"expert": peer}
        )

    def near_copy(shard, other):
        index = 2 * other + core
        view = piece(shard, index)
        return remote(
            view, view, near_send.at[shard, other], piece_recv.at[shard, index], {"expert": sibling}
        )

    peers = [lax.rem(z + k, shards) for k in range(1, shards)]
    others = [lax.rem(chip + k, chips) for k in range(1, chips)]
    for far in peers:
        line_copy(far).start()
    for far in peers:
        small_copy(far).start()
    zero_rows = jnp.zeros((rows - SEQ, width), F32)

    def pad_image(image):
        x_ref[image, :SEQ] = raw_ref[image * SEQ : (image + 1) * SEQ]
        x_ref[image, SEQ:] = zero_rows
        pltpu.make_async_copy(x_ref.at[image], x_hbm.at[image], store_sem.at[0, image]).start()
        grad_ref[image, :SEQ] = raw_grad_ref[image * SEQ : (image + 1) * SEQ]
        grad_ref[image, SEQ:] = zero_rows
        pltpu.make_async_copy(
            grad_ref.at[image], grad_hbm.at[image], store_sem.at[1, image]
        ).start()

    for copy in raws:
        copy.wait()
    pad_image(0)
    for far in peers:
        landed(piece(far, spot), piece_recv.at[far, spot])
        for other in others:
            plane_copy(far, other).start()
        near_copy(far, chip).start()
    line.push(0, own, spread, send_sem, arrived)
    for image in range(1, batches):
        pad_image(image)
    slot_rows_ref[...] = jnp.full(slot_rows_ref.shape, -1, jnp.int32)
    slot_cols_ref[...] = jnp.full(slot_cols_ref.shape, -1, jnp.int32)
    route(cap_pad, cols_ref, rows_ref, limit_ref, slot_rows_ref, slot_cols_ref)
    for far in peers:
        for other in others:
            index = 2 * other + core
            landed(piece(far, index), piece_recv.at[far, index])
            near_copy(far, other).start()
    for far in peers:
        landed(weight_ref.at[rows_of(far), small_cols], small_recv.at[far])
        for k in range(chips):
            index = 2 * k + 1 - core
            landed(piece(far, index), piece_recv.at[far, index])
    weight_store = pltpu.make_async_copy(weight_ref, weight_hbm, load_sem.at[5])
    weight_store.start()
    small_ref[...] = weight_ref[:, 4 * width :].astype(F32).T

    def rows_copy(image, target):
        return remote(
            send_ref.at[image, target],
            received_ref.at[me, image],
            rows_send.at[image, target],
            rows_recv.at[me, image],
            {"expert": target},
        )

    saves = (
        (qkv_ref, qkv_hbm),
        (mixed_ref, mixed_hbm),
        (hidden_ref, hidden_hbm),
        (one_ref, one_hbm),
        (two_ref, two_hbm),
    )
    lane = lax.broadcasted_iota(jnp.int32, (1, 128), 1)
    key_ok = lax.broadcasted_iota(jnp.int32, (1, rows), 1) < SEQ
    slot = lax.broadcasted_iota(jnp.int32, (groups * cap_pad, 1), 0)
    scale = HEAD ** (-0.5)

    def do_image(index, carry):
        x = x_ref[index]
        hat, _ = norm_stats(x)
        one = (hat * small_ref[0:1, :] + small_ref[1:2, :]).astype(BF)
        one_ref[index] = one
        qkv_ref[index] = dot(one, weight_ref[:, : 3 * width]).astype(BF)
        lse = jnp.zeros((rows, 128), F32)
        for pair in range(HEADS // 2):
            low = pair * 128
            query = qkv_ref[index, :, low : low + 128]
            keys = qkv_ref[index, :, width + low : width + low + 128]
            values = qkv_ref[index, :, 2 * width + low : 2 * width + low + 128]
            total = None
            for side in range(2):
                part_of = (lane // HEAD) == side
                scores = dot_nt(jnp.where(part_of, query, jnp.zeros_like(query)), keys) * scale
                scores = jnp.where(key_ok, scores, NEG)
                highest = jnp.max(scores, axis=-1, keepdims=True)
                expo = jnp.exp(scores - highest)
                denom = jnp.sum(expo, axis=-1, keepdims=True)
                weights = (expo / denom).astype(BF)
                lse = jnp.where(lane == 2 * pair + side, highest + jnp.log(denom), lse)
                part = dot(weights, jnp.where(part_of, values, jnp.zeros_like(values)))
                total = part if total is None else total + part
            mixed_ref[index, :, low : low + 128] = total.astype(BF)
        lse_ref[index] = lse
        hidden = x + dot(mixed_ref[index], weight_ref[:, 3 * width : 4 * width])
        hidden_ref[index] = hidden
        hat, _ = norm_stats(hidden)
        two = (hat * small_ref[2:3, :] + small_ref[3:4, :]).astype(BF)
        two_ref[index] = two
        logits = dot(two, weight_ref[:, 4 * width :])
        in_router = (lane >= 4) & (lane < 4 + experts)
        logits = jnp.where(in_router, logits, NEG)
        expo = jnp.exp(logits - jnp.max(logits, axis=-1, keepdims=True))
        probs = expo / jnp.sum(expo, axis=-1, keepdims=True)
        probs_ref[index] = probs
        out_grad = grad_ref[index]
        both = None
        grads = None
        for j in range(2):
            gate = jnp.sum(
                jnp.where(lane - 4 == cols_ref[index, :, j : j + 1], probs, 0.0),
                axis=-1,
                keepdims=True,
            )
            pick = (slot == slot_rows_ref[index, j : j + 1, :]).astype(F32)
            both = pick if both is None else both + pick
            part = dot(pick.astype(BF), (gate * out_grad).astype(BF))
            grads = part if grads is None else grads + part
        sent = dot(both.astype(BF), two).astype(BF)
        send_ref[index, :, 0] = sent.reshape(groups, cap_pad, width)
        send_ref[index, :, 1] = grads.astype(BF).reshape(groups, cap_pad, width)
        for k in range(1, groups):
            rows_copy(index, lax.rem(me + k, groups)).start()
        pltpu.make_async_copy(
            send_ref.at[index, me], received_ref.at[me, index], rows_recv.at[me, index]
        ).start()
        for k, (here, there) in enumerate(saves):
            pltpu.make_async_copy(here.at[index], there.at[index], store_sem.at[2 + k, index]).start()
        return carry

    lax.fori_loop(0, batches, do_image, 0)

    rounds = min(EARLY, shards - 1)
    for round_id in range(1, rounds):
        line.receive(round_id - 1, spread, arrived)
        line.push(round_id, own, spread, send_sem, arrived)

    def finish(image, carry):
        for k in range(groups):
            source = lax.rem(me + k, groups)
            if k:
                rows_copy(image, source).wait_send()
            landed(received_ref.at[source, image], rows_recv.at[source, image])
        pltpu.make_async_copy(x_ref.at[image], x_hbm.at[image], store_sem.at[0, image]).wait()
        pltpu.make_async_copy(grad_ref.at[image], grad_hbm.at[image], store_sem.at[1, image]).wait()
        for k, (here, there) in enumerate(saves):
            pltpu.make_async_copy(here.at[image], there.at[image], store_sem.at[2 + k, image]).wait()
        return carry

    lax.fori_loop(0, batches, finish, 0)
    weight_store.wait()
    for far in peers:
        line_copy(far).wait_send()
        small_copy(far).wait_send()
        for other in others:
            plane_copy(far, other).wait_send()
        for k in range(chips):
            near_copy(far, k).wait_send()
    line.receive(rounds - 1, spread, arrived)
    for round_id in range(rounds):
        line.drain(round_id, own, spread, send_sem, arrived)


def run_front(raw, raw_grad, dense, own, cols, rows_first, limits, experts, cap_pad):
    batches, rows = cols.shape[:2]
    width = raw.shape[1]
    shards = lax.axis_size("dp")
    groups = lax.axis_size("expert")
    body, bias, out = own
    tall = body.shape[0] + bias.shape[0]
    anywhere = pl.BlockSpec(memory_space=pl.ANY)
    inside = pl.BlockSpec(memory_space=pltpu.VMEM)
    dma = pltpu.SemaphoreType.DMA
    chips = PLANE // 2

    def shape(*dims, dtype=BF):
        return jax.ShapeDtypeStruct((batches, rows) + dims, dtype)

    return pl.pallas_call(
        functools.partial(front_kernel, experts, shards),
        out_shape=(
            jax.ShapeDtypeStruct((groups, batches, 2, cap_pad, width), BF),
            shape(width, dtype=F32),
            shape(width, dtype=F32),
            jax.ShapeDtypeStruct((width, 4 * width + SMALL), BF),
            shape(3 * width),
            shape(width),
            shape(width, dtype=F32),
            shape(width),
            shape(width),
            shape(128, dtype=F32),
            shape(SMALL, dtype=F32),
            shape(8, dtype=jnp.int32),
            jax.ShapeDtypeStruct((shards, tall, body.shape[1]), BF),
            jax.ShapeDtypeStruct((shards,) + out.shape, BF),
        ),
        in_specs=[pl.BlockSpec(memory_space=pltpu.SMEM), inside, inside] + [anywhere] * 8,
        out_specs=(anywhere,) * 9 + (inside,) * 3 + (anywhere,) * 2,
        scratch_shapes=[
            pltpu.VMEM(raw.shape, F32),
            pltpu.VMEM(raw.shape, F32),
            pltpu.VMEM((batches, rows, width), F32),
            pltpu.VMEM((batches, rows, width), F32),
            pltpu.VMEM((width, 4 * width + SMALL), BF),
            pltpu.VMEM((batches, rows, 3 * width), BF),
            pltpu.VMEM((batches, rows, width), BF),
            pltpu.VMEM((batches, rows, width), F32),
            pltpu.VMEM((batches, rows, width), BF),
            pltpu.VMEM((batches, rows, width), BF),
            pltpu.VMEM((SMALL, width), F32),
            pltpu.VMEM((batches, 8, rows), jnp.int32),
            pltpu.VMEM((batches, groups, 2, cap_pad, width), BF),
            dma((6,)),
            dma((7, batches)),
            dma((2, EARLY, 3)),
            dma((shards, 2)),
            dma((batches, groups)),
            dma((groups, batches)),
            dma((shards,)),
            dma((shards,)),
            dma((shards,)),
            dma((shards, PLANE)),
            dma((shards, chips)),
            dma((shards, chips)),
        ],
        compiler_params=pltpu.CompilerParams(
            vmem_limit_bytes=VMEM_LIMIT, collective_id=1, has_side_effects=True
        ),
        cost_estimate=pl.CostEstimate(
            flops=8000000000, bytes_accessed=40000000, transcendentals=3000000
        ),
        name="front",
    )(limits, cols, rows_first, raw, raw_grad, *dense, *own)


def pieces_of(tall, span, cuts=2):
    pieces = []
    for kind, extent in enumerate((tall, span)):
        size = ceil_to(-(-extent // cuts), 16)
        for low in range(0, extent, size):
            pieces.append((kind, low, min(size, extent - low)))
    return tuple(pieces)


def moe_kernel(
    shards,
    groups,
    x_hbm,
    own_body,
    own_bias,
    own_out,
    spread_in_ref,
    spread_out_ref,
    back_ref,
    sum_in_ref,
    sum_out_ref,
    far_in_ref,
    far_out_ref,
    rows_ref,
    win_ref,
    wout_ref,
    y_acc,
    dx_acc,
    gin_acc,
    gout_acc,
    part_in_ref,
    part_out_ref,
    land_in_ref,
    land_out_ref,
    rows_sem,
    weight_send,
    arrived,
    sum_send,
    sum_recv,
    back_send,
    back_recv,
    final_sem,
):
    line = Line(shards)
    z = line.me
    me = lax.axis_index("expert")
    _, batches, _, cap_pad, width = rows_ref.shape
    _, tall, span = spread_in_ref.shape
    group = max(1, 512 // (batches * cap_pad))
    while groups % group:
        group -= 1
    blocks = groups // group
    rows = group * batches * cap_pad
    early = min(EARLY, shards - 1)
    spread = (win_ref, wout_ref)
    early_spread = (spread_in_ref, spread_out_ref)
    own = (own_body, own_bias, own_out)
    parts = (part_in_ref, part_out_ref)
    lands = (land_in_ref, land_out_ref)
    pieces = pieces_of(tall, span)

    for k in range(groups):
        source = lax.rem(me + k, groups)
        pltpu.make_async_copy(x_hbm.at[source], rows_ref.at[source], rows_sem.at[source]).start()
    mine = (
        (own_body, win_ref.at[z, pl.ds(0, width)], 0),
        (own_bias, win_ref.at[z, pl.ds(width, tall - width)], 0),
        (own_out, wout_ref.at[z], 1),
    )
    for here, there, part in mine:
        pltpu.make_async_copy(here, there, arrived.at[z, part]).start()
    for far in range(1, early + 1):
        for sign in (-1, 1):
            slot = z + sign * far

            @pl.when((slot >= 0) & (slot < shards))
            def _():
                for part in range(2):
                    pltpu.make_async_copy(
                        early_spread[part].at[slot], spread[part].at[slot], arrived.at[slot, part]
                    ).start()

    line.greet(me, groups)
    if early < shards - 1:
        line.push(early, own, spread, weight_send, arrived, early_spread)

    table = []
    for at in range(shards):
        near = sorted(range(shards), key=lambda q: (abs(q - at), q))
        table.append(near[1:-1] + near[:1] + near[-1:])

    def quarter(step):
        total = 0
        for at in range(shards):
            for s in range(shards):
                hit = jnp.where((z == at) & (step == s), table[at][s], 0)
                total = total + hit
        return total

    def sum_copy(way, q, piece):
        kind, low, size = pieces[piece]
        if way == 0:
            slot = q - 1
            peer = z + 1
        else:
            slot = jnp.where(q == z - 1, shards - 2, q - 1)
            peer = z - 1
        cut = pl.ds(low, size)
        return pltpu.make_async_remote_copy(
            src_ref=parts[kind].at[q, cut],
            dst_ref=lands[kind].at[slot, cut],
            send_sem=sum_send.at[way, q, piece],
            recv_sem=sum_recv.at[slot, piece],
            device_id={"dp": peer},
            device_id_type=MESH,
        )

    def take_sum(slot, q, piece):
        kind, low, size = pieces[piece]
        cut = pl.ds(low, size)
        view = lands[kind].at[slot, cut]
        pltpu.make_async_copy(view, view, sum_recv.at[slot, piece]).wait()
        parts[kind][q, cut] = (
            parts[kind][q, cut].astype(F32) + lands[kind][slot, cut].astype(F32)
        ).astype(BF)

    def back_copy(source):
        return pltpu.make_async_remote_copy(
            src_ref=rows_ref.at[source],
            dst_ref=back_ref.at[me],
            send_sem=back_send.at[source],
            recv_sem=back_recv.at[me],
            device_id={"expert": source},
            device_id_type=MESH,
        )

    def back_start(first):
        for k in range(group):
            source = first + k

            @pl.when(source != me)
            def _():
                back_copy(source).start()

            @pl.when(source == me)
            def _():
                pltpu.make_async_copy(
                    rows_ref.at[source], back_ref.at[source], back_recv.at[source]
                ).start()

    def block_first(block):
        return lax.rem(me // group + 1 + block, blocks) * group

    plain = (shards - 2) * blocks
    inner = (z > 0) & (z < shards - 1)

    def do_item(item, carry):
        late = item >= plain
        rest = item - plain
        step = jnp.where(late, shards - 2 + lax.rem(rest + 2 * blocks, 2), item // blocks)
        block = jnp.where(late, (rest + 2 * blocks) // 2 - blocks, lax.rem(item, blocks))
        q = quarter(step)
        bank = jnp.where(step == shards - 1, 1, 0)

        @pl.when(block == 0)
        def _():
            line.wait_slot(q, spread, arrived)
            for round_id in range(early, shards - 2):
                for way in range(2):
                    forward = 1 - 2 * way

                    @pl.when((q == z - forward * (round_id + 1)) & line.sends(way, round_id + 1))
                    def _():
                        for copy in line.hop(
                            way, round_id + 1, spread, spread, weight_send, arrived
                        ):
                            copy.start()

        @pl.when((step == shards - 2) & (block > 0))
        def _():
            back_start(block_first(block - 1))

        lead = block_first(block)
        low = pl.multiple_of(lead * (batches * cap_pad), rows)
        here = pl.ds(low, rows)
        mine = pl.ds(lead, group)

        @pl.when(step == 0)
        def _():
            for k in range(group):
                view = rows_ref.at[lead + k]
                pltpu.make_async_copy(view, view, rows_sem.at[lead + k]).wait()

        x = rows_ref[mine, :, 0].reshape(rows, width)
        grad = rows_ref[mine, :, 1].reshape(rows, width)
        win = win_ref[q, :width, :]
        wout = wout_ref[q]
        pre = dot(x, win) + win_ref[q, width : width + 1, :].astype(F32)
        cdf = 0.5 * lax.erf(pre * (0.5**0.5)) + 0.5
        active = (pre * cdf).astype(BF)
        slope = cdf + pre * (jnp.exp(-0.5 * pre * pre) * 0.3989422804014327)
        d_pre = (dot_nt(grad, wout) * slope).astype(BF)
        y_part = dot(active, wout)
        dx_part = dot_nt(d_pre, win)

        @pl.when(step == 0)
        def _():
            y_acc[here, :] = y_part
            dx_acc[here, :] = dx_part

        @pl.when(step > 0)
        def _():
            y_acc[here, :] += y_part
            dx_acc[here, :] += dx_part

        gout = dot_tn(active, grad)
        gin = dot_tn(x, d_pre)
        gbias = jnp.sum(d_pre.astype(F32), axis=0, keepdims=True)

        @pl.when(block == 0)
        def _():
            gout_acc[bank] = gout
            gin_acc[bank, :width, :] = gin
            gin_acc[bank, width : width + 1, :] = gbias

        @pl.when(block > 0)
        def _():
            gout_acc[bank] += gout
            gin_acc[bank, :width, :] += gin
            gin_acc[bank, width : width + 1, :] += gbias

        @pl.when(step == shards - 1)
        def _():
            shape = (group, batches, cap_pad, width)
            rows_ref[mine, :, 0] = y_acc[here, :].astype(BF).reshape(shape)
            rows_ref[mine, :, 1] = dx_acc[here, :].astype(BF).reshape(shape)

        @pl.when(block == blocks - 1)
        def _():
            part_in_ref[q, :width, :] = gin_acc[bank, :width, :].astype(BF)
            part_in_ref[q, width:, :] = jnp.broadcast_to(
                gin_acc[bank, width : width + 1, :].astype(BF), (tall - width, span)
            )
            part_out_ref[q] = gout_acc[bank].astype(BF)

            @pl.when((z == 0) & (q > z) & (q < shards - 1))
            def _():
                for piece in range(len(pieces)):
                    sum_copy(0, q, piece).start()

            @pl.when((z == shards - 1) & (q < z) & (q > 0))
            def _():
                for piece in range(len(pieces)):
                    sum_copy(1, q, piece).start()

        return carry

    lax.fori_loop(0, shards * blocks, do_item, 0)
    back_start(block_first(blocks - 1))
    finals = [
        pltpu.make_async_copy(part_in_ref.at[0], far_in_ref.at[0], final_sem.at[0]),
        pltpu.make_async_copy(part_out_ref.at[0], far_out_ref.at[0], final_sem.at[1]),
        pltpu.make_async_copy(part_in_ref.at[shards - 1], far_in_ref.at[1], final_sem.at[2]),
        pltpu.make_async_copy(part_out_ref.at[shards - 1], far_out_ref.at[1], final_sem.at[3]),
        pltpu.make_async_copy(part_in_ref.at[z], sum_in_ref, final_sem.at[4]),
        pltpu.make_async_copy(part_out_ref.at[z], sum_out_ref, final_sem.at[5]),
    ]
    for copy in finals[:4]:
        copy.start()

    def do_forward(turn, carry):
        up = turn
        down = shards - 1 - turn
        for piece in range(len(pieces)):

            @pl.when((up > z) & (z > 0))
            def _():
                take_sum(up - 1, up, piece)
                sum_copy(0, up, piece).start()

            @pl.when((down < z) & (z < shards - 1))
            def _():
                take_sum(down - 1, down, piece)
                sum_copy(1, down, piece).start()

        return carry

    lax.fori_loop(1, shards - 1, do_forward, 0)
    for piece in range(len(pieces)):

        @pl.when(inner)
        def _():
            take_sum(z - 1, z, piece)
            take_sum(shards - 2, z, piece)

    for copy in finals[4:]:
        copy.start()

    def finish_sum(q, carry):
        @pl.when((q > z) & line.has_above)
        def _():
            for piece in range(len(pieces)):
                sum_copy(0, q, piece).wait_send()

        @pl.when((q < z) & line.has_below)
        def _():
            for piece in range(len(pieces)):
                sum_copy(1, q, piece).wait_send()

        return carry

    lax.fori_loop(1, shards - 1, finish_sum, 0)
    for round_id in range(early, shards - 1):
        line.drain(round_id, own, spread, weight_send, arrived)
    for k in range(groups):
        source = lax.rem(me + k, groups)
        if k:
            back_copy(source).wait_send()
        view = back_ref.at[source]
        pltpu.make_async_copy(view, view, back_recv.at[source]).wait()
    for copy in finals:
        copy.wait()


def run_moe(received, own, spread_in, spread_out):
    groups, batches, _, cap_pad, width = received.shape
    shards, tall, span = spread_in.shape
    total = groups * batches * cap_pad
    count = len(pieces_of(tall, span))
    anywhere = pl.BlockSpec(memory_space=pl.ANY)
    return pl.pallas_call(
        functools.partial(moe_kernel, shards, groups),
        out_shape=(
            jax.ShapeDtypeStruct(received.shape, BF),
            jax.ShapeDtypeStruct((tall, span), BF),
            jax.ShapeDtypeStruct((span, width), BF),
            jax.ShapeDtypeStruct((2, tall, span), BF),
            jax.ShapeDtypeStruct((2, span, width), BF),
        ),
        in_specs=[anywhere] * 6,
        out_specs=(anywhere,) * 5,
        scratch_shapes=[
            pltpu.VMEM(received.shape, BF),
            pltpu.VMEM((shards, tall, span), BF),
            pltpu.VMEM((shards, span, width), BF),
            pltpu.VMEM((total, width), F32),
            pltpu.VMEM((total, width), F32),
            pltpu.VMEM((2, ceil_to(width + 1, 8), span), F32),
            pltpu.VMEM((2, span, width), F32),
            pltpu.VMEM((shards, tall, span), BF),
            pltpu.VMEM((shards, span, width), BF),
            pltpu.VMEM((shards - 1, tall, span), BF),
            pltpu.VMEM((shards - 1, span, width), BF),
            pltpu.SemaphoreType.DMA((groups,)),
            pltpu.SemaphoreType.DMA((2, shards, 2)),
            pltpu.SemaphoreType.DMA((shards, 2)),
            pltpu.SemaphoreType.DMA((2, shards, count)),
            pltpu.SemaphoreType.DMA((shards - 1, count)),
            pltpu.SemaphoreType.DMA((groups,)),
            pltpu.SemaphoreType.DMA((groups,)),
            pltpu.SemaphoreType.DMA((6,)),
        ],
        compiler_params=pltpu.CompilerParams(
            vmem_limit_bytes=VMEM_MAX, collective_id=2, has_side_effects=True
        ),
        cost_estimate=pl.CostEstimate(
            flops=12 * total * width * span * shards,
            bytes_accessed=60000000,
            transcendentals=2 * total * span * shards,
        ),
        name="moe",
    )(received, *own, spread_in, spread_out)


def tail_kernel(
    experts,
    x_ref,
    grad_ref,
    weight_ref,
    cols_ref,
    slot_cols_ref,
    back_ref,
    qkv_ref,
    mixed_ref,
    lse_ref,
    hidden_ref,
    one_ref,
    two_ref,
    probs_ref,
    out_ref,
    dx_ref,
    dense_ref,
    small_ref,
    sums_ref,
    d_qkv_ref,
    d_branch_ref,
    d_logits_ref,
    one_all,
    two_all,
    mixed_all,
):
    width = x_ref.shape[-1]
    rows = x_ref.shape[1]
    index = pl.program_id(0)

    @pl.when(index == 0)
    def _():
        small_ref[...] = weight_ref[:, 4 * width :].astype(F32).T
        sums_ref[...] = jnp.zeros_like(sums_ref)

    here = pl.ds(pl.multiple_of(index * rows, rows), rows)
    one_all[here, :] = one_ref[0]
    two_all[here, :] = two_ref[0]
    mixed_all[here, :] = mixed_ref[0]
    out_grad = grad_ref[0]
    hidden = hidden_ref[0]
    probs = probs_ref[0]
    lane = lax.broadcasted_iota(jnp.int32, (1, 128), 1)
    slots = back_ref.shape[0] * back_ref.shape[3]
    slot = lax.broadcasted_iota(jnp.int32, (1, slots), 1)
    answers = back_ref[:, 0, 0].reshape(slots, width)
    answer_grads = back_ref[:, 0, 1].reshape(slots, width)
    result = hidden
    d_probs = jnp.zeros_like(probs)
    both = None
    for j in range(2):
        pick = (slot == slot_cols_ref[0, :, j : j + 1]).astype(F32)
        both = pick if both is None else both + pick
        chosen = lane - 4 == cols_ref[0, :, j : j + 1]
        gate = jnp.sum(jnp.where(chosen, probs, 0.0), axis=-1, keepdims=True)
        picked = dot(pick.astype(BF), answers)
        result = result + gate * picked
        d_gate = jnp.sum(picked * out_grad, axis=-1, keepdims=True)
        d_probs = jnp.where(chosen, d_gate, d_probs)
    out_ref[0] = result
    d_logits = probs * (d_probs - jnp.sum(d_probs * probs, axis=-1, keepdims=True))
    d_logits = d_logits.astype(BF)
    d_logits_ref[here, :] = d_logits
    d_two = dot(both.astype(BF), answer_grads) + dot_nt(d_logits, weight_ref[:, 4 * width :])
    hat, inverse = norm_stats(hidden)
    sums_ref[2:3, :] += jnp.sum(d_two * hat, axis=0, keepdims=True)
    sums_ref[3:4, :] += jnp.sum(d_two, axis=0, keepdims=True)
    d_hat = d_two * small_ref[2:3, :]
    d_hidden = out_grad + inverse * (
        d_hat
        - jnp.mean(d_hat, axis=-1, keepdims=True)
        - hat * jnp.mean(d_hat * hat, axis=-1, keepdims=True)
    )
    d_branch = d_hidden.astype(BF)
    d_branch_ref[here, :] = d_branch
    d_mixed_all = dot_nt(d_branch, weight_ref[:, 3 * width : 4 * width]).astype(BF)
    key_ok = lax.broadcasted_iota(jnp.int32, (1, rows), 1) < SEQ
    scale = HEAD ** (-0.5)
    for pair in range(HEADS // 2):
        low = pair * 128
        query = qkv_ref[0, :, low : low + 128]
        keys = qkv_ref[0, :, width + low : width + low + 128]
        values = qkv_ref[0, :, 2 * width + low : 2 * width + low + 128]
        d_mixed = d_mixed_all[:, low : low + 128]
        d_query = d_keys = d_values = None
        for side in range(2):
            mine = (lane // HEAD) == side
            head = 2 * pair + side

            def own(array):
                return jnp.where(mine, array, jnp.zeros_like(array))

            my_query = own(query)
            my_keys = own(keys)
            my_d_mixed = own(d_mixed)
            scores = dot_nt(my_query, keys) * scale
            scores = jnp.where(key_ok, scores, NEG)
            probs_h = jnp.exp(scores - lse_ref[0, :, head : head + 1])
            d_weights = dot_nt(my_d_mixed, values)
            row_terms = jnp.sum(d_weights * probs_h, axis=-1, keepdims=True)
            d_scores = (probs_h * (d_weights - row_terms) * scale).astype(BF)
            parts = (
                dot(d_scores, my_keys),
                dot_tn(d_scores, my_query),
                dot_tn(probs_h.astype(BF), my_d_mixed),
            )
            if side == 0:
                d_query, d_keys, d_values = parts
            else:
                d_query, d_keys, d_values = (
                    d_query + parts[0],
                    d_keys + parts[1],
                    d_values + parts[2],
                )
        d_qkv_ref[here, low : low + 128] = d_query.astype(BF)
        d_qkv_ref[here, width + low : width + low + 128] = d_keys.astype(BF)
        d_qkv_ref[here, 2 * width + low : 2 * width + low + 128] = d_values.astype(BF)
    d_one = dot_nt(d_qkv_ref[here, :], weight_ref[:, : 3 * width])
    hat, inverse = norm_stats(x_ref[0])
    sums_ref[0:1, :] += jnp.sum(d_one * hat, axis=0, keepdims=True)
    sums_ref[1:2, :] += jnp.sum(d_one, axis=0, keepdims=True)
    d_hat = d_one * small_ref[0:1, :]
    dx_ref[0] = d_hidden + inverse * (
        d_hat
        - jnp.mean(d_hat, axis=-1, keepdims=True)
        - hat * jnp.mean(d_hat * hat, axis=-1, keepdims=True)
    )

    @pl.when(index == pl.num_programs(0) - 1)
    def _():
        dense_ref[:, 4 * width :] = (dot_tn(two_all[...], d_logits_ref[...]) + sums_ref[...].T).astype(BF)
        dense_ref[:, 3 * width : 4 * width] = dot_tn(mixed_all[...], d_branch_ref[...]).astype(BF)
        for part in range(3):
            cut = slice(part * width, (part + 1) * width)
            dense_ref[:, cut] = dot_tn(one_all[...], d_qkv_ref[:, cut]).astype(BF)


def run_tail(x, grad, weight, cols, slot_cols, back, saved, experts):
    batches, rows, width = x.shape
    total = weight.shape[1]
    cap_pad = back.shape[3]
    qkv, mixed, lse, hidden, one, two, probs = saved

    def block(*shape):
        return pl.BlockSpec((1,) + shape, lambda i: (i,) + (0,) * len(shape))

    return pl.pallas_call(
        functools.partial(tail_kernel, experts),
        grid=(batches,),
        out_shape=(
            jax.ShapeDtypeStruct(x.shape, F32),
            jax.ShapeDtypeStruct(x.shape, F32),
            jax.ShapeDtypeStruct((width, total), BF),
        ),
        in_specs=[
            block(rows, width),
            block(rows, width),
            pl.BlockSpec((width, total), lambda i: (0, 0), pipeline_mode=pl.Buffered(1)),
            block(rows, 4),
            block(rows, 8),
            pl.BlockSpec((experts, 1, 2, cap_pad, width), lambda i: (0, i, 0, 0, 0)),
            block(rows, 3 * width),
            block(rows, width),
            block(rows, 128),
            block(rows, width),
            block(rows, width),
            block(rows, width),
            block(rows, SMALL),
        ],
        out_specs=(
            block(rows, width),
            block(rows, width),
            pl.BlockSpec((width, total), lambda i: (0, 0), pipeline_mode=pl.Buffered(1)),
        ),
        scratch_shapes=[
            pltpu.VMEM((SMALL, width), F32),
            pltpu.VMEM((SMALL, width), F32),
            pltpu.VMEM((batches * rows, 3 * width), BF),
            pltpu.VMEM((batches * rows, width), BF),
            pltpu.VMEM((batches * rows, SMALL), BF),
            pltpu.VMEM((batches * rows, width), BF),
            pltpu.VMEM((batches * rows, width), BF),
            pltpu.VMEM((batches * rows, width), BF),
        ],
        compiler_params=params(),
        cost_estimate=pl.CostEstimate(
            flops=16000000000, bytes_accessed=50000000, transcendentals=2000000
        ),
        name="tail",
    )(x, grad, weight, cols, slot_cols, back, qkv, mixed, lse, hidden, one, two, probs)


def reduce_kernel(
    experts,
    shards,
    cols_ref,
    slot_cols_ref,
    lse_ref,
    probs_ref,
    x_hbm,
    grad_hbm,
    weight_hbm,
    back_hbm,
    qkv_hbm,
    mixed_hbm,
    hidden_hbm,
    one_hbm,
    two_hbm,
    far_in_hbm,
    far_out_hbm,
    out_hbm,
    dx_hbm,
    end_in_hbm,
    end_out_hbm,
    qkv_grad_ref,
    proj_grad_ref,
    small_grad_ref,
    x_ref,
    grad_ref,
    weight_ref,
    back_ref,
    qkv_ref,
    mixed_ref,
    hidden_ref,
    one_ref,
    two_ref,
    small_ref,
    sums_ref,
    one_flip,
    d_qkv_ref,
    d_branch_ref,
    d_mixed_ref,
    d_logits_ref,
    tiles_ref,
    near_ref,
    plane_land,
    plane_ref,
    line_land,
    final_ref,
    small_land,
    small_far,
    far_in_ref,
    far_out_ref,
    far_in_land,
    far_out_land,
    load_sem,
    store_sem,
    near_send,
    near_recv,
    plane_send,
    plane_recv,
    line_send,
    line_recv,
    final_send,
    final_recv,
    small_send,
    small_recv,
    far_load,
    far_send,
    far_recv,
):
    batches, rows, width = x_ref.shape
    z = lax.axis_index("dp")
    me = lax.axis_index("expert")
    core = lax.rem(me, 2)
    sibling = me + 1 - 2 * core
    chip = me // 2
    chips = PLANE // 2
    pairs = HEADS // 2
    depth = width // shards
    head_tiles = width // TILE
    own_tiles = (4 * width // TILE) // PLANE

    def loads(kind, image):
        pair = {
            0: (back_hbm.at[:, image], back_ref.at[:, image]),
            1: (hidden_hbm.at[image], hidden_ref.at[image]),
            2: (grad_hbm.at[image], grad_ref.at[image]),
            3: (mixed_hbm.at[image], mixed_ref.at[pl.ds(image * rows, rows)]),
            4: (two_hbm.at[image], two_ref.at[pl.ds(image * rows, rows)]),
            5: (one_hbm.at[image], one_ref.at[pl.ds(image * rows, rows)]),
            6: (qkv_hbm.at[image], qkv_ref.at[pl.ds(image * rows, rows)]),
            7: (x_hbm.at[image], x_ref.at[image]),
        }[kind]
        return pltpu.make_async_copy(pair[0], pair[1], load_sem.at[kind, image])

    weight_load = pltpu.make_async_copy(weight_hbm, weight_ref, load_sem.at[8, 0])
    far_parts = (far_in_ref, far_out_ref)
    far_lands = (far_in_land, far_out_land)
    far_loads = [
        pltpu.make_async_copy(source.at[k], target.at[k], far_load.at[k, part])
        for k in range(2)
        for part, (source, target) in enumerate(
            ((far_in_hbm, far_in_ref), (far_out_hbm, far_out_ref))
        )
    ]

    @pl.when((z == 0) | (z == shards - 1))
    def _():
        for copy in far_loads:
            copy.start()

    for kind in range(3):
        loads(kind, 0).start()
    weight_load.start()
    for image in range(1, batches):
        for kind in range(3):
            loads(kind, image).start()
    @pl.when((z > 0) & (z < shards - 1))
    def _():
        for copy in far_loads:
            copy.start()

    for kind in range(3, 8):
        for image in range(batches):
            loads(kind, image).start()

    barrier = pltpu.get_barrier_semaphore()
    for k in range(1, PLANE):
        pl.semaphore_signal(
            barrier, inc=1, device_id={"expert": lax.rem(me + k, PLANE)}, device_id_type=MESH
        )
    for k in range(1, shards):
        pl.semaphore_signal(
            barrier, inc=1, device_id={"dp": lax.rem(z + k, shards)}, device_id_type=MESH
        )
    pl.semaphore_wait(barrier, PLANE - 1 + shards - 1)

    def remote(source, target, send_sem, recv_sem, peer):
        return pltpu.make_async_remote_copy(
            src_ref=source,
            dst_ref=target,
            send_sem=send_sem,
            recv_sem=recv_sem,
            device_id=peer,
            device_id_type=MESH,
        )

    def landed(view, sem):
        pltpu.make_async_copy(view, view, sem).wait()

    pieces = pieces_of(far_in_ref.shape[1], far_out_ref.shape[1], FAR_CUTS)
    inner = (z > 0) & (z < shards - 1)
    low_half = 2 * z < shards

    def far_copy(k, piece):
        kind, low, size = pieces[piece]
        cut = pl.ds(low, size)
        return remote(
            far_parts[kind].at[k, cut],
            far_lands[kind].at[k, cut],
            far_send.at[k, piece],
            far_recv.at[k, piece],
            {"dp": z + 2 * k - 1},
        )

    def far_take(k, piece):
        kind, low, size = pieces[piece]
        cut = pl.ds(low, size)
        landed(far_lands[kind].at[k, cut], far_recv.at[k, piece])
        far_parts[kind][k, cut] = (
            far_parts[kind][k, cut].astype(F32) + far_lands[kind][k, cut].astype(F32)
        ).astype(BF)

    def far_forward(k, piece):
        far_take(k, piece)
        far_copy(k, piece).start()

    def pass_on(first, piece):
        @pl.when(inner & low_half)
        def _():
            far_forward(1 if first else 0, piece)

        @pl.when(inner & jnp.logical_not(low_half))
        def _():
            far_forward(0 if first else 1, piece)

    @pl.when(z == 0)
    def _():
        for copy in far_loads:
            copy.wait()
        for piece in range(len(pieces)):
            far_copy(1, piece).start()

    @pl.when(z == shards - 1)
    def _():
        for copy in far_loads:
            copy.wait()
        for piece in range(len(pieces)):
            far_copy(0, piece).start()

    def near_copy(tile):
        return remote(
            tiles_ref.at[tile],
            near_ref.at[tile // 2],
            near_send.at[tile],
            near_recv.at[tile],
            {"expert": sibling},
        )

    def plane_copy(tile):
        return remote(
            tiles_ref.at[tile],
            plane_land.at[tile // PLANE, chip],
            plane_send.at[tile],
            plane_recv.at[tile // PLANE, chip],
            {"expert": lax.rem(tile, PLANE)},
        )

    def line_copy(k, far):
        return remote(
            plane_ref.at[k, pl.ds(pl.multiple_of(far * depth, depth), depth)],
            line_land.at[k, z],
            line_send.at[k, far],
            line_recv.at[k, z],
            {"dp": far},
        )

    def final_copy(k, peer):
        tile = me + PLANE * k
        return remote(
            final_ref.at[tile],
            final_ref.at[tile],
            final_send.at[k, peer],
            final_recv.at[tile],
            {"expert": peer},
        )

    def leave(tile):
        @pl.when(lax.rem(tile, 2) != core)
        def _():
            near_copy(tile).start()

    def combine(tile):
        @pl.when(lax.rem(tile, 2) == core)
        def _():
            landed(near_ref.at[tile // 2], near_recv.at[tile])
            tiles_ref[tile] = (
                tiles_ref[tile].astype(F32) + near_ref[tile // 2].astype(F32)
            ).astype(BF)

            @pl.when(lax.rem(tile, PLANE) != me)
            def _():
                plane_copy(tile).start()

    def plane_sum(k):
        total = tiles_ref[me + PLANE * k].astype(F32)
        for j in range(1, chips):
            far = lax.rem(chip + j, chips)
            landed(plane_land.at[k, far], plane_recv.at[k, far])
            total = total + plane_land[k, far].astype(F32)
        plane_ref[k] = total.astype(BF)
        for j in range(1, shards):
            line_copy(k, lax.rem(z + j, shards)).start()

    def line_sum(k):
        mine = pl.ds(pl.multiple_of(z * depth, depth), depth)
        total = plane_ref[k, mine].astype(F32)
        for j in range(1, shards):
            far = lax.rem(z + j, shards)
            landed(line_land.at[k, far], line_recv.at[k, far])
            total = total + line_land[k, far].astype(F32)
        final_ref[me + PLANE * k] = total.astype(BF)
        for j in range(1, PLANE):
            final_copy(k, lax.rem(me + j, PLANE)).start()

    lane = lax.broadcasted_iota(jnp.int32, (1, 128), 1)
    groups, _, _, cap_pad, _ = back_ref.shape
    slots = groups * cap_pad
    slot = lax.broadcasted_iota(jnp.int32, (1, slots), 1)
    sums_ref[...] = jnp.zeros_like(sums_ref)

    def phase_one(image, carry):
        here = pl.ds(pl.multiple_of(image * rows, rows), rows)
        for kind in range(3):
            view = (back_ref.at[:, image], hidden_ref.at[image], grad_ref.at[image])[kind]
            landed(view, load_sem.at[kind, image])

        @pl.when(image == 0)
        def _():
            weight_load.wait()
            small_ref[...] = weight_ref[:, 4 * width :].astype(F32).T

        out_grad = grad_ref[image]
        hidden = hidden_ref[image]
        probs = probs_ref[image]
        answers = back_ref[:, image, 0].reshape(slots, width)
        answer_grads = back_ref[:, image, 1].reshape(slots, width)
        result = hidden
        d_probs = jnp.zeros_like(probs)
        both = None
        for j in range(2):
            pick = (slot == slot_cols_ref[image, :, j : j + 1]).astype(F32)
            both = pick if both is None else both + pick
            chosen = lane - 4 == cols_ref[image, :, j : j + 1]
            gate = jnp.sum(jnp.where(chosen, probs, 0.0), axis=-1, keepdims=True)
            picked = dot(pick.astype(BF), answers)
            result = result + gate * picked
            d_gate = jnp.sum(picked * out_grad, axis=-1, keepdims=True)
            d_probs = jnp.where(chosen, d_gate, d_probs)
        d_logits = probs * (d_probs - jnp.sum(d_probs * probs, axis=-1, keepdims=True))
        d_logits = d_logits.astype(BF)
        d_logits_ref[here, :] = d_logits
        d_two = dot(both.astype(BF), answer_grads) + dot_nt(d_logits, weight_ref[:, 4 * width :])
        hat, inverse = norm_stats(hidden)
        sums_ref[2:3, :] += jnp.sum(d_two * hat, axis=0, keepdims=True)
        sums_ref[3:4, :] += jnp.sum(d_two, axis=0, keepdims=True)
        d_hat = d_two * small_ref[2:3, :]
        d_hidden = out_grad + inverse * (
            d_hat
            - jnp.mean(d_hat, axis=-1, keepdims=True)
            - hat * jnp.mean(d_hat * hat, axis=-1, keepdims=True)
        )
        d_branch = d_hidden.astype(BF)
        d_branch_ref[here, :] = d_branch
        d_mixed_ref[here, :] = dot_nt(d_branch, weight_ref[:, 3 * width : 4 * width]).astype(BF)
        grad_ref[image] = d_hidden
        hidden_ref[image] = result
        pltpu.make_async_copy(hidden_ref.at[image], out_hbm.at[image], store_sem.at[0, image]).start()
        return carry

    lax.fori_loop(0, batches, phase_one, 0)

    @pl.when(inner)
    def _():
        for copy in far_loads:
            copy.wait()

    pass_on(True, 0)
    for kind, view in ((3, mixed_ref), (4, two_ref), (5, one_ref)):
        for image in range(batches):
            landed(view.at[pl.ds(image * rows, rows)], load_sem.at[kind, image])
    proj = dot_tn(mixed_ref[...], d_branch_ref[...]).astype(BF)
    for tile in range(head_tiles):
        tiles_ref[tile] = proj[:, tile * TILE : (tile + 1) * TILE]
    for tile in range(head_tiles):
        leave(tile)
    one_flip[...] = one_ref[...].T
    flipped = dot_tn(d_logits_ref[...], two_ref[...])
    for image in range(batches):
        landed(qkv_ref.at[pl.ds(image * rows, rows)], load_sem.at[6, image])

    key_ok = lax.broadcasted_iota(jnp.int32, (1, rows), 1) < SEQ
    scale = HEAD ** (-0.5)

    def phase_two(pair, carry):
        low = pl.multiple_of(pair * TILE, TILE)
        spots = [pl.ds(pl.multiple_of(part * width + low, TILE), TILE) for part in range(3)]
        for image in range(batches):
            here = pl.ds(image * rows, rows)
            query, keys, values = (qkv_ref[here, spot] for spot in spots)
            d_mixed = d_mixed_ref[here, pl.ds(low, TILE)]
            total = [None, None, None]
            for side in range(2):
                mine = (lane // HEAD) == side

                def own(array):
                    return jnp.where(mine, array, jnp.zeros_like(array))

                my_query = own(query)
                my_d_mixed = own(d_mixed)
                scores = dot_nt(my_query, keys) * scale
                scores = jnp.where(key_ok, scores, NEG)
                log_total = jnp.sum(
                    jnp.where(lane == 2 * pair + side, lse_ref[image], 0.0), axis=-1, keepdims=True
                )
                probs_h = jnp.exp(scores - log_total)
                d_weights = dot_nt(my_d_mixed, values)
                row_terms = jnp.sum(d_weights * probs_h, axis=-1, keepdims=True)
                d_scores = (probs_h * (d_weights - row_terms) * scale).astype(BF)
                fresh = (
                    dot(d_scores, own(keys)),
                    dot_tn(d_scores, my_query),
                    dot_tn(probs_h.astype(BF), my_d_mixed),
                )
                total = [new if old is None else old + new for old, new in zip(total, fresh)]
            for part in range(3):
                d_qkv_ref[here, spots[part]] = total[part].astype(BF)
        first = head_tiles + 3 * pair
        for part in range(3):
            tiles_ref[first + part] = dot(one_flip[...], d_qkv_ref[:, spots[part]]).astype(BF)
        for part in range(3):
            leave(first + part)

        @pl.when(pair == 0)
        def _():
            for tile in range(head_tiles):
                combine(tile)

        @pl.when(pair > 0)
        def _():
            for part in range(3):
                combine(first - 3 + part)

        for turn, first, piece in FAR_TURNS:

            @pl.when(pair == turn)
            def _():
                pass_on(first, piece)

        @pl.when(pair == pairs - 3)
        def _():
            plane_sum(0)

        @pl.when(pair == pairs - 1)
        def _():
            line_sum(0)
            plane_sum(1)

        return carry

    lax.fori_loop(0, pairs, phase_two, 0)
    for part in range(3):
        combine(head_tiles + 3 * (pairs - 1) + part)

    for image in range(batches):
        landed(x_ref.at[image], load_sem.at[7, image])

    def phase_three(image, carry):
        here = pl.ds(pl.multiple_of(image * rows, rows), rows)
        d_one = dot_nt(d_qkv_ref[here, :], weight_ref[:, : 3 * width])
        hat, inverse = norm_stats(x_ref[image])
        sums_ref[0:1, :] += jnp.sum(d_one * hat, axis=0, keepdims=True)
        sums_ref[1:2, :] += jnp.sum(d_one, axis=0, keepdims=True)
        d_hat = d_one * small_ref[0:1, :]
        x_ref[image] = grad_ref[image] + inverse * (
            d_hat
            - jnp.mean(d_hat, axis=-1, keepdims=True)
            - hat * jnp.mean(d_hat * hat, axis=-1, keepdims=True)
        )
        pltpu.make_async_copy(x_ref.at[image], dx_hbm.at[image], store_sem.at[1, image]).start()

        @pl.when(image == batches // 2 - 1)
        def _():
            pass_on(True, 7)
            pass_on(False, 5)
            line_sum(1)
            plane_sum(2)

        return carry

    lax.fori_loop(0, batches, phase_three, 0)

    def small_copy(k):
        peer = lax.rem(me + k, PLANE)
        return remote(
            sums_ref, small_land.at[me], small_send.at[peer], small_recv.at[me], {"expert": peer}
        )

    def small_far_copy(k):
        peer = lax.rem(z + k, shards)
        return remote(
            small_land.at[me],
            small_far.at[z],
            small_send.at[PLANE + peer],
            small_recv.at[PLANE + z],
            {"dp": peer},
        )

    sums_ref[...] += flipped[: sums_ref.shape[0]]
    for k in range(1, PLANE):
        small_copy(k).start()
    pass_on(False, 6)
    line_sum(2)
    total = sums_ref[...]
    for k in range(1, PLANE):
        peer = lax.rem(me + k, PLANE)
        landed(small_land.at[peer], small_recv.at[peer])
        total = total + small_land[peer]
    small_land[me] = total
    for k in range(1, shards):
        small_far_copy(k).start()
    for k in range(1, shards):
        peer = lax.rem(z + k, shards)
        landed(small_far.at[peer], small_recv.at[PLANE + peer])
        total = total + small_far[peer]
    small_grad_ref[...] = total
    pass_on(False, 7)

    def finish(tile, carry):
        @pl.when(lax.rem(tile, PLANE) != me)
        def _():
            landed(final_ref.at[tile], final_recv.at[tile])

        @pl.when(lax.rem(tile, 2) != core)
        def _():
            near_copy(tile).wait_send()

        @pl.when((lax.rem(tile, 2) == core) & (lax.rem(tile, PLANE) != me))
        def _():
            plane_copy(tile).wait_send()

        return carry

    lax.fori_loop(0, 4 * head_tiles, finish, 0)
    for tile in range(head_tiles):
        proj_grad_ref[:, tile * TILE : (tile + 1) * TILE] = final_ref[tile].astype(F32)
    for pair in range(pairs):
        for part in range(3):
            low = part * width + pair * TILE
            qkv_grad_ref[:, low : low + TILE] = final_ref[head_tiles + 3 * pair + part].astype(F32)
    for k in range(own_tiles):
        for j in range(1, shards):
            line_copy(k, lax.rem(z + j, shards)).wait_send()
        for j in range(1, PLANE):
            final_copy(k, lax.rem(me + j, PLANE)).wait_send()
    for k in range(1, PLANE):
        small_copy(k).wait_send()
    for k in range(1, shards):
        small_far_copy(k).wait_send()
    for piece in range(len(pieces)):

        @pl.when(z == 0)
        def _():
            far_take(0, piece)

        @pl.when(z == shards - 1)
        def _():
            far_take(1, piece)

    mine = jnp.where(z == shards - 1, 1, 0)
    ends = [
        pltpu.make_async_copy(far_in_ref.at[mine], end_in_hbm, far_load.at[0, 0]),
        pltpu.make_async_copy(far_out_ref.at[mine], end_out_hbm, far_load.at[0, 1]),
    ]
    for copy in ends:
        copy.start()
    for piece in range(len(pieces)):

        @pl.when(z < shards - 1)
        def _():
            far_copy(1, piece).wait_send()

        @pl.when(z > 0)
        def _():
            far_copy(0, piece).wait_send()

    for copy in ends:
        copy.wait()
    for image in range(batches):
        pltpu.make_async_copy(hidden_ref.at[image], out_hbm.at[image], store_sem.at[0, image]).wait()
        pltpu.make_async_copy(x_ref.at[image], dx_hbm.at[image], store_sem.at[1, image]).wait()


def run_reduce(x, grad, weight, cols, slot_cols, back, saved, far, experts):
    batches, rows, width = x.shape
    total = weight.shape[1]
    shards = lax.axis_size("dp")
    qkv, mixed, lse, hidden, one, two, probs = saved
    depth = width // shards
    tiles = 4 * width // TILE
    own_tiles = tiles // PLANE
    small_rows = ceil_to(4 + experts, 8)
    count = len(pieces_of(far[0].shape[1], far[1].shape[1], FAR_CUTS))
    anywhere = pl.BlockSpec(memory_space=pl.ANY)
    inside = pl.BlockSpec(memory_space=pltpu.VMEM)
    dma = pltpu.SemaphoreType.DMA
    return pl.pallas_call(
        functools.partial(reduce_kernel, experts, shards),
        out_shape=(
            jax.ShapeDtypeStruct(x.shape, F32),
            jax.ShapeDtypeStruct(x.shape, F32),
            jax.ShapeDtypeStruct(far[0].shape[1:], BF),
            jax.ShapeDtypeStruct(far[1].shape[1:], BF),
            jax.ShapeDtypeStruct((depth, 3 * width), F32),
            jax.ShapeDtypeStruct((depth, width), F32),
            jax.ShapeDtypeStruct((small_rows, width), F32),
        ),
        in_specs=[inside] * 4 + [anywhere] * 11,
        out_specs=(anywhere,) * 4 + (inside,) * 3,
        scratch_shapes=[
            pltpu.VMEM(x.shape, F32),
            pltpu.VMEM(x.shape, F32),
            pltpu.VMEM(weight.shape, BF),
            pltpu.VMEM(back.shape, BF),
            pltpu.VMEM((batches * rows, 3 * width), BF),
            pltpu.VMEM((batches * rows, width), BF),
            pltpu.VMEM(x.shape, F32),
            pltpu.VMEM((batches * rows, width), BF),
            pltpu.VMEM((batches * rows, width), BF),
            pltpu.VMEM((SMALL, width), F32),
            pltpu.VMEM((small_rows, width), F32),
            pltpu.VMEM((width, batches * rows), BF),
            pltpu.VMEM((batches * rows, 3 * width), BF),
            pltpu.VMEM((batches * rows, width), BF),
            pltpu.VMEM((batches * rows, width), BF),
            pltpu.VMEM((batches * rows, SMALL), BF),
            pltpu.VMEM((tiles, width, TILE), BF),
            pltpu.VMEM((tiles // 2, width, TILE), BF),
            pltpu.VMEM((own_tiles, PLANE // 2, width, TILE), BF),
            pltpu.VMEM((own_tiles, width, TILE), BF),
            pltpu.VMEM((own_tiles, shards, depth, TILE), BF),
            pltpu.VMEM((tiles, depth, TILE), BF),
            pltpu.VMEM((PLANE, small_rows, width), F32),
            pltpu.VMEM((shards, small_rows, width), F32),
            pltpu.VMEM(far[0].shape, BF),
            pltpu.VMEM(far[1].shape, BF),
            pltpu.VMEM(far[0].shape, BF),
            pltpu.VMEM(far[1].shape, BF),
            dma((9, batches)),
            dma((2, batches)),
            dma((tiles,)),
            dma((tiles,)),
            dma((tiles,)),
            dma((own_tiles, PLANE // 2)),
            dma((own_tiles, shards)),
            dma((own_tiles, shards)),
            dma((own_tiles, PLANE)),
            dma((tiles,)),
            dma((PLANE + shards,)),
            dma((PLANE + shards,)),
            dma((2, 2)),
            dma((2, count)),
            dma((2, count)),
        ],
        compiler_params=pltpu.CompilerParams(
            vmem_limit_bytes=VMEM_MAX, collective_id=3, has_side_effects=True
        ),
        cost_estimate=pl.CostEstimate(
            flops=16000000000, bytes_accessed=50000000, transcendentals=2000000
        ),
        name="tail",
    )(cols, slot_cols, lse, probs, x, grad, weight, back, qkv, mixed, hidden, one, two, *far)


def last_turn(far_in, far_out):
    at = lax.axis_index("dp") // (lax.axis_size("dp") - 1)
    return [lax.psum(far.astype(F32), "dp").astype(BF)[at] for far in (far_in, far_out)]


def per_device(
    inputs,
    gain_one,
    shift_one,
    qkv_weight,
    proj_weight,
    gain_two,
    shift_two,
    router_weight,
    expert_in,
    expert_bias,
    expert_out,
    out_grad,
    routes,
    priority,
    capacity,
):
    batches = priority.shape[0]
    count = inputs.shape[0] // batches
    width = inputs.shape[1]
    experts = router_weight.shape[1]
    groups = lax.axis_size("expert")
    cap_pad = ceil_to(max(2, (5 * count + 2 * experts - 1) // (2 * experts)), 16)
    depth = qkv_weight.shape[0]
    both = ("dp", "expert")

    vectors = jnp.stack([gain_one, shift_one, gain_two, shift_two], axis=1)
    small = jnp.concatenate([vectors, router_weight], axis=1)
    small = jnp.pad(small, ((0, 0), (0, SMALL - small.shape[1])))
    dense = (qkv_weight, proj_weight, small)
    own = (expert_in[0], jnp.pad(expert_bias, ((0, BIAS_ROWS - 1), (0, 0))), expert_out[0])
    cols = jnp.concatenate([routes, priority.reshape(batches * SEQ, 2)], axis=1)
    cols = cols.reshape(batches, SEQ, 4)
    cols = jnp.pad(cols, ((0, 0), (0, SEQ_PAD - SEQ), (0, 0)), constant_values=-1)
    rows_first = jnp.swapaxes(cols, 1, 2)
    received, x, grad, weight, qkv, mixed, hidden, one, two, lse, probs, slot_cols, *spread = run_front(
        inputs, out_grad, dense, own, cols, rows_first, capacity, experts, cap_pad
    )
    saved = (qkv, mixed, lse, hidden, one, two, probs)
    back, sum_in, sum_out, far_in, far_out = run_moe(received, own, *spread)
    z = lax.axis_index("dp")
    at_end = (z == 0) | (z == lax.axis_size("dp") - 1)
    spot = 4 * width
    if groups == PLANE:
        outputs, inputs_grad, end_in, end_out, qkv_grad, proj_grad, small_grad = run_reduce(
            x, grad, weight, cols, slot_cols, back, saved, (far_in, far_out), experts
        )
        small_grad = lax.dynamic_slice_in_dim(
            small_grad, lax.axis_index("dp") * depth, depth, axis=1
        )
        vectors = [small_grad[k] for k in range(4)]
        router_grad = small_grad[4 : 4 + experts].T
    else:
        outputs, inputs_grad, dense = run_tail(
            x, grad, weight, cols, slot_cols, back, saved, experts
        )
        end_in, end_out = last_turn(far_in, far_out)
        dense = lax.psum_scatter(dense, both, scatter_dimension=0, tiled=True)
        dense = lax.all_gather(dense, "expert", axis=0, tiled=True).astype(F32)
        qkv_grad = dense[:, : 3 * width]
        proj_grad = dense[:, 3 * width : spot]
        vectors = [dense[:, spot + k] for k in range(4)]
        router_grad = dense[:, spot + 4 : spot + 4 + experts]
    grad_in = jnp.where(at_end, end_in, sum_in).astype(F32)
    grad_out = jnp.where(at_end, end_out, sum_out).astype(F32)
    return (
        outputs[:, :SEQ].reshape(batches * SEQ, width),
        inputs_grad[:, :SEQ].reshape(batches * SEQ, width),
        vectors[0],
        vectors[1],
        qkv_grad,
        proj_grad,
        vectors[2],
        vectors[3],
        router_grad,
        grad_in[None, :width],
        grad_in[None, width],
        grad_out[None],
    )


def solution(mesh):
    token = P(("dp", "expert"), None)
    vector = P("dp")
    matrix = P("dp", None)
    return jax.shard_map(
        per_device,
        mesh=mesh,
        in_specs=(
            token,
            vector,
            vector,
            matrix,
            matrix,
            vector,
            vector,
            matrix,
            P("expert", None, "dp"),
            P("expert", "dp"),
            P("expert", "dp", None),
            token,
            token,
            token,
            P(("dp", "expert")),
        ),
        out_specs=(
            token,
            token,
            vector,
            vector,
            matrix,
            matrix,
            vector,
            vector,
            matrix,
            P("expert", None, "dp"),
            P("expert", "dp"),
            P("expert", "dp", None),
        ),
        check_vma=False,
    )
```

```python
import functools

import jax
import jax.numpy as jnp
from jax import lax
from jax.experimental import pallas as pl
from jax.experimental.pallas import tpu as pltpu
from jax.sharding import PartitionSpec as P

HEADS = 12
HEAD = 64
SEQ = 197
SEQ_PAD = 208
EPS = 1e-06
BF = jnp.bfloat16
F32 = jnp.float32
SMALL = 128
MESH = pl.DeviceIdType.MESH
EARLY_PIECES = range(3)
LATE_PIECES = range(3, 4)
EARLY_FAR = 2
FAR_CUTS = 4
FAR_TURNS = (
    (0, True, 4),
    (0, False, 2),
    (1, True, 5),
    (1, False, 3),
    (3, True, 6),
    (3, False, 4),
    (4, True, 7),
    (4, False, 5),
)
TILE = 128
PLANE = 8
BIAS_ROWS = 16
NEG = -1e30
VMEM_LIMIT = 60 * 1024 * 1024
VMEM_MAX = 67043328


def ceil_to(value, step):
    return (value + step - 1) // step * step


def dot(a, b):
    return jnp.dot(a, b, preferred_element_type=F32)


def dot_nt(a, b):
    return lax.dot_general(a, b, (((1,), (1,)), ((), ())), preferred_element_type=F32)


def dot_tn(a, b):
    return lax.dot_general(a, b, (((0,), (0,)), ((), ())), preferred_element_type=F32)


def params(count=1):
    return pltpu.CompilerParams(
        dimension_semantics=("arbitrary",) * count, vmem_limit_bytes=VMEM_LIMIT
    )


class Line:
    def __init__(self, shards):
        self.shards = shards
        self.me = lax.axis_index("dp")
        self.has_below = self.me > 0
        self.has_above = self.me < shards - 1

    def greet(self, me, groups):
        barrier = pltpu.get_barrier_semaphore()
        for k in range(1, groups):
            pl.semaphore_signal(
                barrier, inc=1, device_id={"expert": lax.rem(me + k, groups)}, device_id_type=MESH
            )
        for k in range(1, self.shards):
            pl.semaphore_signal(
                barrier,
                inc=1,
                device_id={"dp": lax.rem(self.me + k, self.shards)},
                device_id_type=MESH,
            )
        pl.semaphore_wait(barrier, groups - 1 + self.shards - 1)

    def views(self, pair, slot):
        tall, span = pair[0].shape[1:]
        return [
            pair[kind].at[slot, pl.ds(low, size)] for kind, low, size in pieces_of(tall, span)
        ]

    def hop(self, way, round_id, source, target, send_sem, arrived, some=range(4)):
        step = 1 - 2 * way
        slot = self.me - step * round_id
        places = self.views(target, slot)
        if round_id == 0:
            body, bias, out = source
            tall, span = target[0].shape[1:]
            moves = []
            for piece, (kind, low, size) in enumerate(pieces_of(tall, span)):
                own = out if kind else body
                here = min(size, own.shape[0] - low)
                moves.append((own.at[pl.ds(low, here)], target[kind].at[slot, pl.ds(low, here)], piece))
                if here < size:
                    moves.append((bias, target[kind].at[slot, pl.ds(low + here, size - here)], piece))
        else:
            origins = self.views(source, slot)
            moves = [(origins[piece], places[piece], piece) for piece in some]
        return [
            pltpu.make_async_remote_copy(
                src_ref=origin,
                dst_ref=place,
                send_sem=send_sem.at[way, round_id, k if round_id == 0 else piece],
                recv_sem=arrived.at[slot, piece],
                device_id={"dp": self.me + step},
                device_id_type=MESH,
            )
            for k, (origin, place, piece) in enumerate(moves)
        ]

    def sends(self, way, round_id):
        if way == 0:
            return (self.me >= round_id) & self.has_above
        return (self.me + round_id < self.shards) & self.has_below

    def push(self, round_id, source, target, send_sem, arrived, some=range(4)):
        for way in range(2):

            @pl.when(self.sends(way, round_id))
            def _():
                for copy in self.hop(way, round_id, source, target, send_sem, arrived, some):
                    copy.start()

    def drain(self, round_id, source, target, send_sem, arrived, some=range(4)):
        for way in range(2):

            @pl.when(self.sends(way, round_id))
            def _():
                for copy in self.hop(way, round_id, source, target, send_sem, arrived, some):
                    copy.wait_send()

    def receive(self, round_id, target, arrived, some=range(4)):
        far = round_id + 1

        @pl.when(self.me >= far)
        def _():
            self.wait_slot(self.me - far, target, arrived, some)

        @pl.when(self.me + far < self.shards)
        def _():
            self.wait_slot(self.me + far, target, arrived, some)

    def wait_slot(self, slot, target, arrived, some=range(4)):
        places = self.views(target, slot)
        for piece in some:
            pltpu.make_async_copy(places[piece], places[piece], arrived.at[slot, piece]).wait()


def route(cap_pad, cols_ref, rows_ref, limit_ref, slot_rows_ref, slot_cols_ref):
    for b in range(cols_ref.shape[0]):
        limit = limit_ref[b]
        col = [cols_ref[b, :, k : k + 1] for k in range(4)]
        row = [rows_ref[b, k : k + 1, :] for k in range(4)]
        for j in range(2):
            rank_row = 0
            rank_col = 0
            for k in range(2):
                hit = (col[k] == row[j]) & (col[2 + k] < row[2 + j])
                rank_row = rank_row + jnp.sum(hit.astype(jnp.int32), axis=0, keepdims=True)
                hit = (row[k] == col[j]) & (row[2 + k] < col[2 + j])
                rank_col = rank_col + jnp.sum(hit.astype(jnp.int32), axis=1, keepdims=True)
            keep_row = (rank_row < limit) & (row[j] >= 0)
            keep_col = (rank_col < limit) & (col[j] >= 0)
            slot_rows_ref[b, j : j + 1, :] = jnp.where(keep_row, row[j] * cap_pad + rank_row, -1)
            slot_cols_ref[b, :, j : j + 1] = jnp.where(keep_col, col[j] * cap_pad + rank_col, -1)


def norm_stats(values):
    average = jnp.mean(values, axis=-1, keepdims=True)
    centered = values - average
    spread = jnp.mean(centered * centered, axis=-1, keepdims=True)
    inverse = lax.rsqrt(spread + EPS)
    return centered * inverse, inverse


def front_kernel(
    experts,
    shards,
    limit_ref,
    cols_ref,
    rows_ref,
    raw_hbm,
    raw_grad_hbm,
    qkv_own,
    proj_own,
    small_own,
    own_body,
    own_bias,
    own_out,
    received_ref,
    x_hbm,
    grad_hbm,
    weight_hbm,
    qkv_hbm,
    mixed_hbm,
    hidden_hbm,
    one_hbm,
    two_hbm,
    lse_ref,
    probs_ref,
    slot_cols_ref,
    vectors_ref,
    spread_in_ref,
    spread_out_ref,
    raw_ref,
    raw_grad_ref,
    x_ref,
    grad_ref,
    weight_ref,
    qkv_ref,
    mixed_ref,
    hidden_ref,
    one_ref,
    two_ref,
    small_land,
    slot_rows_ref,
    send_ref,
    load_sem,
    store_sem,
    send_sem,
    arrived,
    rows_send,
    rows_recv,
    small_send,
    small_recv,
    line_send,
    piece_recv,
    plane_send,
    near_send,
):
    batches, rows, width = x_ref.shape
    groups = received_ref.shape[0]
    cap_pad = received_ref.shape[3]
    me = lax.axis_index("expert")
    line = Line(shards)
    z = line.me
    own = (own_body, own_bias, own_out)
    spread = (spread_in_ref, spread_out_ref)
    depth = width // shards
    piece_width = 4 * width // PLANE
    base = me // PLANE * PLANE
    spot = me - base
    core = lax.rem(me, 2)
    sibling = me + 1 - 2 * core
    chip = spot // 2
    chips = PLANE // 2
    cut = 3 * width // piece_width

    def remote(source, target, send, recv, peer):
        return pltpu.make_async_remote_copy(
            src_ref=source,
            dst_ref=target,
            send_sem=send,
            recv_sem=recv,
            device_id=peer,
            device_id_type=MESH,
        )

    def landed(view, sem):
        pltpu.make_async_copy(view, view, sem).wait()

    def rows_of(shard):
        return pl.ds(pl.multiple_of(shard * depth, depth), depth)

    def piece(shard, index):
        low = pl.multiple_of(index * piece_width, piece_width)
        return weight_ref.at[rows_of(shard), pl.ds(low, piece_width)]

    raws = [
        pltpu.make_async_copy(raw_hbm, raw_ref, load_sem.at[0]),
        pltpu.make_async_copy(raw_grad_hbm, raw_grad_ref, load_sem.at[1]),
    ]
    mine = [
        pltpu.make_async_copy(
            qkv_own, weight_ref.at[rows_of(z), pl.ds(0, 3 * width)], load_sem.at[2]
        ),
        pltpu.make_async_copy(
            proj_own, weight_ref.at[rows_of(z), pl.ds(3 * width, width)], load_sem.at[3]
        ),
        pltpu.make_async_copy(small_own, small_land.at[z], load_sem.at[4]),
    ]
    for copy in mine:
        copy.start()
    for copy in raws:
        copy.start()
    line.greet(me, groups)
    for copy in mine:
        copy.wait()

    def small_copy(far):
        view = small_land.at[z]
        return remote(view, view, small_send.at[far], small_recv.at[z], {"dp": far})

    def line_copy(far):
        view = piece(z, spot)
        return remote(view, view, line_send.at[far], piece_recv.at[z, spot], {"dp": far})

    def plane_copy(shard, other):
        view = piece(shard, spot)
        peer = base + 2 * other + core
        return remote(
            view, view, plane_send.at[shard, other], piece_recv.at[shard, spot], {"expert": peer}
        )

    def near_copy(shard, other):
        index = 2 * other + core
        view = piece(shard, index)
        return remote(
            view, view, near_send.at[shard, other], piece_recv.at[shard, index], {"expert": sibling}
        )

    peers = [lax.rem(z + k, shards) for k in range(1, shards)]
    others = [lax.rem(chip + k, chips) for k in range(1, chips)]
    for far in peers:
        line_copy(far).start()
    for far in peers:
        small_copy(far).start()
    line.push(0, own, spread, send_sem, arrived)
    zero_rows = jnp.zeros((rows - SEQ, width), F32)

    def pad_image(image):
        x_ref[image, :SEQ] = raw_ref[image * SEQ : (image + 1) * SEQ]
        x_ref[image, SEQ:] = zero_rows
        pltpu.make_async_copy(x_ref.at[image], x_hbm.at[image], store_sem.at[0, image]).start()
        grad_ref[image, :SEQ] = raw_grad_ref[image * SEQ : (image + 1) * SEQ]
        grad_ref[image, SEQ:] = zero_rows
        pltpu.make_async_copy(
            grad_ref.at[image], grad_hbm.at[image], store_sem.at[1, image]
        ).start()

    for copy in raws:
        copy.wait()
    pad_image(0)
    for far in peers:
        landed(piece(far, spot), piece_recv.at[far, spot])
        for other in others:
            plane_copy(far, other).start()
        near_copy(far, chip).start()
    for image in range(1, batches):
        pad_image(image)
    slot_rows_ref[...] = jnp.full(slot_rows_ref.shape, -1, jnp.int32)
    slot_cols_ref[...] = jnp.full(slot_cols_ref.shape, -1, jnp.int32)
    route(cap_pad, cols_ref, rows_ref, limit_ref, slot_rows_ref, slot_cols_ref)
    slot_cols_ref[:, :, 2:4] = cols_ref[:, :, 0:2]
    for far in peers:
        for other in others:
            index = 2 * other + core
            landed(piece(far, index), piece_recv.at[far, index])
            near_copy(far, other).start()
    for far in peers:
        landed(small_land.at[far], small_recv.at[far])
        for k in range(chips):
            index = 2 * k + 1 - core
            landed(piece(far, index), piece_recv.at[far, index])
    weight_store = pltpu.make_async_copy(weight_ref, weight_hbm, load_sem.at[5])
    weight_store.start()
    used = small_land.shape[1]
    small_rows = jnp.concatenate(
        [small_land[shard, :, :depth].astype(F32) for shard in range(shards)], axis=1
    )
    vectors_ref[...] = jnp.zeros_like(vectors_ref)
    vectors_ref[:used] = small_rows.astype(BF)
    gain_one, shift_one, gain_two, shift_two = (small_rows[k : k + 1] for k in range(4))

    def rows_copy(image, target):
        return remote(
            send_ref.at[image, target],
            received_ref.at[me, image],
            rows_send.at[image, target],
            rows_recv.at[me, image],
            {"expert": target},
        )

    saves = (
        (qkv_ref, qkv_hbm),
        (mixed_ref, mixed_hbm),
        (hidden_ref, hidden_hbm),
        (one_ref, one_hbm),
        (two_ref, two_hbm),
    )
    lane = lax.broadcasted_iota(jnp.int32, (1, 128), 1)
    key_ok = lax.broadcasted_iota(jnp.int32, (1, rows), 1) < SEQ
    slot = lax.broadcasted_iota(jnp.int32, (groups * cap_pad, 1), 0)
    scale = HEAD ** (-0.5)

    def do_image(index, carry):
        x = x_ref[index]
        hat, _ = norm_stats(x)
        one = (hat * gain_one + shift_one).astype(BF)
        one_ref[index] = one
        qkv_ref[index] = dot(one, weight_ref[:, : 3 * width]).astype(BF)
        lse = jnp.zeros((rows, 128), F32)
        for pair in range(HEADS // 2):
            low = pair * 128
            query = qkv_ref[index, :, low : low + 128]
            keys = qkv_ref[index, :, width + low : width + low + 128]
            values = qkv_ref[index, :, 2 * width + low : 2 * width + low + 128]
            total = None
            for side in range(2):
                part_of = (lane // HEAD) == side
                scores = dot_nt(jnp.where(part_of, query, jnp.zeros_like(query)), keys) * scale
                scores = jnp.where(key_ok, scores, NEG)
                highest = jnp.max(scores, axis=-1, keepdims=True)
                expo = jnp.exp(scores - highest)
                denom = jnp.sum(expo, axis=-1, keepdims=True)
                weights = (expo / denom).astype(BF)
                lse = jnp.where(lane == 2 * pair + side, highest + jnp.log(denom), lse)
                part = dot(weights, jnp.where(part_of, values, jnp.zeros_like(values)))
                total = part if total is None else total + part
            mixed_ref[index, :, low : low + 128] = total.astype(BF)
        lse_ref[index] = lse
        hidden = x + dot(mixed_ref[index], weight_ref[:, 3 * width : 4 * width])
        hidden_ref[index] = hidden
        hat, _ = norm_stats(hidden)
        two = (hat * gain_two + shift_two).astype(BF)
        two_ref[index] = two
        logits = dot_nt(two, vectors_ref[...])
        in_router = (lane >= 4) & (lane < 4 + experts)
        logits = jnp.where(in_router, logits, NEG)
        expo = jnp.exp(logits - jnp.max(logits, axis=-1, keepdims=True))
        probs = expo / jnp.sum(expo, axis=-1, keepdims=True)
        probs_ref[index] = probs
        out_grad = grad_ref[index]
        both = None
        grads = None
        for j in range(2):
            gate = jnp.sum(
                jnp.where(lane - 4 == cols_ref[index, :, j : j + 1], probs, 0.0),
                axis=-1,
                keepdims=True,
            )
            pick = (slot == slot_rows_ref[index, j : j + 1, :]).astype(F32)
            both = pick if both is None else both + pick
            part = dot(pick.astype(BF), (gate * out_grad).astype(BF))
            grads = part if grads is None else grads + part
        sent = dot(both.astype(BF), two).astype(BF)
        send_ref[index, :, 0] = sent.reshape(groups, cap_pad, width)
        send_ref[index, :, 1] = grads.astype(BF).reshape(groups, cap_pad, width)
        for k in range(1, groups):
            rows_copy(index, lax.rem(me + k, groups)).start()
        pltpu.make_async_copy(
            send_ref.at[index, me], received_ref.at[me, index], rows_recv.at[me, index]
        ).start()
        for k, (here, there) in enumerate(saves):
            pltpu.make_async_copy(here.at[index], there.at[index], store_sem.at[2 + k, index]).start()
        return carry

    lax.fori_loop(0, batches, do_image, 0)

    line.receive(0, spread, arrived)
    line.push(1, spread, spread, send_sem, arrived, EARLY_PIECES)

    def finish(image, carry):
        for k in range(groups):
            source = lax.rem(me + k, groups)
            if k:
                rows_copy(image, source).wait_send()
            landed(received_ref.at[source, image], rows_recv.at[source, image])
        pltpu.make_async_copy(x_ref.at[image], x_hbm.at[image], store_sem.at[0, image]).wait()
        pltpu.make_async_copy(grad_ref.at[image], grad_hbm.at[image], store_sem.at[1, image]).wait()
        for k, (here, there) in enumerate(saves):
            pltpu.make_async_copy(here.at[image], there.at[image], store_sem.at[2 + k, image]).wait()
        return carry

    lax.fori_loop(0, batches, finish, 0)
    weight_store.wait()
    for far in peers:
        line_copy(far).wait_send()
        small_copy(far).wait_send()
        for other in others:
            plane_copy(far, other).wait_send()
        for k in range(chips):
            near_copy(far, k).wait_send()
    line.receive(1, spread, arrived, EARLY_PIECES)
    line.drain(0, own, spread, send_sem, arrived)
    line.drain(1, spread, spread, send_sem, arrived, EARLY_PIECES)


def run_front(raw, raw_grad, dense, own, cols, rows_first, limits, experts, cap_pad):
    batches, rows = cols.shape[:2]
    width = raw.shape[1]
    shards = lax.axis_size("dp")
    groups = lax.axis_size("expert")
    body, bias, out = own
    tall = body.shape[0] + bias.shape[0]
    anywhere = pl.BlockSpec(memory_space=pl.ANY)
    inside = pl.BlockSpec(memory_space=pltpu.VMEM)
    dma = pltpu.SemaphoreType.DMA
    chips = PLANE // 2

    def shape(*dims, dtype=BF):
        return jax.ShapeDtypeStruct((batches, rows) + dims, dtype)

    return pl.pallas_call(
        functools.partial(front_kernel, experts, shards),
        out_shape=(
            jax.ShapeDtypeStruct((groups, batches, 2, cap_pad, width), BF),
            shape(width, dtype=F32),
            shape(width, dtype=F32),
            jax.ShapeDtypeStruct((width, 4 * width), BF),
            shape(3 * width),
            shape(width),
            shape(width, dtype=F32),
            shape(width),
            shape(width),
            shape(128, dtype=F32),
            shape(SMALL, dtype=F32),
            shape(8, dtype=jnp.int32),
            jax.ShapeDtypeStruct((SMALL, width), BF),
            jax.ShapeDtypeStruct((shards, tall, body.shape[1]), BF),
            jax.ShapeDtypeStruct((shards,) + out.shape, BF),
        ),
        in_specs=[pl.BlockSpec(memory_space=pltpu.SMEM), inside, inside] + [anywhere] * 8,
        out_specs=(anywhere,) * 9 + (inside,) * 4 + (anywhere,) * 2,
        scratch_shapes=[
            pltpu.VMEM(raw.shape, F32),
            pltpu.VMEM(raw.shape, F32),
            pltpu.VMEM((batches, rows, width), F32),
            pltpu.VMEM((batches, rows, width), F32),
            pltpu.VMEM((width, 4 * width), BF),
            pltpu.VMEM((batches, rows, 3 * width), BF),
            pltpu.VMEM((batches, rows, width), BF),
            pltpu.VMEM((batches, rows, width), F32),
            pltpu.VMEM((batches, rows, width), BF),
            pltpu.VMEM((batches, rows, width), BF),
            pltpu.VMEM((shards,) + dense[2].shape, BF),
            pltpu.VMEM((batches, 8, rows), jnp.int32),
            pltpu.VMEM((batches, groups, 2, cap_pad, width), BF),
            dma((6,)),
            dma((7, batches)),
            dma((2, 2, 5)),
            dma((shards, 4)),
            dma((batches, groups)),
            dma((groups, batches)),
            dma((shards,)),
            dma((shards,)),
            dma((shards,)),
            dma((shards, PLANE)),
            dma((shards, chips)),
            dma((shards, chips)),
        ],
        compiler_params=pltpu.CompilerParams(
            vmem_limit_bytes=VMEM_LIMIT, collective_id=1, has_side_effects=True
        ),
        cost_estimate=pl.CostEstimate(
            flops=8000000000, bytes_accessed=40000000, transcendentals=3000000
        ),
        name="front",
    )(limits, cols, rows_first, raw, raw_grad, *dense, *own)


def pieces_of(tall, span, cuts=2):
    pieces = []
    for kind, extent in enumerate((tall, span)):
        size = ceil_to(-(-extent // cuts), 16)
        for low in range(0, extent, size):
            pieces.append((kind, low, min(size, extent - low)))
    return tuple(pieces)


def moe_kernel(
    shards,
    groups,
    x_hbm,
    own_body,
    own_bias,
    own_out,
    spread_in_ref,
    spread_out_ref,
    back_ref,
    sum_in_ref,
    sum_out_ref,
    far_in_ref,
    far_out_ref,
    rows_ref,
    win_ref,
    wout_ref,
    y_acc,
    dx_acc,
    gin_acc,
    gout_acc,
    part_in_ref,
    part_out_ref,
    land_in_ref,
    land_out_ref,
    far_land,
    rows_sem,
    own_sem,
    far_send,
    far_recv,
    weight_send,
    arrived,
    sum_send,
    sum_recv,
    back_send,
    back_recv,
    final_sem,
):
    line = Line(shards)
    z = line.me
    me = lax.axis_index("expert")
    _, batches, _, cap_pad, width = rows_ref.shape
    _, tall, span = spread_in_ref.shape
    group = max(1, 512 // (batches * cap_pad))
    while groups % group:
        group -= 1
    blocks = groups // group
    rows = group * batches * cap_pad
    spread = (win_ref, wout_ref)
    early_spread = (spread_in_ref, spread_out_ref)
    own = (own_body, own_bias, own_out)
    parts = (part_in_ref, part_out_ref)
    lands = (land_in_ref, land_out_ref)
    pieces = pieces_of(tall, span)
    far_pieces = pieces_of(tall, span, FAR_CUTS)

    for k in range(groups):
        source = lax.rem(me + k, groups)
        pltpu.make_async_copy(x_hbm.at[source], rows_ref.at[source], rows_sem.at[source]).start()
    own_places = (
        (own_body, win_ref.at[z, pl.ds(0, width)], 0),
        (own_bias, win_ref.at[z, pl.ds(width, tall - width)], 1),
        (own_out, wout_ref.at[z], 2),
    )
    own_loads = [
        pltpu.make_async_copy(here, there, own_sem.at[k]) for here, there, k in own_places
    ]

    def fetch(far, some):
        for sign in (-1, 1):
            slot = z + sign * far

            @pl.when((slot >= 0) & (slot < shards))
            def _():
                origins = line.views(early_spread, slot)
                places = line.views(spread, slot)
                for piece in some:
                    pltpu.make_async_copy(
                        origins[piece], places[piece], arrived.at[slot, piece]
                    ).start()

    fetch(1, range(4))
    fetch(2, EARLY_PIECES)
    for copy in own_loads:
        copy.start()

    line.greet(me, groups)
    line.push(1, early_spread, spread, weight_send, arrived, LATE_PIECES)
    line.push(2, early_spread, spread, weight_send, arrived, EARLY_PIECES)

    table = []
    for at in range(shards):
        near = sorted(range(shards), key=lambda q: (abs(q - at), q))
        table.append(near[1:-1] + near[:1] + near[-1:])

    def quarter(step):
        total = 0
        for at in range(shards):
            for s in range(shards):
                hit = jnp.where((z == at) & (step == s), table[at][s], 0)
                total = total + hit
        return total

    def sum_copy(way, q, piece):
        kind, low, size = pieces[piece]
        if way == 0:
            slot = q - 1
            peer = z + 1
        else:
            slot = jnp.where(q == z - 1, shards - 2, q - 1)
            peer = z - 1
        cut = pl.ds(low, size)
        return pltpu.make_async_remote_copy(
            src_ref=parts[kind].at[q, cut],
            dst_ref=lands[kind].at[slot, cut],
            send_sem=sum_send.at[way, q, piece],
            recv_sem=sum_recv.at[slot, piece],
            device_id={"dp": peer},
            device_id_type=MESH,
        )

    def take_sum(slot, q, piece):
        kind, low, size = pieces[piece]
        cut = pl.ds(low, size)
        view = lands[kind].at[slot, cut]
        pltpu.make_async_copy(view, view, sum_recv.at[slot, piece]).wait()
        parts[kind][q, cut] = (
            parts[kind][q, cut].astype(F32) + lands[kind][slot, cut].astype(F32)
        ).astype(BF)

    def back_copy(source):
        return pltpu.make_async_remote_copy(
            src_ref=rows_ref.at[source],
            dst_ref=back_ref.at[me],
            send_sem=back_send.at[source],
            recv_sem=back_recv.at[me],
            device_id={"expert": source},
            device_id_type=MESH,
        )

    def back_start(first):
        for k in range(group):
            source = first + k

            @pl.when(source != me)
            def _():
                back_copy(source).start()

            @pl.when(source == me)
            def _():
                pltpu.make_async_copy(
                    rows_ref.at[source], back_ref.at[source], back_recv.at[source]
                ).start()

    def block_first(block):
        lead = me // group
        if blocks == 4:
            order = (3 - lead, lead + 1 - 2 * lax.rem(lead, 2), lax.rem(lead + 2, 4), lead)
            picked = 0
            for k in range(4):
                picked = picked + jnp.where(block == k, order[k], 0)
            return picked * group
        return lax.rem(lead + 1 + block, blocks) * group

    plain = (shards - 2) * blocks
    late_item = max(1, blocks - 1)
    inner = (z > 0) & (z < shards - 1)

    def do_item(item, carry):
        late = item >= plain
        rest = item - plain
        step = jnp.where(late, shards - 2 + lax.rem(rest + 2 * blocks, 2), item // blocks)
        block = jnp.where(late, (rest + 2 * blocks) // 2 - blocks, lax.rem(item, blocks))
        q = quarter(step)
        bank = jnp.where(step == shards - 1, 1, 0)

        @pl.when(block == 0)
        def _():
            far = jnp.abs(q - z)

            @pl.when(far == 0)
            def _():
                for copy in own_loads:
                    copy.wait()

            @pl.when(far == 2)
            def _():
                line.wait_slot(q, spread, arrived, EARLY_PIECES)

            @pl.when((far == 1) | (far > 2))
            def _():
                line.wait_slot(q, spread, arrived)

            for distance in range(3, shards - 1):
                for way in range(2):
                    forward = 1 - 2 * way

                    @pl.when((q == z - forward * distance) & line.sends(way, distance))
                    def _():
                        for copy in line.hop(way, distance, spread, spread, weight_send, arrived):
                            copy.start()

        @pl.when(item == late_item)
        def _():
            line.receive(1, spread, arrived, LATE_PIECES)
            line.push(2, spread, spread, weight_send, arrived, LATE_PIECES)

        @pl.when((step == shards - 2) & (block > 0))
        def _():
            back_start(block_first(block - 1))

        lead = block_first(block)
        low = pl.multiple_of(lead * (batches * cap_pad), rows)
        here = pl.ds(low, rows)
        mine = pl.ds(lead, group)

        @pl.when(step == 0)
        def _():
            for k in range(group):
                view = rows_ref.at[lead + k]
                pltpu.make_async_copy(view, view, rows_sem.at[lead + k]).wait()

        x = rows_ref[mine, :, 0].reshape(rows, width)
        grad = rows_ref[mine, :, 1].reshape(rows, width)
        win = win_ref[q, :width, :]
        wout = wout_ref[q]
        pre = dot(x, win) + win_ref[q, width : width + 1, :].astype(F32)
        cdf = 0.5 * lax.erf(pre * (0.5**0.5)) + 0.5
        active = (pre * cdf).astype(BF)
        slope = cdf + pre * (jnp.exp(-0.5 * pre * pre) * 0.3989422804014327)
        d_pre = (dot_nt(grad, wout) * slope).astype(BF)
        y_part = dot(active, wout)
        dx_part = dot_nt(d_pre, win)

        @pl.when(step == 0)
        def _():
            y_acc[here, :] = y_part
            dx_acc[here, :] = dx_part

        @pl.when(step > 0)
        def _():
            y_acc[here, :] += y_part
            dx_acc[here, :] += dx_part

        gout = dot_tn(active, grad)
        gin = dot_tn(x, d_pre)
        gbias = jnp.sum(d_pre.astype(F32), axis=0, keepdims=True)

        @pl.when(block == 0)
        def _():
            gout_acc[bank] = gout
            gin_acc[bank, :width, :] = gin
            gin_acc[bank, width : width + 1, :] = gbias

        @pl.when(block > 0)
        def _():
            gout_acc[bank] += gout
            gin_acc[bank, :width, :] += gin
            gin_acc[bank, width : width + 1, :] += gbias

        @pl.when(step == shards - 1)
        def _():
            shape = (group, batches, cap_pad, width)
            rows_ref[mine, :, 0] = y_acc[here, :].astype(BF).reshape(shape)
            rows_ref[mine, :, 1] = dx_acc[here, :].astype(BF).reshape(shape)

        @pl.when(block == blocks - 1)
        def _():
            part_in_ref[q, :width, :] = gin_acc[bank, :width, :].astype(BF)
            part_in_ref[q, width:, :] = jnp.broadcast_to(
                gin_acc[bank, width : width + 1, :].astype(BF), (tall - width, span)
            )
            part_out_ref[q] = gout_acc[bank].astype(BF)

            @pl.when((z == 0) & (q > z) & (q < shards - 1))
            def _():
                for piece in range(len(pieces)):
                    sum_copy(0, q, piece).start()

            @pl.when((z == shards - 1) & (q < z) & (q > 0))
            def _():
                for piece in range(len(pieces)):
                    sum_copy(1, q, piece).start()

        return carry

    lax.fori_loop(0, shards * blocks, do_item, 0)
    back_start(block_first(blocks - 1))

    def early_far(k, piece):
        _, low, size = far_pieces[piece]
        cut = pl.ds(low, size)
        return pltpu.make_async_remote_copy(
            src_ref=part_in_ref.at[(shards - 1) * k, cut],
            dst_ref=far_land.at[k, cut],
            send_sem=far_send.at[piece],
            recv_sem=far_recv.at[piece],
            device_id={"dp": z + 2 * k - 1},
            device_id_type=MESH,
        )

    def early_add(k, piece):
        _, low, size = far_pieces[piece]
        cut = pl.ds(low, size)
        view = far_land.at[k, cut]
        pltpu.make_async_copy(view, view, far_recv.at[piece]).wait()
        part_in_ref[(shards - 1) * k, cut] = (
            part_in_ref[(shards - 1) * k, cut].astype(F32) + far_land[k, cut].astype(F32)
        ).astype(BF)

    for piece in range(EARLY_FAR):

        @pl.when(z == 0)
        def _():
            early_far(1, piece).start()

        @pl.when(z == shards - 1)
        def _():
            early_far(0, piece).start()

    finals = [
        pltpu.make_async_copy(part_in_ref.at[0], far_in_ref.at[0], final_sem.at[0]),
        pltpu.make_async_copy(part_out_ref.at[0], far_out_ref.at[0], final_sem.at[1]),
        pltpu.make_async_copy(part_in_ref.at[shards - 1], far_in_ref.at[1], final_sem.at[2]),
        pltpu.make_async_copy(part_out_ref.at[shards - 1], far_out_ref.at[1], final_sem.at[3]),
        pltpu.make_async_copy(part_in_ref.at[z], sum_in_ref, final_sem.at[4]),
        pltpu.make_async_copy(part_out_ref.at[z], sum_out_ref, final_sem.at[5]),
    ]
    def do_forward(turn, carry):
        up = turn
        down = shards - 1 - turn
        for piece in range(len(pieces)):

            @pl.when((up > z) & (z > 0))
            def _():
                take_sum(up - 1, up, piece)
                sum_copy(0, up, piece).start()

            @pl.when((down < z) & (z < shards - 1))
            def _():
                take_sum(down - 1, down, piece)
                sum_copy(1, down, piece).start()

        return carry

    lax.fori_loop(1, shards - 1, do_forward, 0)
    for piece in range(len(pieces)):

        @pl.when(inner)
        def _():
            take_sum(z - 1, z, piece)
            take_sum(shards - 2, z, piece)

    for copy in finals[4:]:
        copy.start()
    for piece in range(EARLY_FAR):

        @pl.when(z == 1)
        def _():
            early_add(1, piece)

        @pl.when(z == shards - 2)
        def _():
            early_add(0, piece)

    for copy in finals[:4]:
        copy.start()

    def finish_sum(q, carry):
        @pl.when((q > z) & line.has_above)
        def _():
            for piece in range(len(pieces)):
                sum_copy(0, q, piece).wait_send()

        @pl.when((q < z) & line.has_below)
        def _():
            for piece in range(len(pieces)):
                sum_copy(1, q, piece).wait_send()

        return carry

    lax.fori_loop(1, shards - 1, finish_sum, 0)
    line.drain(1, spread, spread, weight_send, arrived, LATE_PIECES)
    for round_id in range(2, shards - 1):
        line.drain(round_id, spread, spread, weight_send, arrived)
    for piece in range(EARLY_FAR):

        @pl.when(z == 0)
        def _():
            early_far(1, piece).wait_send()

        @pl.when(z == shards - 1)
        def _():
            early_far(0, piece).wait_send()

    for k in range(groups):
        source = lax.rem(me + k, groups)
        if k:
            back_copy(source).wait_send()
        view = back_ref.at[source]
        pltpu.make_async_copy(view, view, back_recv.at[source]).wait()
    for copy in finals:
        copy.wait()


def run_moe(received, own, spread_in, spread_out):
    groups, batches, _, cap_pad, width = received.shape
    shards, tall, span = spread_in.shape
    total = groups * batches * cap_pad
    count = len(pieces_of(tall, span))
    early_rows = sum(pieces_of(tall, span, FAR_CUTS)[EARLY_FAR - 1][1:])
    anywhere = pl.BlockSpec(memory_space=pl.ANY)
    return pl.pallas_call(
        functools.partial(moe_kernel, shards, groups),
        out_shape=(
            jax.ShapeDtypeStruct(received.shape, BF),
            jax.ShapeDtypeStruct((tall, span), BF),
            jax.ShapeDtypeStruct((span, width), BF),
            jax.ShapeDtypeStruct((2, tall, span), BF),
            jax.ShapeDtypeStruct((2, span, width), BF),
        ),
        in_specs=[anywhere] * 6,
        out_specs=(anywhere,) * 5,
        scratch_shapes=[
            pltpu.VMEM(received.shape, BF),
            pltpu.VMEM((shards, tall, span), BF),
            pltpu.VMEM((shards, span, width), BF),
            pltpu.VMEM((total, width), F32),
            pltpu.VMEM((total, width), F32),
            pltpu.VMEM((2, ceil_to(width + 1, 8), span), F32),
            pltpu.VMEM((2, span, width), F32),
            pltpu.VMEM((shards, tall, span), BF),
            pltpu.VMEM((shards, span, width), BF),
            pltpu.VMEM((shards - 1, tall, span), BF),
            pltpu.VMEM((shards - 1, span, width), BF),
            pltpu.VMEM((2, early_rows, span), BF),
            pltpu.SemaphoreType.DMA((groups,)),
            pltpu.SemaphoreType.DMA((3,)),
            pltpu.SemaphoreType.DMA((EARLY_FAR,)),
            pltpu.SemaphoreType.DMA((EARLY_FAR,)),
            pltpu.SemaphoreType.DMA((2, shards, 4)),
            pltpu.SemaphoreType.DMA((shards, 4)),
            pltpu.SemaphoreType.DMA((2, shards, count)),
            pltpu.SemaphoreType.DMA((shards - 1, count)),
            pltpu.SemaphoreType.DMA((groups,)),
            pltpu.SemaphoreType.DMA((groups,)),
            pltpu.SemaphoreType.DMA((6,)),
        ],
        compiler_params=pltpu.CompilerParams(
            vmem_limit_bytes=VMEM_MAX, collective_id=2, has_side_effects=True
        ),
        cost_estimate=pl.CostEstimate(
            flops=12 * total * width * span * shards,
            bytes_accessed=60000000,
            transcendentals=2 * total * span * shards,
        ),
        name="moe",
    )(received, *own, spread_in, spread_out)


def tail_kernel(
    experts,
    x_ref,
    grad_ref,
    weight_ref,
    cols_ref,
    slot_cols_ref,
    back_ref,
    qkv_ref,
    mixed_ref,
    lse_ref,
    hidden_ref,
    one_ref,
    two_ref,
    probs_ref,
    out_ref,
    dx_ref,
    dense_ref,
    small_ref,
    sums_ref,
    d_qkv_ref,
    d_branch_ref,
    d_logits_ref,
    one_all,
    two_all,
    mixed_all,
):
    width = x_ref.shape[-1]
    rows = x_ref.shape[1]
    index = pl.program_id(0)

    @pl.when(index == 0)
    def _():
        small_ref[...] = weight_ref[:, 4 * width :].astype(F32).T
        sums_ref[...] = jnp.zeros_like(sums_ref)

    here = pl.ds(pl.multiple_of(index * rows, rows), rows)
    one_all[here, :] = one_ref[0]
    two_all[here, :] = two_ref[0]
    mixed_all[here, :] = mixed_ref[0]
    out_grad = grad_ref[0]
    hidden = hidden_ref[0]
    probs = probs_ref[0]
    lane = lax.broadcasted_iota(jnp.int32, (1, 128), 1)
    slots = back_ref.shape[0] * back_ref.shape[3]
    slot = lax.broadcasted_iota(jnp.int32, (1, slots), 1)
    answers = back_ref[:, 0, 0].reshape(slots, width)
    answer_grads = back_ref[:, 0, 1].reshape(slots, width)
    result = hidden
    d_probs = jnp.zeros_like(probs)
    both = None
    for j in range(2):
        pick = (slot == slot_cols_ref[0, :, j : j + 1]).astype(F32)
        both = pick if both is None else both + pick
        chosen = lane - 4 == cols_ref[0, :, j : j + 1]
        gate = jnp.sum(jnp.where(chosen, probs, 0.0), axis=-1, keepdims=True)
        picked = dot(pick.astype(BF), answers)
        result = result + gate * picked
        d_gate = jnp.sum(picked * out_grad, axis=-1, keepdims=True)
        d_probs = jnp.where(chosen, d_gate, d_probs)
    out_ref[0] = result
    d_logits = probs * (d_probs - jnp.sum(d_probs * probs, axis=-1, keepdims=True))
    d_logits = d_logits.astype(BF)
    d_logits_ref[here, :] = d_logits
    d_two = dot(both.astype(BF), answer_grads) + dot_nt(d_logits, weight_ref[:, 4 * width :])
    hat, inverse = norm_stats(hidden)
    sums_ref[2:3, :] += jnp.sum(d_two * hat, axis=0, keepdims=True)
    sums_ref[3:4, :] += jnp.sum(d_two, axis=0, keepdims=True)
    d_hat = d_two * small_ref[2:3, :]
    d_hidden = out_grad + inverse * (
        d_hat
        - jnp.mean(d_hat, axis=-1, keepdims=True)
        - hat * jnp.mean(d_hat * hat, axis=-1, keepdims=True)
    )
    d_branch = d_hidden.astype(BF)
    d_branch_ref[here, :] = d_branch
    d_mixed_all = dot_nt(d_branch, weight_ref[:, 3 * width : 4 * width]).astype(BF)
    key_ok = lax.broadcasted_iota(jnp.int32, (1, rows), 1) < SEQ
    scale = HEAD ** (-0.5)
    for pair in range(HEADS // 2):
        low = pair * 128
        query = qkv_ref[0, :, low : low + 128]
        keys = qkv_ref[0, :, width + low : width + low + 128]
        values = qkv_ref[0, :, 2 * width + low : 2 * width + low + 128]
        d_mixed = d_mixed_all[:, low : low + 128]
        d_query = d_keys = d_values = None
        for side in range(2):
            mine = (lane // HEAD) == side
            head = 2 * pair + side

            def own(array):
                return jnp.where(mine, array, jnp.zeros_like(array))

            my_query = own(query)
            my_keys = own(keys)
            my_d_mixed = own(d_mixed)
            scores = dot_nt(my_query, keys) * scale
            scores = jnp.where(key_ok, scores, NEG)
            probs_h = jnp.exp(scores - lse_ref[0, :, head : head + 1])
            d_weights = dot_nt(my_d_mixed, values)
            row_terms = jnp.sum(d_weights * probs_h, axis=-1, keepdims=True)
            d_scores = (probs_h * (d_weights - row_terms) * scale).astype(BF)
            parts = (
                dot(d_scores, my_keys),
                dot_tn(d_scores, my_query),
                dot_tn(probs_h.astype(BF), my_d_mixed),
            )
            if side == 0:
                d_query, d_keys, d_values = parts
            else:
                d_query, d_keys, d_values = (
                    d_query + parts[0],
                    d_keys + parts[1],
                    d_values + parts[2],
                )
        d_qkv_ref[here, low : low + 128] = d_query.astype(BF)
        d_qkv_ref[here, width + low : width + low + 128] = d_keys.astype(BF)
        d_qkv_ref[here, 2 * width + low : 2 * width + low + 128] = d_values.astype(BF)
    d_one = dot_nt(d_qkv_ref[here, :], weight_ref[:, : 3 * width])
    hat, inverse = norm_stats(x_ref[0])
    sums_ref[0:1, :] += jnp.sum(d_one * hat, axis=0, keepdims=True)
    sums_ref[1:2, :] += jnp.sum(d_one, axis=0, keepdims=True)
    d_hat = d_one * small_ref[0:1, :]
    dx_ref[0] = d_hidden + inverse * (
        d_hat
        - jnp.mean(d_hat, axis=-1, keepdims=True)
        - hat * jnp.mean(d_hat * hat, axis=-1, keepdims=True)
    )

    @pl.when(index == pl.num_programs(0) - 1)
    def _():
        dense_ref[:, 4 * width :] = (dot_tn(two_all[...], d_logits_ref[...]) + sums_ref[...].T).astype(BF)
        dense_ref[:, 3 * width : 4 * width] = dot_tn(mixed_all[...], d_branch_ref[...]).astype(BF)
        for part in range(3):
            cut = slice(part * width, (part + 1) * width)
            dense_ref[:, cut] = dot_tn(one_all[...], d_qkv_ref[:, cut]).astype(BF)


def run_tail(x, grad, weight, cols, slot_cols, back, saved, experts):
    batches, rows, width = x.shape
    total = weight.shape[1]
    cap_pad = back.shape[3]
    qkv, mixed, lse, hidden, one, two, probs = saved

    def block(*shape):
        return pl.BlockSpec((1,) + shape, lambda i: (i,) + (0,) * len(shape))

    return pl.pallas_call(
        functools.partial(tail_kernel, experts),
        grid=(batches,),
        out_shape=(
            jax.ShapeDtypeStruct(x.shape, F32),
            jax.ShapeDtypeStruct(x.shape, F32),
            jax.ShapeDtypeStruct((width, total), BF),
        ),
        in_specs=[
            block(rows, width),
            block(rows, width),
            pl.BlockSpec((width, total), lambda i: (0, 0), pipeline_mode=pl.Buffered(1)),
            block(rows, 4),
            block(rows, 8),
            pl.BlockSpec((experts, 1, 2, cap_pad, width), lambda i: (0, i, 0, 0, 0)),
            block(rows, 3 * width),
            block(rows, width),
            block(rows, 128),
            block(rows, width),
            block(rows, width),
            block(rows, width),
            block(rows, SMALL),
        ],
        out_specs=(
            block(rows, width),
            block(rows, width),
            pl.BlockSpec((width, total), lambda i: (0, 0), pipeline_mode=pl.Buffered(1)),
        ),
        scratch_shapes=[
            pltpu.VMEM((SMALL, width), F32),
            pltpu.VMEM((SMALL, width), F32),
            pltpu.VMEM((batches * rows, 3 * width), BF),
            pltpu.VMEM((batches * rows, width), BF),
            pltpu.VMEM((batches * rows, SMALL), BF),
            pltpu.VMEM((batches * rows, width), BF),
            pltpu.VMEM((batches * rows, width), BF),
            pltpu.VMEM((batches * rows, width), BF),
        ],
        compiler_params=params(),
        cost_estimate=pl.CostEstimate(
            flops=16000000000, bytes_accessed=50000000, transcendentals=2000000
        ),
        name="tail",
    )(x, grad, weight, cols, slot_cols, back, qkv, mixed, lse, hidden, one, two, probs)


def reduce_kernel(
    experts,
    shards,
    slot_cols_ref,
    lse_ref,
    probs_ref,
    vectors_ref,
    x_hbm,
    grad_hbm,
    weight_hbm,
    back_hbm,
    qkv_hbm,
    mixed_hbm,
    hidden_hbm,
    one_hbm,
    two_hbm,
    far_in_hbm,
    far_out_hbm,
    out_hbm,
    dx_hbm,
    end_in_hbm,
    end_out_hbm,
    qkv_grad_ref,
    proj_grad_ref,
    small_grad_ref,
    x_ref,
    grad_ref,
    weight_ref,
    back_ref,
    qkv_ref,
    mixed_ref,
    hidden_ref,
    one_ref,
    two_ref,
    raw_ref,
    sums_ref,
    one_flip,
    d_qkv_ref,
    d_branch_ref,
    d_mixed_ref,
    d_logits_ref,
    tiles_ref,
    near_ref,
    plane_land,
    plane_ref,
    line_land,
    final_ref,
    small_land,
    small_far,
    far_in_ref,
    far_out_ref,
    far_in_land,
    far_out_land,
    load_sem,
    store_sem,
    near_send,
    near_recv,
    plane_send,
    plane_recv,
    line_send,
    line_recv,
    final_send,
    final_recv,
    small_send,
    small_recv,
    far_load,
    far_send,
    far_recv,
):
    batches, rows, width = x_ref.shape
    z = lax.axis_index("dp")
    me = lax.axis_index("expert")
    core = lax.rem(me, 2)
    sibling = me + 1 - 2 * core
    chip = me // 2
    chips = PLANE // 2
    pairs = HEADS // 2
    depth = width // shards
    head_tiles = width // TILE
    own_tiles = (4 * width // TILE) // PLANE

    def loads(kind, image):
        pair = {
            0: (back_hbm.at[:, image], back_ref.at[:, image]),
            1: (hidden_hbm.at[image], hidden_ref.at[image]),
            2: (grad_hbm.at[image], grad_ref.at[image]),
            3: (mixed_hbm.at[image], mixed_ref.at[pl.ds(image * rows, rows)]),
            4: (two_hbm.at[image], two_ref.at[pl.ds(image * rows, rows)]),
            5: (one_hbm.at[image], one_ref.at[pl.ds(image * rows, rows)]),
            6: (qkv_hbm.at[image], qkv_ref.at[pl.ds(image * rows, rows)]),
            7: (x_hbm.at[image], x_ref.at[image]),
        }[kind]
        return pltpu.make_async_copy(pair[0], pair[1], load_sem.at[kind, image])

    weight_load = pltpu.make_async_copy(weight_hbm, weight_ref, load_sem.at[8, 0])
    far_parts = (far_in_ref, far_out_ref)
    far_lands = (far_in_land, far_out_land)
    far_loads = [
        pltpu.make_async_copy(source.at[k], target.at[k], far_load.at[k, part])
        for k in range(2)
        for part, (source, target) in enumerate(
            ((far_in_hbm, far_in_ref), (far_out_hbm, far_out_ref))
        )
    ]

    for copy in far_loads:
        copy.start()
    for kind in range(3):
        loads(kind, 0).start()
    weight_load.start()
    for image in range(1, batches):
        for kind in range(3):
            loads(kind, image).start()
    for kind in range(3, 8):
        for image in range(batches):
            loads(kind, image).start()

    barrier = pltpu.get_barrier_semaphore()
    for k in range(1, PLANE):
        pl.semaphore_signal(
            barrier, inc=1, device_id={"expert": lax.rem(me + k, PLANE)}, device_id_type=MESH
        )
    for k in range(1, shards):
        pl.semaphore_signal(
            barrier, inc=1, device_id={"dp": lax.rem(z + k, shards)}, device_id_type=MESH
        )
    pl.semaphore_wait(barrier, PLANE - 1 + shards - 1)

    def remote(source, target, send_sem, recv_sem, peer):
        return pltpu.make_async_remote_copy(
            src_ref=source,
            dst_ref=target,
            send_sem=send_sem,
            recv_sem=recv_sem,
            device_id=peer,
            device_id_type=MESH,
        )

    def landed(view, sem):
        pltpu.make_async_copy(view, view, sem).wait()

    pieces = pieces_of(far_in_ref.shape[1], far_out_ref.shape[1], FAR_CUTS)
    inner = (z > 0) & (z < shards - 1)
    low_half = 2 * z < shards

    def far_copy(k, piece):
        kind, low, size = pieces[piece]
        cut = pl.ds(low, size)
        return remote(
            far_parts[kind].at[k, cut],
            far_lands[kind].at[k, cut],
            far_send.at[k, piece],
            far_recv.at[k, piece],
            {"dp": z + 2 * k - 1},
        )

    def far_take(k, piece):
        kind, low, size = pieces[piece]
        cut = pl.ds(low, size)
        landed(far_lands[kind].at[k, cut], far_recv.at[k, piece])
        far_parts[kind][k, cut] = (
            far_parts[kind][k, cut].astype(F32) + far_lands[kind][k, cut].astype(F32)
        ).astype(BF)

    def far_forward(k, piece):
        if piece < EARLY_FAR:
            @pl.when(z != (1 if k else shards - 2))
            def _():
                far_take(k, piece)

        else:
            far_take(k, piece)
        far_copy(k, piece).start()

    def pass_on(first, piece):
        @pl.when(inner & low_half)
        def _():
            far_forward(1 if first else 0, piece)

        @pl.when(inner & jnp.logical_not(low_half))
        def _():
            far_forward(0 if first else 1, piece)

    for copy in far_loads:
        copy.wait()

    @pl.when(z == 0)
    def _():
        for piece in range(EARLY_FAR, len(pieces)):
            far_copy(1, piece).start()

    @pl.when(z == shards - 1)
    def _():
        for piece in range(EARLY_FAR, len(pieces)):
            far_copy(0, piece).start()

    def near_copy(tile):
        return remote(
            tiles_ref.at[tile],
            near_ref.at[tile // 2],
            near_send.at[tile],
            near_recv.at[tile],
            {"expert": sibling},
        )

    def plane_copy(tile):
        owner = lax.rem(tile, PLANE) // 2
        place = lax.rem(chip - owner + 2 * chips - 1, chips)
        return remote(
            tiles_ref.at[tile],
            plane_land.at[tile // PLANE, place],
            plane_send.at[tile],
            plane_recv.at[tile // PLANE, place],
            {"expert": lax.rem(tile, PLANE)},
        )

    def line_copy(k, far):
        return remote(
            plane_ref.at[k, pl.ds(pl.multiple_of(far * depth, depth), depth)],
            line_land.at[k, z],
            line_send.at[k, far],
            line_recv.at[k, z],
            {"dp": far},
        )

    def final_copy(k, peer):
        tile = me + PLANE * k
        return remote(
            final_ref.at[tile],
            final_ref.at[tile],
            final_send.at[k, peer],
            final_recv.at[tile],
            {"expert": peer},
        )

    def leave(tile):
        @pl.when(lax.rem(tile, 2) != core)
        def _():
            near_copy(tile).start()

    def combine(tile):
        @pl.when(lax.rem(tile, 2) == core)
        def _():
            landed(near_ref.at[tile // 2], near_recv.at[tile])
            tiles_ref[tile] = (
                tiles_ref[tile].astype(F32) + near_ref[tile // 2].astype(F32)
            ).astype(BF)

            @pl.when(lax.rem(tile, PLANE) != me)
            def _():
                plane_copy(tile).start()

    def plane_sum(k):
        total = tiles_ref[me + PLANE * k].astype(F32)
        for j in range(1, chips):
            landed(plane_land.at[k, j - 1], plane_recv.at[k, j - 1])
            total = total + plane_land[k, j - 1].astype(F32)
        plane_ref[k] = total.astype(BF)
        for j in range(1, shards):
            line_copy(k, lax.rem(z + j, shards)).start()

    def line_sum(k):
        mine = pl.ds(pl.multiple_of(z * depth, depth), depth)
        total = plane_ref[k, mine].astype(F32)
        for j in range(1, shards):
            far = lax.rem(z + j, shards)
            landed(line_land.at[k, far], line_recv.at[k, far])
            total = total + line_land[k, far].astype(F32)
        final_ref[me + PLANE * k] = total.astype(BF)
        for j in range(1, PLANE):
            final_copy(k, lax.rem(me + j, PLANE)).start()

    pass_on(True, 0)
    pass_on(True, 1)

    lane = lax.broadcasted_iota(jnp.int32, (1, 128), 1)
    groups, _, _, cap_pad, _ = back_ref.shape
    slots = groups * cap_pad
    slot = lax.broadcasted_iota(jnp.int32, (1, slots), 1)
    sums_ref[...] = jnp.zeros_like(sums_ref)
    small_rows = vectors_ref[:8].astype(F32)
    gain_one = small_rows[0:1]
    gain_two = small_rows[2:3]

    def phase_one(image, carry):
        here = pl.ds(pl.multiple_of(image * rows, rows), rows)
        for kind in range(3):
            view = (back_ref.at[:, image], hidden_ref.at[image], grad_ref.at[image])[kind]
            landed(view, load_sem.at[kind, image])

        @pl.when(image == 0)
        def _():
            weight_load.wait()

        out_grad = grad_ref[image]
        hidden = hidden_ref[image]
        probs = probs_ref[image]
        answers = back_ref[:, image, 0].reshape(slots, width)
        answer_grads = back_ref[:, image, 1].reshape(slots, width)
        result = hidden
        d_probs = jnp.zeros_like(probs)
        both = None
        for j in range(2):
            pick = (slot == slot_cols_ref[image, :, j : j + 1]).astype(F32)
            both = pick if both is None else both + pick
            chosen = lane - 4 == slot_cols_ref[image, :, 2 + j : 3 + j]
            gate = jnp.sum(jnp.where(chosen, probs, 0.0), axis=-1, keepdims=True)
            picked = dot(pick.astype(BF), answers)
            result = result + gate * picked
            d_gate = jnp.sum(picked * out_grad, axis=-1, keepdims=True)
            d_probs = jnp.where(chosen, d_gate, d_probs)
        d_logits = probs * (d_probs - jnp.sum(d_probs * probs, axis=-1, keepdims=True))
        d_logits = d_logits.astype(BF)
        d_logits_ref[here, :] = d_logits
        d_two = dot(both.astype(BF), answer_grads) + dot(d_logits, vectors_ref[...])
        hat, inverse = norm_stats(hidden)
        sums_ref[2:3, :] += jnp.sum(d_two * hat, axis=0, keepdims=True)
        sums_ref[3:4, :] += jnp.sum(d_two, axis=0, keepdims=True)
        d_hat = d_two * gain_two
        d_hidden = out_grad + inverse * (
            d_hat
            - jnp.mean(d_hat, axis=-1, keepdims=True)
            - hat * jnp.mean(d_hat * hat, axis=-1, keepdims=True)
        )
        d_branch = d_hidden.astype(BF)
        d_branch_ref[here, :] = d_branch
        d_mixed_ref[here, :] = dot_nt(d_branch, weight_ref[:, 3 * width : 4 * width]).astype(BF)
        grad_ref[image] = d_hidden
        hidden_ref[image] = result
        return carry

    lax.fori_loop(0, batches, phase_one, 0)
    for image in range(batches):
        raw_ref[image * SEQ : (image + 1) * SEQ] = hidden_ref[image, :SEQ]
    out_store = pltpu.make_async_copy(raw_ref, out_hbm, store_sem.at[0, 0])
    out_store.start()
    pass_on(True, 2)
    pass_on(True, 3)
    pass_on(False, 0)
    for kind, view in ((3, mixed_ref), (4, two_ref), (5, one_ref)):
        for image in range(batches):
            landed(view.at[pl.ds(image * rows, rows)], load_sem.at[kind, image])
    proj = dot_tn(mixed_ref[...], d_branch_ref[...]).astype(BF)
    for tile in range(head_tiles):
        tiles_ref[tile] = proj[:, tile * TILE : (tile + 1) * TILE]
    for tile in range(head_tiles):
        leave(tile)
    one_flip[...] = one_ref[...].T
    flipped = dot_tn(d_logits_ref[...], two_ref[...])
    for image in range(batches):
        landed(qkv_ref.at[pl.ds(image * rows, rows)], load_sem.at[6, image])

    pass_on(False, 1)

    key_ok = lax.broadcasted_iota(jnp.int32, (1, rows), 1) < SEQ
    scale = HEAD ** (-0.5)

    def phase_two(pair, carry):
        low = pl.multiple_of(pair * TILE, TILE)
        spots = [pl.ds(pl.multiple_of(part * width + low, TILE), TILE) for part in range(3)]
        for image in range(batches):
            here = pl.ds(image * rows, rows)
            query, keys, values = (qkv_ref[here, spot] for spot in spots)
            d_mixed = d_mixed_ref[here, pl.ds(low, TILE)]
            total = [None, None, None]
            for side in range(2):
                mine = (lane // HEAD) == side

                def own(array):
                    return jnp.where(mine, array, jnp.zeros_like(array))

                my_query = own(query)
                my_d_mixed = own(d_mixed)
                scores = dot_nt(my_query, keys) * scale
                scores = jnp.where(key_ok, scores, NEG)
                log_total = jnp.sum(
                    jnp.where(lane == 2 * pair + side, lse_ref[image], 0.0), axis=-1, keepdims=True
                )
                probs_h = jnp.exp(scores - log_total)
                d_weights = dot_nt(my_d_mixed, values)
                row_terms = jnp.sum(d_weights * probs_h, axis=-1, keepdims=True)
                d_scores = (probs_h * (d_weights - row_terms) * scale).astype(BF)
                fresh = (
                    dot(d_scores, own(keys)),
                    dot_tn(d_scores, my_query),
                    dot_tn(probs_h.astype(BF), my_d_mixed),
                )
                total = [new if old is None else old + new for old, new in zip(total, fresh)]
            for part in range(3):
                d_qkv_ref[here, spots[part]] = total[part].astype(BF)
        first = head_tiles + 3 * pair
        for part in range(3):
            tiles_ref[first + part] = dot(one_flip[...], d_qkv_ref[:, spots[part]]).astype(BF)
        for part in range(3):
            leave(first + part)

        @pl.when(pair == 0)
        def _():
            for tile in range(head_tiles):
                combine(tile)

        @pl.when(pair > 0)
        def _():
            for part in range(3):
                combine(first - 3 + part)

        for turn, first, piece in FAR_TURNS:

            @pl.when(pair == turn)
            def _():
                pass_on(first, piece)

        @pl.when(pair == pairs - 3)
        def _():
            plane_sum(0)

        @pl.when(pair == pairs - 1)
        def _():
            line_sum(0)
            plane_sum(1)

        return carry

    lax.fori_loop(0, pairs, phase_two, 0)
    for part in range(3):
        combine(head_tiles + 3 * (pairs - 1) + part)

    for image in range(batches):
        landed(x_ref.at[image], load_sem.at[7, image])

    def phase_three(image, carry):
        here = pl.ds(pl.multiple_of(image * rows, rows), rows)
        d_one = dot_nt(d_qkv_ref[here, :], weight_ref[:, : 3 * width])
        hat, inverse = norm_stats(x_ref[image])
        sums_ref[0:1, :] += jnp.sum(d_one * hat, axis=0, keepdims=True)
        sums_ref[1:2, :] += jnp.sum(d_one, axis=0, keepdims=True)
        d_hat = d_one * gain_one
        x_ref[image] = grad_ref[image] + inverse * (
            d_hat
            - jnp.mean(d_hat, axis=-1, keepdims=True)
            - hat * jnp.mean(d_hat * hat, axis=-1, keepdims=True)
        )

        @pl.when(image == batches // 2 - 1)
        def _():
            pass_on(False, 6)
            line_sum(1)
            plane_sum(2)

        return carry

    lax.fori_loop(0, batches, phase_three, 0)
    out_store.wait()
    for image in range(batches):
        raw_ref[image * SEQ : (image + 1) * SEQ] = x_ref[image, :SEQ]
    dx_store = pltpu.make_async_copy(raw_ref, dx_hbm, store_sem.at[1, 0])
    dx_store.start()

    def small_copy(k):
        peer = lax.rem(me + k, PLANE)
        return remote(
            sums_ref, small_land.at[me], small_send.at[peer], small_recv.at[me], {"expert": peer}
        )

    def small_far_copy(k):
        peer = lax.rem(z + k, shards)
        return remote(
            small_land.at[me],
            small_far.at[z],
            small_send.at[PLANE + peer],
            small_recv.at[PLANE + z],
            {"dp": peer},
        )

    sums_ref[...] += flipped[: sums_ref.shape[0]]
    for k in range(1, PLANE):
        small_copy(k).start()
    pass_on(False, 7)
    line_sum(2)
    total = sums_ref[...]
    for k in range(1, PLANE):
        peer = lax.rem(me + k, PLANE)
        landed(small_land.at[peer], small_recv.at[peer])
        total = total + small_land[peer]
    small_land[me] = total
    for k in range(1, shards):
        small_far_copy(k).start()
    for k in range(1, shards):
        peer = lax.rem(z + k, shards)
        landed(small_far.at[peer], small_recv.at[PLANE + peer])
        total = total + small_far[peer]
    small_grad_ref[...] = total

    def finish(tile, carry):
        @pl.when(lax.rem(tile, PLANE) != me)
        def _():
            landed(final_ref.at[tile], final_recv.at[tile])

        @pl.when(lax.rem(tile, 2) != core)
        def _():
            near_copy(tile).wait_send()

        @pl.when((lax.rem(tile, 2) == core) & (lax.rem(tile, PLANE) != me))
        def _():
            plane_copy(tile).wait_send()

        return carry

    lax.fori_loop(0, 4 * head_tiles, finish, 0)
    for tile in range(head_tiles):
        proj_grad_ref[:, tile * TILE : (tile + 1) * TILE] = final_ref[tile].astype(F32)
    for pair in range(pairs):
        for part in range(3):
            low = part * width + pair * TILE
            qkv_grad_ref[:, low : low + TILE] = final_ref[head_tiles + 3 * pair + part].astype(F32)
    for k in range(own_tiles):
        for j in range(1, shards):
            line_copy(k, lax.rem(z + j, shards)).wait_send()
        for j in range(1, PLANE):
            final_copy(k, lax.rem(me + j, PLANE)).wait_send()
    for k in range(1, PLANE):
        small_copy(k).wait_send()
    for k in range(1, shards):
        small_far_copy(k).wait_send()
    for piece in range(len(pieces)):

        @pl.when(z == 0)
        def _():
            far_take(0, piece)

        @pl.when(z == shards - 1)
        def _():
            far_take(1, piece)

    mine = jnp.where(z == shards - 1, 1, 0)
    ends = [
        pltpu.make_async_copy(far_in_ref.at[mine], end_in_hbm, far_load.at[0, 0]),
        pltpu.make_async_copy(far_out_ref.at[mine], end_out_hbm, far_load.at[0, 1]),
    ]
    for copy in ends:
        copy.start()
    for piece in range(len(pieces)):

        first = 1 if piece < EARLY_FAR else 0

        @pl.when((z < shards - 1) & (z >= first))
        def _():
            far_copy(1, piece).wait_send()

        @pl.when((z > 0) & (z < shards - first))
        def _():
            far_copy(0, piece).wait_send()

    for copy in ends:
        copy.wait()
    dx_store.wait()


def run_reduce(x, grad, weight, vectors, slot_cols, back, saved, far, experts):
    batches, rows, width = x.shape
    shards = lax.axis_size("dp")
    qkv, mixed, lse, hidden, one, two, probs = saved
    depth = width // shards
    tiles = 4 * width // TILE
    own_tiles = tiles // PLANE
    small_rows = ceil_to(4 + experts, 8)
    count = len(pieces_of(far[0].shape[1], far[1].shape[1], FAR_CUTS))
    anywhere = pl.BlockSpec(memory_space=pl.ANY)
    inside = pl.BlockSpec(memory_space=pltpu.VMEM)
    dma = pltpu.SemaphoreType.DMA
    return pl.pallas_call(
        functools.partial(reduce_kernel, experts, shards),
        out_shape=(
            jax.ShapeDtypeStruct((batches * SEQ, width), F32),
            jax.ShapeDtypeStruct((batches * SEQ, width), F32),
            jax.ShapeDtypeStruct(far[0].shape[1:], BF),
            jax.ShapeDtypeStruct(far[1].shape[1:], BF),
            jax.ShapeDtypeStruct((depth, 3 * width), F32),
            jax.ShapeDtypeStruct((depth, width), F32),
            jax.ShapeDtypeStruct((small_rows, width), F32),
        ),
        in_specs=[inside] * 4 + [anywhere] * 11,
        out_specs=(anywhere,) * 4 + (inside,) * 3,
        scratch_shapes=[
            pltpu.VMEM(x.shape, F32),
            pltpu.VMEM(x.shape, F32),
            pltpu.VMEM(weight.shape, BF),
            pltpu.VMEM(back.shape, BF),
            pltpu.VMEM((batches * rows, 3 * width), BF),
            pltpu.VMEM((batches * rows, width), BF),
            pltpu.VMEM(x.shape, F32),
            pltpu.VMEM((batches * rows, width), BF),
            pltpu.VMEM((batches * rows, width), BF),
            pltpu.VMEM((batches * SEQ, width), F32),
            pltpu.VMEM((small_rows, width), F32),
            pltpu.VMEM((width, batches * rows), BF),
            pltpu.VMEM((batches * rows, 3 * width), BF),
            pltpu.VMEM((batches * rows, width), BF),
            pltpu.VMEM((batches * rows, width), BF),
            pltpu.VMEM((batches * rows, SMALL), BF),
            pltpu.VMEM((tiles, width, TILE), BF),
            pltpu.VMEM((tiles // 2, width, TILE), BF),
            pltpu.VMEM((own_tiles, PLANE // 2 - 1, width, TILE), BF),
            pltpu.VMEM((own_tiles, width, TILE), BF),
            pltpu.VMEM((own_tiles, shards, depth, TILE), BF),
            pltpu.VMEM((tiles, depth, TILE), BF),
            pltpu.VMEM((PLANE, small_rows, width), F32),
            pltpu.VMEM((shards, small_rows, width), F32),
            pltpu.VMEM(far[0].shape, BF),
            pltpu.VMEM(far[1].shape, BF),
            pltpu.VMEM(far[0].shape, BF),
            pltpu.VMEM(far[1].shape, BF),
            dma((9, batches)),
            dma((2, batches)),
            dma((tiles,)),
            dma((tiles,)),
            dma((tiles,)),
            dma((own_tiles, PLANE // 2 - 1)),
            dma((own_tiles, shards)),
            dma((own_tiles, shards)),
            dma((own_tiles, PLANE)),
            dma((tiles,)),
            dma((PLANE + shards,)),
            dma((PLANE + shards,)),
            dma((2, 2)),
            dma((2, count)),
            dma((2, count)),
        ],
        compiler_params=pltpu.CompilerParams(
            vmem_limit_bytes=VMEM_MAX, collective_id=3, has_side_effects=True
        ),
        cost_estimate=pl.CostEstimate(
            flops=16000000000, bytes_accessed=50000000, transcendentals=2000000
        ),
        name="tail",
    )(slot_cols, lse, probs, vectors, x, grad, weight, back, qkv, mixed, hidden, one, two, *far)


def last_turn(far_in, far_out):
    at = lax.axis_index("dp") // (lax.axis_size("dp") - 1)
    return [lax.psum(far.astype(F32), "dp").astype(BF)[at] for far in (far_in, far_out)]


def per_device(
    inputs,
    gain_one,
    shift_one,
    qkv_weight,
    proj_weight,
    gain_two,
    shift_two,
    router_weight,
    expert_in,
    expert_bias,
    expert_out,
    out_grad,
    routes,
    priority,
    capacity,
):
    batches = priority.shape[0]
    count = inputs.shape[0] // batches
    width = inputs.shape[1]
    experts = router_weight.shape[1]
    groups = lax.axis_size("expert")
    cap_pad = ceil_to(max(2, (5 * count + 2 * experts - 1) // (2 * experts)), 16)
    depth = qkv_weight.shape[0]
    both = ("dp", "expert")

    used, wide = 4 + experts, gain_one.shape[0]
    small = jnp.concatenate(
        [gain_one, shift_one, gain_two, shift_two, router_weight.T.reshape(-1)]
    ).reshape(used, wide)
    small = jnp.pad(small, ((0, ceil_to(used, 16) - used), (0, ceil_to(wide, 128) - wide)))
    dense = (qkv_weight, proj_weight, small)
    own = (expert_in[0], jnp.pad(expert_bias, ((0, BIAS_ROWS - 1), (0, 0))), expert_out[0])
    cols = jnp.concatenate([routes, priority.reshape(batches * SEQ, 2)], axis=1)
    cols = cols.reshape(batches, SEQ, 4)
    cols = jnp.pad(cols, ((0, 0), (0, SEQ_PAD - SEQ), (0, 0)), constant_values=-1)
    rows_first = jnp.swapaxes(cols, 1, 2)
    received, x, grad, weight, qkv, mixed, hidden, one, two, lse, probs, slot_cols, rows_small, *spread = run_front(
        inputs, out_grad, dense, own, cols, rows_first, capacity, experts, cap_pad
    )
    saved = (qkv, mixed, lse, hidden, one, two, probs)
    back, sum_in, sum_out, far_in, far_out = run_moe(received, own, *spread)
    z = lax.axis_index("dp")
    at_end = (z == 0) | (z == lax.axis_size("dp") - 1)
    spot = 4 * width
    if groups == PLANE:
        outputs, inputs_grad, end_in, end_out, qkv_grad, proj_grad, small_grad = run_reduce(
            x, grad, weight, rows_small, slot_cols, back, saved, (far_in, far_out), experts
        )
        small_grad = lax.dynamic_slice_in_dim(
            small_grad, lax.axis_index("dp") * depth, depth, axis=1
        )
        vectors = [small_grad[k] for k in range(4)]
        router_grad = small_grad[4 : 4 + experts].T
    else:
        weight = jnp.concatenate([weight, rows_small.T], axis=1)
        outputs, inputs_grad, dense = run_tail(
            x, grad, weight, cols, slot_cols, back, saved, experts
        )
        end_in, end_out = last_turn(far_in, far_out)
        outputs, inputs_grad = (
            full[:, :SEQ].reshape(batches * SEQ, width) for full in (outputs, inputs_grad)
        )
        dense = lax.psum_scatter(dense, both, scatter_dimension=0, tiled=True)
        dense = lax.all_gather(dense, "expert", axis=0, tiled=True).astype(F32)
        qkv_grad = dense[:, : 3 * width]
        proj_grad = dense[:, 3 * width : spot]
        vectors = [dense[:, spot + k] for k in range(4)]
        router_grad = dense[:, spot + 4 : spot + 4 + experts]
    grad_in = jnp.where(at_end, end_in[:width], sum_in[:width]).astype(F32)
    grad_bias = jnp.where(at_end, end_in[width], sum_in[width]).astype(F32)
    grad_out = jnp.where(at_end, end_out, sum_out).astype(F32)
    return (
        outputs,
        inputs_grad,
        vectors[0],
        vectors[1],
        qkv_grad,
        proj_grad,
        vectors[2],
        vectors[3],
        router_grad,
        grad_in[None],
        grad_bias[None],
        grad_out[None],
    )


def solution(mesh):
    token = P(("dp", "expert"), None)
    vector = P("dp")
    matrix = P("dp", None)
    return jax.shard_map(
        per_device,
        mesh=mesh,
        in_specs=(
            token,
            vector,
            vector,
            matrix,
            matrix,
            vector,
            vector,
            matrix,
            P("expert", None, "dp"),
            P("expert", "dp"),
            P("expert", "dp", None),
            token,
            token,
            token,
            P(("dp", "expert")),
        ),
        out_specs=(
            token,
            token,
            vector,
            vector,
            matrix,
            matrix,
            vector,
            vector,
            matrix,
            P("expert", None, "dp"),
            P("expert", "dp"),
            P("expert", "dp", None),
        ),
        check_vma=False,
    )
```

```python
import functools

import jax
import jax.numpy as jnp
from jax import lax
from jax.experimental import pallas as pl
from jax.experimental.pallas import tpu as pltpu
from jax.sharding import PartitionSpec as P

HEADS = 12
HEAD = 64
SEQ = 197
SEQ_PAD = 208
EPS = 1e-06
BF = jnp.bfloat16
F32 = jnp.float32
SMALL = 128
MESH = pl.DeviceIdType.MESH
EARLY_PIECES = range(2)
LATE_PIECES = range(2, 4)
EARLY_FAR = 2
FAR_CUTS = 4
FAR_TURNS = (
    (0, True, 3),
    (1, True, 4),
    (1, False, 2),
    (2, True, 5),
    (3, False, 3),
    (4, True, 6),
    (4, False, 4),
    (5, True, 7),
    (5, False, 5),
)
TILE = 128
PLANE = 8
BIAS_ROWS = 16
NEG = -1e30
VMEM_LIMIT = 60 * 1024 * 1024
VMEM_MAX = 67043328


def ceil_to(value, step):
    return (value + step - 1) // step * step


def dot(a, b):
    return jnp.dot(a, b, preferred_element_type=F32)


def dot_nt(a, b):
    return lax.dot_general(a, b, (((1,), (1,)), ((), ())), preferred_element_type=F32)


def dot_tn(a, b):
    return lax.dot_general(a, b, (((0,), (0,)), ((), ())), preferred_element_type=F32)


def params(count=1):
    return pltpu.CompilerParams(
        dimension_semantics=("arbitrary",) * count, vmem_limit_bytes=VMEM_LIMIT
    )


class Line:
    def __init__(self, shards):
        self.shards = shards
        self.me = lax.axis_index("dp")
        self.has_below = self.me > 0
        self.has_above = self.me < shards - 1

    def greet(self, me, groups):
        barrier = pltpu.get_barrier_semaphore()
        for k in range(1, groups):
            pl.semaphore_signal(
                barrier, inc=1, device_id={"expert": lax.rem(me + k, groups)}, device_id_type=MESH
            )
        for k in range(1, self.shards):
            pl.semaphore_signal(
                barrier,
                inc=1,
                device_id={"dp": lax.rem(self.me + k, self.shards)},
                device_id_type=MESH,
            )
        pl.semaphore_wait(barrier, groups - 1 + self.shards - 1)

    def views(self, pair, slot):
        tall, span = pair[0].shape[1:]
        return [
            pair[kind].at[slot, pl.ds(low, size)] for kind, low, size in pieces_of(tall, span)
        ]

    def hop(self, way, round_id, source, target, send_sem, arrived, some=range(4)):
        step = 1 - 2 * way
        slot = self.me - step * round_id
        places = self.views(target, slot)
        if round_id == 0:
            body, bias, out = source
            tall, span = target[0].shape[1:]
            moves = []
            for piece, (kind, low, size) in enumerate(pieces_of(tall, span)):
                own = out if kind else body
                here = min(size, own.shape[0] - low)
                moves.append((own.at[pl.ds(low, here)], target[kind].at[slot, pl.ds(low, here)], piece))
                if here < size:
                    moves.append((bias, target[kind].at[slot, pl.ds(low + here, size - here)], piece))
        else:
            origins = self.views(source, slot)
            moves = [(origins[piece], places[piece], piece) for piece in some]
        return [
            pltpu.make_async_remote_copy(
                src_ref=origin,
                dst_ref=place,
                send_sem=send_sem.at[way, round_id, k if round_id == 0 else piece],
                recv_sem=arrived.at[slot, piece],
                device_id={"dp": self.me + step},
                device_id_type=MESH,
            )
            for k, (origin, place, piece) in enumerate(moves)
        ]

    def sends(self, way, round_id):
        if way == 0:
            return (self.me >= round_id) & self.has_above
        return (self.me + round_id < self.shards) & self.has_below

    def push(self, round_id, source, target, send_sem, arrived, some=range(4)):
        for way in range(2):

            @pl.when(self.sends(way, round_id))
            def _():
                for copy in self.hop(way, round_id, source, target, send_sem, arrived, some):
                    copy.start()

    def drain(self, round_id, source, target, send_sem, arrived, some=range(4)):
        for way in range(2):

            @pl.when(self.sends(way, round_id))
            def _():
                for copy in self.hop(way, round_id, source, target, send_sem, arrived, some):
                    copy.wait_send()

    def receive(self, round_id, target, arrived, some=range(4)):
        far = round_id + 1

        @pl.when(self.me >= far)
        def _():
            self.wait_slot(self.me - far, target, arrived, some)

        @pl.when(self.me + far < self.shards)
        def _():
            self.wait_slot(self.me + far, target, arrived, some)

    def wait_slot(self, slot, target, arrived, some=range(4)):
        places = self.views(target, slot)
        for piece in some:
            pltpu.make_async_copy(places[piece], places[piece], arrived.at[slot, piece]).wait()


def route(cap_pad, cols_ref, rows_ref, limit_ref, slot_rows_ref, slot_cols_ref):
    for b in range(cols_ref.shape[0]):
        limit = limit_ref[b]
        col = [cols_ref[b, :, k : k + 1] for k in range(4)]
        row = [rows_ref[b, k : k + 1, :] for k in range(4)]
        for j in range(2):
            rank_row = 0
            rank_col = 0
            for k in range(2):
                hit = (col[k] == row[j]) & (col[2 + k] < row[2 + j])
                rank_row = rank_row + jnp.sum(hit.astype(jnp.int32), axis=0, keepdims=True)
                hit = (row[k] == col[j]) & (row[2 + k] < col[2 + j])
                rank_col = rank_col + jnp.sum(hit.astype(jnp.int32), axis=1, keepdims=True)
            keep_row = (rank_row < limit) & (row[j] >= 0)
            keep_col = (rank_col < limit) & (col[j] >= 0)
            slot_rows_ref[b, j : j + 1, :] = jnp.where(keep_row, row[j] * cap_pad + rank_row, -1)
            slot_cols_ref[b, :, j : j + 1] = jnp.where(keep_col, col[j] * cap_pad + rank_col, -1)


def norm_stats(values):
    average = jnp.mean(values, axis=-1, keepdims=True)
    centered = values - average
    spread = jnp.mean(centered * centered, axis=-1, keepdims=True)
    inverse = lax.rsqrt(spread + EPS)
    return centered * inverse, inverse


def front_kernel(
    experts,
    shards,
    limit_ref,
    cols_ref,
    rows_ref,
    raw_hbm,
    raw_grad_hbm,
    qkv_own,
    proj_own,
    small_own_ref,
    own_body,
    own_bias,
    own_out,
    received_ref,
    last_hbm,
    x_hbm,
    grad_hbm,
    weight_hbm,
    qkv_hbm,
    mixed_hbm,
    hidden_hbm,
    one_hbm,
    two_hbm,
    lse_ref,
    probs_ref,
    slot_cols_ref,
    vectors_ref,
    spread_in_ref,
    spread_out_ref,
    raw_ref,
    raw_grad_ref,
    x_ref,
    grad_ref,
    weight_ref,
    qkv_ref,
    mixed_ref,
    hidden_ref,
    one_ref,
    two_ref,
    small_land,
    slot_rows_ref,
    send_ref,
    load_sem,
    store_sem,
    send_sem,
    arrived,
    rows_send,
    rows_recv,
    small_send,
    small_recv,
    line_send,
    piece_recv,
    plane_send,
    near_send,
):
    batches, rows, width = x_ref.shape
    groups = received_ref.shape[0]
    cap_pad = received_ref.shape[3]
    me = lax.axis_index("expert")
    line = Line(shards)
    z = line.me
    own = (own_body, own_bias, own_out)
    spread = (spread_in_ref, spread_out_ref)
    depth = width // shards
    piece_width = 4 * width // PLANE
    base = me // PLANE * PLANE
    spot = me - base
    core = lax.rem(me, 2)
    sibling = me + 1 - 2 * core
    chip = spot // 2
    chips = PLANE // 2
    cut = 3 * width // piece_width

    def remote(source, target, send, recv, peer):
        return pltpu.make_async_remote_copy(
            src_ref=source,
            dst_ref=target,
            send_sem=send,
            recv_sem=recv,
            device_id=peer,
            device_id_type=MESH,
        )

    def landed(view, sem):
        pltpu.make_async_copy(view, view, sem).wait()

    def rows_of(shard):
        return pl.ds(pl.multiple_of(shard * depth, depth), depth)

    def piece(shard, index):
        low = pl.multiple_of(index * piece_width, piece_width)
        return weight_ref.at[rows_of(shard), pl.ds(low, piece_width)]

    raws = [
        pltpu.make_async_copy(raw_hbm, raw_ref, load_sem.at[0]),
        pltpu.make_async_copy(raw_grad_hbm, raw_grad_ref, load_sem.at[1]),
    ]
    mine = [
        pltpu.make_async_copy(
            qkv_own, weight_ref.at[rows_of(z), pl.ds(0, 3 * width)], load_sem.at[2]
        ),
        pltpu.make_async_copy(
            proj_own, weight_ref.at[rows_of(z), pl.ds(3 * width, width)], load_sem.at[3]
        ),
    ]
    for copy in mine:
        copy.start()
    for copy in raws:
        copy.start()
    small_land[z, :, :depth] = (
        small_own_ref[...].astype(F32).T[: small_land.shape[1]].astype(BF)
    )
    line.greet(me, groups)
    for copy in mine:
        copy.wait()

    def small_copy(far):
        view = small_land.at[z]
        return remote(view, view, small_send.at[far], small_recv.at[z], {"dp": far})

    def line_copy(far):
        view = piece(z, spot)
        return remote(view, view, line_send.at[far], piece_recv.at[z, spot], {"dp": far})

    def plane_copy(shard, other):
        view = piece(shard, spot)
        peer = base + 2 * other + core
        return remote(
            view, view, plane_send.at[shard, other], piece_recv.at[shard, spot], {"expert": peer}
        )

    def near_copy(shard, other):
        index = 2 * other + core
        view = piece(shard, index)
        return remote(
            view, view, near_send.at[shard, other], piece_recv.at[shard, index], {"expert": sibling}
        )

    peers = [lax.rem(z + k, shards) for k in range(1, shards)]
    others = [lax.rem(chip + k, chips) for k in range(1, chips)]
    for far in peers:
        line_copy(far).start()
    for far in peers:
        small_copy(far).start()
    line.push(0, own, spread, send_sem, arrived)
    zero_rows = jnp.zeros((rows - SEQ, width), F32)

    def pad_image(image):
        x_ref[image, :SEQ] = raw_ref[image * SEQ : (image + 1) * SEQ]
        x_ref[image, SEQ:] = zero_rows
        pltpu.make_async_copy(x_ref.at[image], x_hbm.at[image], store_sem.at[0, image]).start()
        grad_ref[image, :SEQ] = raw_grad_ref[image * SEQ : (image + 1) * SEQ]
        grad_ref[image, SEQ:] = zero_rows
        pltpu.make_async_copy(
            grad_ref.at[image], grad_hbm.at[image], store_sem.at[1, image]
        ).start()

    for copy in raws:
        copy.wait()
    pad_image(0)
    for far in peers:
        landed(piece(far, spot), piece_recv.at[far, spot])
        for other in others:
            plane_copy(far, other).start()
        near_copy(far, chip).start()
    for image in range(1, batches):
        pad_image(image)
    slot_rows_ref[...] = jnp.full(slot_rows_ref.shape, -1, jnp.int32)
    slot_cols_ref[...] = jnp.full(slot_cols_ref.shape, -1, jnp.int32)
    route(cap_pad, cols_ref, rows_ref, limit_ref, slot_rows_ref, slot_cols_ref)
    slot_cols_ref[:, :, 2:4] = cols_ref[:, :, 0:2]
    for far in peers:
        for other in others:
            index = 2 * other + core
            landed(piece(far, index), piece_recv.at[far, index])
            near_copy(far, other).start()
    for far in peers:
        landed(small_land.at[far], small_recv.at[far])
        for k in range(chips):
            index = 2 * k + 1 - core
            landed(piece(far, index), piece_recv.at[far, index])
    weight_store = pltpu.make_async_copy(weight_ref, weight_hbm, load_sem.at[5])
    weight_store.start()
    used = small_land.shape[1]
    small_rows = jnp.concatenate(
        [small_land[shard, :, :depth].astype(F32) for shard in range(shards)], axis=1
    )
    vectors_ref[...] = jnp.zeros_like(vectors_ref)
    vectors_ref[:used] = small_rows.astype(BF)
    gain_one, shift_one, gain_two, shift_two = (small_rows[k : k + 1] for k in range(4))

    def rows_copy(image, target):
        return remote(
            send_ref.at[image, target],
            received_ref.at[me, image],
            rows_send.at[image, target],
            rows_recv.at[me, image],
            {"expert": target},
        )

    last = batches - 1
    last_store = pltpu.make_async_copy(send_ref.at[last], last_hbm, load_sem.at[4])
    saves = (
        (qkv_ref, qkv_hbm),
        (mixed_ref, mixed_hbm),
        (hidden_ref, hidden_hbm),
        (one_ref, one_hbm),
        (two_ref, two_hbm),
    )
    lane = lax.broadcasted_iota(jnp.int32, (1, 128), 1)
    key_ok = lax.broadcasted_iota(jnp.int32, (1, rows), 1) < SEQ
    slot = lax.broadcasted_iota(jnp.int32, (groups * cap_pad, 1), 0)
    scale = HEAD ** (-0.5)

    def do_image(index, carry):
        x = x_ref[index]
        hat, _ = norm_stats(x)
        one = (hat * gain_one + shift_one).astype(BF)
        one_ref[index] = one
        qkv_ref[index] = dot(one, weight_ref[:, : 3 * width]).astype(BF)
        lse = jnp.zeros((rows, 128), F32)
        for pair in range(HEADS // 2):
            low = pair * 128
            query = qkv_ref[index, :, low : low + 128]
            keys = qkv_ref[index, :, width + low : width + low + 128]
            values = qkv_ref[index, :, 2 * width + low : 2 * width + low + 128]
            total = None
            for side in range(2):
                part_of = (lane // HEAD) == side
                scores = dot_nt(jnp.where(part_of, query, jnp.zeros_like(query)), keys) * scale
                scores = jnp.where(key_ok, scores, NEG)
                highest = jnp.max(scores, axis=-1, keepdims=True)
                expo = jnp.exp(scores - highest)
                denom = jnp.sum(expo, axis=-1, keepdims=True)
                weights = (expo / denom).astype(BF)
                lse = jnp.where(lane == 2 * pair + side, highest + jnp.log(denom), lse)
                part = dot(weights, jnp.where(part_of, values, jnp.zeros_like(values)))
                total = part if total is None else total + part
            mixed_ref[index, :, low : low + 128] = total.astype(BF)
        lse_ref[index] = lse
        hidden = x + dot(mixed_ref[index], weight_ref[:, 3 * width : 4 * width])
        hidden_ref[index] = hidden
        hat, _ = norm_stats(hidden)
        two = (hat * gain_two + shift_two).astype(BF)
        two_ref[index] = two
        logits = dot_nt(two, vectors_ref[...])
        in_router = (lane >= 4) & (lane < 4 + experts)
        logits = jnp.where(in_router, logits, NEG)
        expo = jnp.exp(logits - jnp.max(logits, axis=-1, keepdims=True))
        probs = expo / jnp.sum(expo, axis=-1, keepdims=True)
        probs_ref[index] = probs
        out_grad = grad_ref[index]
        both = None
        grads = None
        for j in range(2):
            gate = jnp.sum(
                jnp.where(lane - 4 == cols_ref[index, :, j : j + 1], probs, 0.0),
                axis=-1,
                keepdims=True,
            )
            pick = (slot == slot_rows_ref[index, j : j + 1, :]).astype(F32)
            both = pick if both is None else both + pick
            part = dot(pick.astype(BF), (gate * out_grad).astype(BF))
            grads = part if grads is None else grads + part
        sent = dot(both.astype(BF), two).astype(BF)
        send_ref[index, :, 0] = sent.reshape(groups, cap_pad, width)
        send_ref[index, :, 1] = grads.astype(BF).reshape(groups, cap_pad, width)

        @pl.when(index < last)
        def _():
            for k in range(1, groups):
                rows_copy(index, lax.rem(me + k, groups)).start()
            pltpu.make_async_copy(
                send_ref.at[index, me], received_ref.at[me, index], rows_recv.at[me, index]
            ).start()

        @pl.when(index == last)
        def _():
            last_store.start()

        for k, (here, there) in enumerate(saves):
            pltpu.make_async_copy(here.at[index], there.at[index], store_sem.at[2 + k, index]).start()
        return carry

    lax.fori_loop(0, batches, do_image, 0)

    line.receive(0, spread, arrived)
    line.push(1, spread, spread, send_sem, arrived, EARLY_PIECES)

    def finish(image, carry):
        @pl.when(image < last)
        def _():
            for k in range(groups):
                source = lax.rem(me + k, groups)
                if k:
                    rows_copy(image, source).wait_send()
                landed(received_ref.at[source, image], rows_recv.at[source, image])

        pltpu.make_async_copy(x_ref.at[image], x_hbm.at[image], store_sem.at[0, image]).wait()
        pltpu.make_async_copy(grad_ref.at[image], grad_hbm.at[image], store_sem.at[1, image]).wait()
        for k, (here, there) in enumerate(saves):
            pltpu.make_async_copy(here.at[image], there.at[image], store_sem.at[2 + k, image]).wait()
        return carry

    lax.fori_loop(0, batches, finish, 0)
    weight_store.wait()
    last_store.wait()
    for far in peers:
        line_copy(far).wait_send()
        small_copy(far).wait_send()
        for other in others:
            plane_copy(far, other).wait_send()
        for k in range(chips):
            near_copy(far, k).wait_send()
    line.receive(1, spread, arrived, EARLY_PIECES)
    line.drain(0, own, spread, send_sem, arrived)
    line.drain(1, spread, spread, send_sem, arrived, EARLY_PIECES)


def run_front(raw, raw_grad, dense, own, cols, rows_first, limits, experts, cap_pad):
    batches, rows = cols.shape[:2]
    width = raw.shape[1]
    shards = lax.axis_size("dp")
    groups = lax.axis_size("expert")
    body, bias, out = own
    tall = body.shape[0] + bias.shape[0]
    anywhere = pl.BlockSpec(memory_space=pl.ANY)
    inside = pl.BlockSpec(memory_space=pltpu.VMEM)
    dma = pltpu.SemaphoreType.DMA
    chips = PLANE // 2

    def shape(*dims, dtype=BF):
        return jax.ShapeDtypeStruct((batches, rows) + dims, dtype)

    return pl.pallas_call(
        functools.partial(front_kernel, experts, shards),
        out_shape=(
            jax.ShapeDtypeStruct((groups, batches, 2, cap_pad, width), BF),
            jax.ShapeDtypeStruct((groups, 2, cap_pad, width), BF),
            shape(width, dtype=F32),
            shape(width, dtype=F32),
            jax.ShapeDtypeStruct((width, 4 * width), BF),
            shape(3 * width),
            shape(width),
            shape(width, dtype=F32),
            shape(width),
            shape(width),
            shape(128, dtype=F32),
            shape(SMALL, dtype=F32),
            shape(8, dtype=jnp.int32),
            jax.ShapeDtypeStruct((SMALL, width), BF),
            jax.ShapeDtypeStruct((shards, tall, body.shape[1]), BF),
            jax.ShapeDtypeStruct((shards,) + out.shape, BF),
        ),
        in_specs=[pl.BlockSpec(memory_space=pltpu.SMEM), inside, inside]
        + [anywhere] * 4
        + [inside]
        + [anywhere] * 3,
        out_specs=(anywhere,) * 10 + (inside,) * 4 + (anywhere,) * 2,
        scratch_shapes=[
            pltpu.VMEM(raw.shape, F32),
            pltpu.VMEM(raw.shape, F32),
            pltpu.VMEM((batches, rows, width), F32),
            pltpu.VMEM((batches, rows, width), F32),
            pltpu.VMEM((width, 4 * width), BF),
            pltpu.VMEM((batches, rows, 3 * width), BF),
            pltpu.VMEM((batches, rows, width), BF),
            pltpu.VMEM((batches, rows, width), F32),
            pltpu.VMEM((batches, rows, width), BF),
            pltpu.VMEM((batches, rows, width), BF),
            pltpu.VMEM((shards, ceil_to(4 + experts, 16), ceil_to(dense[2].shape[0], 128)), BF),
            pltpu.VMEM((batches, 8, rows), jnp.int32),
            pltpu.VMEM((batches, groups, 2, cap_pad, width), BF),
            dma((6,)),
            dma((7, batches)),
            dma((2, 2, 5)),
            dma((shards, 4)),
            dma((batches, groups)),
            dma((groups, batches)),
            dma((shards,)),
            dma((shards,)),
            dma((shards,)),
            dma((shards, PLANE)),
            dma((shards, chips)),
            dma((shards, chips)),
        ],
        compiler_params=pltpu.CompilerParams(
            vmem_limit_bytes=VMEM_LIMIT, collective_id=1, has_side_effects=True
        ),
        cost_estimate=pl.CostEstimate(
            flops=8000000000, bytes_accessed=40000000, transcendentals=3000000
        ),
        name="front",
    )(limits, cols, rows_first, raw, raw_grad, *dense, *own)


def pieces_of(tall, span, cuts=2):
    pieces = []
    for kind, extent in enumerate((tall, span)):
        size = ceil_to(-(-extent // cuts), 16)
        for low in range(0, extent, size):
            pieces.append((kind, low, min(size, extent - low)))
    return tuple(pieces)


def moe_kernel(
    shards,
    groups,
    x_hbm,
    last_hbm,
    own_body,
    own_bias,
    own_out,
    spread_in_ref,
    spread_out_ref,
    back_ref,
    sum_in_ref,
    sum_out_ref,
    far_in_ref,
    far_out_ref,
    rows_ref,
    win_ref,
    wout_ref,
    y_acc,
    dx_acc,
    gin_acc,
    gout_acc,
    part_in_ref,
    part_out_ref,
    land_in_ref,
    land_out_ref,
    far_land,
    rows_sem,
    last_send,
    last_recv,
    own_sem,
    far_send,
    far_recv,
    weight_send,
    arrived,
    sum_send,
    sum_recv,
    back_send,
    back_recv,
    final_sem,
):
    line = Line(shards)
    z = line.me
    me = lax.axis_index("expert")
    _, batches, _, cap_pad, width = rows_ref.shape
    _, tall, span = spread_in_ref.shape
    blocks = batches
    rows = groups * cap_pad
    last = batches - 1
    spread = (win_ref, wout_ref)
    early_spread = (spread_in_ref, spread_out_ref)
    own = (own_body, own_bias, own_out)
    parts = (part_in_ref, part_out_ref)
    lands = (land_in_ref, land_out_ref)
    pieces = pieces_of(tall, span)
    far_pieces = pieces_of(tall, span, FAR_CUTS)

    for image in range(last):
        pltpu.make_async_copy(x_hbm.at[:, image], rows_ref.at[:, image], rows_sem.at[image]).start()
    pltpu.make_async_copy(last_hbm.at[me], rows_ref.at[me, last], last_recv.at[me]).start()
    own_places = (
        (own_body, win_ref.at[z, pl.ds(0, width)], 0),
        (own_bias, win_ref.at[z, pl.ds(width, tall - width)], 1),
        (own_out, wout_ref.at[z], 2),
    )
    own_loads = [
        pltpu.make_async_copy(here, there, own_sem.at[k]) for here, there, k in own_places
    ]

    def fetch(far, some):
        for sign in (-1, 1):
            slot = z + sign * far

            @pl.when((slot >= 0) & (slot < shards))
            def _():
                origins = line.views(early_spread, slot)
                places = line.views(spread, slot)
                for piece in some:
                    pltpu.make_async_copy(
                        origins[piece], places[piece], arrived.at[slot, piece]
                    ).start()

    fetch(1, range(4))
    fetch(2, EARLY_PIECES)
    for copy in own_loads:
        copy.start()

    line.greet(me, groups)

    def last_copy(target):
        return pltpu.make_async_remote_copy(
            src_ref=last_hbm.at[target],
            dst_ref=rows_ref.at[me, last],
            send_sem=last_send.at[target],
            recv_sem=last_recv.at[me],
            device_id={"expert": target},
            device_id_type=MESH,
        )

    for k in range(1, groups):
        last_copy(lax.rem(me + k, groups)).start()
    line.push(1, early_spread, spread, weight_send, arrived, LATE_PIECES)
    line.push(2, early_spread, spread, weight_send, arrived, EARLY_PIECES)

    table = []
    for at in range(shards):
        near = sorted(range(shards), key=lambda q: (abs(q - at), q))
        table.append(near[1:-1] + near[:1] + near[-1:])

    def quarter(step):
        total = 0
        for at in range(shards):
            for s in range(shards):
                hit = jnp.where((z == at) & (step == s), table[at][s], 0)
                total = total + hit
        return total

    def sum_copy(way, q, piece):
        kind, low, size = pieces[piece]
        if way == 0:
            slot = q - 1
            peer = z + 1
        else:
            slot = jnp.where(q == z - 1, shards - 2, q - 1)
            peer = z - 1
        cut = pl.ds(low, size)
        return pltpu.make_async_remote_copy(
            src_ref=parts[kind].at[q, cut],
            dst_ref=lands[kind].at[slot, cut],
            send_sem=sum_send.at[way, q, piece],
            recv_sem=sum_recv.at[slot, piece],
            device_id={"dp": peer},
            device_id_type=MESH,
        )

    def take_sum(slot, q, piece):
        kind, low, size = pieces[piece]
        cut = pl.ds(low, size)
        view = lands[kind].at[slot, cut]
        pltpu.make_async_copy(view, view, sum_recv.at[slot, piece]).wait()
        parts[kind][q, cut] = (
            parts[kind][q, cut].astype(F32) + lands[kind][slot, cut].astype(F32)
        ).astype(BF)

    def back_copy(target, image):
        return pltpu.make_async_remote_copy(
            src_ref=rows_ref.at[target, image],
            dst_ref=back_ref.at[me, image],
            send_sem=back_send.at[target, image],
            recv_sem=back_recv.at[me, image],
            device_id={"expert": target},
            device_id_type=MESH,
        )

    def back_start(image):
        for k in range(1, groups):
            back_copy(lax.rem(me + k, groups), image).start()
        pltpu.make_async_copy(
            rows_ref.at[me, image], back_ref.at[me, image], back_recv.at[me, image]
        ).start()

    plain = (shards - 2) * blocks
    late_item = blocks
    inner = (z > 0) & (z < shards - 1)

    def do_item(item, carry):
        late = item >= plain
        rest = item - plain
        step = jnp.where(late, shards - 2 + lax.rem(rest + 2 * blocks, 2), item // blocks)
        block = jnp.where(late, (rest + 2 * blocks) // 2 - blocks, lax.rem(item, blocks))
        q = quarter(step)
        bank = jnp.where(step == shards - 1, 1, 0)

        @pl.when(block == 0)
        def _():
            far = jnp.abs(q - z)

            @pl.when(far == 0)
            def _():
                for copy in own_loads:
                    copy.wait()

            @pl.when(far == 2)
            def _():
                line.wait_slot(q, spread, arrived, EARLY_PIECES)

            @pl.when((far == 1) | (far > 2))
            def _():
                line.wait_slot(q, spread, arrived)

            for distance in range(3, shards - 1):
                for way in range(2):
                    forward = 1 - 2 * way

                    @pl.when((q == z - forward * distance) & line.sends(way, distance))
                    def _():
                        for copy in line.hop(way, distance, spread, spread, weight_send, arrived):
                            copy.start()

        @pl.when(item == late_item)
        def _():
            line.receive(1, spread, arrived, LATE_PIECES)
            line.push(2, spread, spread, weight_send, arrived, LATE_PIECES)

        @pl.when((step == shards - 2) & (block > 0))
        def _():
            back_start(block - 1)

        here = pl.ds(pl.multiple_of(block * rows, rows), rows)

        @pl.when((step == 0) & (block < last))
        def _():
            view = rows_ref.at[:, block]
            pltpu.make_async_copy(view, view, rows_sem.at[block]).wait()

        @pl.when((step == 0) & (block == last))
        def _():
            for source in range(groups):
                view = rows_ref.at[source, last]
                pltpu.make_async_copy(view, view, last_recv.at[source]).wait()

        x = rows_ref[:, block, 0].reshape(rows, width)
        grad = rows_ref[:, block, 1].reshape(rows, width)
        win = win_ref[q, :width, :]
        wout = wout_ref[q]
        pre = dot(x, win) + win_ref[q, width : width + 1, :].astype(F32)
        cdf = 0.5 * lax.erf(pre * (0.5**0.5)) + 0.5
        active = (pre * cdf).astype(BF)
        slope = cdf + pre * (jnp.exp(-0.5 * pre * pre) * 0.3989422804014327)
        d_pre = (dot_nt(grad, wout) * slope).astype(BF)
        y_part = dot(active, wout)
        dx_part = dot_nt(d_pre, win)

        @pl.when(step == 0)
        def _():
            y_acc[here, :] = y_part
            dx_acc[here, :] = dx_part

        @pl.when(step > 0)
        def _():
            y_acc[here, :] += y_part
            dx_acc[here, :] += dx_part

        gout = dot_tn(active, grad)
        gin = dot_tn(x, d_pre)
        gbias = jnp.sum(d_pre.astype(F32), axis=0, keepdims=True)

        @pl.when(block == 0)
        def _():
            gout_acc[bank] = gout
            gin_acc[bank, :width, :] = gin
            gin_acc[bank, width : width + 1, :] = gbias

        @pl.when(block > 0)
        def _():
            gout_acc[bank] += gout
            gin_acc[bank, :width, :] += gin
            gin_acc[bank, width : width + 1, :] += gbias

        @pl.when(step == shards - 1)
        def _():
            shape = (groups, cap_pad, width)
            rows_ref[:, block, 0] = y_acc[here, :].astype(BF).reshape(shape)
            rows_ref[:, block, 1] = dx_acc[here, :].astype(BF).reshape(shape)

        @pl.when(block == blocks - 1)
        def _():
            part_in_ref[q, :width, :] = gin_acc[bank, :width, :].astype(BF)
            part_in_ref[q, width:, :] = jnp.broadcast_to(
                gin_acc[bank, width : width + 1, :].astype(BF), (tall - width, span)
            )
            part_out_ref[q] = gout_acc[bank].astype(BF)

            @pl.when((z == 0) & (q > z) & (q < shards - 1))
            def _():
                for piece in range(len(pieces)):
                    sum_copy(0, q, piece).start()

            @pl.when((z == shards - 1) & (q < z) & (q > 0))
            def _():
                for piece in range(len(pieces)):
                    sum_copy(1, q, piece).start()

        return carry

    lax.fori_loop(0, shards * blocks, do_item, 0)
    back_start(blocks - 1)

    def early_far(k, piece):
        _, low, size = far_pieces[piece]
        cut = pl.ds(low, size)
        return pltpu.make_async_remote_copy(
            src_ref=part_in_ref.at[(shards - 1) * k, cut],
            dst_ref=far_land.at[k, cut],
            send_sem=far_send.at[piece],
            recv_sem=far_recv.at[piece],
            device_id={"dp": z + 2 * k - 1},
            device_id_type=MESH,
        )

    def early_add(k, piece):
        _, low, size = far_pieces[piece]
        cut = pl.ds(low, size)
        view = far_land.at[k, cut]
        pltpu.make_async_copy(view, view, far_recv.at[piece]).wait()
        part_in_ref[(shards - 1) * k, cut] = (
            part_in_ref[(shards - 1) * k, cut].astype(F32) + far_land[k, cut].astype(F32)
        ).astype(BF)

    for piece in range(EARLY_FAR):

        @pl.when(z == 0)
        def _():
            early_far(1, piece).start()

        @pl.when(z == shards - 1)
        def _():
            early_far(0, piece).start()

    finals = [
        pltpu.make_async_copy(part_in_ref.at[0], far_in_ref.at[0], final_sem.at[0]),
        pltpu.make_async_copy(part_out_ref.at[0], far_out_ref.at[0], final_sem.at[1]),
        pltpu.make_async_copy(part_in_ref.at[shards - 1], far_in_ref.at[1], final_sem.at[2]),
        pltpu.make_async_copy(part_out_ref.at[shards - 1], far_out_ref.at[1], final_sem.at[3]),
        pltpu.make_async_copy(part_in_ref.at[z], sum_in_ref, final_sem.at[4]),
        pltpu.make_async_copy(part_out_ref.at[z], sum_out_ref, final_sem.at[5]),
    ]
    def do_forward(turn, carry):
        up = turn
        down = shards - 1 - turn
        for piece in range(len(pieces)):

            @pl.when((up > z) & (z > 0))
            def _():
                take_sum(up - 1, up, piece)
                sum_copy(0, up, piece).start()

            @pl.when((down < z) & (z < shards - 1))
            def _():
                take_sum(down - 1, down, piece)
                sum_copy(1, down, piece).start()

        return carry

    lax.fori_loop(1, shards - 1, do_forward, 0)
    for piece in range(len(pieces)):

        @pl.when(inner)
        def _():
            take_sum(z - 1, z, piece)
            take_sum(shards - 2, z, piece)

    for copy in finals[4:]:
        copy.start()
    for piece in range(EARLY_FAR):

        @pl.when(z == 1)
        def _():
            early_add(1, piece)

        @pl.when(z == shards - 2)
        def _():
            early_add(0, piece)

    for copy in finals[:4]:
        copy.start()

    def finish_sum(q, carry):
        @pl.when((q > z) & line.has_above)
        def _():
            for piece in range(len(pieces)):
                sum_copy(0, q, piece).wait_send()

        @pl.when((q < z) & line.has_below)
        def _():
            for piece in range(len(pieces)):
                sum_copy(1, q, piece).wait_send()

        return carry

    lax.fori_loop(1, shards - 1, finish_sum, 0)
    line.drain(1, spread, spread, weight_send, arrived, LATE_PIECES)
    for round_id in range(2, shards - 1):
        line.drain(round_id, spread, spread, weight_send, arrived)
    for piece in range(EARLY_FAR):

        @pl.when(z == 0)
        def _():
            early_far(1, piece).wait_send()

        @pl.when(z == shards - 1)
        def _():
            early_far(0, piece).wait_send()

    for k in range(1, groups):
        last_copy(lax.rem(me + k, groups)).wait_send()

    def finish_back(image, carry):
        for k in range(groups):
            source = lax.rem(me + k, groups)
            if k:
                back_copy(source, image).wait_send()
            view = back_ref.at[source, image]
            pltpu.make_async_copy(view, view, back_recv.at[source, image]).wait()
        return carry

    lax.fori_loop(0, batches, finish_back, 0)
    for copy in finals:
        copy.wait()


def run_moe(received, last, own, spread_in, spread_out):
    groups, batches, _, cap_pad, width = received.shape
    shards, tall, span = spread_in.shape
    total = groups * batches * cap_pad
    count = len(pieces_of(tall, span))
    early_rows = sum(pieces_of(tall, span, FAR_CUTS)[EARLY_FAR - 1][1:])
    anywhere = pl.BlockSpec(memory_space=pl.ANY)
    return pl.pallas_call(
        functools.partial(moe_kernel, shards, groups),
        out_shape=(
            jax.ShapeDtypeStruct(received.shape, BF),
            jax.ShapeDtypeStruct((tall, span), BF),
            jax.ShapeDtypeStruct((span, width), BF),
            jax.ShapeDtypeStruct((2, tall, span), BF),
            jax.ShapeDtypeStruct((2, span, width), BF),
        ),
        in_specs=[anywhere] * 7,
        out_specs=(anywhere,) * 5,
        scratch_shapes=[
            pltpu.VMEM(received.shape, BF),
            pltpu.VMEM((shards, tall, span), BF),
            pltpu.VMEM((shards, span, width), BF),
            pltpu.VMEM((total, width), F32),
            pltpu.VMEM((total, width), F32),
            pltpu.VMEM((2, ceil_to(width + 1, 8), span), F32),
            pltpu.VMEM((2, span, width), F32),
            pltpu.VMEM((shards, tall, span), BF),
            pltpu.VMEM((shards, span, width), BF),
            pltpu.VMEM((shards - 1, tall, span), BF),
            pltpu.VMEM((shards - 1, span, width), BF),
            pltpu.VMEM((2, early_rows, span), BF),
            pltpu.SemaphoreType.DMA((batches,)),
            pltpu.SemaphoreType.DMA((groups,)),
            pltpu.SemaphoreType.DMA((groups,)),
            pltpu.SemaphoreType.DMA((3,)),
            pltpu.SemaphoreType.DMA((EARLY_FAR,)),
            pltpu.SemaphoreType.DMA((EARLY_FAR,)),
            pltpu.SemaphoreType.DMA((2, shards, 4)),
            pltpu.SemaphoreType.DMA((shards, 4)),
            pltpu.SemaphoreType.DMA((2, shards, count)),
            pltpu.SemaphoreType.DMA((shards - 1, count)),
            pltpu.SemaphoreType.DMA((groups, batches)),
            pltpu.SemaphoreType.DMA((groups, batches)),
            pltpu.SemaphoreType.DMA((6,)),
        ],
        compiler_params=pltpu.CompilerParams(
            vmem_limit_bytes=VMEM_MAX, collective_id=2, has_side_effects=True
        ),
        cost_estimate=pl.CostEstimate(
            flops=12 * total * width * span * shards,
            bytes_accessed=60000000,
            transcendentals=2 * total * span * shards,
        ),
        name="moe",
    )(received, last, *own, spread_in, spread_out)


def tail_kernel(
    experts,
    x_ref,
    grad_ref,
    weight_ref,
    cols_ref,
    slot_cols_ref,
    back_ref,
    qkv_ref,
    mixed_ref,
    lse_ref,
    hidden_ref,
    one_ref,
    two_ref,
    probs_ref,
    out_ref,
    dx_ref,
    dense_ref,
    small_ref,
    sums_ref,
    d_qkv_ref,
    d_branch_ref,
    d_logits_ref,
    one_all,
    two_all,
    mixed_all,
):
    width = x_ref.shape[-1]
    rows = x_ref.shape[1]
    index = pl.program_id(0)

    @pl.when(index == 0)
    def _():
        small_ref[...] = weight_ref[:, 4 * width :].astype(F32).T
        sums_ref[...] = jnp.zeros_like(sums_ref)

    here = pl.ds(pl.multiple_of(index * rows, rows), rows)
    one_all[here, :] = one_ref[0]
    two_all[here, :] = two_ref[0]
    mixed_all[here, :] = mixed_ref[0]
    out_grad = grad_ref[0]
    hidden = hidden_ref[0]
    probs = probs_ref[0]
    lane = lax.broadcasted_iota(jnp.int32, (1, 128), 1)
    slots = back_ref.shape[0] * back_ref.shape[3]
    slot = lax.broadcasted_iota(jnp.int32, (1, slots), 1)
    answers = back_ref[:, 0, 0].reshape(slots, width)
    answer_grads = back_ref[:, 0, 1].reshape(slots, width)
    result = hidden
    d_probs = jnp.zeros_like(probs)
    both = None
    for j in range(2):
        pick = (slot == slot_cols_ref[0, :, j : j + 1]).astype(F32)
        both = pick if both is None else both + pick
        chosen = lane - 4 == cols_ref[0, :, j : j + 1]
        gate = jnp.sum(jnp.where(chosen, probs, 0.0), axis=-1, keepdims=True)
        picked = dot(pick.astype(BF), answers)
        result = result + gate * picked
        d_gate = jnp.sum(picked * out_grad, axis=-1, keepdims=True)
        d_probs = jnp.where(chosen, d_gate, d_probs)
    out_ref[0] = result
    d_logits = probs * (d_probs - jnp.sum(d_probs * probs, axis=-1, keepdims=True))
    d_logits = d_logits.astype(BF)
    d_logits_ref[here, :] = d_logits
    d_two = dot(both.astype(BF), answer_grads) + dot_nt(d_logits, weight_ref[:, 4 * width :])
    hat, inverse = norm_stats(hidden)
    sums_ref[2:3, :] += jnp.sum(d_two * hat, axis=0, keepdims=True)
    sums_ref[3:4, :] += jnp.sum(d_two, axis=0, keepdims=True)
    d_hat = d_two * small_ref[2:3, :]
    d_hidden = out_grad + inverse * (
        d_hat
        - jnp.mean(d_hat, axis=-1, keepdims=True)
        - hat * jnp.mean(d_hat * hat, axis=-1, keepdims=True)
    )
    d_branch = d_hidden.astype(BF)
    d_branch_ref[here, :] = d_branch
    d_mixed_all = dot_nt(d_branch, weight_ref[:, 3 * width : 4 * width]).astype(BF)
    key_ok = lax.broadcasted_iota(jnp.int32, (1, rows), 1) < SEQ
    scale = HEAD ** (-0.5)
    for pair in range(HEADS // 2):
        low = pair * 128
        query = qkv_ref[0, :, low : low + 128]
        keys = qkv_ref[0, :, width + low : width + low + 128]
        values = qkv_ref[0, :, 2 * width + low : 2 * width + low + 128]
        d_mixed = d_mixed_all[:, low : low + 128]
        d_query = d_keys = d_values = None
        for side in range(2):
            mine = (lane // HEAD) == side
            head = 2 * pair + side

            def own(array):
                return jnp.where(mine, array, jnp.zeros_like(array))

            my_query = own(query)
            my_keys = own(keys)
            my_d_mixed = own(d_mixed)
            scores = dot_nt(my_query, keys) * scale
            scores = jnp.where(key_ok, scores, NEG)
            probs_h = jnp.exp(scores - lse_ref[0, :, head : head + 1])
            d_weights = dot_nt(my_d_mixed, values)
            row_terms = jnp.sum(d_weights * probs_h, axis=-1, keepdims=True)
            d_scores = (probs_h * (d_weights - row_terms) * scale).astype(BF)
            parts = (
                dot(d_scores, my_keys),
                dot_tn(d_scores, my_query),
                dot_tn(probs_h.astype(BF), my_d_mixed),
            )
            if side == 0:
                d_query, d_keys, d_values = parts
            else:
                d_query, d_keys, d_values = (
                    d_query + parts[0],
                    d_keys + parts[1],
                    d_values + parts[2],
                )
        d_qkv_ref[here, low : low + 128] = d_query.astype(BF)
        d_qkv_ref[here, width + low : width + low + 128] = d_keys.astype(BF)
        d_qkv_ref[here, 2 * width + low : 2 * width + low + 128] = d_values.astype(BF)
    d_one = dot_nt(d_qkv_ref[here, :], weight_ref[:, : 3 * width])
    hat, inverse = norm_stats(x_ref[0])
    sums_ref[0:1, :] += jnp.sum(d_one * hat, axis=0, keepdims=True)
    sums_ref[1:2, :] += jnp.sum(d_one, axis=0, keepdims=True)
    d_hat = d_one * small_ref[0:1, :]
    dx_ref[0] = d_hidden + inverse * (
        d_hat
        - jnp.mean(d_hat, axis=-1, keepdims=True)
        - hat * jnp.mean(d_hat * hat, axis=-1, keepdims=True)
    )

    @pl.when(index == pl.num_programs(0) - 1)
    def _():
        dense_ref[:, 4 * width :] = (dot_tn(two_all[...], d_logits_ref[...]) + sums_ref[...].T).astype(BF)
        dense_ref[:, 3 * width : 4 * width] = dot_tn(mixed_all[...], d_branch_ref[...]).astype(BF)
        for part in range(3):
            cut = slice(part * width, (part + 1) * width)
            dense_ref[:, cut] = dot_tn(one_all[...], d_qkv_ref[:, cut]).astype(BF)


def run_tail(x, grad, weight, cols, slot_cols, back, saved, experts):
    batches, rows, width = x.shape
    total = weight.shape[1]
    cap_pad = back.shape[3]
    qkv, mixed, lse, hidden, one, two, probs = saved

    def block(*shape):
        return pl.BlockSpec((1,) + shape, lambda i: (i,) + (0,) * len(shape))

    return pl.pallas_call(
        functools.partial(tail_kernel, experts),
        grid=(batches,),
        out_shape=(
            jax.ShapeDtypeStruct(x.shape, F32),
            jax.ShapeDtypeStruct(x.shape, F32),
            jax.ShapeDtypeStruct((width, total), BF),
        ),
        in_specs=[
            block(rows, width),
            block(rows, width),
            pl.BlockSpec((width, total), lambda i: (0, 0), pipeline_mode=pl.Buffered(1)),
            block(rows, 4),
            block(rows, 8),
            pl.BlockSpec((experts, 1, 2, cap_pad, width), lambda i: (0, i, 0, 0, 0)),
            block(rows, 3 * width),
            block(rows, width),
            block(rows, 128),
            block(rows, width),
            block(rows, width),
            block(rows, width),
            block(rows, SMALL),
        ],
        out_specs=(
            block(rows, width),
            block(rows, width),
            pl.BlockSpec((width, total), lambda i: (0, 0), pipeline_mode=pl.Buffered(1)),
        ),
        scratch_shapes=[
            pltpu.VMEM((SMALL, width), F32),
            pltpu.VMEM((SMALL, width), F32),
            pltpu.VMEM((batches * rows, 3 * width), BF),
            pltpu.VMEM((batches * rows, width), BF),
            pltpu.VMEM((batches * rows, SMALL), BF),
            pltpu.VMEM((batches * rows, width), BF),
            pltpu.VMEM((batches * rows, width), BF),
            pltpu.VMEM((batches * rows, width), BF),
        ],
        compiler_params=params(),
        cost_estimate=pl.CostEstimate(
            flops=16000000000, bytes_accessed=50000000, transcendentals=2000000
        ),
        name="tail",
    )(x, grad, weight, cols, slot_cols, back, qkv, mixed, lse, hidden, one, two, probs)


def reduce_kernel(
    experts,
    shards,
    slot_cols_ref,
    lse_ref,
    probs_ref,
    vectors_ref,
    x_hbm,
    grad_hbm,
    weight_hbm,
    back_hbm,
    qkv_hbm,
    mixed_hbm,
    hidden_hbm,
    one_hbm,
    two_hbm,
    far_in_hbm,
    far_out_hbm,
    out_hbm,
    dx_hbm,
    end_in_hbm,
    end_out_hbm,
    qkv_grad_ref,
    proj_grad_ref,
    small_grad_ref,
    x_ref,
    grad_ref,
    weight_ref,
    back_ref,
    qkv_ref,
    mixed_ref,
    hidden_ref,
    one_ref,
    two_ref,
    raw_ref,
    sums_ref,
    one_flip,
    d_qkv_ref,
    d_branch_ref,
    d_mixed_ref,
    d_logits_ref,
    tiles_ref,
    near_ref,
    plane_land,
    plane_ref,
    line_land,
    final_ref,
    small_land,
    small_far,
    far_in_ref,
    far_out_ref,
    far_in_land,
    far_out_land,
    load_sem,
    store_sem,
    near_send,
    near_recv,
    plane_send,
    plane_recv,
    line_send,
    line_recv,
    final_send,
    final_recv,
    small_send,
    small_recv,
    far_load,
    far_send,
    far_recv,
):
    batches, rows, width = x_ref.shape
    z = lax.axis_index("dp")
    me = lax.axis_index("expert")
    core = lax.rem(me, 2)
    sibling = me + 1 - 2 * core
    chip = me // 2
    chips = PLANE // 2
    pairs = HEADS // 2
    depth = width // shards
    head_tiles = width // TILE
    own_tiles = (4 * width // TILE) // PLANE

    def loads(kind, image):
        pair = {
            0: (back_hbm.at[:, image], back_ref.at[:, image]),
            1: (hidden_hbm.at[image], hidden_ref.at[image]),
            2: (grad_hbm.at[image], grad_ref.at[image]),
            3: (mixed_hbm.at[image], mixed_ref.at[pl.ds(image * rows, rows)]),
            4: (two_hbm.at[image], two_ref.at[pl.ds(image * rows, rows)]),
            5: (one_hbm.at[image], one_ref.at[pl.ds(image * rows, rows)]),
            6: (qkv_hbm.at[image], qkv_ref.at[pl.ds(image * rows, rows)]),
            7: (x_hbm.at[image], x_ref.at[image]),
        }[kind]
        return pltpu.make_async_copy(pair[0], pair[1], load_sem.at[kind, image])

    weight_load = pltpu.make_async_copy(weight_hbm, weight_ref, load_sem.at[8, 0])
    far_parts = (far_in_ref, far_out_ref)
    far_lands = (far_in_land, far_out_land)
    far_loads = [
        pltpu.make_async_copy(source.at[k], target.at[k], far_load.at[k, part])
        for k in range(2)
        for part, (source, target) in enumerate(
            ((far_in_hbm, far_in_ref), (far_out_hbm, far_out_ref))
        )
    ]

    for copy in far_loads:
        copy.start()
    for kind in range(3):
        loads(kind, 0).start()
    weight_load.start()
    for image in range(1, batches):
        for kind in range(3):
            loads(kind, image).start()
    for kind in range(3, 8):
        for image in range(batches):
            loads(kind, image).start()

    barrier = pltpu.get_barrier_semaphore()
    for k in range(1, PLANE):
        pl.semaphore_signal(
            barrier, inc=1, device_id={"expert": lax.rem(me + k, PLANE)}, device_id_type=MESH
        )
    for k in range(1, shards):
        pl.semaphore_signal(
            barrier, inc=1, device_id={"dp": lax.rem(z + k, shards)}, device_id_type=MESH
        )
    pl.semaphore_wait(barrier, PLANE - 1 + shards - 1)

    def remote(source, target, send_sem, recv_sem, peer):
        return pltpu.make_async_remote_copy(
            src_ref=source,
            dst_ref=target,
            send_sem=send_sem,
            recv_sem=recv_sem,
            device_id=peer,
            device_id_type=MESH,
        )

    def landed(view, sem):
        pltpu.make_async_copy(view, view, sem).wait()

    pieces = pieces_of(far_in_ref.shape[1], far_out_ref.shape[1], FAR_CUTS)
    inner = (z > 0) & (z < shards - 1)
    low_half = 2 * z < shards

    def far_copy(k, piece):
        kind, low, size = pieces[piece]
        cut = pl.ds(low, size)
        return remote(
            far_parts[kind].at[k, cut],
            far_lands[kind].at[k, cut],
            far_send.at[k, piece],
            far_recv.at[k, piece],
            {"dp": z + 2 * k - 1},
        )

    def far_take(k, piece):
        kind, low, size = pieces[piece]
        cut = pl.ds(low, size)
        landed(far_lands[kind].at[k, cut], far_recv.at[k, piece])
        far_parts[kind][k, cut] = (
            far_parts[kind][k, cut].astype(F32) + far_lands[kind][k, cut].astype(F32)
        ).astype(BF)

    def far_forward(k, piece):
        if piece < EARLY_FAR:
            @pl.when(z != (1 if k else shards - 2))
            def _():
                far_take(k, piece)

        else:
            far_take(k, piece)
        far_copy(k, piece).start()

    def pass_on(first, piece):
        @pl.when(inner & low_half)
        def _():
            far_forward(1 if first else 0, piece)

        @pl.when(inner & jnp.logical_not(low_half))
        def _():
            far_forward(0 if first else 1, piece)

    for copy in far_loads:
        copy.wait()

    @pl.when(z == 0)
    def _():
        for piece in range(EARLY_FAR, len(pieces)):
            far_copy(1, piece).start()

    @pl.when(z == shards - 1)
    def _():
        for piece in range(EARLY_FAR, len(pieces)):
            far_copy(0, piece).start()

    def near_copy(tile):
        return remote(
            tiles_ref.at[tile],
            near_ref.at[tile // 2],
            near_send.at[tile],
            near_recv.at[tile],
            {"expert": sibling},
        )

    def plane_copy(tile):
        owner = lax.rem(tile, PLANE) // 2
        place = lax.rem(chip - owner + 2 * chips - 1, chips)
        return remote(
            tiles_ref.at[tile],
            plane_land.at[tile // PLANE, place],
            plane_send.at[tile],
            plane_recv.at[tile // PLANE, place],
            {"expert": lax.rem(tile, PLANE)},
        )

    def line_copy(k, far):
        return remote(
            plane_ref.at[k, pl.ds(pl.multiple_of(far * depth, depth), depth)],
            line_land.at[k, z],
            line_send.at[k, far],
            line_recv.at[k, z],
            {"dp": far},
        )

    def final_copy(k, peer):
        tile = me + PLANE * k
        return remote(
            final_ref.at[tile],
            final_ref.at[tile],
            final_send.at[k, peer],
            final_recv.at[tile],
            {"expert": peer},
        )

    def leave(tile):
        @pl.when(lax.rem(tile, 2) != core)
        def _():
            near_copy(tile).start()

    def combine(tile):
        @pl.when(lax.rem(tile, 2) == core)
        def _():
            landed(near_ref.at[tile // 2], near_recv.at[tile])
            tiles_ref[tile] = (
                tiles_ref[tile].astype(F32) + near_ref[tile // 2].astype(F32)
            ).astype(BF)

            @pl.when(lax.rem(tile, PLANE) != me)
            def _():
                plane_copy(tile).start()

    def plane_sum(k):
        total = tiles_ref[me + PLANE * k].astype(F32)
        for j in range(1, chips):
            landed(plane_land.at[k, j - 1], plane_recv.at[k, j - 1])
            total = total + plane_land[k, j - 1].astype(F32)
        plane_ref[k] = total.astype(BF)
        for j in range(1, shards):
            line_copy(k, lax.rem(z + j, shards)).start()

    def line_sum(k):
        mine = pl.ds(pl.multiple_of(z * depth, depth), depth)
        total = plane_ref[k, mine].astype(F32)
        for j in range(1, shards):
            far = lax.rem(z + j, shards)
            landed(line_land.at[k, far], line_recv.at[k, far])
            total = total + line_land[k, far].astype(F32)
        final_ref[me + PLANE * k] = total.astype(BF)
        for j in range(1, PLANE):
            final_copy(k, lax.rem(me + j, PLANE)).start()

    pass_on(True, 0)
    pass_on(True, 1)

    lane = lax.broadcasted_iota(jnp.int32, (1, 128), 1)
    groups, _, _, cap_pad, _ = back_ref.shape
    slots = groups * cap_pad
    slot = lax.broadcasted_iota(jnp.int32, (1, slots), 1)
    sums_ref[...] = jnp.zeros_like(sums_ref)
    small_rows = vectors_ref[:8].astype(F32)
    gain_one = small_rows[0:1]
    gain_two = small_rows[2:3]

    def phase_one(image, carry):
        here = pl.ds(pl.multiple_of(image * rows, rows), rows)
        for kind in range(3):
            view = (back_ref.at[:, image], hidden_ref.at[image], grad_ref.at[image])[kind]
            landed(view, load_sem.at[kind, image])

        @pl.when(image == 0)
        def _():
            weight_load.wait()

        out_grad = grad_ref[image]
        hidden = hidden_ref[image]
        probs = probs_ref[image]
        answers = back_ref[:, image, 0].reshape(slots, width)
        answer_grads = back_ref[:, image, 1].reshape(slots, width)
        result = hidden
        d_probs = jnp.zeros_like(probs)
        both = None
        for j in range(2):
            pick = (slot == slot_cols_ref[image, :, j : j + 1]).astype(F32)
            both = pick if both is None else both + pick
            chosen = lane - 4 == slot_cols_ref[image, :, 2 + j : 3 + j]
            gate = jnp.sum(jnp.where(chosen, probs, 0.0), axis=-1, keepdims=True)
            picked = dot(pick.astype(BF), answers)
            result = result + gate * picked
            d_gate = jnp.sum(picked * out_grad, axis=-1, keepdims=True)
            d_probs = jnp.where(chosen, d_gate, d_probs)
        d_logits = probs * (d_probs - jnp.sum(d_probs * probs, axis=-1, keepdims=True))
        d_logits = d_logits.astype(BF)
        d_logits_ref[here, :] = d_logits
        d_two = dot(both.astype(BF), answer_grads) + dot(d_logits, vectors_ref[...])
        hat, inverse = norm_stats(hidden)
        sums_ref[2:3, :] += jnp.sum(d_two * hat, axis=0, keepdims=True)
        sums_ref[3:4, :] += jnp.sum(d_two, axis=0, keepdims=True)
        d_hat = d_two * gain_two
        d_hidden = out_grad + inverse * (
            d_hat
            - jnp.mean(d_hat, axis=-1, keepdims=True)
            - hat * jnp.mean(d_hat * hat, axis=-1, keepdims=True)
        )
        d_branch = d_hidden.astype(BF)
        d_branch_ref[here, :] = d_branch
        d_mixed_ref[here, :] = dot_nt(d_branch, weight_ref[:, 3 * width : 4 * width]).astype(BF)
        grad_ref[image] = d_hidden
        hidden_ref[image] = result
        return carry

    lax.fori_loop(0, batches, phase_one, 0)
    for image in range(batches):
        raw_ref[image * SEQ : (image + 1) * SEQ] = hidden_ref[image, :SEQ]
    out_store = pltpu.make_async_copy(raw_ref, out_hbm, store_sem.at[0, 0])
    out_store.start()
    pass_on(True, 2)
    pass_on(False, 0)
    for kind, view in ((3, mixed_ref), (4, two_ref), (5, one_ref)):
        for image in range(batches):
            landed(view.at[pl.ds(image * rows, rows)], load_sem.at[kind, image])
    proj = dot_tn(mixed_ref[...], d_branch_ref[...]).astype(BF)
    for tile in range(head_tiles):
        tiles_ref[tile] = proj[:, tile * TILE : (tile + 1) * TILE]
    for tile in range(head_tiles):
        leave(tile)
    one_flip[...] = one_ref[...].T
    flipped = dot_tn(d_logits_ref[...], two_ref[...])
    for image in range(batches):
        landed(qkv_ref.at[pl.ds(image * rows, rows)], load_sem.at[6, image])

    pass_on(False, 1)

    key_ok = lax.broadcasted_iota(jnp.int32, (1, rows), 1) < SEQ
    scale = HEAD ** (-0.5)

    def phase_two(pair, carry):
        low = pl.multiple_of(pair * TILE, TILE)
        spots = [pl.ds(pl.multiple_of(part * width + low, TILE), TILE) for part in range(3)]
        for image in range(batches):
            here = pl.ds(image * rows, rows)
            query, keys, values = (qkv_ref[here, spot] for spot in spots)
            d_mixed = d_mixed_ref[here, pl.ds(low, TILE)]
            total = [None, None, None]
            for side in range(2):
                mine = (lane // HEAD) == side

                def own(array):
                    return jnp.where(mine, array, jnp.zeros_like(array))

                my_query = own(query)
                my_d_mixed = own(d_mixed)
                scores = dot_nt(my_query, keys) * scale
                scores = jnp.where(key_ok, scores, NEG)
                log_total = jnp.sum(
                    jnp.where(lane == 2 * pair + side, lse_ref[image], 0.0), axis=-1, keepdims=True
                )
                probs_h = jnp.exp(scores - log_total)
                d_weights = dot_nt(my_d_mixed, values)
                row_terms = jnp.sum(d_weights * probs_h, axis=-1, keepdims=True)
                d_scores = (probs_h * (d_weights - row_terms) * scale).astype(BF)
                fresh = (
                    dot(d_scores, own(keys)),
                    dot_tn(d_scores, my_query),
                    dot_tn(probs_h.astype(BF), my_d_mixed),
                )
                total = [new if old is None else old + new for old, new in zip(total, fresh)]
            for part in range(3):
                d_qkv_ref[here, spots[part]] = total[part].astype(BF)
        first = head_tiles + 3 * pair
        for part in range(3):
            tiles_ref[first + part] = dot(one_flip[...], d_qkv_ref[:, spots[part]]).astype(BF)
        for part in range(3):
            leave(first + part)

        @pl.when(pair == 0)
        def _():
            for tile in range(head_tiles):
                combine(tile)

        @pl.when(pair > 0)
        def _():
            for part in range(3):
                combine(first - 3 + part)

        for turn, first, piece in FAR_TURNS:

            @pl.when(pair == turn)
            def _():
                pass_on(first, piece)

        @pl.when(pair == pairs - 3)
        def _():
            plane_sum(0)

        @pl.when(pair == pairs - 1)
        def _():
            line_sum(0)
            plane_sum(1)

        return carry

    lax.fori_loop(0, pairs, phase_two, 0)
    for part in range(3):
        combine(head_tiles + 3 * (pairs - 1) + part)

    for image in range(batches):
        landed(x_ref.at[image], load_sem.at[7, image])

    def phase_three(image, carry):
        here = pl.ds(pl.multiple_of(image * rows, rows), rows)
        d_one = dot_nt(d_qkv_ref[here, :], weight_ref[:, : 3 * width])
        hat, inverse = norm_stats(x_ref[image])
        sums_ref[0:1, :] += jnp.sum(d_one * hat, axis=0, keepdims=True)
        sums_ref[1:2, :] += jnp.sum(d_one, axis=0, keepdims=True)
        d_hat = d_one * gain_one
        x_ref[image] = grad_ref[image] + inverse * (
            d_hat
            - jnp.mean(d_hat, axis=-1, keepdims=True)
            - hat * jnp.mean(d_hat * hat, axis=-1, keepdims=True)
        )

        @pl.when(image == batches // 2 - 1)
        def _():
            pass_on(False, 6)
            line_sum(1)
            plane_sum(2)

        return carry

    lax.fori_loop(0, batches, phase_three, 0)
    out_store.wait()
    for image in range(batches):
        raw_ref[image * SEQ : (image + 1) * SEQ] = x_ref[image, :SEQ]
    dx_store = pltpu.make_async_copy(raw_ref, dx_hbm, store_sem.at[1, 0])
    dx_store.start()

    def small_copy(k):
        peer = lax.rem(me + k, PLANE)
        return remote(
            sums_ref, small_land.at[me], small_send.at[peer], small_recv.at[me], {"expert": peer}
        )

    def small_far_copy(k):
        peer = lax.rem(z + k, shards)
        return remote(
            small_land.at[me],
            small_far.at[z],
            small_send.at[PLANE + peer],
            small_recv.at[PLANE + z],
            {"dp": peer},
        )

    sums_ref[...] += flipped[: sums_ref.shape[0]]
    for k in range(1, PLANE):
        small_copy(k).start()
    pass_on(False, 7)
    line_sum(2)
    total = sums_ref[...]
    for k in range(1, PLANE):
        peer = lax.rem(me + k, PLANE)
        landed(small_land.at[peer], small_recv.at[peer])
        total = total + small_land[peer]
    small_land[me] = total
    for k in range(1, shards):
        small_far_copy(k).start()
    for k in range(1, shards):
        peer = lax.rem(z + k, shards)
        landed(small_far.at[peer], small_recv.at[PLANE + peer])
        total = total + small_far[peer]
    small_grad_ref[...] = total

    def finish(tile, carry):
        @pl.when(lax.rem(tile, PLANE) != me)
        def _():
            landed(final_ref.at[tile], final_recv.at[tile])

        @pl.when(lax.rem(tile, 2) != core)
        def _():
            near_copy(tile).wait_send()

        @pl.when((lax.rem(tile, 2) == core) & (lax.rem(tile, PLANE) != me))
        def _():
            plane_copy(tile).wait_send()

        return carry

    lax.fori_loop(0, 4 * head_tiles, finish, 0)
    for tile in range(head_tiles):
        proj_grad_ref[:, tile * TILE : (tile + 1) * TILE] = final_ref[tile].astype(F32)
    for pair in range(pairs):
        for part in range(3):
            low = part * width + pair * TILE
            qkv_grad_ref[:, low : low + TILE] = final_ref[head_tiles + 3 * pair + part].astype(F32)
    for k in range(own_tiles):
        for j in range(1, shards):
            line_copy(k, lax.rem(z + j, shards)).wait_send()
        for j in range(1, PLANE):
            final_copy(k, lax.rem(me + j, PLANE)).wait_send()
    for k in range(1, PLANE):
        small_copy(k).wait_send()
    for k in range(1, shards):
        small_far_copy(k).wait_send()
    for piece in range(len(pieces)):

        @pl.when(z == 0)
        def _():
            far_take(0, piece)

        @pl.when(z == shards - 1)
        def _():
            far_take(1, piece)

    mine = jnp.where(z == shards - 1, 1, 0)
    ends = [
        pltpu.make_async_copy(far_in_ref.at[mine], end_in_hbm, far_load.at[0, 0]),
        pltpu.make_async_copy(far_out_ref.at[mine], end_out_hbm, far_load.at[0, 1]),
    ]
    for copy in ends:
        copy.start()
    for piece in range(len(pieces)):

        first = 1 if piece < EARLY_FAR else 0

        @pl.when((z < shards - 1) & (z >= first))
        def _():
            far_copy(1, piece).wait_send()

        @pl.when((z > 0) & (z < shards - first))
        def _():
            far_copy(0, piece).wait_send()

    for copy in ends:
        copy.wait()
    dx_store.wait()


def run_reduce(x, grad, weight, vectors, slot_cols, back, saved, far, experts):
    batches, rows, width = x.shape
    shards = lax.axis_size("dp")
    qkv, mixed, lse, hidden, one, two, probs = saved
    depth = width // shards
    tiles = 4 * width // TILE
    own_tiles = tiles // PLANE
    small_rows = ceil_to(4 + experts, 8)
    count = len(pieces_of(far[0].shape[1], far[1].shape[1], FAR_CUTS))
    anywhere = pl.BlockSpec(memory_space=pl.ANY)
    inside = pl.BlockSpec(memory_space=pltpu.VMEM)
    dma = pltpu.SemaphoreType.DMA
    return pl.pallas_call(
        functools.partial(reduce_kernel, experts, shards),
        out_shape=(
            jax.ShapeDtypeStruct((batches * SEQ, width), F32),
            jax.ShapeDtypeStruct((batches * SEQ, width), F32),
            jax.ShapeDtypeStruct(far[0].shape[1:], BF),
            jax.ShapeDtypeStruct(far[1].shape[1:], BF),
            jax.ShapeDtypeStruct((depth, 3 * width), F32),
            jax.ShapeDtypeStruct((depth, width), F32),
            jax.ShapeDtypeStruct((small_rows, width), F32),
        ),
        in_specs=[inside] * 4 + [anywhere] * 11,
        out_specs=(anywhere,) * 4 + (inside,) * 3,
        scratch_shapes=[
            pltpu.VMEM(x.shape, F32),
            pltpu.VMEM(x.shape, F32),
            pltpu.VMEM(weight.shape, BF),
            pltpu.VMEM(back.shape, BF),
            pltpu.VMEM((batches * rows, 3 * width), BF),
            pltpu.VMEM((batches * rows, width), BF),
            pltpu.VMEM(x.shape, F32),
            pltpu.VMEM((batches * rows, width), BF),
            pltpu.VMEM((batches * rows, width), BF),
            pltpu.VMEM((batches * SEQ, width), F32),
            pltpu.VMEM((small_rows, width), F32),
            pltpu.VMEM((width, batches * rows), BF),
            pltpu.VMEM((batches * rows, 3 * width), BF),
            pltpu.VMEM((batches * rows, width), BF),
            pltpu.VMEM((batches * rows, width), BF),
            pltpu.VMEM((batches * rows, SMALL), BF),
            pltpu.VMEM((tiles, width, TILE), BF),
            pltpu.VMEM((tiles // 2, width, TILE), BF),
            pltpu.VMEM((own_tiles, PLANE // 2 - 1, width, TILE), BF),
            pltpu.VMEM((own_tiles, width, TILE), BF),
            pltpu.VMEM((own_tiles, shards, depth, TILE), BF),
            pltpu.VMEM((tiles, depth, TILE), BF),
            pltpu.VMEM((PLANE, small_rows, width), F32),
            pltpu.VMEM((shards, small_rows, width), F32),
            pltpu.VMEM(far[0].shape, BF),
            pltpu.VMEM(far[1].shape, BF),
            pltpu.VMEM(far[0].shape, BF),
            pltpu.VMEM(far[1].shape, BF),
            dma((9, batches)),
            dma((2, batches)),
            dma((tiles,)),
            dma((tiles,)),
            dma((tiles,)),
            dma((own_tiles, PLANE // 2 - 1)),
            dma((own_tiles, shards)),
            dma((own_tiles, shards)),
            dma((own_tiles, PLANE)),
            dma((tiles,)),
            dma((PLANE + shards,)),
            dma((PLANE + shards,)),
            dma((2, 2)),
            dma((2, count)),
            dma((2, count)),
        ],
        compiler_params=pltpu.CompilerParams(
            vmem_limit_bytes=VMEM_MAX, collective_id=3, has_side_effects=True
        ),
        cost_estimate=pl.CostEstimate(
            flops=16000000000, bytes_accessed=50000000, transcendentals=2000000
        ),
        name="tail",
    )(slot_cols, lse, probs, vectors, x, grad, weight, back, qkv, mixed, hidden, one, two, *far)


def last_turn(far_in, far_out):
    at = lax.axis_index("dp") // (lax.axis_size("dp") - 1)
    return [lax.psum(far.astype(F32), "dp").astype(BF)[at] for far in (far_in, far_out)]


def per_device(
    inputs,
    gain_one,
    shift_one,
    qkv_weight,
    proj_weight,
    gain_two,
    shift_two,
    router_weight,
    expert_in,
    expert_bias,
    expert_out,
    out_grad,
    routes,
    priority,
    capacity,
):
    batches = priority.shape[0]
    count = inputs.shape[0] // batches
    width = inputs.shape[1]
    experts = router_weight.shape[1]
    groups = lax.axis_size("expert")
    cap_pad = ceil_to(max(2, (5 * count + 2 * experts - 1) // (2 * experts)), 16)
    depth = qkv_weight.shape[0]
    both = ("dp", "expert")

    vectors = jnp.stack([gain_one, shift_one, gain_two, shift_two], axis=1)
    small = jnp.concatenate([vectors, router_weight], axis=1)
    small = jnp.pad(small, ((0, 0), (0, SMALL - small.shape[1])))
    dense = (qkv_weight, proj_weight, small)
    own = (expert_in[0], jnp.pad(expert_bias, ((0, BIAS_ROWS - 1), (0, 0))), expert_out[0])
    cols = jnp.concatenate([routes, priority.reshape(batches * SEQ, 2)], axis=1)
    cols = cols.reshape(batches, SEQ, 4)
    cols = jnp.pad(cols, ((0, 0), (0, SEQ_PAD - SEQ), (0, 0)), constant_values=-1)
    rows_first = jnp.swapaxes(cols, 1, 2)
    received, last, x, grad, weight, qkv, mixed, hidden, one, two, lse, probs, slot_cols, rows_small, *spread = run_front(
        inputs, out_grad, dense, own, cols, rows_first, capacity, experts, cap_pad
    )
    saved = (qkv, mixed, lse, hidden, one, two, probs)
    back, sum_in, sum_out, far_in, far_out = run_moe(received, last, own, *spread)
    z = lax.axis_index("dp")
    at_end = (z == 0) | (z == lax.axis_size("dp") - 1)
    spot = 4 * width
    if groups == PLANE:
        outputs, inputs_grad, end_in, end_out, qkv_grad, proj_grad, small_grad = run_reduce(
            x, grad, weight, rows_small, slot_cols, back, saved, (far_in, far_out), experts
        )
        small_grad = lax.dynamic_slice_in_dim(
            small_grad, lax.axis_index("dp") * depth, depth, axis=1
        )
        vectors = [small_grad[k] for k in range(4)]
        router_grad = small_grad[4 : 4 + experts].T
    else:
        weight = jnp.concatenate([weight, rows_small.T], axis=1)
        outputs, inputs_grad, dense = run_tail(
            x, grad, weight, cols, slot_cols, back, saved, experts
        )
        end_in, end_out = last_turn(far_in, far_out)
        outputs, inputs_grad = (
            full[:, :SEQ].reshape(batches * SEQ, width) for full in (outputs, inputs_grad)
        )
        dense = lax.psum_scatter(dense, both, scatter_dimension=0, tiled=True)
        dense = lax.all_gather(dense, "expert", axis=0, tiled=True).astype(F32)
        qkv_grad = dense[:, : 3 * width]
        proj_grad = dense[:, 3 * width : spot]
        vectors = [dense[:, spot + k] for k in range(4)]
        router_grad = dense[:, spot + 4 : spot + 4 + experts]
    grad_in = jnp.where(at_end, end_in[:width], sum_in[:width]).astype(F32)
    grad_bias = jnp.where(at_end, end_in[width], sum_in[width]).astype(F32)
    grad_out = jnp.where(at_end, end_out, sum_out).astype(F32)
    return (
        outputs,
        inputs_grad,
        vectors[0],
        vectors[1],
        qkv_grad,
        proj_grad,
        vectors[2],
        vectors[3],
        router_grad,
        grad_in[None],
        grad_bias[None],
        grad_out[None],
    )


def solution(mesh):
    token = P(("dp", "expert"), None)
    vector = P("dp")
    matrix = P("dp", None)
    return jax.shard_map(
        per_device,
        mesh=mesh,
        in_specs=(
            token,
            vector,
            vector,
            matrix,
            matrix,
            vector,
            vector,
            matrix,
            P("expert", None, "dp"),
            P("expert", "dp"),
            P("expert", "dp", None),
            token,
            token,
            token,
            P(("dp", "expert")),
        ),
        out_specs=(
            token,
            token,
            vector,
            vector,
            matrix,
            matrix,
            vector,
            vector,
            matrix,
            P("expert", None, "dp"),
            P("expert", "dp"),
            P("expert", "dp", None),
        ),
        check_vma=False,
    )
```

```python
import functools

import jax
import jax.numpy as jnp
from jax import lax
from jax.experimental import pallas as pl
from jax.experimental.pallas import tpu as pltpu
from jax.sharding import PartitionSpec as P

HEADS = 12
HEAD = 64
SEQ = 197
SEQ_PAD = 208
EPS = 1e-06
BF = jnp.bfloat16
F32 = jnp.float32
SMALL = 128
MESH = pl.DeviceIdType.MESH
EARLY_PIECES = range(2)
LATE_PIECES = range(2, 4)
EARLY_FAR = 3
FAR_CUTS = 4
FAR_TURNS = (
    (0, True, 3),
    (1, True, 4),
    (1, False, 2),
    (2, True, 5),
    (3, False, 3),
    (4, True, 6),
    (4, False, 4),
    (5, True, 7),
    (5, False, 5),
)
TILE = 128
PLANE = 8
BIAS_ROWS = 16
NEG = -1e30
VMEM_LIMIT = 60 * 1024 * 1024
VMEM_MAX = 67043328


def ceil_to(value, step):
    return (value + step - 1) // step * step


def dot(a, b):
    return jnp.dot(a, b, preferred_element_type=F32)


def dot_nt(a, b):
    return lax.dot_general(a, b, (((1,), (1,)), ((), ())), preferred_element_type=F32)


def dot_tn(a, b):
    return lax.dot_general(a, b, (((0,), (0,)), ((), ())), preferred_element_type=F32)


def params(count=1):
    return pltpu.CompilerParams(
        dimension_semantics=("arbitrary",) * count, vmem_limit_bytes=VMEM_LIMIT
    )


class Line:
    def __init__(self, shards):
        self.shards = shards
        self.me = lax.axis_index("dp")
        self.has_below = self.me > 0
        self.has_above = self.me < shards - 1

    def greet(self, me, groups):
        barrier = pltpu.get_barrier_semaphore()
        for k in range(1, groups):
            pl.semaphore_signal(
                barrier, inc=1, device_id={"expert": lax.rem(me + k, groups)}, device_id_type=MESH
            )
        for k in range(1, self.shards):
            pl.semaphore_signal(
                barrier,
                inc=1,
                device_id={"dp": lax.rem(self.me + k, self.shards)},
                device_id_type=MESH,
            )
        pl.semaphore_wait(barrier, groups - 1 + self.shards - 1)

    def views(self, pair, slot):
        tall, span = pair[0].shape[1:]
        return [
            pair[kind].at[slot, pl.ds(low, size)] for kind, low, size in pieces_of(tall, span)
        ]

    def hop(self, way, round_id, source, target, send_sem, arrived, some=range(4)):
        step = 1 - 2 * way
        slot = self.me - step * round_id
        places = self.views(target, slot)
        if round_id == 0:
            body, bias, out = source
            tall, span = target[0].shape[1:]
            moves = []
            for piece, (kind, low, size) in enumerate(pieces_of(tall, span)):
                own = out if kind else body
                here = min(size, own.shape[0] - low)
                moves.append((own.at[pl.ds(low, here)], target[kind].at[slot, pl.ds(low, here)], piece))
                if here < size:
                    moves.append((bias, target[kind].at[slot, pl.ds(low + here, size - here)], piece))
        else:
            origins = self.views(source, slot)
            moves = [(origins[piece], places[piece], piece) for piece in some]
        return [
            pltpu.make_async_remote_copy(
                src_ref=origin,
                dst_ref=place,
                send_sem=send_sem.at[way, round_id, k if round_id == 0 else piece],
                recv_sem=arrived.at[slot, piece],
                device_id={"dp": self.me + step},
                device_id_type=MESH,
            )
            for k, (origin, place, piece) in enumerate(moves)
        ]

    def sends(self, way, round_id):
        if way == 0:
            return (self.me >= round_id) & self.has_above
        return (self.me + round_id < self.shards) & self.has_below

    def push(self, round_id, source, target, send_sem, arrived, some=range(4)):
        for way in range(2):

            @pl.when(self.sends(way, round_id))
            def _():
                for copy in self.hop(way, round_id, source, target, send_sem, arrived, some):
                    copy.start()

    def drain(self, round_id, source, target, send_sem, arrived, some=range(4)):
        for way in range(2):

            @pl.when(self.sends(way, round_id))
            def _():
                for copy in self.hop(way, round_id, source, target, send_sem, arrived, some):
                    copy.wait_send()

    def receive(self, round_id, target, arrived, some=range(4)):
        far = round_id + 1

        @pl.when(self.me >= far)
        def _():
            self.wait_slot(self.me - far, target, arrived, some)

        @pl.when(self.me + far < self.shards)
        def _():
            self.wait_slot(self.me + far, target, arrived, some)

    def wait_slot(self, slot, target, arrived, some=range(4)):
        places = self.views(target, slot)
        for piece in some:
            pltpu.make_async_copy(places[piece], places[piece], arrived.at[slot, piece]).wait()


def route(cap_pad, cols_ref, rows_ref, limit_ref, slot_rows_ref, slot_cols_ref):
    for b in range(cols_ref.shape[0]):
        limit = limit_ref[b]
        col = [cols_ref[b, :, k : k + 1] for k in range(4)]
        row = [rows_ref[b, k : k + 1, :] for k in range(4)]
        for j in range(2):
            rank_row = 0
            rank_col = 0
            for k in range(2):
                hit = (col[k] == row[j]) & (col[2 + k] < row[2 + j])
                rank_row = rank_row + jnp.sum(hit.astype(jnp.int32), axis=0, keepdims=True)
                hit = (row[k] == col[j]) & (row[2 + k] < col[2 + j])
                rank_col = rank_col + jnp.sum(hit.astype(jnp.int32), axis=1, keepdims=True)
            keep_row = (rank_row < limit) & (row[j] >= 0)
            keep_col = (rank_col < limit) & (col[j] >= 0)
            slot_rows_ref[b, j : j + 1, :] = jnp.where(keep_row, row[j] * cap_pad + rank_row, -1)
            slot_cols_ref[b, :, j : j + 1] = jnp.where(keep_col, col[j] * cap_pad + rank_col, -1)


def norm_stats(values):
    average = jnp.mean(values, axis=-1, keepdims=True)
    centered = values - average
    spread = jnp.mean(centered * centered, axis=-1, keepdims=True)
    inverse = lax.rsqrt(spread + EPS)
    return centered * inverse, inverse


def front_kernel(
    experts,
    shards,
    limit_ref,
    cols_ref,
    rows_ref,
    raw_hbm,
    raw_grad_hbm,
    qkv_own,
    proj_own,
    small_own_ref,
    own_body,
    own_bias,
    own_out,
    received_ref,
    last_hbm,
    x_hbm,
    grad_hbm,
    weight_hbm,
    qkv_hbm,
    mixed_hbm,
    hidden_hbm,
    one_hbm,
    two_hbm,
    lse_ref,
    probs_ref,
    slot_cols_ref,
    vectors_ref,
    spread_in_ref,
    spread_out_ref,
    raw_ref,
    raw_grad_ref,
    x_ref,
    grad_ref,
    weight_ref,
    qkv_ref,
    mixed_ref,
    hidden_ref,
    one_ref,
    two_ref,
    small_land,
    slot_rows_ref,
    send_ref,
    load_sem,
    store_sem,
    send_sem,
    arrived,
    rows_send,
    rows_recv,
    small_send,
    small_recv,
    line_send,
    piece_recv,
    plane_send,
    near_send,
):
    batches, rows, width = x_ref.shape
    groups = received_ref.shape[0]
    cap_pad = received_ref.shape[3]
    me = lax.axis_index("expert")
    line = Line(shards)
    z = line.me
    own = (own_body, own_bias, own_out)
    spread = (spread_in_ref, spread_out_ref)
    depth = width // shards
    piece_width = 4 * width // PLANE
    base = me // PLANE * PLANE
    spot = me - base
    core = lax.rem(me, 2)
    sibling = me + 1 - 2 * core
    chip = spot // 2
    chips = PLANE // 2
    cut = 3 * width // piece_width

    def remote(source, target, send, recv, peer):
        return pltpu.make_async_remote_copy(
            src_ref=source,
            dst_ref=target,
            send_sem=send,
            recv_sem=recv,
            device_id=peer,
            device_id_type=MESH,
        )

    def landed(view, sem):
        pltpu.make_async_copy(view, view, sem).wait()

    def rows_of(shard):
        return pl.ds(pl.multiple_of(shard * depth, depth), depth)

    def piece(shard, index):
        low = pl.multiple_of(index * piece_width, piece_width)
        return weight_ref.at[rows_of(shard), pl.ds(low, piece_width)]

    raws = [
        pltpu.make_async_copy(raw_hbm, raw_ref, load_sem.at[0]),
        pltpu.make_async_copy(raw_grad_hbm, raw_grad_ref, load_sem.at[1]),
    ]
    mine = [
        pltpu.make_async_copy(
            qkv_own, weight_ref.at[rows_of(z), pl.ds(0, 3 * width)], load_sem.at[2]
        ),
        pltpu.make_async_copy(
            proj_own, weight_ref.at[rows_of(z), pl.ds(3 * width, width)], load_sem.at[3]
        ),
    ]
    for copy in mine:
        copy.start()
    for copy in raws:
        copy.start()
    small_land[z, :, :depth] = (
        small_own_ref[...].astype(F32).T[: small_land.shape[1]].astype(BF)
    )
    line.greet(me, groups)
    for copy in mine:
        copy.wait()

    def small_copy(far):
        view = small_land.at[z]
        return remote(view, view, small_send.at[far], small_recv.at[z], {"dp": far})

    def line_copy(far):
        view = piece(z, spot)
        return remote(view, view, line_send.at[far], piece_recv.at[z, spot], {"dp": far})

    def plane_copy(shard, other):
        view = piece(shard, spot)
        peer = base + 2 * other + core
        return remote(
            view, view, plane_send.at[shard, other], piece_recv.at[shard, spot], {"expert": peer}
        )

    def near_copy(shard, other):
        index = 2 * other + core
        view = piece(shard, index)
        return remote(
            view, view, near_send.at[shard, other], piece_recv.at[shard, index], {"expert": sibling}
        )

    peers = [lax.rem(z + k, shards) for k in range(1, shards)]
    others = [lax.rem(chip + k, chips) for k in range(1, chips)]
    for far in peers:
        line_copy(far).start()
    for far in peers:
        small_copy(far).start()
    line.push(0, own, spread, send_sem, arrived)
    zero_rows = jnp.zeros((rows - SEQ, width), F32)

    def pad_image(image):
        x_ref[image, :SEQ] = raw_ref[image * SEQ : (image + 1) * SEQ]
        x_ref[image, SEQ:] = zero_rows
        pltpu.make_async_copy(x_ref.at[image], x_hbm.at[image], store_sem.at[0, image]).start()
        grad_ref[image, :SEQ] = raw_grad_ref[image * SEQ : (image + 1) * SEQ]
        grad_ref[image, SEQ:] = zero_rows
        pltpu.make_async_copy(
            grad_ref.at[image], grad_hbm.at[image], store_sem.at[1, image]
        ).start()

    for copy in raws:
        copy.wait()
    pad_image(0)
    for far in peers:
        landed(piece(far, spot), piece_recv.at[far, spot])
        for other in others:
            plane_copy(far, other).start()
        near_copy(far, chip).start()
    for image in range(1, batches):
        pad_image(image)
    slot_rows_ref[...] = jnp.full(slot_rows_ref.shape, -1, jnp.int32)
    slot_cols_ref[...] = jnp.full(slot_cols_ref.shape, -1, jnp.int32)
    route(cap_pad, cols_ref, rows_ref, limit_ref, slot_rows_ref, slot_cols_ref)
    slot_cols_ref[:, :, 2:4] = cols_ref[:, :, 0:2]
    for far in peers:
        for other in others:
            index = 2 * other + core
            landed(piece(far, index), piece_recv.at[far, index])
            near_copy(far, other).start()
    for far in peers:
        landed(small_land.at[far], small_recv.at[far])
        for k in range(chips):
            index = 2 * k + 1 - core
            landed(piece(far, index), piece_recv.at[far, index])
    weight_store = pltpu.make_async_copy(weight_ref, weight_hbm, load_sem.at[5])
    weight_store.start()
    used = small_land.shape[1]
    small_rows = jnp.concatenate(
        [small_land[shard, :, :depth].astype(F32) for shard in range(shards)], axis=1
    )
    vectors_ref[...] = jnp.zeros_like(vectors_ref)
    vectors_ref[:used] = small_rows.astype(BF)
    gain_one, shift_one, gain_two, shift_two = (small_rows[k : k + 1] for k in range(4))

    def rows_copy(image, target):
        return remote(
            send_ref.at[image, target],
            received_ref.at[me, image],
            rows_send.at[image, target],
            rows_recv.at[me, image],
            {"expert": target},
        )

    last = batches - 1
    last_store = pltpu.make_async_copy(send_ref.at[last], last_hbm, load_sem.at[4])
    saves = (
        (qkv_ref, qkv_hbm),
        (mixed_ref, mixed_hbm),
        (hidden_ref, hidden_hbm),
        (one_ref, one_hbm),
        (two_ref, two_hbm),
    )
    lane = lax.broadcasted_iota(jnp.int32, (1, 128), 1)
    key_ok = lax.broadcasted_iota(jnp.int32, (1, rows), 1) < SEQ
    slot = lax.broadcasted_iota(jnp.int32, (groups * cap_pad, 1), 0)
    scale = HEAD ** (-0.5)

    def do_image(index, carry):
        x = x_ref[index]
        hat, _ = norm_stats(x)
        one = (hat * gain_one + shift_one).astype(BF)
        one_ref[index] = one
        qkv_ref[index] = dot(one, weight_ref[:, : 3 * width]).astype(BF)
        lse = jnp.zeros((rows, 128), F32)
        for pair in range(HEADS // 2):
            low = pair * 128
            query = qkv_ref[index, :, low : low + 128]
            keys = qkv_ref[index, :, width + low : width + low + 128]
            values = qkv_ref[index, :, 2 * width + low : 2 * width + low + 128]
            total = None
            for side in range(2):
                part_of = (lane // HEAD) == side
                scores = dot_nt(jnp.where(part_of, query, jnp.zeros_like(query)), keys) * scale
                scores = jnp.where(key_ok, scores, NEG)
                highest = jnp.max(scores, axis=-1, keepdims=True)
                expo = jnp.exp(scores - highest)
                denom = jnp.sum(expo, axis=-1, keepdims=True)
                weights = (expo / denom).astype(BF)
                lse = jnp.where(lane == 2 * pair + side, highest + jnp.log(denom), lse)
                part = dot(weights, jnp.where(part_of, values, jnp.zeros_like(values)))
                total = part if total is None else total + part
            mixed_ref[index, :, low : low + 128] = total.astype(BF)
        lse_ref[index] = lse
        hidden = x + dot(mixed_ref[index], weight_ref[:, 3 * width : 4 * width])
        hidden_ref[index] = hidden
        hat, _ = norm_stats(hidden)
        two = (hat * gain_two + shift_two).astype(BF)
        two_ref[index] = two
        logits = dot_nt(two, vectors_ref[...])
        in_router = (lane >= 4) & (lane < 4 + experts)
        logits = jnp.where(in_router, logits, NEG)
        expo = jnp.exp(logits - jnp.max(logits, axis=-1, keepdims=True))
        probs = expo / jnp.sum(expo, axis=-1, keepdims=True)
        probs_ref[index] = probs
        out_grad = grad_ref[index]
        both = None
        grads = None
        for j in range(2):
            gate = jnp.sum(
                jnp.where(lane - 4 == cols_ref[index, :, j : j + 1], probs, 0.0),
                axis=-1,
                keepdims=True,
            )
            pick = (slot == slot_rows_ref[index, j : j + 1, :]).astype(F32)
            both = pick if both is None else both + pick
            part = dot(pick.astype(BF), (gate * out_grad).astype(BF))
            grads = part if grads is None else grads + part
        sent = dot(both.astype(BF), two).astype(BF)
        send_ref[index, :, 0] = sent.reshape(groups, cap_pad, width)
        send_ref[index, :, 1] = grads.astype(BF).reshape(groups, cap_pad, width)

        @pl.when(index < last)
        def _():
            for k in range(1, groups):
                rows_copy(index, lax.rem(me + k, groups)).start()
            pltpu.make_async_copy(
                send_ref.at[index, me], received_ref.at[me, index], rows_recv.at[me, index]
            ).start()

        @pl.when(index == last)
        def _():
            last_store.start()

        for k, (here, there) in enumerate(saves):
            pltpu.make_async_copy(here.at[index], there.at[index], store_sem.at[2 + k, index]).start()
        return carry

    lax.fori_loop(0, batches, do_image, 0)

    line.receive(0, spread, arrived)
    line.push(1, spread, spread, send_sem, arrived, EARLY_PIECES)

    def finish(image, carry):
        @pl.when(image < last)
        def _():
            for k in range(groups):
                source = lax.rem(me + k, groups)
                if k:
                    rows_copy(image, source).wait_send()
                landed(received_ref.at[source, image], rows_recv.at[source, image])

        pltpu.make_async_copy(x_ref.at[image], x_hbm.at[image], store_sem.at[0, image]).wait()
        pltpu.make_async_copy(grad_ref.at[image], grad_hbm.at[image], store_sem.at[1, image]).wait()
        for k, (here, there) in enumerate(saves):
            pltpu.make_async_copy(here.at[image], there.at[image], store_sem.at[2 + k, image]).wait()
        return carry

    lax.fori_loop(0, batches, finish, 0)
    weight_store.wait()
    last_store.wait()
    for far in peers:
        line_copy(far).wait_send()
        small_copy(far).wait_send()
        for other in others:
            plane_copy(far, other).wait_send()
        for k in range(chips):
            near_copy(far, k).wait_send()
    line.receive(1, spread, arrived, EARLY_PIECES)
    line.drain(0, own, spread, send_sem, arrived)
    line.drain(1, spread, spread, send_sem, arrived, EARLY_PIECES)


def run_front(raw, raw_grad, dense, own, cols, rows_first, limits, experts, cap_pad):
    batches, rows = cols.shape[:2]
    width = raw.shape[1]
    shards = lax.axis_size("dp")
    groups = lax.axis_size("expert")
    body, bias, out = own
    tall = body.shape[0] + bias.shape[0]
    anywhere = pl.BlockSpec(memory_space=pl.ANY)
    inside = pl.BlockSpec(memory_space=pltpu.VMEM)
    dma = pltpu.SemaphoreType.DMA
    chips = PLANE // 2

    def shape(*dims, dtype=BF):
        return jax.ShapeDtypeStruct((batches, rows) + dims, dtype)

    return pl.pallas_call(
        functools.partial(front_kernel, experts, shards),
        out_shape=(
            jax.ShapeDtypeStruct((groups, batches, 2, cap_pad, width), BF),
            jax.ShapeDtypeStruct((groups, 2, cap_pad, width), BF),
            shape(width, dtype=F32),
            shape(width, dtype=F32),
            jax.ShapeDtypeStruct((width, 4 * width), BF),
            shape(3 * width),
            shape(width),
            shape(width, dtype=F32),
            shape(width),
            shape(width),
            shape(128, dtype=F32),
            shape(SMALL, dtype=F32),
            shape(8, dtype=jnp.int32),
            jax.ShapeDtypeStruct((SMALL, width), BF),
            jax.ShapeDtypeStruct((shards, tall, body.shape[1]), BF),
            jax.ShapeDtypeStruct((shards,) + out.shape, BF),
        ),
        in_specs=[pl.BlockSpec(memory_space=pltpu.SMEM), inside, inside]
        + [anywhere] * 4
        + [inside]
        + [anywhere] * 3,
        out_specs=(anywhere,) * 10 + (inside,) * 4 + (anywhere,) * 2,
        scratch_shapes=[
            pltpu.VMEM(raw.shape, F32),
            pltpu.VMEM(raw.shape, F32),
            pltpu.VMEM((batches, rows, width), F32),
            pltpu.VMEM((batches, rows, width), F32),
            pltpu.VMEM((width, 4 * width), BF),
            pltpu.VMEM((batches, rows, 3 * width), BF),
            pltpu.VMEM((batches, rows, width), BF),
            pltpu.VMEM((batches, rows, width), F32),
            pltpu.VMEM((batches, rows, width), BF),
            pltpu.VMEM((batches, rows, width), BF),
            pltpu.VMEM((shards, ceil_to(4 + experts, 16), ceil_to(dense[2].shape[0], 128)), BF),
            pltpu.VMEM((batches, 8, rows), jnp.int32),
            pltpu.VMEM((batches, groups, 2, cap_pad, width), BF),
            dma((6,)),
            dma((7, batches)),
            dma((2, 2, 5)),
            dma((shards, 4)),
            dma((batches, groups)),
            dma((groups, batches)),
            dma((shards,)),
            dma((shards,)),
            dma((shards,)),
            dma((shards, PLANE)),
            dma((shards, chips)),
            dma((shards, chips)),
        ],
        compiler_params=pltpu.CompilerParams(
            vmem_limit_bytes=VMEM_LIMIT, collective_id=1, has_side_effects=True
        ),
        cost_estimate=pl.CostEstimate(
            flops=8000000000, bytes_accessed=40000000, transcendentals=3000000
        ),
        name="front",
    )(limits, cols, rows_first, raw, raw_grad, *dense, *own)


def pieces_of(tall, span, cuts=2):
    pieces = []
    for kind, extent in enumerate((tall, span)):
        size = ceil_to(-(-extent // cuts), 16)
        for low in range(0, extent, size):
            pieces.append((kind, low, min(size, extent - low)))
    return tuple(pieces)


def moe_kernel(
    shards,
    groups,
    x_hbm,
    last_hbm,
    own_body,
    own_bias,
    own_out,
    spread_in_ref,
    spread_out_ref,
    back_ref,
    sum_in_ref,
    sum_out_ref,
    far_in_ref,
    far_out_ref,
    rows_ref,
    win_ref,
    wout_ref,
    y_acc,
    dx_acc,
    gin_acc,
    gout_acc,
    part_in_ref,
    part_out_ref,
    land_in_ref,
    land_out_ref,
    far_land,
    rows_sem,
    last_send,
    last_recv,
    own_sem,
    far_send,
    far_recv,
    weight_send,
    arrived,
    sum_send,
    sum_recv,
    back_send,
    back_recv,
    final_sem,
):
    line = Line(shards)
    z = line.me
    me = lax.axis_index("expert")
    _, batches, _, cap_pad, width = rows_ref.shape
    _, tall, span = spread_in_ref.shape
    blocks = batches
    rows = groups * cap_pad
    last = batches - 1
    spread = (win_ref, wout_ref)
    early_spread = (spread_in_ref, spread_out_ref)
    own = (own_body, own_bias, own_out)
    parts = (part_in_ref, part_out_ref)
    lands = (land_in_ref, land_out_ref)
    pieces = pieces_of(tall, span)
    far_pieces = pieces_of(tall, span, FAR_CUTS)

    for image in range(last):
        pltpu.make_async_copy(x_hbm.at[:, image], rows_ref.at[:, image], rows_sem.at[image]).start()
    pltpu.make_async_copy(last_hbm.at[me], rows_ref.at[me, last], last_recv.at[me]).start()
    own_places = (
        (own_body, win_ref.at[z, pl.ds(0, width)], 0),
        (own_bias, win_ref.at[z, pl.ds(width, tall - width)], 1),
        (own_out, wout_ref.at[z], 2),
    )
    own_loads = [
        pltpu.make_async_copy(here, there, own_sem.at[k]) for here, there, k in own_places
    ]

    def fetch(far, some):
        for sign in (-1, 1):
            slot = z + sign * far

            @pl.when((slot >= 0) & (slot < shards))
            def _():
                origins = line.views(early_spread, slot)
                places = line.views(spread, slot)
                for piece in some:
                    pltpu.make_async_copy(
                        origins[piece], places[piece], arrived.at[slot, piece]
                    ).start()

    fetch(1, range(4))
    fetch(2, EARLY_PIECES)
    for copy in own_loads:
        copy.start()

    line.greet(me, groups)

    def last_copy(target):
        return pltpu.make_async_remote_copy(
            src_ref=last_hbm.at[target],
            dst_ref=rows_ref.at[me, last],
            send_sem=last_send.at[target],
            recv_sem=last_recv.at[me],
            device_id={"expert": target},
            device_id_type=MESH,
        )

    for k in range(1, groups):
        last_copy(lax.rem(me + k, groups)).start()
    line.push(1, early_spread, spread, weight_send, arrived, LATE_PIECES)
    line.push(2, early_spread, spread, weight_send, arrived, EARLY_PIECES)

    table = []
    for at in range(shards):
        near = sorted(range(shards), key=lambda q: (abs(q - at), q))
        table.append(near[1:-1] + near[:1] + near[-1:])

    def quarter(step):
        total = 0
        for at in range(shards):
            for s in range(shards):
                hit = jnp.where((z == at) & (step == s), table[at][s], 0)
                total = total + hit
        return total

    def sum_copy(way, q, piece):
        kind, low, size = pieces[piece]
        if way == 0:
            slot = q - 1
            peer = z + 1
        else:
            slot = jnp.where(q == z - 1, shards - 2, q - 1)
            peer = z - 1
        cut = pl.ds(low, size)
        return pltpu.make_async_remote_copy(
            src_ref=parts[kind].at[q, cut],
            dst_ref=lands[kind].at[slot, cut],
            send_sem=sum_send.at[way, q, piece],
            recv_sem=sum_recv.at[slot, piece],
            device_id={"dp": peer},
            device_id_type=MESH,
        )

    def take_sum(slot, q, piece):
        kind, low, size = pieces[piece]
        cut = pl.ds(low, size)
        view = lands[kind].at[slot, cut]
        pltpu.make_async_copy(view, view, sum_recv.at[slot, piece]).wait()
        parts[kind][q, cut] = (
            parts[kind][q, cut].astype(F32) + lands[kind][slot, cut].astype(F32)
        ).astype(BF)

    def back_copy(target, image):
        return pltpu.make_async_remote_copy(
            src_ref=rows_ref.at[target, image],
            dst_ref=back_ref.at[me, image],
            send_sem=back_send.at[target, image],
            recv_sem=back_recv.at[me, image],
            device_id={"expert": target},
            device_id_type=MESH,
        )

    def back_start(image):
        for k in range(1, groups):
            back_copy(lax.rem(me + k, groups), image).start()
        pltpu.make_async_copy(
            rows_ref.at[me, image], back_ref.at[me, image], back_recv.at[me, image]
        ).start()

    plain = (shards - 2) * blocks
    late_item = blocks
    inner = (z > 0) & (z < shards - 1)

    def do_item(item, carry):
        late = item >= plain
        rest = item - plain
        step = jnp.where(late, shards - 2 + lax.rem(rest + 2 * blocks, 2), item // blocks)
        block = jnp.where(late, (rest + 2 * blocks) // 2 - blocks, lax.rem(item, blocks))
        q = quarter(step)
        bank = jnp.where(step == shards - 1, 1, 0)

        @pl.when(block == 0)
        def _():
            far = jnp.abs(q - z)

            @pl.when(far == 0)
            def _():
                for copy in own_loads:
                    copy.wait()

            @pl.when(far == 2)
            def _():
                line.wait_slot(q, spread, arrived, EARLY_PIECES)

            @pl.when((far == 1) | (far > 2))
            def _():
                line.wait_slot(q, spread, arrived)

            for distance in range(3, shards - 1):
                for way in range(2):
                    forward = 1 - 2 * way

                    @pl.when((q == z - forward * distance) & line.sends(way, distance))
                    def _():
                        for copy in line.hop(way, distance, spread, spread, weight_send, arrived):
                            copy.start()

        @pl.when(item == late_item)
        def _():
            line.receive(1, spread, arrived, LATE_PIECES)
            line.push(2, spread, spread, weight_send, arrived, LATE_PIECES)

        @pl.when((step == shards - 2) & (block > 0))
        def _():
            back_start(block - 1)

        here = pl.ds(pl.multiple_of(block * rows, rows), rows)

        @pl.when((step == 0) & (block < last))
        def _():
            view = rows_ref.at[:, block]
            pltpu.make_async_copy(view, view, rows_sem.at[block]).wait()

        @pl.when((step == 0) & (block == last))
        def _():
            for source in range(groups):
                view = rows_ref.at[source, last]
                pltpu.make_async_copy(view, view, last_recv.at[source]).wait()

        x = rows_ref[:, block, 0].reshape(rows, width)
        grad = rows_ref[:, block, 1].reshape(rows, width)
        win = win_ref[q, :width, :]
        wout = wout_ref[q]
        pre = dot(x, win) + win_ref[q, width : width + 1, :].astype(F32)
        cdf = 0.5 * lax.erf(pre * (0.5**0.5)) + 0.5
        active = (pre * cdf).astype(BF)
        slope = cdf + pre * (jnp.exp(-0.5 * pre * pre) * 0.3989422804014327)
        d_pre = (dot_nt(grad, wout) * slope).astype(BF)
        y_part = dot(active, wout)
        dx_part = dot_nt(d_pre, win)

        @pl.when(step == 0)
        def _():
            y_acc[here, :] = y_part
            dx_acc[here, :] = dx_part

        @pl.when(step > 0)
        def _():
            y_acc[here, :] += y_part
            dx_acc[here, :] += dx_part

        gout = dot_tn(active, grad)
        gin = dot_tn(x, d_pre)
        gbias = jnp.sum(d_pre.astype(F32), axis=0, keepdims=True)

        @pl.when(block == 0)
        def _():
            gout_acc[bank] = gout
            gin_acc[bank, :width, :] = gin
            gin_acc[bank, width : width + 1, :] = gbias

        @pl.when(block > 0)
        def _():
            gout_acc[bank] += gout
            gin_acc[bank, :width, :] += gin
            gin_acc[bank, width : width + 1, :] += gbias

        @pl.when(step == shards - 1)
        def _():
            shape = (groups, cap_pad, width)
            rows_ref[:, block, 0] = y_acc[here, :].astype(BF).reshape(shape)
            rows_ref[:, block, 1] = dx_acc[here, :].astype(BF).reshape(shape)

        @pl.when(block == blocks - 1)
        def _():
            part_in_ref[q, :width, :] = gin_acc[bank, :width, :].astype(BF)
            part_in_ref[q, width:, :] = jnp.broadcast_to(
                gin_acc[bank, width : width + 1, :].astype(BF), (tall - width, span)
            )
            part_out_ref[q] = gout_acc[bank].astype(BF)

            @pl.when((z == 0) & (q > z) & (q < shards - 1))
            def _():
                for piece in range(len(pieces)):
                    sum_copy(0, q, piece).start()

            @pl.when((z == shards - 1) & (q < z) & (q > 0))
            def _():
                for piece in range(len(pieces)):
                    sum_copy(1, q, piece).start()

        return carry

    lax.fori_loop(0, shards * blocks, do_item, 0)
    back_start(blocks - 1)

    def early_far(k, piece):
        _, low, size = far_pieces[piece]
        cut = pl.ds(low, size)
        return pltpu.make_async_remote_copy(
            src_ref=part_in_ref.at[(shards - 1) * k, cut],
            dst_ref=far_land.at[k, cut],
            send_sem=far_send.at[piece],
            recv_sem=far_recv.at[piece],
            device_id={"dp": z + 2 * k - 1},
            device_id_type=MESH,
        )

    def early_add(k, piece):
        _, low, size = far_pieces[piece]
        cut = pl.ds(low, size)
        view = far_land.at[k, cut]
        pltpu.make_async_copy(view, view, far_recv.at[piece]).wait()
        part_in_ref[(shards - 1) * k, cut] = (
            part_in_ref[(shards - 1) * k, cut].astype(F32) + far_land[k, cut].astype(F32)
        ).astype(BF)

    for piece in range(EARLY_FAR):

        @pl.when(z == 0)
        def _():
            early_far(1, piece).start()

        @pl.when(z == shards - 1)
        def _():
            early_far(0, piece).start()

    finals = [
        pltpu.make_async_copy(part_in_ref.at[0], far_in_ref.at[0], final_sem.at[0]),
        pltpu.make_async_copy(part_out_ref.at[0], far_out_ref.at[0], final_sem.at[1]),
        pltpu.make_async_copy(part_in_ref.at[shards - 1], far_in_ref.at[1], final_sem.at[2]),
        pltpu.make_async_copy(part_out_ref.at[shards - 1], far_out_ref.at[1], final_sem.at[3]),
        pltpu.make_async_copy(part_in_ref.at[z], sum_in_ref, final_sem.at[4]),
        pltpu.make_async_copy(part_out_ref.at[z], sum_out_ref, final_sem.at[5]),
    ]
    def do_forward(turn, carry):
        up = turn
        down = shards - 1 - turn
        for piece in range(len(pieces)):

            @pl.when((up > z) & (z > 0))
            def _():
                take_sum(up - 1, up, piece)
                sum_copy(0, up, piece).start()

            @pl.when((down < z) & (z < shards - 1))
            def _():
                take_sum(down - 1, down, piece)
                sum_copy(1, down, piece).start()

        return carry

    lax.fori_loop(1, shards - 1, do_forward, 0)
    for piece in range(len(pieces)):

        @pl.when(inner)
        def _():
            take_sum(z - 1, z, piece)
            take_sum(shards - 2, z, piece)

    for copy in finals[4:]:
        copy.start()
    for piece in range(EARLY_FAR):

        @pl.when(z == 1)
        def _():
            early_add(1, piece)

        @pl.when(z == shards - 2)
        def _():
            early_add(0, piece)

    for copy in finals[:4]:
        copy.start()

    def finish_sum(q, carry):
        @pl.when((q > z) & line.has_above)
        def _():
            for piece in range(len(pieces)):
                sum_copy(0, q, piece).wait_send()

        @pl.when((q < z) & line.has_below)
        def _():
            for piece in range(len(pieces)):
                sum_copy(1, q, piece).wait_send()

        return carry

    lax.fori_loop(1, shards - 1, finish_sum, 0)
    line.drain(1, spread, spread, weight_send, arrived, LATE_PIECES)
    for round_id in range(2, shards - 1):
        line.drain(round_id, spread, spread, weight_send, arrived)
    for piece in range(EARLY_FAR):

        @pl.when(z == 0)
        def _():
            early_far(1, piece).wait_send()

        @pl.when(z == shards - 1)
        def _():
            early_far(0, piece).wait_send()

    for k in range(1, groups):
        last_copy(lax.rem(me + k, groups)).wait_send()

    def finish_back(image, carry):
        for k in range(groups):
            source = lax.rem(me + k, groups)
            if k:
                back_copy(source, image).wait_send()
            view = back_ref.at[source, image]
            pltpu.make_async_copy(view, view, back_recv.at[source, image]).wait()
        return carry

    lax.fori_loop(0, batches, finish_back, 0)
    for copy in finals:
        copy.wait()


def run_moe(received, last, own, spread_in, spread_out):
    groups, batches, _, cap_pad, width = received.shape
    shards, tall, span = spread_in.shape
    total = groups * batches * cap_pad
    count = len(pieces_of(tall, span))
    early_rows = sum(pieces_of(tall, span, FAR_CUTS)[EARLY_FAR - 1][1:])
    anywhere = pl.BlockSpec(memory_space=pl.ANY)
    return pl.pallas_call(
        functools.partial(moe_kernel, shards, groups),
        out_shape=(
            jax.ShapeDtypeStruct(received.shape, BF),
            jax.ShapeDtypeStruct((tall, span), BF),
            jax.ShapeDtypeStruct((span, width), BF),
            jax.ShapeDtypeStruct((2, tall, span), BF),
            jax.ShapeDtypeStruct((2, span, width), BF),
        ),
        in_specs=[anywhere] * 7,
        out_specs=(anywhere,) * 5,
        scratch_shapes=[
            pltpu.VMEM(received.shape, BF),
            pltpu.VMEM((shards, tall, span), BF),
            pltpu.VMEM((shards, span, width), BF),
            pltpu.VMEM((total, width), F32),
            pltpu.VMEM((total, width), F32),
            pltpu.VMEM((2, ceil_to(width + 1, 8), span), F32),
            pltpu.VMEM((2, span, width), F32),
            pltpu.VMEM((shards, tall, span), BF),
            pltpu.VMEM((shards, span, width), BF),
            pltpu.VMEM((shards - 1, tall, span), BF),
            pltpu.VMEM((shards - 1, span, width), BF),
            pltpu.VMEM((2, early_rows, span), BF),
            pltpu.SemaphoreType.DMA((batches,)),
            pltpu.SemaphoreType.DMA((groups,)),
            pltpu.SemaphoreType.DMA((groups,)),
            pltpu.SemaphoreType.DMA((3,)),
            pltpu.SemaphoreType.DMA((EARLY_FAR,)),
            pltpu.SemaphoreType.DMA((EARLY_FAR,)),
            pltpu.SemaphoreType.DMA((2, shards, 4)),
            pltpu.SemaphoreType.DMA((shards, 4)),
            pltpu.SemaphoreType.DMA((2, shards, count)),
            pltpu.SemaphoreType.DMA((shards - 1, count)),
            pltpu.SemaphoreType.DMA((groups, batches)),
            pltpu.SemaphoreType.DMA((groups, batches)),
            pltpu.SemaphoreType.DMA((6,)),
        ],
        compiler_params=pltpu.CompilerParams(
            vmem_limit_bytes=VMEM_MAX, collective_id=2, has_side_effects=True
        ),
        cost_estimate=pl.CostEstimate(
            flops=12 * total * width * span * shards,
            bytes_accessed=60000000,
            transcendentals=2 * total * span * shards,
        ),
        name="moe",
    )(received, last, *own, spread_in, spread_out)


def tail_kernel(
    experts,
    x_ref,
    grad_ref,
    weight_ref,
    cols_ref,
    slot_cols_ref,
    back_ref,
    qkv_ref,
    mixed_ref,
    lse_ref,
    hidden_ref,
    one_ref,
    two_ref,
    probs_ref,
    out_ref,
    dx_ref,
    dense_ref,
    small_ref,
    sums_ref,
    d_qkv_ref,
    d_branch_ref,
    d_logits_ref,
    one_all,
    two_all,
    mixed_all,
):
    width = x_ref.shape[-1]
    rows = x_ref.shape[1]
    index = pl.program_id(0)

    @pl.when(index == 0)
    def _():
        small_ref[...] = weight_ref[:, 4 * width :].astype(F32).T
        sums_ref[...] = jnp.zeros_like(sums_ref)

    here = pl.ds(pl.multiple_of(index * rows, rows), rows)
    one_all[here, :] = one_ref[0]
    two_all[here, :] = two_ref[0]
    mixed_all[here, :] = mixed_ref[0]
    out_grad = grad_ref[0]
    hidden = hidden_ref[0]
    probs = probs_ref[0]
    lane = lax.broadcasted_iota(jnp.int32, (1, 128), 1)
    slots = back_ref.shape[0] * back_ref.shape[3]
    slot = lax.broadcasted_iota(jnp.int32, (1, slots), 1)
    answers = back_ref[:, 0, 0].reshape(slots, width)
    answer_grads = back_ref[:, 0, 1].reshape(slots, width)
    result = hidden
    d_probs = jnp.zeros_like(probs)
    both = None
    for j in range(2):
        pick = (slot == slot_cols_ref[0, :, j : j + 1]).astype(F32)
        both = pick if both is None else both + pick
        chosen = lane - 4 == cols_ref[0, :, j : j + 1]
        gate = jnp.sum(jnp.where(chosen, probs, 0.0), axis=-1, keepdims=True)
        picked = dot(pick.astype(BF), answers)
        result = result + gate * picked
        d_gate = jnp.sum(picked * out_grad, axis=-1, keepdims=True)
        d_probs = jnp.where(chosen, d_gate, d_probs)
    out_ref[0] = result
    d_logits = probs * (d_probs - jnp.sum(d_probs * probs, axis=-1, keepdims=True))
    d_logits = d_logits.astype(BF)
    d_logits_ref[here, :] = d_logits
    d_two = dot(both.astype(BF), answer_grads) + dot_nt(d_logits, weight_ref[:, 4 * width :])
    hat, inverse = norm_stats(hidden)
    sums_ref[2:3, :] += jnp.sum(d_two * hat, axis=0, keepdims=True)
    sums_ref[3:4, :] += jnp.sum(d_two, axis=0, keepdims=True)
    d_hat = d_two * small_ref[2:3, :]
    d_hidden = out_grad + inverse * (
        d_hat
        - jnp.mean(d_hat, axis=-1, keepdims=True)
        - hat * jnp.mean(d_hat * hat, axis=-1, keepdims=True)
    )
    d_branch = d_hidden.astype(BF)
    d_branch_ref[here, :] = d_branch
    d_mixed_all = dot_nt(d_branch, weight_ref[:, 3 * width : 4 * width]).astype(BF)
    key_ok = lax.broadcasted_iota(jnp.int32, (1, rows), 1) < SEQ
    scale = HEAD ** (-0.5)
    for pair in range(HEADS // 2):
        low = pair * 128
        query = qkv_ref[0, :, low : low + 128]
        keys = qkv_ref[0, :, width + low : width + low + 128]
        values = qkv_ref[0, :, 2 * width + low : 2 * width + low + 128]
        d_mixed = d_mixed_all[:, low : low + 128]
        d_query = d_keys = d_values = None
        for side in range(2):
            mine = (lane // HEAD) == side
            head = 2 * pair + side

            def own(array):
                return jnp.where(mine, array, jnp.zeros_like(array))

            my_query = own(query)
            my_keys = own(keys)
            my_d_mixed = own(d_mixed)
            scores = dot_nt(my_query, keys) * scale
            scores = jnp.where(key_ok, scores, NEG)
            probs_h = jnp.exp(scores - lse_ref[0, :, head : head + 1])
            d_weights = dot_nt(my_d_mixed, values)
            row_terms = jnp.sum(d_weights * probs_h, axis=-1, keepdims=True)
            d_scores = (probs_h * (d_weights - row_terms) * scale).astype(BF)
            parts = (
                dot(d_scores, my_keys),
                dot_tn(d_scores, my_query),
                dot_tn(probs_h.astype(BF), my_d_mixed),
            )
            if side == 0:
                d_query, d_keys, d_values = parts
            else:
                d_query, d_keys, d_values = (
                    d_query + parts[0],
                    d_keys + parts[1],
                    d_values + parts[2],
                )
        d_qkv_ref[here, low : low + 128] = d_query.astype(BF)
        d_qkv_ref[here, width + low : width + low + 128] = d_keys.astype(BF)
        d_qkv_ref[here, 2 * width + low : 2 * width + low + 128] = d_values.astype(BF)
    d_one = dot_nt(d_qkv_ref[here, :], weight_ref[:, : 3 * width])
    hat, inverse = norm_stats(x_ref[0])
    sums_ref[0:1, :] += jnp.sum(d_one * hat, axis=0, keepdims=True)
    sums_ref[1:2, :] += jnp.sum(d_one, axis=0, keepdims=True)
    d_hat = d_one * small_ref[0:1, :]
    dx_ref[0] = d_hidden + inverse * (
        d_hat
        - jnp.mean(d_hat, axis=-1, keepdims=True)
        - hat * jnp.mean(d_hat * hat, axis=-1, keepdims=True)
    )

    @pl.when(index == pl.num_programs(0) - 1)
    def _():
        dense_ref[:, 4 * width :] = (dot_tn(two_all[...], d_logits_ref[...]) + sums_ref[...].T).astype(BF)
        dense_ref[:, 3 * width : 4 * width] = dot_tn(mixed_all[...], d_branch_ref[...]).astype(BF)
        for part in range(3):
            cut = slice(part * width, (part + 1) * width)
            dense_ref[:, cut] = dot_tn(one_all[...], d_qkv_ref[:, cut]).astype(BF)


def run_tail(x, grad, weight, cols, slot_cols, back, saved, experts):
    batches, rows, width = x.shape
    total = weight.shape[1]
    cap_pad = back.shape[3]
    qkv, mixed, lse, hidden, one, two, probs = saved

    def block(*shape):
        return pl.BlockSpec((1,) + shape, lambda i: (i,) + (0,) * len(shape))

    return pl.pallas_call(
        functools.partial(tail_kernel, experts),
        grid=(batches,),
        out_shape=(
            jax.ShapeDtypeStruct(x.shape, F32),
            jax.ShapeDtypeStruct(x.shape, F32),
            jax.ShapeDtypeStruct((width, total), BF),
        ),
        in_specs=[
            block(rows, width),
            block(rows, width),
            pl.BlockSpec((width, total), lambda i: (0, 0), pipeline_mode=pl.Buffered(1)),
            block(rows, 4),
            block(rows, 8),
            pl.BlockSpec((experts, 1, 2, cap_pad, width), lambda i: (0, i, 0, 0, 0)),
            block(rows, 3 * width),
            block(rows, width),
            block(rows, 128),
            block(rows, width),
            block(rows, width),
            block(rows, width),
            block(rows, SMALL),
        ],
        out_specs=(
            block(rows, width),
            block(rows, width),
            pl.BlockSpec((width, total), lambda i: (0, 0), pipeline_mode=pl.Buffered(1)),
        ),
        scratch_shapes=[
            pltpu.VMEM((SMALL, width), F32),
            pltpu.VMEM((SMALL, width), F32),
            pltpu.VMEM((batches * rows, 3 * width), BF),
            pltpu.VMEM((batches * rows, width), BF),
            pltpu.VMEM((batches * rows, SMALL), BF),
            pltpu.VMEM((batches * rows, width), BF),
            pltpu.VMEM((batches * rows, width), BF),
            pltpu.VMEM((batches * rows, width), BF),
        ],
        compiler_params=params(),
        cost_estimate=pl.CostEstimate(
            flops=16000000000, bytes_accessed=50000000, transcendentals=2000000
        ),
        name="tail",
    )(x, grad, weight, cols, slot_cols, back, qkv, mixed, lse, hidden, one, two, probs)


def reduce_kernel(
    experts,
    shards,
    slot_cols_ref,
    lse_ref,
    probs_ref,
    vectors_ref,
    x_hbm,
    grad_hbm,
    weight_hbm,
    back_hbm,
    qkv_hbm,
    mixed_hbm,
    hidden_hbm,
    one_hbm,
    two_hbm,
    far_in_hbm,
    far_out_hbm,
    out_hbm,
    dx_hbm,
    end_in_hbm,
    end_out_hbm,
    qkv_grad_ref,
    proj_grad_ref,
    small_grad_ref,
    x_ref,
    grad_ref,
    weight_ref,
    back_ref,
    qkv_ref,
    mixed_ref,
    hidden_ref,
    one_ref,
    two_ref,
    raw_ref,
    sums_ref,
    one_flip,
    d_qkv_ref,
    d_branch_ref,
    d_mixed_ref,
    d_logits_ref,
    tiles_ref,
    near_ref,
    plane_land,
    plane_ref,
    line_land,
    final_ref,
    small_land,
    small_far,
    far_in_ref,
    far_out_ref,
    far_in_land,
    far_out_land,
    load_sem,
    store_sem,
    near_send,
    near_recv,
    plane_send,
    plane_recv,
    line_send,
    line_recv,
    final_send,
    final_recv,
    small_send,
    small_recv,
    far_load,
    far_send,
    far_recv,
):
    batches, rows, width = x_ref.shape
    z = lax.axis_index("dp")
    me = lax.axis_index("expert")
    core = lax.rem(me, 2)
    sibling = me + 1 - 2 * core
    chip = me // 2
    chips = PLANE // 2
    pairs = HEADS // 2
    depth = width // shards
    head_tiles = width // TILE
    own_tiles = (4 * width // TILE) // PLANE

    def loads(kind, image):
        pair = {
            0: (back_hbm.at[:, image], back_ref.at[:, image]),
            1: (hidden_hbm.at[image], hidden_ref.at[image]),
            2: (grad_hbm.at[image], grad_ref.at[image]),
            3: (mixed_hbm.at[image], mixed_ref.at[pl.ds(image * rows, rows)]),
            4: (two_hbm.at[image], two_ref.at[pl.ds(image * rows, rows)]),
            5: (one_hbm.at[image], one_ref.at[pl.ds(image * rows, rows)]),
            6: (qkv_hbm.at[image], qkv_ref.at[pl.ds(image * rows, rows)]),
            7: (x_hbm.at[image], x_ref.at[image]),
        }[kind]
        return pltpu.make_async_copy(pair[0], pair[1], load_sem.at[kind, image])

    weight_load = pltpu.make_async_copy(weight_hbm, weight_ref, load_sem.at[8, 0])
    far_parts = (far_in_ref, far_out_ref)
    far_lands = (far_in_land, far_out_land)
    far_loads = [
        pltpu.make_async_copy(source.at[k], target.at[k], far_load.at[k, part])
        for k in range(2)
        for part, (source, target) in enumerate(
            ((far_in_hbm, far_in_ref), (far_out_hbm, far_out_ref))
        )
    ]

    for copy in far_loads:
        copy.start()
    for kind in range(3):
        loads(kind, 0).start()
    weight_load.start()
    for image in range(1, batches):
        for kind in range(3):
            loads(kind, image).start()
    for kind in range(3, 8):
        for image in range(batches):
            loads(kind, image).start()

    barrier = pltpu.get_barrier_semaphore()
    for k in range(1, PLANE):
        pl.semaphore_signal(
            barrier, inc=1, device_id={"expert": lax.rem(me + k, PLANE)}, device_id_type=MESH
        )
    for k in range(1, shards):
        pl.semaphore_signal(
            barrier, inc=1, device_id={"dp": lax.rem(z + k, shards)}, device_id_type=MESH
        )
    pl.semaphore_wait(barrier, PLANE - 1 + shards - 1)

    def remote(source, target, send_sem, recv_sem, peer):
        return pltpu.make_async_remote_copy(
            src_ref=source,
            dst_ref=target,
            send_sem=send_sem,
            recv_sem=recv_sem,
            device_id=peer,
            device_id_type=MESH,
        )

    def landed(view, sem):
        pltpu.make_async_copy(view, view, sem).wait()

    pieces = pieces_of(far_in_ref.shape[1], far_out_ref.shape[1], FAR_CUTS)
    inner = (z > 0) & (z < shards - 1)
    low_half = 2 * z < shards

    def far_copy(k, piece):
        kind, low, size = pieces[piece]
        cut = pl.ds(low, size)
        return remote(
            far_parts[kind].at[k, cut],
            far_lands[kind].at[k, cut],
            far_send.at[k, piece],
            far_recv.at[k, piece],
            {"dp": z + 2 * k - 1},
        )

    def far_take(k, piece):
        kind, low, size = pieces[piece]
        cut = pl.ds(low, size)
        landed(far_lands[kind].at[k, cut], far_recv.at[k, piece])
        far_parts[kind][k, cut] = (
            far_parts[kind][k, cut].astype(F32) + far_lands[kind][k, cut].astype(F32)
        ).astype(BF)

    def far_forward(k, piece):
        if piece < EARLY_FAR:
            @pl.when(z != (1 if k else shards - 2))
            def _():
                far_take(k, piece)

        else:
            far_take(k, piece)
        far_copy(k, piece).start()

    def pass_on(first, piece):
        @pl.when(inner & low_half)
        def _():
            far_forward(1 if first else 0, piece)

        @pl.when(inner & jnp.logical_not(low_half))
        def _():
            far_forward(0 if first else 1, piece)

    for copy in far_loads:
        copy.wait()

    @pl.when(z == 0)
    def _():
        for piece in range(EARLY_FAR, len(pieces)):
            far_copy(1, piece).start()

    @pl.when(z == shards - 1)
    def _():
        for piece in range(EARLY_FAR, len(pieces)):
            far_copy(0, piece).start()

    def near_copy(tile):
        return remote(
            tiles_ref.at[tile],
            near_ref.at[tile // 2],
            near_send.at[tile],
            near_recv.at[tile],
            {"expert": sibling},
        )

    def plane_copy(tile):
        owner = lax.rem(tile, PLANE) // 2
        place = lax.rem(chip - owner + 2 * chips - 1, chips)
        return remote(
            tiles_ref.at[tile],
            plane_land.at[tile // PLANE, place],
            plane_send.at[tile],
            plane_recv.at[tile // PLANE, place],
            {"expert": lax.rem(tile, PLANE)},
        )

    def line_copy(k, far):
        return remote(
            plane_ref.at[k, pl.ds(pl.multiple_of(far * depth, depth), depth)],
            line_land.at[k, z],
            line_send.at[k, far],
            line_recv.at[k, z],
            {"dp": far},
        )

    def final_copy(k, peer):
        tile = me + PLANE * k
        return remote(
            final_ref.at[tile],
            final_ref.at[tile],
            final_send.at[k, peer],
            final_recv.at[tile],
            {"expert": peer},
        )

    def leave(tile):
        @pl.when(lax.rem(tile, 2) != core)
        def _():
            near_copy(tile).start()

    def combine(tile):
        @pl.when(lax.rem(tile, 2) == core)
        def _():
            landed(near_ref.at[tile // 2], near_recv.at[tile])
            tiles_ref[tile] = (
                tiles_ref[tile].astype(F32) + near_ref[tile // 2].astype(F32)
            ).astype(BF)

            @pl.when(lax.rem(tile, PLANE) != me)
            def _():
                plane_copy(tile).start()

    def plane_sum(k):
        total = tiles_ref[me + PLANE * k].astype(F32)
        for j in range(1, chips):
            landed(plane_land.at[k, j - 1], plane_recv.at[k, j - 1])
            total = total + plane_land[k, j - 1].astype(F32)
        plane_ref[k] = total.astype(BF)
        for j in range(1, shards):
            line_copy(k, lax.rem(z + j, shards)).start()

    def line_sum(k):
        mine = pl.ds(pl.multiple_of(z * depth, depth), depth)
        total = plane_ref[k, mine].astype(F32)
        for j in range(1, shards):
            far = lax.rem(z + j, shards)
            landed(line_land.at[k, far], line_recv.at[k, far])
            total = total + line_land[k, far].astype(F32)
        final_ref[me + PLANE * k] = total.astype(BF)
        for j in range(1, PLANE):
            final_copy(k, lax.rem(me + j, PLANE)).start()

    pass_on(True, 0)
    pass_on(True, 1)

    lane = lax.broadcasted_iota(jnp.int32, (1, 128), 1)
    groups, _, _, cap_pad, _ = back_ref.shape
    slots = groups * cap_pad
    slot = lax.broadcasted_iota(jnp.int32, (1, slots), 1)
    sums_ref[...] = jnp.zeros_like(sums_ref)
    small_rows = vectors_ref[:8].astype(F32)
    gain_one = small_rows[0:1]
    gain_two = small_rows[2:3]

    def phase_one(image, carry):
        here = pl.ds(pl.multiple_of(image * rows, rows), rows)
        for kind in range(3):
            view = (back_ref.at[:, image], hidden_ref.at[image], grad_ref.at[image])[kind]
            landed(view, load_sem.at[kind, image])

        @pl.when(image == 0)
        def _():
            weight_load.wait()

        out_grad = grad_ref[image]
        hidden = hidden_ref[image]
        probs = probs_ref[image]
        answers = back_ref[:, image, 0].reshape(slots, width)
        answer_grads = back_ref[:, image, 1].reshape(slots, width)
        result = hidden
        d_probs = jnp.zeros_like(probs)
        both = None
        for j in range(2):
            pick = (slot == slot_cols_ref[image, :, j : j + 1]).astype(F32)
            both = pick if both is None else both + pick
            chosen = lane - 4 == slot_cols_ref[image, :, 2 + j : 3 + j]
            gate = jnp.sum(jnp.where(chosen, probs, 0.0), axis=-1, keepdims=True)
            picked = dot(pick.astype(BF), answers)
            result = result + gate * picked
            d_gate = jnp.sum(picked * out_grad, axis=-1, keepdims=True)
            d_probs = jnp.where(chosen, d_gate, d_probs)
        d_logits = probs * (d_probs - jnp.sum(d_probs * probs, axis=-1, keepdims=True))
        d_logits = d_logits.astype(BF)
        d_logits_ref[here, :] = d_logits
        d_two = dot(both.astype(BF), answer_grads) + dot(d_logits, vectors_ref[...])
        hat, inverse = norm_stats(hidden)
        sums_ref[2:3, :] += jnp.sum(d_two * hat, axis=0, keepdims=True)
        sums_ref[3:4, :] += jnp.sum(d_two, axis=0, keepdims=True)
        d_hat = d_two * gain_two
        d_hidden = out_grad + inverse * (
            d_hat
            - jnp.mean(d_hat, axis=-1, keepdims=True)
            - hat * jnp.mean(d_hat * hat, axis=-1, keepdims=True)
        )
        d_branch = d_hidden.astype(BF)
        d_branch_ref[here, :] = d_branch
        d_mixed_ref[here, :] = dot_nt(d_branch, weight_ref[:, 3 * width : 4 * width]).astype(BF)
        grad_ref[image] = d_hidden
        hidden_ref[image] = result
        return carry

    lax.fori_loop(0, batches, phase_one, 0)
    for image in range(batches):
        raw_ref[image * SEQ : (image + 1) * SEQ] = hidden_ref[image, :SEQ]
    out_store = pltpu.make_async_copy(raw_ref, out_hbm, store_sem.at[0, 0])
    out_store.start()
    pass_on(True, 2)
    pass_on(False, 0)
    for kind, view in ((3, mixed_ref), (4, two_ref), (5, one_ref)):
        for image in range(batches):
            landed(view.at[pl.ds(image * rows, rows)], load_sem.at[kind, image])
    proj = dot_tn(mixed_ref[...], d_branch_ref[...]).astype(BF)
    for tile in range(head_tiles):
        tiles_ref[tile] = proj[:, tile * TILE : (tile + 1) * TILE]
    for tile in range(head_tiles):
        leave(tile)
    one_flip[...] = one_ref[...].T
    flipped = dot_tn(d_logits_ref[...], two_ref[...])
    for image in range(batches):
        landed(qkv_ref.at[pl.ds(image * rows, rows)], load_sem.at[6, image])

    pass_on(False, 1)

    key_ok = lax.broadcasted_iota(jnp.int32, (1, rows), 1) < SEQ
    scale = HEAD ** (-0.5)

    def phase_two(pair, carry):
        low = pl.multiple_of(pair * TILE, TILE)
        spots = [pl.ds(pl.multiple_of(part * width + low, TILE), TILE) for part in range(3)]
        for image in range(batches):
            here = pl.ds(image * rows, rows)
            query, keys, values = (qkv_ref[here, spot] for spot in spots)
            d_mixed = d_mixed_ref[here, pl.ds(low, TILE)]
            total = [None, None, None]
            for side in range(2):
                mine = (lane // HEAD) == side

                def own(array):
                    return jnp.where(mine, array, jnp.zeros_like(array))

                my_query = own(query)
                my_d_mixed = own(d_mixed)
                scores = dot_nt(my_query, keys) * scale
                scores = jnp.where(key_ok, scores, NEG)
                log_total = jnp.sum(
                    jnp.where(lane == 2 * pair + side, lse_ref[image], 0.0), axis=-1, keepdims=True
                )
                probs_h = jnp.exp(scores - log_total)
                d_weights = dot_nt(my_d_mixed, values)
                row_terms = jnp.sum(d_weights * probs_h, axis=-1, keepdims=True)
                d_scores = (probs_h * (d_weights - row_terms) * scale).astype(BF)
                fresh = (
                    dot(d_scores, own(keys)),
                    dot_tn(d_scores, my_query),
                    dot_tn(probs_h.astype(BF), my_d_mixed),
                )
                total = [new if old is None else old + new for old, new in zip(total, fresh)]
            for part in range(3):
                d_qkv_ref[here, spots[part]] = total[part].astype(BF)
        first = head_tiles + 3 * pair
        for part in range(3):
            tiles_ref[first + part] = dot(one_flip[...], d_qkv_ref[:, spots[part]]).astype(BF)
        for part in range(3):
            leave(first + part)

        @pl.when(pair == 0)
        def _():
            for tile in range(head_tiles):
                combine(tile)

        @pl.when(pair > 0)
        def _():
            for part in range(3):
                combine(first - 3 + part)

        for turn, first, piece in FAR_TURNS:

            @pl.when(pair == turn)
            def _():
                pass_on(first, piece)

        @pl.when(pair == pairs - 3)
        def _():
            plane_sum(0)

        @pl.when(pair == pairs - 1)
        def _():
            line_sum(0)
            plane_sum(1)

        return carry

    lax.fori_loop(0, pairs, phase_two, 0)
    for part in range(3):
        combine(head_tiles + 3 * (pairs - 1) + part)

    for image in range(batches):
        landed(x_ref.at[image], load_sem.at[7, image])

    def phase_three(image, carry):
        here = pl.ds(pl.multiple_of(image * rows, rows), rows)
        d_one = dot_nt(d_qkv_ref[here, :], weight_ref[:, : 3 * width])
        hat, inverse = norm_stats(x_ref[image])
        sums_ref[0:1, :] += jnp.sum(d_one * hat, axis=0, keepdims=True)
        sums_ref[1:2, :] += jnp.sum(d_one, axis=0, keepdims=True)
        d_hat = d_one * gain_one
        x_ref[image] = grad_ref[image] + inverse * (
            d_hat
            - jnp.mean(d_hat, axis=-1, keepdims=True)
            - hat * jnp.mean(d_hat * hat, axis=-1, keepdims=True)
        )

        @pl.when(image == batches // 2 - 1)
        def _():
            pass_on(False, 6)
            line_sum(1)
            plane_sum(2)

        return carry

    lax.fori_loop(0, batches, phase_three, 0)
    out_store.wait()
    for image in range(batches):
        raw_ref[image * SEQ : (image + 1) * SEQ] = x_ref[image, :SEQ]
    dx_store = pltpu.make_async_copy(raw_ref, dx_hbm, store_sem.at[1, 0])
    dx_store.start()

    def small_copy(k):
        peer = lax.rem(me + k, PLANE)
        return remote(
            sums_ref, small_land.at[me], small_send.at[peer], small_recv.at[me], {"expert": peer}
        )

    def small_far_copy(k):
        peer = lax.rem(z + k, shards)
        return remote(
            small_land.at[me],
            small_far.at[z],
            small_send.at[PLANE + peer],
            small_recv.at[PLANE + z],
            {"dp": peer},
        )

    sums_ref[...] += flipped[: sums_ref.shape[0]]
    for k in range(1, PLANE):
        small_copy(k).start()
    pass_on(False, 7)
    line_sum(2)
    total = sums_ref[...]
    for k in range(1, PLANE):
        peer = lax.rem(me + k, PLANE)
        landed(small_land.at[peer], small_recv.at[peer])
        total = total + small_land[peer]
    small_land[me] = total
    for k in range(1, shards):
        small_far_copy(k).start()
    for k in range(1, shards):
        peer = lax.rem(z + k, shards)
        landed(small_far.at[peer], small_recv.at[PLANE + peer])
        total = total + small_far[peer]
    small_grad_ref[...] = total

    def finish(tile, carry):
        @pl.when(lax.rem(tile, PLANE) != me)
        def _():
            landed(final_ref.at[tile], final_recv.at[tile])

        @pl.when(lax.rem(tile, 2) != core)
        def _():
            near_copy(tile).wait_send()

        @pl.when((lax.rem(tile, 2) == core) & (lax.rem(tile, PLANE) != me))
        def _():
            plane_copy(tile).wait_send()

        return carry

    lax.fori_loop(0, 4 * head_tiles, finish, 0)
    for tile in range(head_tiles):
        proj_grad_ref[:, tile * TILE : (tile + 1) * TILE] = final_ref[tile].astype(F32)
    for pair in range(pairs):
        for part in range(3):
            low = part * width + pair * TILE
            qkv_grad_ref[:, low : low + TILE] = final_ref[head_tiles + 3 * pair + part].astype(F32)
    for k in range(own_tiles):
        for j in range(1, shards):
            line_copy(k, lax.rem(z + j, shards)).wait_send()
        for j in range(1, PLANE):
            final_copy(k, lax.rem(me + j, PLANE)).wait_send()
    for k in range(1, PLANE):
        small_copy(k).wait_send()
    for k in range(1, shards):
        small_far_copy(k).wait_send()
    for piece in range(len(pieces)):

        @pl.when(z == 0)
        def _():
            far_take(0, piece)

        @pl.when(z == shards - 1)
        def _():
            far_take(1, piece)

    mine = jnp.where(z == shards - 1, 1, 0)
    ends = [
        pltpu.make_async_copy(far_in_ref.at[mine], end_in_hbm, far_load.at[0, 0]),
        pltpu.make_async_copy(far_out_ref.at[mine], end_out_hbm, far_load.at[0, 1]),
    ]
    for copy in ends:
        copy.start()
    for piece in range(len(pieces)):

        first = 1 if piece < EARLY_FAR else 0

        @pl.when((z < shards - 1) & (z >= first))
        def _():
            far_copy(1, piece).wait_send()

        @pl.when((z > 0) & (z < shards - first))
        def _():
            far_copy(0, piece).wait_send()

    for copy in ends:
        copy.wait()
    dx_store.wait()


def run_reduce(x, grad, weight, vectors, slot_cols, back, saved, far, experts):
    batches, rows, width = x.shape
    shards = lax.axis_size("dp")
    qkv, mixed, lse, hidden, one, two, probs = saved
    depth = width // shards
    tiles = 4 * width // TILE
    own_tiles = tiles // PLANE
    small_rows = ceil_to(4 + experts, 8)
    count = len(pieces_of(far[0].shape[1], far[1].shape[1], FAR_CUTS))
    anywhere = pl.BlockSpec(memory_space=pl.ANY)
    inside = pl.BlockSpec(memory_space=pltpu.VMEM)
    dma = pltpu.SemaphoreType.DMA
    return pl.pallas_call(
        functools.partial(reduce_kernel, experts, shards),
        out_shape=(
            jax.ShapeDtypeStruct((batches * SEQ, width), F32),
            jax.ShapeDtypeStruct((batches * SEQ, width), F32),
            jax.ShapeDtypeStruct(far[0].shape[1:], BF),
            jax.ShapeDtypeStruct(far[1].shape[1:], BF),
            jax.ShapeDtypeStruct((depth, 3 * width), F32),
            jax.ShapeDtypeStruct((depth, width), F32),
            jax.ShapeDtypeStruct((small_rows, width), F32),
        ),
        in_specs=[inside] * 4 + [anywhere] * 11,
        out_specs=(anywhere,) * 4 + (inside,) * 3,
        scratch_shapes=[
            pltpu.VMEM(x.shape, F32),
            pltpu.VMEM(x.shape, F32),
            pltpu.VMEM(weight.shape, BF),
            pltpu.VMEM(back.shape, BF),
            pltpu.VMEM((batches * rows, 3 * width), BF),
            pltpu.VMEM((batches * rows, width), BF),
            pltpu.VMEM(x.shape, F32),
            pltpu.VMEM((batches * rows, width), BF),
            pltpu.VMEM((batches * rows, width), BF),
            pltpu.VMEM((batches * SEQ, width), F32),
            pltpu.VMEM((small_rows, width), F32),
            pltpu.VMEM((width, batches * rows), BF),
            pltpu.VMEM((batches * rows, 3 * width), BF),
            pltpu.VMEM((batches * rows, width), BF),
            pltpu.VMEM((batches * rows, width), BF),
            pltpu.VMEM((batches * rows, SMALL), BF),
            pltpu.VMEM((tiles, width, TILE), BF),
            pltpu.VMEM((tiles // 2, width, TILE), BF),
            pltpu.VMEM((own_tiles, PLANE // 2 - 1, width, TILE), BF),
            pltpu.VMEM((own_tiles, width, TILE), BF),
            pltpu.VMEM((own_tiles, shards, depth, TILE), BF),
            pltpu.VMEM((tiles, depth, TILE), BF),
            pltpu.VMEM((PLANE, small_rows, width), F32),
            pltpu.VMEM((shards, small_rows, width), F32),
            pltpu.VMEM(far[0].shape, BF),
            pltpu.VMEM(far[1].shape, BF),
            pltpu.VMEM(far[0].shape, BF),
            pltpu.VMEM(far[1].shape, BF),
            dma((9, batches)),
            dma((2, batches)),
            dma((tiles,)),
            dma((tiles,)),
            dma((tiles,)),
            dma((own_tiles, PLANE // 2 - 1)),
            dma((own_tiles, shards)),
            dma((own_tiles, shards)),
            dma((own_tiles, PLANE)),
            dma((tiles,)),
            dma((PLANE + shards,)),
            dma((PLANE + shards,)),
            dma((2, 2)),
            dma((2, count)),
            dma((2, count)),
        ],
        compiler_params=pltpu.CompilerParams(
            vmem_limit_bytes=VMEM_MAX, collective_id=3, has_side_effects=True
        ),
        cost_estimate=pl.CostEstimate(
            flops=16000000000, bytes_accessed=50000000, transcendentals=2000000
        ),
        name="tail",
    )(slot_cols, lse, probs, vectors, x, grad, weight, back, qkv, mixed, hidden, one, two, *far)


def last_turn(far_in, far_out):
    at = lax.axis_index("dp") // (lax.axis_size("dp") - 1)
    return [lax.psum(far.astype(F32), "dp").astype(BF)[at] for far in (far_in, far_out)]


def per_device(
    inputs,
    gain_one,
    shift_one,
    qkv_weight,
    proj_weight,
    gain_two,
    shift_two,
    router_weight,
    expert_in,
    expert_bias,
    expert_out,
    out_grad,
    routes,
    priority,
    capacity,
):
    batches = priority.shape[0]
    count = inputs.shape[0] // batches
    width = inputs.shape[1]
    experts = router_weight.shape[1]
    groups = lax.axis_size("expert")
    cap_pad = ceil_to(max(2, (5 * count + 2 * experts - 1) // (2 * experts)), 16)
    depth = qkv_weight.shape[0]
    both = ("dp", "expert")

    vectors = jnp.stack([gain_one, shift_one, gain_two, shift_two], axis=1)
    small = jnp.concatenate([vectors, router_weight], axis=1)
    small = jnp.pad(small, ((0, 0), (0, SMALL - small.shape[1])))
    dense = (qkv_weight, proj_weight, small)
    own = (expert_in[0], jnp.pad(expert_bias, ((0, BIAS_ROWS - 1), (0, 0))), expert_out[0])
    cols = jnp.concatenate([routes, priority.reshape(batches * SEQ, 2)], axis=1)
    cols = cols.reshape(batches, SEQ, 4)
    cols = jnp.pad(cols, ((0, 0), (0, SEQ_PAD - SEQ), (0, 0)), constant_values=-1)
    rows_first = jnp.swapaxes(cols, 1, 2)
    received, last, x, grad, weight, qkv, mixed, hidden, one, two, lse, probs, slot_cols, rows_small, *spread = run_front(
        inputs, out_grad, dense, own, cols, rows_first, capacity, experts, cap_pad
    )
    saved = (qkv, mixed, lse, hidden, one, two, probs)
    back, sum_in, sum_out, far_in, far_out = run_moe(received, last, own, *spread)
    z = lax.axis_index("dp")
    at_end = (z == 0) | (z == lax.axis_size("dp") - 1)
    spot = 4 * width
    if groups == PLANE:
        outputs, inputs_grad, end_in, end_out, qkv_grad, proj_grad, small_grad = run_reduce(
            x, grad, weight, rows_small, slot_cols, back, saved, (far_in, far_out), experts
        )
        small_grad = lax.dynamic_slice_in_dim(
            small_grad, lax.axis_index("dp") * depth, depth, axis=1
        )
        vectors = [small_grad[k] for k in range(4)]
        router_grad = small_grad[4 : 4 + experts].T
    else:
        weight = jnp.concatenate([weight, rows_small.T], axis=1)
        outputs, inputs_grad, dense = run_tail(
            x, grad, weight, cols, slot_cols, back, saved, experts
        )
        end_in, end_out = last_turn(far_in, far_out)
        outputs, inputs_grad = (
            full[:, :SEQ].reshape(batches * SEQ, width) for full in (outputs, inputs_grad)
        )
        dense = lax.psum_scatter(dense, both, scatter_dimension=0, tiled=True)
        dense = lax.all_gather(dense, "expert", axis=0, tiled=True).astype(F32)
        qkv_grad = dense[:, : 3 * width]
        proj_grad = dense[:, 3 * width : spot]
        vectors = [dense[:, spot + k] for k in range(4)]
        router_grad = dense[:, spot + 4 : spot + 4 + experts]
    grad_in = jnp.where(at_end, end_in[:width], sum_in[:width]).astype(F32)
    grad_bias = jnp.where(at_end, end_in[width], sum_in[width]).astype(F32)
    grad_out = jnp.where(at_end, end_out, sum_out).astype(F32)
    return (
        outputs,
        inputs_grad,
        vectors[0],
        vectors[1],
        qkv_grad,
        proj_grad,
        vectors[2],
        vectors[3],
        router_grad,
        grad_in[None],
        grad_bias[None],
        grad_out[None],
    )


def solution(mesh):
    token = P(("dp", "expert"), None)
    vector = P("dp")
    matrix = P("dp", None)
    return jax.shard_map(
        per_device,
        mesh=mesh,
        in_specs=(
            token,
            vector,
            vector,
            matrix,
            matrix,
            vector,
            vector,
            matrix,
            P("expert", None, "dp"),
            P("expert", "dp"),
            P("expert", "dp", None),
            token,
            token,
            token,
            P(("dp", "expert")),
        ),
        out_specs=(
            token,
            token,
            vector,
            vector,
            matrix,
            matrix,
            vector,
            vector,
            matrix,
            P("expert", None, "dp"),
            P("expert", "dp"),
            P("expert", "dp", None),
        ),
        check_vma=False,
    )
```

```python
import functools

import jax
import jax.numpy as jnp
from jax import lax
from jax.experimental import pallas as pl
from jax.experimental.pallas import tpu as pltpu
from jax.sharding import PartitionSpec as P

HEADS = 12
HEAD = 64
SEQ = 197
SEQ_PAD = 208
EPS = 1e-06
BF = jnp.bfloat16
F32 = jnp.float32
SMALL = 128
MESH = pl.DeviceIdType.MESH
EARLY_PIECES = range(2)
LATE_PIECES = range(2, 4)
EARLY_FAR = 3
FAR_CUTS = 4
FAR_TURNS = (
    (0, True, 3),
    (1, True, 4),
    (1, False, 2),
    (2, True, 5),
    (3, False, 3),
    (4, True, 6),
    (4, False, 4),
    (5, True, 7),
    (5, False, 5),
)
TILE = 128
PLANE = 8
BIAS_ROWS = 16
NEG = -1e30
VMEM_LIMIT = 60 * 1024 * 1024
VMEM_MAX = 67043328


def ceil_to(value, step):
    return (value + step - 1) // step * step


def dot(a, b):
    return jnp.dot(a, b, preferred_element_type=F32)


def dot_nt(a, b):
    return lax.dot_general(a, b, (((1,), (1,)), ((), ())), preferred_element_type=F32)


def dot_tn(a, b):
    return lax.dot_general(a, b, (((0,), (0,)), ((), ())), preferred_element_type=F32)


def params(count=1):
    return pltpu.CompilerParams(
        dimension_semantics=("arbitrary",) * count, vmem_limit_bytes=VMEM_LIMIT
    )


class Line:
    def __init__(self, shards):
        self.shards = shards
        self.me = lax.axis_index("dp")
        self.has_below = self.me > 0
        self.has_above = self.me < shards - 1

    def greet(self, me, groups):
        barrier = pltpu.get_barrier_semaphore()
        for k in range(1, groups):
            pl.semaphore_signal(
                barrier, inc=1, device_id={"expert": lax.rem(me + k, groups)}, device_id_type=MESH
            )
        for k in range(1, self.shards):
            pl.semaphore_signal(
                barrier,
                inc=1,
                device_id={"dp": lax.rem(self.me + k, self.shards)},
                device_id_type=MESH,
            )
        pl.semaphore_wait(barrier, groups - 1 + self.shards - 1)

    def views(self, pair, slot):
        tall, span = pair[0].shape[1:]
        return [
            pair[kind].at[slot, pl.ds(low, size)] for kind, low, size in pieces_of(tall, span)
        ]

    def hop(self, way, round_id, source, target, send_sem, arrived, some=range(4)):
        step = 1 - 2 * way
        slot = self.me - step * round_id
        places = self.views(target, slot)
        if round_id == 0:
            body, bias, out = source
            tall, span = target[0].shape[1:]
            moves = []
            for piece, (kind, low, size) in enumerate(pieces_of(tall, span)):
                own = out if kind else body
                here = min(size, own.shape[0] - low)
                moves.append((own.at[pl.ds(low, here)], target[kind].at[slot, pl.ds(low, here)], piece))
                if here < size:
                    moves.append((bias, target[kind].at[slot, pl.ds(low + here, size - here)], piece))
        else:
            origins = self.views(source, slot)
            moves = [(origins[piece], places[piece], piece) for piece in some]
        return [
            pltpu.make_async_remote_copy(
                src_ref=origin,
                dst_ref=place,
                send_sem=send_sem.at[way, round_id, k if round_id == 0 else piece],
                recv_sem=arrived.at[slot, piece],
                device_id={"dp": self.me + step},
                device_id_type=MESH,
            )
            for k, (origin, place, piece) in enumerate(moves)
        ]

    def sends(self, way, round_id):
        if way == 0:
            return (self.me >= round_id) & self.has_above
        return (self.me + round_id < self.shards) & self.has_below

    def push(self, round_id, source, target, send_sem, arrived, some=range(4)):
        for way in range(2):

            @pl.when(self.sends(way, round_id))
            def _():
                for copy in self.hop(way, round_id, source, target, send_sem, arrived, some):
                    copy.start()

    def drain(self, round_id, source, target, send_sem, arrived, some=range(4)):
        for way in range(2):

            @pl.when(self.sends(way, round_id))
            def _():
                for copy in self.hop(way, round_id, source, target, send_sem, arrived, some):
                    copy.wait_send()

    def receive(self, round_id, target, arrived, some=range(4)):
        far = round_id + 1

        @pl.when(self.me >= far)
        def _():
            self.wait_slot(self.me - far, target, arrived, some)

        @pl.when(self.me + far < self.shards)
        def _():
            self.wait_slot(self.me + far, target, arrived, some)

    def wait_slot(self, slot, target, arrived, some=range(4)):
        places = self.views(target, slot)
        for piece in some:
            pltpu.make_async_copy(places[piece], places[piece], arrived.at[slot, piece]).wait()


def route(cap_pad, cols_ref, rows_ref, limit_ref, slot_rows_ref, slot_cols_ref):
    for b in range(cols_ref.shape[0]):
        limit = limit_ref[b]
        col = [cols_ref[b, :, k : k + 1] for k in range(4)]
        row = [rows_ref[b, k : k + 1, :] for k in range(4)]
        for j in range(2):
            rank_row = 0
            rank_col = 0
            for k in range(2):
                hit = (col[k] == row[j]) & (col[2 + k] < row[2 + j])
                rank_row = rank_row + jnp.sum(hit.astype(jnp.int32), axis=0, keepdims=True)
                hit = (row[k] == col[j]) & (row[2 + k] < col[2 + j])
                rank_col = rank_col + jnp.sum(hit.astype(jnp.int32), axis=1, keepdims=True)
            keep_row = (rank_row < limit) & (row[j] >= 0)
            keep_col = (rank_col < limit) & (col[j] >= 0)
            slot_rows_ref[b, j : j + 1, :] = jnp.where(keep_row, row[j] * cap_pad + rank_row, -1)
            slot_cols_ref[b, :, j : j + 1] = jnp.where(keep_col, col[j] * cap_pad + rank_col, -1)


def norm_stats(values):
    average = jnp.mean(values, axis=-1, keepdims=True)
    centered = values - average
    spread = jnp.mean(centered * centered, axis=-1, keepdims=True)
    inverse = lax.rsqrt(spread + EPS)
    return centered * inverse, inverse


def front_kernel(
    experts,
    shards,
    limit_ref,
    cols_ref,
    rows_ref,
    raw_hbm,
    raw_grad_hbm,
    qkv_own,
    proj_own,
    small_own_ref,
    own_body,
    own_bias,
    own_out,
    received_ref,
    last_hbm,
    x_hbm,
    grad_hbm,
    weight_hbm,
    qkv_hbm,
    mixed_hbm,
    hidden_hbm,
    one_hbm,
    two_hbm,
    lse_ref,
    probs_ref,
    slot_cols_ref,
    vectors_ref,
    spread_in_ref,
    spread_out_ref,
    raw_ref,
    raw_grad_ref,
    x_ref,
    grad_ref,
    weight_ref,
    qkv_ref,
    mixed_ref,
    hidden_ref,
    one_ref,
    two_ref,
    small_land,
    slot_rows_ref,
    send_ref,
    load_sem,
    store_sem,
    send_sem,
    arrived,
    rows_send,
    rows_recv,
    small_send,
    small_recv,
    line_send,
    piece_recv,
    plane_send,
    near_send,
):
    batches, rows, width = x_ref.shape
    groups = received_ref.shape[0]
    cap_pad = received_ref.shape[3]
    me = lax.axis_index("expert")
    line = Line(shards)
    z = line.me
    own = (own_body, own_bias, own_out)
    spread = (spread_in_ref, spread_out_ref)
    depth = width // shards
    piece_width = 4 * width // PLANE
    base = me // PLANE * PLANE
    spot = me - base
    core = lax.rem(me, 2)
    sibling = me + 1 - 2 * core
    chip = spot // 2
    chips = PLANE // 2
    cut = 3 * width // piece_width

    def remote(source, target, send, recv, peer):
        return pltpu.make_async_remote_copy(
            src_ref=source,
            dst_ref=target,
            send_sem=send,
            recv_sem=recv,
            device_id=peer,
            device_id_type=MESH,
        )

    def landed(view, sem):
        pltpu.make_async_copy(view, view, sem).wait()

    def rows_of(shard):
        return pl.ds(pl.multiple_of(shard * depth, depth), depth)

    def piece(shard, index):
        low = pl.multiple_of(index * piece_width, piece_width)
        return weight_ref.at[rows_of(shard), pl.ds(low, piece_width)]

    raws = [
        pltpu.make_async_copy(raw_hbm, raw_ref, load_sem.at[0]),
        pltpu.make_async_copy(raw_grad_hbm, raw_grad_ref, load_sem.at[1]),
    ]
    mine = [
        pltpu.make_async_copy(
            qkv_own, weight_ref.at[rows_of(z), pl.ds(0, 3 * width)], load_sem.at[2]
        ),
        pltpu.make_async_copy(
            proj_own, weight_ref.at[rows_of(z), pl.ds(3 * width, width)], load_sem.at[3]
        ),
    ]
    for copy in mine:
        copy.start()
    for copy in raws:
        copy.start()
    small_land[z, :, :depth] = (
        small_own_ref[...].astype(F32).T[: small_land.shape[1]].astype(BF)
    )
    line.greet(me, groups)
    for copy in mine:
        copy.wait()

    def small_copy(far):
        view = small_land.at[z]
        return remote(view, view, small_send.at[far], small_recv.at[z], {"dp": far})

    def line_copy(far):
        view = piece(z, spot)
        return remote(view, view, line_send.at[far], piece_recv.at[z, spot], {"dp": far})

    def plane_copy(shard, other):
        view = piece(shard, spot)
        peer = base + 2 * other + core
        return remote(
            view, view, plane_send.at[shard, other], piece_recv.at[shard, spot], {"expert": peer}
        )

    def near_copy(shard, other):
        index = 2 * other + core
        view = piece(shard, index)
        return remote(
            view, view, near_send.at[shard, other], piece_recv.at[shard, index], {"expert": sibling}
        )

    peers = [lax.rem(z + k, shards) for k in range(1, shards)]
    others = [lax.rem(chip + k, chips) for k in range(1, chips)]
    for far in peers:
        line_copy(far).start()
    for far in peers:
        small_copy(far).start()
    line.push(0, own, spread, send_sem, arrived)
    zero_rows = jnp.zeros((rows - SEQ, width), F32)

    def pad_image(image):
        x_ref[image, :SEQ] = raw_ref[image * SEQ : (image + 1) * SEQ]
        x_ref[image, SEQ:] = zero_rows
        pltpu.make_async_copy(x_ref.at[image], x_hbm.at[image], store_sem.at[0, image]).start()
        grad_ref[image, :SEQ] = raw_grad_ref[image * SEQ : (image + 1) * SEQ]
        grad_ref[image, SEQ:] = zero_rows
        pltpu.make_async_copy(
            grad_ref.at[image], grad_hbm.at[image], store_sem.at[1, image]
        ).start()

    for copy in raws:
        copy.wait()
    pad_image(0)
    for far in peers:
        landed(piece(far, spot), piece_recv.at[far, spot])
        for other in others:
            plane_copy(far, other).start()
        near_copy(far, chip).start()
    for image in range(1, batches):
        pad_image(image)
    slot_rows_ref[...] = jnp.full(slot_rows_ref.shape, -1, jnp.int32)
    slot_cols_ref[...] = jnp.full(slot_cols_ref.shape, -1, jnp.int32)
    route(cap_pad, cols_ref, rows_ref, limit_ref, slot_rows_ref, slot_cols_ref)
    slot_cols_ref[:, :, 2:4] = cols_ref[:, :, 0:2]
    for far in peers:
        for other in others:
            index = 2 * other + core
            landed(piece(far, index), piece_recv.at[far, index])
            near_copy(far, other).start()
    for far in peers:
        landed(small_land.at[far], small_recv.at[far])
        for k in range(chips):
            index = 2 * k + 1 - core
            landed(piece(far, index), piece_recv.at[far, index])
    weight_store = pltpu.make_async_copy(weight_ref, weight_hbm, load_sem.at[5])
    weight_store.start()
    used = small_land.shape[1]
    small_rows = jnp.concatenate(
        [small_land[shard, :, :depth].astype(F32) for shard in range(shards)], axis=1
    )
    vectors_ref[...] = jnp.zeros_like(vectors_ref)
    vectors_ref[:used] = small_rows.astype(BF)
    gain_one, shift_one, gain_two, shift_two = (small_rows[k : k + 1] for k in range(4))

    def rows_copy(image, target):
        return remote(
            send_ref.at[image, target],
            received_ref.at[me, image],
            rows_send.at[image, target],
            rows_recv.at[me, image],
            {"expert": target},
        )

    last = batches - 1
    last_store = pltpu.make_async_copy(send_ref.at[last], last_hbm, load_sem.at[4])
    saves = (
        (qkv_ref, qkv_hbm),
        (mixed_ref, mixed_hbm),
        (hidden_ref, hidden_hbm),
        (one_ref, one_hbm),
        (two_ref, two_hbm),
    )
    lane = lax.broadcasted_iota(jnp.int32, (1, 128), 1)
    key_ok = lax.broadcasted_iota(jnp.int32, (1, rows), 1) < SEQ
    slot = lax.broadcasted_iota(jnp.int32, (groups * cap_pad, 1), 0)
    scale = HEAD ** (-0.5)

    def do_image(index, carry):
        x = x_ref[index]
        hat, _ = norm_stats(x)
        one = (hat * gain_one + shift_one).astype(BF)
        one_ref[index] = one
        qkv_ref[index] = dot(one, weight_ref[:, : 3 * width]).astype(BF)
        lse = jnp.zeros((rows, 128), F32)
        for pair in range(HEADS // 2):
            low = pair * 128
            query = qkv_ref[index, :, low : low + 128]
            keys = qkv_ref[index, :, width + low : width + low + 128]
            values = qkv_ref[index, :, 2 * width + low : 2 * width + low + 128]
            total = None
            for side in range(2):
                part_of = (lane // HEAD) == side
                scores = dot_nt(jnp.where(part_of, query, jnp.zeros_like(query)), keys) * scale
                scores = jnp.where(key_ok, scores, NEG)
                highest = jnp.max(scores, axis=-1, keepdims=True)
                expo = jnp.exp(scores - highest)
                denom = jnp.sum(expo, axis=-1, keepdims=True)
                weights = (expo / denom).astype(BF)
                lse = jnp.where(lane == 2 * pair + side, highest + jnp.log(denom), lse)
                part = dot(weights, jnp.where(part_of, values, jnp.zeros_like(values)))
                total = part if total is None else total + part
            mixed_ref[index, :, low : low + 128] = total.astype(BF)
        lse_ref[index] = lse
        hidden = x + dot(mixed_ref[index], weight_ref[:, 3 * width : 4 * width])
        hidden_ref[index] = hidden
        hat, _ = norm_stats(hidden)
        two = (hat * gain_two + shift_two).astype(BF)
        two_ref[index] = two
        logits = dot_nt(two, vectors_ref[...])
        in_router = (lane >= 4) & (lane < 4 + experts)
        logits = jnp.where(in_router, logits, NEG)
        expo = jnp.exp(logits - jnp.max(logits, axis=-1, keepdims=True))
        probs = expo / jnp.sum(expo, axis=-1, keepdims=True)
        probs_ref[index] = probs
        out_grad = grad_ref[index]
        both = None
        grads = None
        for j in range(2):
            gate = jnp.sum(
                jnp.where(lane - 4 == cols_ref[index, :, j : j + 1], probs, 0.0),
                axis=-1,
                keepdims=True,
            )
            pick = (slot == slot_rows_ref[index, j : j + 1, :]).astype(F32)
            both = pick if both is None else both + pick
            part = dot(pick.astype(BF), (gate * out_grad).astype(BF))
            grads = part if grads is None else grads + part
        sent = dot(both.astype(BF), two).astype(BF)
        send_ref[index, :, 0] = sent.reshape(groups, cap_pad, width)
        send_ref[index, :, 1] = grads.astype(BF).reshape(groups, cap_pad, width)

        @pl.when(index < last)
        def _():
            for k in range(1, groups):
                rows_copy(index, lax.rem(me + k, groups)).start()
            pltpu.make_async_copy(
                send_ref.at[index, me], received_ref.at[me, index], rows_recv.at[me, index]
            ).start()

        @pl.when(index == last)
        def _():
            last_store.start()

        for k, (here, there) in enumerate(saves):
            pltpu.make_async_copy(here.at[index], there.at[index], store_sem.at[2 + k, index]).start()
        return carry

    lax.fori_loop(0, batches, do_image, 0)

    line.receive(0, spread, arrived)
    line.push(1, spread, spread, send_sem, arrived, EARLY_PIECES)

    def finish(image, carry):
        @pl.when(image < last)
        def _():
            for k in range(groups):
                source = lax.rem(me + k, groups)
                if k:
                    rows_copy(image, source).wait_send()
                landed(received_ref.at[source, image], rows_recv.at[source, image])

        pltpu.make_async_copy(x_ref.at[image], x_hbm.at[image], store_sem.at[0, image]).wait()
        pltpu.make_async_copy(grad_ref.at[image], grad_hbm.at[image], store_sem.at[1, image]).wait()
        for k, (here, there) in enumerate(saves):
            pltpu.make_async_copy(here.at[image], there.at[image], store_sem.at[2 + k, image]).wait()
        return carry

    lax.fori_loop(0, batches, finish, 0)
    weight_store.wait()
    last_store.wait()
    for far in peers:
        line_copy(far).wait_send()
        small_copy(far).wait_send()
        for other in others:
            plane_copy(far, other).wait_send()
        for k in range(chips):
            near_copy(far, k).wait_send()
    line.receive(1, spread, arrived, EARLY_PIECES)
    line.drain(0, own, spread, send_sem, arrived)
    line.drain(1, spread, spread, send_sem, arrived, EARLY_PIECES)


def run_front(raw, raw_grad, dense, own, cols, rows_first, limits, experts, cap_pad):
    batches, rows = cols.shape[:2]
    width = raw.shape[1]
    shards = lax.axis_size("dp")
    groups = lax.axis_size("expert")
    body, bias, out = own
    tall = body.shape[0] + bias.shape[0]
    anywhere = pl.BlockSpec(memory_space=pl.ANY)
    inside = pl.BlockSpec(memory_space=pltpu.VMEM)
    dma = pltpu.SemaphoreType.DMA
    chips = PLANE // 2

    def shape(*dims, dtype=BF):
        return jax.ShapeDtypeStruct((batches, rows) + dims, dtype)

    return pl.pallas_call(
        functools.partial(front_kernel, experts, shards),
        out_shape=(
            jax.ShapeDtypeStruct((groups, batches, 2, cap_pad, width), BF),
            jax.ShapeDtypeStruct((groups, 2, cap_pad, width), BF),
            shape(width, dtype=F32),
            shape(width, dtype=F32),
            jax.ShapeDtypeStruct((width, 4 * width), BF),
            shape(3 * width),
            shape(width),
            shape(width, dtype=F32),
            shape(width),
            shape(width),
            shape(128, dtype=F32),
            shape(SMALL, dtype=F32),
            shape(8, dtype=jnp.int32),
            jax.ShapeDtypeStruct((SMALL, width), BF),
            jax.ShapeDtypeStruct((shards, tall, body.shape[1]), BF),
            jax.ShapeDtypeStruct((shards,) + out.shape, BF),
        ),
        in_specs=[pl.BlockSpec(memory_space=pltpu.SMEM), inside, inside]
        + [anywhere] * 4
        + [inside]
        + [anywhere] * 3,
        out_specs=(anywhere,) * 10 + (inside,) * 4 + (anywhere,) * 2,
        scratch_shapes=[
            pltpu.VMEM(raw.shape, F32),
            pltpu.VMEM(raw.shape, F32),
            pltpu.VMEM((batches, rows, width), F32),
            pltpu.VMEM((batches, rows, width), F32),
            pltpu.VMEM((width, 4 * width), BF),
            pltpu.VMEM((batches, rows, 3 * width), BF),
            pltpu.VMEM((batches, rows, width), BF),
            pltpu.VMEM((batches, rows, width), F32),
            pltpu.VMEM((batches, rows, width), BF),
            pltpu.VMEM((batches, rows, width), BF),
            pltpu.VMEM((shards, ceil_to(4 + experts, 16), ceil_to(dense[2].shape[0], 128)), BF),
            pltpu.VMEM((batches, 8, rows), jnp.int32),
            pltpu.VMEM((batches, groups, 2, cap_pad, width), BF),
            dma((6,)),
            dma((7, batches)),
            dma((2, 2, 5)),
            dma((shards, 4)),
            dma((batches, groups)),
            dma((groups, batches)),
            dma((shards,)),
            dma((shards,)),
            dma((shards,)),
            dma((shards, PLANE)),
            dma((shards, chips)),
            dma((shards, chips)),
        ],
        compiler_params=pltpu.CompilerParams(
            vmem_limit_bytes=VMEM_LIMIT, collective_id=1, has_side_effects=True
        ),
        cost_estimate=pl.CostEstimate(
            flops=8000000000, bytes_accessed=40000000, transcendentals=3000000
        ),
        name="front",
    )(limits, cols, rows_first, raw, raw_grad, *dense, *own)


def pieces_of(tall, span, cuts=2):
    pieces = []
    for kind, extent in enumerate((tall, span)):
        size = ceil_to(-(-extent // cuts), 16)
        for low in range(0, extent, size):
            pieces.append((kind, low, min(size, extent - low)))
    return tuple(pieces)


def moe_kernel(
    shards,
    groups,
    x_hbm,
    last_hbm,
    own_body,
    own_bias,
    own_out,
    spread_in_ref,
    spread_out_ref,
    back_ref,
    sum_in_ref,
    sum_out_ref,
    far_in_ref,
    far_out_ref,
    rows_ref,
    win_ref,
    wout_ref,
    y_acc,
    dx_acc,
    gin_acc,
    gout_acc,
    part_in_ref,
    part_out_ref,
    land_in_ref,
    land_out_ref,
    far_land,
    rows_sem,
    last_send,
    last_recv,
    own_sem,
    far_send,
    far_recv,
    weight_send,
    arrived,
    sum_send,
    sum_recv,
    back_send,
    back_recv,
    final_sem,
):
    line = Line(shards)
    z = line.me
    me = lax.axis_index("expert")
    _, batches, _, cap_pad, width = rows_ref.shape
    _, tall, span = spread_in_ref.shape
    blocks = batches
    rows = groups * cap_pad
    last = batches - 1
    spread = (win_ref, wout_ref)
    early_spread = (spread_in_ref, spread_out_ref)
    own = (own_body, own_bias, own_out)
    parts = (part_in_ref, part_out_ref)
    lands = (land_in_ref, land_out_ref)
    pieces = pieces_of(tall, span)
    far_pieces = pieces_of(tall, span, FAR_CUTS)

    for image in range(last):
        pltpu.make_async_copy(x_hbm.at[:, image], rows_ref.at[:, image], rows_sem.at[image]).start()
    pltpu.make_async_copy(last_hbm.at[me], rows_ref.at[me, last], last_recv.at[me]).start()
    own_places = (
        (own_body, win_ref.at[z, pl.ds(0, width)], 0),
        (own_bias, win_ref.at[z, pl.ds(width, tall - width)], 1),
        (own_out, wout_ref.at[z], 2),
    )
    own_loads = [
        pltpu.make_async_copy(here, there, own_sem.at[k]) for here, there, k in own_places
    ]

    def fetch(far, some):
        for sign in (-1, 1):
            slot = z + sign * far

            @pl.when((slot >= 0) & (slot < shards))
            def _():
                origins = line.views(early_spread, slot)
                places = line.views(spread, slot)
                for piece in some:
                    pltpu.make_async_copy(
                        origins[piece], places[piece], arrived.at[slot, piece]
                    ).start()

    fetch(1, range(4))
    fetch(2, EARLY_PIECES)
    for copy in own_loads:
        copy.start()

    line.greet(me, groups)

    def last_copy(target):
        return pltpu.make_async_remote_copy(
            src_ref=last_hbm.at[target],
            dst_ref=rows_ref.at[me, last],
            send_sem=last_send.at[target],
            recv_sem=last_recv.at[me],
            device_id={"expert": target},
            device_id_type=MESH,
        )

    for k in range(1, groups):
        last_copy(lax.rem(me + k, groups)).start()
    line.push(1, early_spread, spread, weight_send, arrived, LATE_PIECES)
    line.push(2, early_spread, spread, weight_send, arrived, EARLY_PIECES)

    table = []
    for at in range(shards):
        near = sorted(range(shards), key=lambda q: (abs(q - at), q))
        table.append(near[1:-1] + near[:1] + near[-1:])

    def quarter(step):
        total = 0
        for at in range(shards):
            for s in range(shards):
                hit = jnp.where((z == at) & (step == s), table[at][s], 0)
                total = total + hit
        return total

    def sum_copy(way, q, piece):
        kind, low, size = pieces[piece]
        if way == 0:
            slot = q - 1
            peer = z + 1
        else:
            slot = jnp.where(q == z - 1, shards - 2, q - 1)
            peer = z - 1
        cut = pl.ds(low, size)
        return pltpu.make_async_remote_copy(
            src_ref=parts[kind].at[q, cut],
            dst_ref=lands[kind].at[slot, cut],
            send_sem=sum_send.at[way, q, piece],
            recv_sem=sum_recv.at[slot, piece],
            device_id={"dp": peer},
            device_id_type=MESH,
        )

    def take_sum(slot, q, piece):
        kind, low, size = pieces[piece]
        cut = pl.ds(low, size)
        view = lands[kind].at[slot, cut]
        pltpu.make_async_copy(view, view, sum_recv.at[slot, piece]).wait()
        parts[kind][q, cut] = (
            parts[kind][q, cut].astype(F32) + lands[kind][slot, cut].astype(F32)
        ).astype(BF)

    def back_copy(target, image):
        return pltpu.make_async_remote_copy(
            src_ref=rows_ref.at[target, image],
            dst_ref=back_ref.at[me, image],
            send_sem=back_send.at[target, image],
            recv_sem=back_recv.at[me, image],
            device_id={"expert": target},
            device_id_type=MESH,
        )

    def back_start(image):
        for k in range(1, groups):
            back_copy(lax.rem(me + k, groups), image).start()
        pltpu.make_async_copy(
            rows_ref.at[me, image], back_ref.at[me, image], back_recv.at[me, image]
        ).start()

    plain = (shards - 2) * blocks
    late_item = blocks
    inner = (z > 0) & (z < shards - 1)

    def do_item(item, carry):
        late = item >= plain
        rest = item - plain
        step = jnp.where(late, shards - 2 + lax.rem(rest + 2 * blocks, 2), item // blocks)
        block = jnp.where(late, (rest + 2 * blocks) // 2 - blocks, lax.rem(item, blocks))
        q = quarter(step)
        bank = jnp.where(step == shards - 1, 1, 0)

        @pl.when(block == 0)
        def _():
            far = jnp.abs(q - z)

            @pl.when(far == 0)
            def _():
                for copy in own_loads:
                    copy.wait()

            @pl.when(far == 2)
            def _():
                line.wait_slot(q, spread, arrived, EARLY_PIECES)

            @pl.when((far == 1) | (far > 2))
            def _():
                line.wait_slot(q, spread, arrived)

            for distance in range(3, shards - 1):
                for way in range(2):
                    forward = 1 - 2 * way

                    @pl.when((q == z - forward * distance) & line.sends(way, distance))
                    def _():
                        for copy in line.hop(way, distance, spread, spread, weight_send, arrived):
                            copy.start()

        @pl.when(item == late_item)
        def _():
            line.receive(1, spread, arrived, LATE_PIECES)
            line.push(2, spread, spread, weight_send, arrived, LATE_PIECES)

        @pl.when((step == shards - 2) & (block > 0))
        def _():
            back_start(block - 1)

        here = pl.ds(pl.multiple_of(block * rows, rows), rows)

        @pl.when((step == 0) & (block < last))
        def _():
            view = rows_ref.at[:, block]
            pltpu.make_async_copy(view, view, rows_sem.at[block]).wait()

        @pl.when((step == 0) & (block == last))
        def _():
            for source in range(groups):
                view = rows_ref.at[source, last]
                pltpu.make_async_copy(view, view, last_recv.at[source]).wait()

        x = rows_ref[:, block, 0].reshape(rows, width)
        grad = rows_ref[:, block, 1].reshape(rows, width)
        win = win_ref[q, :width, :]
        wout = wout_ref[q]
        pre = dot(x, win) + win_ref[q, width : width + 1, :].astype(F32)
        cdf = 0.5 * lax.erf(pre * (0.5**0.5)) + 0.5
        active = (pre * cdf).astype(BF)
        slope = cdf + pre * (jnp.exp(-0.5 * pre * pre) * 0.3989422804014327)
        d_pre = (dot_nt(grad, wout) * slope).astype(BF)
        y_part = dot(active, wout)
        dx_part = dot_nt(d_pre, win)

        @pl.when(step == 0)
        def _():
            y_acc[here, :] = y_part
            dx_acc[here, :] = dx_part

        @pl.when(step > 0)
        def _():
            y_acc[here, :] += y_part
            dx_acc[here, :] += dx_part

        gout = dot_tn(active, grad)
        gin = dot_tn(x, d_pre)
        gbias = jnp.sum(d_pre.astype(F32), axis=0, keepdims=True)

        @pl.when(block == 0)
        def _():
            gout_acc[bank] = gout
            gin_acc[bank, :width, :] = gin
            gin_acc[bank, width : width + 1, :] = gbias

        @pl.when(block > 0)
        def _():
            gout_acc[bank] += gout
            gin_acc[bank, :width, :] += gin
            gin_acc[bank, width : width + 1, :] += gbias

        @pl.when(step == shards - 1)
        def _():
            shape = (groups, cap_pad, width)
            rows_ref[:, block, 0] = y_acc[here, :].astype(BF).reshape(shape)
            rows_ref[:, block, 1] = dx_acc[here, :].astype(BF).reshape(shape)

        @pl.when(block == blocks - 1)
        def _():
            part_in_ref[q, :width, :] = gin_acc[bank, :width, :].astype(BF)
            part_in_ref[q, width:, :] = jnp.broadcast_to(
                gin_acc[bank, width : width + 1, :].astype(BF), (tall - width, span)
            )
            part_out_ref[q] = gout_acc[bank].astype(BF)

            @pl.when((z == 0) & (q > z) & (q < shards - 1))
            def _():
                for piece in range(len(pieces)):
                    sum_copy(0, q, piece).start()

            @pl.when((z == shards - 1) & (q < z) & (q > 0))
            def _():
                for piece in range(len(pieces)):
                    sum_copy(1, q, piece).start()

        return carry

    lax.fori_loop(0, shards * blocks, do_item, 0)
    back_start(blocks - 1)

    def early_far(k, piece):
        _, low, size = far_pieces[piece]
        cut = pl.ds(low, size)
        return pltpu.make_async_remote_copy(
            src_ref=part_in_ref.at[(shards - 1) * k, cut],
            dst_ref=far_land.at[k, cut],
            send_sem=far_send.at[piece],
            recv_sem=far_recv.at[piece],
            device_id={"dp": z + 2 * k - 1},
            device_id_type=MESH,
        )

    def early_add(k, piece):
        _, low, size = far_pieces[piece]
        cut = pl.ds(low, size)
        view = far_land.at[k, cut]
        pltpu.make_async_copy(view, view, far_recv.at[piece]).wait()
        part_in_ref[(shards - 1) * k, cut] = (
            part_in_ref[(shards - 1) * k, cut].astype(F32) + far_land[k, cut].astype(F32)
        ).astype(BF)

    for piece in range(EARLY_FAR):

        @pl.when(z == 0)
        def _():
            early_far(1, piece).start()

        @pl.when(z == shards - 1)
        def _():
            early_far(0, piece).start()

    finals = [
        pltpu.make_async_copy(part_in_ref.at[0], far_in_ref.at[0], final_sem.at[0]),
        pltpu.make_async_copy(part_out_ref.at[0], far_out_ref.at[0], final_sem.at[1]),
        pltpu.make_async_copy(part_in_ref.at[shards - 1], far_in_ref.at[1], final_sem.at[2]),
        pltpu.make_async_copy(part_out_ref.at[shards - 1], far_out_ref.at[1], final_sem.at[3]),
        pltpu.make_async_copy(part_in_ref.at[z], sum_in_ref, final_sem.at[4]),
        pltpu.make_async_copy(part_out_ref.at[z], sum_out_ref, final_sem.at[5]),
    ]
    def do_forward(turn, carry):
        up = turn
        down = shards - 1 - turn
        for piece in range(len(pieces)):

            @pl.when((up > z) & (z > 0))
            def _():
                take_sum(up - 1, up, piece)
                sum_copy(0, up, piece).start()

            @pl.when((down < z) & (z < shards - 1))
            def _():
                take_sum(down - 1, down, piece)
                sum_copy(1, down, piece).start()

        return carry

    lax.fori_loop(1, shards - 1, do_forward, 0)
    for piece in range(len(pieces)):

        @pl.when(inner)
        def _():
            take_sum(z - 1, z, piece)
            take_sum(shards - 2, z, piece)

    for copy in finals[4:]:
        copy.start()
    for piece in range(EARLY_FAR):

        @pl.when(z == 1)
        def _():
            early_add(1, piece)

        @pl.when(z == shards - 2)
        def _():
            early_add(0, piece)

    for copy in finals[:4]:
        copy.start()

    def finish_sum(q, carry):
        @pl.when((q > z) & line.has_above)
        def _():
            for piece in range(len(pieces)):
                sum_copy(0, q, piece).wait_send()

        @pl.when((q < z) & line.has_below)
        def _():
            for piece in range(len(pieces)):
                sum_copy(1, q, piece).wait_send()

        return carry

    lax.fori_loop(1, shards - 1, finish_sum, 0)
    line.drain(1, spread, spread, weight_send, arrived, LATE_PIECES)
    for round_id in range(2, shards - 1):
        line.drain(round_id, spread, spread, weight_send, arrived)
    for piece in range(EARLY_FAR):

        @pl.when(z == 0)
        def _():
            early_far(1, piece).wait_send()

        @pl.when(z == shards - 1)
        def _():
            early_far(0, piece).wait_send()

    for k in range(1, groups):
        last_copy(lax.rem(me + k, groups)).wait_send()

    def finish_back(image, carry):
        for k in range(groups):
            source = lax.rem(me + k, groups)
            if k:
                back_copy(source, image).wait_send()
            view = back_ref.at[source, image]
            pltpu.make_async_copy(view, view, back_recv.at[source, image]).wait()
        return carry

    lax.fori_loop(0, batches, finish_back, 0)
    for copy in finals:
        copy.wait()


def run_moe(received, last, own, spread_in, spread_out):
    groups, batches, _, cap_pad, width = received.shape
    shards, tall, span = spread_in.shape
    total = groups * batches * cap_pad
    count = len(pieces_of(tall, span))
    early_rows = sum(pieces_of(tall, span, FAR_CUTS)[EARLY_FAR - 1][1:])
    anywhere = pl.BlockSpec(memory_space=pl.ANY)
    return pl.pallas_call(
        functools.partial(moe_kernel, shards, groups),
        out_shape=(
            jax.ShapeDtypeStruct(received.shape, BF),
            jax.ShapeDtypeStruct((tall, span), BF),
            jax.ShapeDtypeStruct((span, width), BF),
            jax.ShapeDtypeStruct((2, tall, span), BF),
            jax.ShapeDtypeStruct((2, span, width), BF),
        ),
        in_specs=[anywhere] * 7,
        out_specs=(anywhere,) * 5,
        scratch_shapes=[
            pltpu.VMEM(received.shape, BF),
            pltpu.VMEM((shards, tall, span), BF),
            pltpu.VMEM((shards, span, width), BF),
            pltpu.VMEM((total, width), F32),
            pltpu.VMEM((total, width), F32),
            pltpu.VMEM((2, ceil_to(width + 1, 8), span), F32),
            pltpu.VMEM((2, span, width), F32),
            pltpu.VMEM((shards, tall, span), BF),
            pltpu.VMEM((shards, span, width), BF),
            pltpu.VMEM((shards - 1, tall, span), BF),
            pltpu.VMEM((shards - 1, span, width), BF),
            pltpu.VMEM((2, early_rows, span), BF),
            pltpu.SemaphoreType.DMA((batches,)),
            pltpu.SemaphoreType.DMA((groups,)),
            pltpu.SemaphoreType.DMA((groups,)),
            pltpu.SemaphoreType.DMA((3,)),
            pltpu.SemaphoreType.DMA((EARLY_FAR,)),
            pltpu.SemaphoreType.DMA((EARLY_FAR,)),
            pltpu.SemaphoreType.DMA((2, shards, 4)),
            pltpu.SemaphoreType.DMA((shards, 4)),
            pltpu.SemaphoreType.DMA((2, shards, count)),
            pltpu.SemaphoreType.DMA((shards - 1, count)),
            pltpu.SemaphoreType.DMA((groups, batches)),
            pltpu.SemaphoreType.DMA((groups, batches)),
            pltpu.SemaphoreType.DMA((6,)),
        ],
        compiler_params=pltpu.CompilerParams(
            vmem_limit_bytes=VMEM_MAX, collective_id=2, has_side_effects=True
        ),
        cost_estimate=pl.CostEstimate(
            flops=12 * total * width * span * shards,
            bytes_accessed=60000000,
            transcendentals=2 * total * span * shards,
        ),
        name="moe",
    )(received, last, *own, spread_in, spread_out)


def tail_kernel(
    experts,
    x_ref,
    grad_ref,
    weight_ref,
    cols_ref,
    slot_cols_ref,
    back_ref,
    qkv_ref,
    mixed_ref,
    lse_ref,
    hidden_ref,
    one_ref,
    two_ref,
    probs_ref,
    out_ref,
    dx_ref,
    dense_ref,
    small_ref,
    sums_ref,
    d_qkv_ref,
    d_branch_ref,
    d_logits_ref,
    one_all,
    two_all,
    mixed_all,
):
    width = x_ref.shape[-1]
    rows = x_ref.shape[1]
    index = pl.program_id(0)

    @pl.when(index == 0)
    def _():
        small_ref[...] = weight_ref[:, 4 * width :].astype(F32).T
        sums_ref[...] = jnp.zeros_like(sums_ref)

    here = pl.ds(pl.multiple_of(index * rows, rows), rows)
    one_all[here, :] = one_ref[0]
    two_all[here, :] = two_ref[0]
    mixed_all[here, :] = mixed_ref[0]
    out_grad = grad_ref[0]
    hidden = hidden_ref[0]
    probs = probs_ref[0]
    lane = lax.broadcasted_iota(jnp.int32, (1, 128), 1)
    slots = back_ref.shape[0] * back_ref.shape[3]
    slot = lax.broadcasted_iota(jnp.int32, (1, slots), 1)
    answers = back_ref[:, 0, 0].reshape(slots, width)
    answer_grads = back_ref[:, 0, 1].reshape(slots, width)
    result = hidden
    d_probs = jnp.zeros_like(probs)
    both = None
    for j in range(2):
        pick = (slot == slot_cols_ref[0, :, j : j + 1]).astype(F32)
        both = pick if both is None else both + pick
        chosen = lane - 4 == cols_ref[0, :, j : j + 1]
        gate = jnp.sum(jnp.where(chosen, probs, 0.0), axis=-1, keepdims=True)
        picked = dot(pick.astype(BF), answers)
        result = result + gate * picked
        d_gate = jnp.sum(picked * out_grad, axis=-1, keepdims=True)
        d_probs = jnp.where(chosen, d_gate, d_probs)
    out_ref[0] = result
    d_logits = probs * (d_probs - jnp.sum(d_probs * probs, axis=-1, keepdims=True))
    d_logits = d_logits.astype(BF)
    d_logits_ref[here, :] = d_logits
    d_two = dot(both.astype(BF), answer_grads) + dot_nt(d_logits, weight_ref[:, 4 * width :])
    hat, inverse = norm_stats(hidden)
    sums_ref[2:3, :] += jnp.sum(d_two * hat, axis=0, keepdims=True)
    sums_ref[3:4, :] += jnp.sum(d_two, axis=0, keepdims=True)
    d_hat = d_two * small_ref[2:3, :]
    d_hidden = out_grad + inverse * (
        d_hat
        - jnp.mean(d_hat, axis=-1, keepdims=True)
        - hat * jnp.mean(d_hat * hat, axis=-1, keepdims=True)
    )
    d_branch = d_hidden.astype(BF)
    d_branch_ref[here, :] = d_branch
    d_mixed_all = dot_nt(d_branch, weight_ref[:, 3 * width : 4 * width]).astype(BF)
    key_ok = lax.broadcasted_iota(jnp.int32, (1, rows), 1) < SEQ
    scale = HEAD ** (-0.5)
    for pair in range(HEADS // 2):
        low = pair * 128
        query = qkv_ref[0, :, low : low + 128]
        keys = qkv_ref[0, :, width + low : width + low + 128]
        values = qkv_ref[0, :, 2 * width + low : 2 * width + low + 128]
        d_mixed = d_mixed_all[:, low : low + 128]
        d_query = d_keys = d_values = None
        for side in range(2):
            mine = (lane // HEAD) == side
            head = 2 * pair + side

            def own(array):
                return jnp.where(mine, array, jnp.zeros_like(array))

            my_query = own(query)
            my_keys = own(keys)
            my_d_mixed = own(d_mixed)
            scores = dot_nt(my_query, keys) * scale
            scores = jnp.where(key_ok, scores, NEG)
            probs_h = jnp.exp(scores - lse_ref[0, :, head : head + 1])
            d_weights = dot_nt(my_d_mixed, values)
            row_terms = jnp.sum(d_weights * probs_h, axis=-1, keepdims=True)
            d_scores = (probs_h * (d_weights - row_terms) * scale).astype(BF)
            parts = (
                dot(d_scores, my_keys),
                dot_tn(d_scores, my_query),
                dot_tn(probs_h.astype(BF), my_d_mixed),
            )
            if side == 0:
                d_query, d_keys, d_values = parts
            else:
                d_query, d_keys, d_values = (
                    d_query + parts[0],
                    d_keys + parts[1],
                    d_values + parts[2],
                )
        d_qkv_ref[here, low : low + 128] = d_query.astype(BF)
        d_qkv_ref[here, width + low : width + low + 128] = d_keys.astype(BF)
        d_qkv_ref[here, 2 * width + low : 2 * width + low + 128] = d_values.astype(BF)
    d_one = dot_nt(d_qkv_ref[here, :], weight_ref[:, : 3 * width])
    hat, inverse = norm_stats(x_ref[0])
    sums_ref[0:1, :] += jnp.sum(d_one * hat, axis=0, keepdims=True)
    sums_ref[1:2, :] += jnp.sum(d_one, axis=0, keepdims=True)
    d_hat = d_one * small_ref[0:1, :]
    dx_ref[0] = d_hidden + inverse * (
        d_hat
        - jnp.mean(d_hat, axis=-1, keepdims=True)
        - hat * jnp.mean(d_hat * hat, axis=-1, keepdims=True)
    )

    @pl.when(index == pl.num_programs(0) - 1)
    def _():
        dense_ref[:, 4 * width :] = (dot_tn(two_all[...], d_logits_ref[...]) + sums_ref[...].T).astype(BF)
        dense_ref[:, 3 * width : 4 * width] = dot_tn(mixed_all[...], d_branch_ref[...]).astype(BF)
        for part in range(3):
            cut = slice(part * width, (part + 1) * width)
            dense_ref[:, cut] = dot_tn(one_all[...], d_qkv_ref[:, cut]).astype(BF)


def run_tail(x, grad, weight, cols, slot_cols, back, saved, experts):
    batches, rows, width = x.shape
    total = weight.shape[1]
    cap_pad = back.shape[3]
    qkv, mixed, lse, hidden, one, two, probs = saved

    def block(*shape):
        return pl.BlockSpec((1,) + shape, lambda i: (i,) + (0,) * len(shape))

    return pl.pallas_call(
        functools.partial(tail_kernel, experts),
        grid=(batches,),
        out_shape=(
            jax.ShapeDtypeStruct(x.shape, F32),
            jax.ShapeDtypeStruct(x.shape, F32),
            jax.ShapeDtypeStruct((width, total), BF),
        ),
        in_specs=[
            block(rows, width),
            block(rows, width),
            pl.BlockSpec((width, total), lambda i: (0, 0), pipeline_mode=pl.Buffered(1)),
            block(rows, 4),
            block(rows, 8),
            pl.BlockSpec((experts, 1, 2, cap_pad, width), lambda i: (0, i, 0, 0, 0)),
            block(rows, 3 * width),
            block(rows, width),
            block(rows, 128),
            block(rows, width),
            block(rows, width),
            block(rows, width),
            block(rows, SMALL),
        ],
        out_specs=(
            block(rows, width),
            block(rows, width),
            pl.BlockSpec((width, total), lambda i: (0, 0), pipeline_mode=pl.Buffered(1)),
        ),
        scratch_shapes=[
            pltpu.VMEM((SMALL, width), F32),
            pltpu.VMEM((SMALL, width), F32),
            pltpu.VMEM((batches * rows, 3 * width), BF),
            pltpu.VMEM((batches * rows, width), BF),
            pltpu.VMEM((batches * rows, SMALL), BF),
            pltpu.VMEM((batches * rows, width), BF),
            pltpu.VMEM((batches * rows, width), BF),
            pltpu.VMEM((batches * rows, width), BF),
        ],
        compiler_params=params(),
        cost_estimate=pl.CostEstimate(
            flops=16000000000, bytes_accessed=50000000, transcendentals=2000000
        ),
        name="tail",
    )(x, grad, weight, cols, slot_cols, back, qkv, mixed, lse, hidden, one, two, probs)


def reduce_kernel(
    experts,
    shards,
    slot_cols_ref,
    lse_ref,
    probs_ref,
    vectors_ref,
    x_hbm,
    grad_hbm,
    weight_hbm,
    back_hbm,
    qkv_hbm,
    mixed_hbm,
    hidden_hbm,
    one_hbm,
    two_hbm,
    far_in_hbm,
    far_out_hbm,
    out_hbm,
    dx_hbm,
    end_in_hbm,
    end_out_hbm,
    qkv_grad_ref,
    proj_grad_ref,
    small_grad_ref,
    x_ref,
    grad_ref,
    weight_ref,
    back_ref,
    qkv_ref,
    mixed_ref,
    hidden_ref,
    one_ref,
    two_ref,
    raw_ref,
    sums_ref,
    one_flip,
    d_qkv_ref,
    d_branch_ref,
    d_mixed_ref,
    d_logits_ref,
    tiles_ref,
    near_ref,
    plane_land,
    plane_ref,
    line_land,
    final_ref,
    small_land,
    small_far,
    far_in_ref,
    far_out_ref,
    far_in_land,
    far_out_land,
    load_sem,
    store_sem,
    near_send,
    near_recv,
    plane_send,
    plane_recv,
    line_send,
    line_recv,
    final_send,
    final_recv,
    small_send,
    small_recv,
    far_load,
    far_send,
    far_recv,
):
    batches, rows, width = x_ref.shape
    z = lax.axis_index("dp")
    me = lax.axis_index("expert")
    core = lax.rem(me, 2)
    sibling = me + 1 - 2 * core
    chip = me // 2
    chips = PLANE // 2
    pairs = HEADS // 2
    depth = width // shards
    head_tiles = width // TILE
    own_tiles = (4 * width // TILE) // PLANE

    def loads(kind, image):
        pair = {
            0: (back_hbm.at[:, image], back_ref.at[:, image]),
            1: (hidden_hbm.at[image], hidden_ref.at[image]),
            2: (grad_hbm.at[image], grad_ref.at[image]),
            3: (mixed_hbm.at[image], mixed_ref.at[pl.ds(image * rows, rows)]),
            4: (two_hbm.at[image], two_ref.at[pl.ds(image * rows, rows)]),
            5: (one_hbm.at[image], one_ref.at[pl.ds(image * rows, rows)]),
            6: (qkv_hbm.at[image], qkv_ref.at[pl.ds(image * rows, rows)]),
            7: (x_hbm.at[image], x_ref.at[image]),
        }[kind]
        return pltpu.make_async_copy(pair[0], pair[1], load_sem.at[kind, image])

    weight_load = pltpu.make_async_copy(weight_hbm, weight_ref, load_sem.at[8, 0])
    far_parts = (far_in_ref, far_out_ref)
    far_lands = (far_in_land, far_out_land)
    far_loads = [
        pltpu.make_async_copy(source.at[k], target.at[k], far_load.at[k, part])
        for k in range(2)
        for part, (source, target) in enumerate(
            ((far_in_hbm, far_in_ref), (far_out_hbm, far_out_ref))
        )
    ]

    for copy in far_loads:
        copy.start()
    for kind in range(3):
        loads(kind, 0).start()
    weight_load.start()
    for image in range(1, batches):
        for kind in range(3):
            loads(kind, image).start()
    for kind in range(3, 8):
        for image in range(batches):
            loads(kind, image).start()

    barrier = pltpu.get_barrier_semaphore()
    for k in range(1, PLANE):
        pl.semaphore_signal(
            barrier, inc=1, device_id={"expert": lax.rem(me + k, PLANE)}, device_id_type=MESH
        )
    for k in range(1, shards):
        pl.semaphore_signal(
            barrier, inc=1, device_id={"dp": lax.rem(z + k, shards)}, device_id_type=MESH
        )
    pl.semaphore_wait(barrier, PLANE - 1 + shards - 1)

    def remote(source, target, send_sem, recv_sem, peer):
        return pltpu.make_async_remote_copy(
            src_ref=source,
            dst_ref=target,
            send_sem=send_sem,
            recv_sem=recv_sem,
            device_id=peer,
            device_id_type=MESH,
        )

    def landed(view, sem):
        pltpu.make_async_copy(view, view, sem).wait()

    pieces = pieces_of(far_in_ref.shape[1], far_out_ref.shape[1], FAR_CUTS)
    inner = (z > 0) & (z < shards - 1)
    low_half = 2 * z < shards

    def far_copy(k, piece):
        kind, low, size = pieces[piece]
        cut = pl.ds(low, size)
        return remote(
            far_parts[kind].at[k, cut],
            far_lands[kind].at[k, cut],
            far_send.at[k, piece],
            far_recv.at[k, piece],
            {"dp": z + 2 * k - 1},
        )

    def far_take(k, piece):
        kind, low, size = pieces[piece]
        cut = pl.ds(low, size)
        landed(far_lands[kind].at[k, cut], far_recv.at[k, piece])
        far_parts[kind][k, cut] = (
            far_parts[kind][k, cut].astype(F32) + far_lands[kind][k, cut].astype(F32)
        ).astype(BF)

    def far_forward(k, piece):
        if piece < EARLY_FAR:
            @pl.when(z != (1 if k else shards - 2))
            def _():
                far_take(k, piece)

        else:
            far_take(k, piece)
        far_copy(k, piece).start()

    def pass_on(first, piece):
        @pl.when(inner & low_half)
        def _():
            far_forward(1 if first else 0, piece)

        @pl.when(inner & jnp.logical_not(low_half))
        def _():
            far_forward(0 if first else 1, piece)

    for copy in far_loads:
        copy.wait()

    @pl.when(z == 0)
    def _():
        for piece in range(EARLY_FAR, len(pieces)):
            far_copy(1, piece).start()

    @pl.when(z == shards - 1)
    def _():
        for piece in range(EARLY_FAR, len(pieces)):
            far_copy(0, piece).start()

    def near_copy(tile):
        return remote(
            tiles_ref.at[tile],
            near_ref.at[tile // 2],
            near_send.at[tile],
            near_recv.at[tile],
            {"expert": sibling},
        )

    def plane_copy(tile):
        owner = lax.rem(tile, PLANE) // 2
        place = lax.rem(chip - owner + 2 * chips - 1, chips)
        return remote(
            tiles_ref.at[tile],
            plane_land.at[tile // PLANE, place],
            plane_send.at[tile],
            plane_recv.at[tile // PLANE, place],
            {"expert": lax.rem(tile, PLANE)},
        )

    def line_copy(k, far):
        return remote(
            plane_ref.at[k, pl.ds(pl.multiple_of(far * depth, depth), depth)],
            line_land.at[k, z],
            line_send.at[k, far],
            line_recv.at[k, z],
            {"dp": far},
        )

    def final_copy(k, peer):
        tile = me + PLANE * k
        return remote(
            final_ref.at[tile],
            final_ref.at[tile],
            final_send.at[k, peer],
            final_recv.at[tile],
            {"expert": peer},
        )

    def leave(tile):
        @pl.when(lax.rem(tile, 2) != core)
        def _():
            near_copy(tile).start()

    def combine(tile):
        @pl.when(lax.rem(tile, 2) == core)
        def _():
            landed(near_ref.at[tile // 2], near_recv.at[tile])
            tiles_ref[tile] = (
                tiles_ref[tile].astype(F32) + near_ref[tile // 2].astype(F32)
            ).astype(BF)

            @pl.when(lax.rem(tile, PLANE) != me)
            def _():
                plane_copy(tile).start()

    def plane_sum(k):
        total = tiles_ref[me + PLANE * k].astype(F32)
        for j in range(1, chips):
            landed(plane_land.at[k, j - 1], plane_recv.at[k, j - 1])
            total = total + plane_land[k, j - 1].astype(F32)
        plane_ref[k] = total.astype(BF)
        for j in range(1, shards):
            line_copy(k, lax.rem(z + j, shards)).start()

    def line_sum(k):
        mine = pl.ds(pl.multiple_of(z * depth, depth), depth)
        total = plane_ref[k, mine].astype(F32)
        for j in range(1, shards):
            far = lax.rem(z + j, shards)
            landed(line_land.at[k, far], line_recv.at[k, far])
            total = total + line_land[k, far].astype(F32)
        final_ref[me + PLANE * k] = total.astype(BF)
        for j in range(1, PLANE):
            final_copy(k, lax.rem(me + j, PLANE)).start()

    pass_on(True, 0)
    pass_on(True, 1)

    pass_on(True, 2)

    lane = lax.broadcasted_iota(jnp.int32, (1, 128), 1)
    groups, _, _, cap_pad, _ = back_ref.shape
    slots = groups * cap_pad
    slot = lax.broadcasted_iota(jnp.int32, (1, slots), 1)
    sums_ref[...] = jnp.zeros_like(sums_ref)
    small_rows = vectors_ref[:8].astype(F32)
    gain_one = small_rows[0:1]
    gain_two = small_rows[2:3]

    def phase_one(image, carry):
        here = pl.ds(pl.multiple_of(image * rows, rows), rows)
        for kind in range(3):
            view = (back_ref.at[:, image], hidden_ref.at[image], grad_ref.at[image])[kind]
            landed(view, load_sem.at[kind, image])

        @pl.when(image == 0)
        def _():
            weight_load.wait()

        out_grad = grad_ref[image]
        hidden = hidden_ref[image]
        probs = probs_ref[image]
        answers = back_ref[:, image, 0].reshape(slots, width)
        answer_grads = back_ref[:, image, 1].reshape(slots, width)
        result = hidden
        d_probs = jnp.zeros_like(probs)
        both = None
        for j in range(2):
            pick = (slot == slot_cols_ref[image, :, j : j + 1]).astype(F32)
            both = pick if both is None else both + pick
            chosen = lane - 4 == slot_cols_ref[image, :, 2 + j : 3 + j]
            gate = jnp.sum(jnp.where(chosen, probs, 0.0), axis=-1, keepdims=True)
            picked = dot(pick.astype(BF), answers)
            result = result + gate * picked
            d_gate = jnp.sum(picked * out_grad, axis=-1, keepdims=True)
            d_probs = jnp.where(chosen, d_gate, d_probs)
        d_logits = probs * (d_probs - jnp.sum(d_probs * probs, axis=-1, keepdims=True))
        d_logits = d_logits.astype(BF)
        d_logits_ref[here, :] = d_logits
        d_two = dot(both.astype(BF), answer_grads) + dot(d_logits, vectors_ref[...])
        hat, inverse = norm_stats(hidden)
        sums_ref[2:3, :] += jnp.sum(d_two * hat, axis=0, keepdims=True)
        sums_ref[3:4, :] += jnp.sum(d_two, axis=0, keepdims=True)
        d_hat = d_two * gain_two
        d_hidden = out_grad + inverse * (
            d_hat
            - jnp.mean(d_hat, axis=-1, keepdims=True)
            - hat * jnp.mean(d_hat * hat, axis=-1, keepdims=True)
        )
        d_branch = d_hidden.astype(BF)
        d_branch_ref[here, :] = d_branch
        d_mixed_ref[here, :] = dot_nt(d_branch, weight_ref[:, 3 * width : 4 * width]).astype(BF)
        grad_ref[image] = d_hidden
        hidden_ref[image] = result
        return carry

    lax.fori_loop(0, batches, phase_one, 0)
    for image in range(batches):
        raw_ref[image * SEQ : (image + 1) * SEQ] = hidden_ref[image, :SEQ]
    out_store = pltpu.make_async_copy(raw_ref, out_hbm, store_sem.at[0, 0])
    out_store.start()
    pass_on(False, 0)
    for kind, view in ((3, mixed_ref), (4, two_ref), (5, one_ref)):
        for image in range(batches):
            landed(view.at[pl.ds(image * rows, rows)], load_sem.at[kind, image])
    proj = dot_tn(mixed_ref[...], d_branch_ref[...]).astype(BF)
    for tile in range(head_tiles):
        tiles_ref[tile] = proj[:, tile * TILE : (tile + 1) * TILE]
    for tile in range(head_tiles):
        leave(tile)
    one_flip[...] = one_ref[...].T
    flipped = dot_tn(d_logits_ref[...], two_ref[...])
    for image in range(batches):
        landed(qkv_ref.at[pl.ds(image * rows, rows)], load_sem.at[6, image])

    pass_on(False, 1)

    key_ok = lax.broadcasted_iota(jnp.int32, (1, rows), 1) < SEQ
    scale = HEAD ** (-0.5)

    def phase_two(pair, carry):
        low = pl.multiple_of(pair * TILE, TILE)
        spots = [pl.ds(pl.multiple_of(part * width + low, TILE), TILE) for part in range(3)]
        for image in range(batches):
            here = pl.ds(image * rows, rows)
            query, keys, values = (qkv_ref[here, spot] for spot in spots)
            d_mixed = d_mixed_ref[here, pl.ds(low, TILE)]
            total = [None, None, None]
            for side in range(2):
                mine = (lane // HEAD) == side

                def own(array):
                    return jnp.where(mine, array, jnp.zeros_like(array))

                my_query = own(query)
                my_d_mixed = own(d_mixed)
                scores = dot_nt(my_query, keys) * scale
                scores = jnp.where(key_ok, scores, NEG)
                log_total = jnp.sum(
                    jnp.where(lane == 2 * pair + side, lse_ref[image], 0.0), axis=-1, keepdims=True
                )
                probs_h = jnp.exp(scores - log_total)
                d_weights = dot_nt(my_d_mixed, values)
                row_terms = jnp.sum(d_weights * probs_h, axis=-1, keepdims=True)
                d_scores = (probs_h * (d_weights - row_terms) * scale).astype(BF)
                fresh = (
                    dot(d_scores, own(keys)),
                    dot_tn(d_scores, my_query),
                    dot_tn(probs_h.astype(BF), my_d_mixed),
                )
                total = [new if old is None else old + new for old, new in zip(total, fresh)]
            for part in range(3):
                d_qkv_ref[here, spots[part]] = total[part].astype(BF)
        first = head_tiles + 3 * pair
        fresh_tiles = dot(
            one_flip[...], jnp.concatenate([d_qkv_ref[:, spot] for spot in spots], axis=1)
        ).astype(BF)
        for part in range(3):
            tiles_ref[first + part] = fresh_tiles[:, part * TILE : (part + 1) * TILE]
        for part in range(3):
            leave(first + part)

        @pl.when(pair == 0)
        def _():
            for tile in range(head_tiles):
                combine(tile)

        @pl.when(pair > 0)
        def _():
            for part in range(3):
                combine(first - 3 + part)

        for turn, first, piece in FAR_TURNS:

            @pl.when(pair == turn)
            def _():
                pass_on(first, piece)

        @pl.when(pair == pairs - 3)
        def _():
            plane_sum(0)

        @pl.when(pair == pairs - 1)
        def _():
            line_sum(0)
            plane_sum(1)

        return carry

    lax.fori_loop(0, pairs, phase_two, 0)
    for part in range(3):
        combine(head_tiles + 3 * (pairs - 1) + part)

    for image in range(batches):
        landed(x_ref.at[image], load_sem.at[7, image])

    def phase_three(image, carry):
        here = pl.ds(pl.multiple_of(image * rows, rows), rows)
        d_one = dot_nt(d_qkv_ref[here, :], weight_ref[:, : 3 * width])
        hat, inverse = norm_stats(x_ref[image])
        sums_ref[0:1, :] += jnp.sum(d_one * hat, axis=0, keepdims=True)
        sums_ref[1:2, :] += jnp.sum(d_one, axis=0, keepdims=True)
        d_hat = d_one * gain_one
        x_ref[image] = grad_ref[image] + inverse * (
            d_hat
            - jnp.mean(d_hat, axis=-1, keepdims=True)
            - hat * jnp.mean(d_hat * hat, axis=-1, keepdims=True)
        )

        @pl.when(image == batches // 2 - 1)
        def _():
            pass_on(False, 6)
            line_sum(1)
            plane_sum(2)

        return carry

    lax.fori_loop(0, batches, phase_three, 0)
    out_store.wait()
    for image in range(batches):
        raw_ref[image * SEQ : (image + 1) * SEQ] = x_ref[image, :SEQ]
    dx_store = pltpu.make_async_copy(raw_ref, dx_hbm, store_sem.at[1, 0])
    dx_store.start()

    def small_copy(k):
        peer = lax.rem(me + k, PLANE)
        return remote(
            sums_ref, small_land.at[me], small_send.at[peer], small_recv.at[me], {"expert": peer}
        )

    def small_far_copy(k):
        peer = lax.rem(z + k, shards)
        return remote(
            small_land.at[me],
            small_far.at[z],
            small_send.at[PLANE + peer],
            small_recv.at[PLANE + z],
            {"dp": peer},
        )

    sums_ref[...] += flipped[: sums_ref.shape[0]]
    for k in range(1, PLANE):
        small_copy(k).start()
    pass_on(False, 7)
    line_sum(2)
    total = sums_ref[...]
    for k in range(1, PLANE):
        peer = lax.rem(me + k, PLANE)
        landed(small_land.at[peer], small_recv.at[peer])
        total = total + small_land[peer]
    small_land[me] = total
    for k in range(1, shards):
        small_far_copy(k).start()
    for k in range(1, shards):
        peer = lax.rem(z + k, shards)
        landed(small_far.at[peer], small_recv.at[PLANE + peer])
        total = total + small_far[peer]
    small_grad_ref[...] = total

    def finish(tile, carry):
        @pl.when(lax.rem(tile, PLANE) != me)
        def _():
            landed(final_ref.at[tile], final_recv.at[tile])

        @pl.when(lax.rem(tile, 2) != core)
        def _():
            near_copy(tile).wait_send()

        @pl.when((lax.rem(tile, 2) == core) & (lax.rem(tile, PLANE) != me))
        def _():
            plane_copy(tile).wait_send()

        return carry

    lax.fori_loop(0, 4 * head_tiles, finish, 0)
    for tile in range(head_tiles):
        proj_grad_ref[:, tile * TILE : (tile + 1) * TILE] = final_ref[tile].astype(F32)
    for pair in range(pairs):
        for part in range(3):
            low = part * width + pair * TILE
            qkv_grad_ref[:, low : low + TILE] = final_ref[head_tiles + 3 * pair + part].astype(F32)
    for k in range(own_tiles):
        for j in range(1, shards):
            line_copy(k, lax.rem(z + j, shards)).wait_send()
        for j in range(1, PLANE):
            final_copy(k, lax.rem(me + j, PLANE)).wait_send()
    for k in range(1, PLANE):
        small_copy(k).wait_send()
    for k in range(1, shards):
        small_far_copy(k).wait_send()
    for piece in range(len(pieces)):

        @pl.when(z == 0)
        def _():
            far_take(0, piece)

        @pl.when(z == shards - 1)
        def _():
            far_take(1, piece)

    mine = jnp.where(z == shards - 1, 1, 0)
    ends = [
        pltpu.make_async_copy(far_in_ref.at[mine], end_in_hbm, far_load.at[0, 0]),
        pltpu.make_async_copy(far_out_ref.at[mine], end_out_hbm, far_load.at[0, 1]),
    ]
    for copy in ends:
        copy.start()
    for piece in range(len(pieces)):

        first = 1 if piece < EARLY_FAR else 0

        @pl.when((z < shards - 1) & (z >= first))
        def _():
            far_copy(1, piece).wait_send()

        @pl.when((z > 0) & (z < shards - first))
        def _():
            far_copy(0, piece).wait_send()

    for copy in ends:
        copy.wait()
    dx_store.wait()


def run_reduce(x, grad, weight, vectors, slot_cols, back, saved, far, experts):
    batches, rows, width = x.shape
    shards = lax.axis_size("dp")
    qkv, mixed, lse, hidden, one, two, probs = saved
    depth = width // shards
    tiles = 4 * width // TILE
    own_tiles = tiles // PLANE
    small_rows = ceil_to(4 + experts, 8)
    count = len(pieces_of(far[0].shape[1], far[1].shape[1], FAR_CUTS))
    anywhere = pl.BlockSpec(memory_space=pl.ANY)
    inside = pl.BlockSpec(memory_space=pltpu.VMEM)
    dma = pltpu.SemaphoreType.DMA
    return pl.pallas_call(
        functools.partial(reduce_kernel, experts, shards),
        out_shape=(
            jax.ShapeDtypeStruct((batches * SEQ, width), F32),
            jax.ShapeDtypeStruct((batches * SEQ, width), F32),
            jax.ShapeDtypeStruct(far[0].shape[1:], BF),
            jax.ShapeDtypeStruct(far[1].shape[1:], BF),
            jax.ShapeDtypeStruct((depth, 3 * width), F32),
            jax.ShapeDtypeStruct((depth, width), F32),
            jax.ShapeDtypeStruct((small_rows, width), F32),
        ),
        in_specs=[inside] * 4 + [anywhere] * 11,
        out_specs=(anywhere,) * 4 + (inside,) * 3,
        scratch_shapes=[
            pltpu.VMEM(x.shape, F32),
            pltpu.VMEM(x.shape, F32),
            pltpu.VMEM(weight.shape, BF),
            pltpu.VMEM(back.shape, BF),
            pltpu.VMEM((batches * rows, 3 * width), BF),
            pltpu.VMEM((batches * rows, width), BF),
            pltpu.VMEM(x.shape, F32),
            pltpu.VMEM((batches * rows, width), BF),
            pltpu.VMEM((batches * rows, width), BF),
            pltpu.VMEM((batches * SEQ, width), F32),
            pltpu.VMEM((small_rows, width), F32),
            pltpu.VMEM((width, batches * rows), BF),
            pltpu.VMEM((batches * rows, 3 * width), BF),
            pltpu.VMEM((batches * rows, width), BF),
            pltpu.VMEM((batches * rows, width), BF),
            pltpu.VMEM((batches * rows, SMALL), BF),
            pltpu.VMEM((tiles, width, TILE), BF),
            pltpu.VMEM((tiles // 2, width, TILE), BF),
            pltpu.VMEM((own_tiles, PLANE // 2 - 1, width, TILE), BF),
            pltpu.VMEM((own_tiles, width, TILE), BF),
            pltpu.VMEM((own_tiles, shards, depth, TILE), BF),
            pltpu.VMEM((tiles, depth, TILE), BF),
            pltpu.VMEM((PLANE, small_rows, width), F32),
            pltpu.VMEM((shards, small_rows, width), F32),
            pltpu.VMEM(far[0].shape, BF),
            pltpu.VMEM(far[1].shape, BF),
            pltpu.VMEM(far[0].shape, BF),
            pltpu.VMEM(far[1].shape, BF),
            dma((9, batches)),
            dma((2, batches)),
            dma((tiles,)),
            dma((tiles,)),
            dma((tiles,)),
            dma((own_tiles, PLANE // 2 - 1)),
            dma((own_tiles, shards)),
            dma((own_tiles, shards)),
            dma((own_tiles, PLANE)),
            dma((tiles,)),
            dma((PLANE + shards,)),
            dma((PLANE + shards,)),
            dma((2, 2)),
            dma((2, count)),
            dma((2, count)),
        ],
        compiler_params=pltpu.CompilerParams(
            vmem_limit_bytes=VMEM_MAX, collective_id=3, has_side_effects=True
        ),
        cost_estimate=pl.CostEstimate(
            flops=16000000000, bytes_accessed=50000000, transcendentals=2000000
        ),
        name="tail",
    )(slot_cols, lse, probs, vectors, x, grad, weight, back, qkv, mixed, hidden, one, two, *far)


def last_turn(far_in, far_out):
    at = lax.axis_index("dp") // (lax.axis_size("dp") - 1)
    return [lax.psum(far.astype(F32), "dp").astype(BF)[at] for far in (far_in, far_out)]


def per_device(
    inputs,
    gain_one,
    shift_one,
    qkv_weight,
    proj_weight,
    gain_two,
    shift_two,
    router_weight,
    expert_in,
    expert_bias,
    expert_out,
    out_grad,
    routes,
    priority,
    capacity,
):
    batches = priority.shape[0]
    count = inputs.shape[0] // batches
    width = inputs.shape[1]
    experts = router_weight.shape[1]
    groups = lax.axis_size("expert")
    cap_pad = ceil_to(max(2, (5 * count + 2 * experts - 1) // (2 * experts)), 16)
    depth = qkv_weight.shape[0]
    both = ("dp", "expert")

    vectors = jnp.stack([gain_one, shift_one, gain_two, shift_two], axis=1)
    small = jnp.concatenate([vectors, router_weight], axis=1)
    small = jnp.pad(small, ((0, 0), (0, SMALL - small.shape[1])))
    dense = (qkv_weight, proj_weight, small)
    own = (expert_in[0], jnp.pad(expert_bias, ((0, BIAS_ROWS - 1), (0, 0))), expert_out[0])
    cols = jnp.concatenate([routes, priority.reshape(batches * SEQ, 2)], axis=1)
    cols = cols.reshape(batches, SEQ, 4)
    cols = jnp.pad(cols, ((0, 0), (0, SEQ_PAD - SEQ), (0, 0)), constant_values=-1)
    rows_first = jnp.swapaxes(cols, 1, 2)
    received, last, x, grad, weight, qkv, mixed, hidden, one, two, lse, probs, slot_cols, rows_small, *spread = run_front(
        inputs, out_grad, dense, own, cols, rows_first, capacity, experts, cap_pad
    )
    saved = (qkv, mixed, lse, hidden, one, two, probs)
    back, sum_in, sum_out, far_in, far_out = run_moe(received, last, own, *spread)
    z = lax.axis_index("dp")
    at_end = (z == 0) | (z == lax.axis_size("dp") - 1)
    spot = 4 * width
    if groups == PLANE:
        outputs, inputs_grad, end_in, end_out, qkv_grad, proj_grad, small_grad = run_reduce(
            x, grad, weight, rows_small, slot_cols, back, saved, (far_in, far_out), experts
        )
        small_grad = lax.dynamic_slice_in_dim(
            small_grad, lax.axis_index("dp") * depth, depth, axis=1
        )
        vectors = [small_grad[k] for k in range(4)]
        router_grad = small_grad[4 : 4 + experts].T
    else:
        weight = jnp.concatenate([weight, rows_small.T], axis=1)
        outputs, inputs_grad, dense = run_tail(
            x, grad, weight, cols, slot_cols, back, saved, experts
        )
        end_in, end_out = last_turn(far_in, far_out)
        outputs, inputs_grad = (
            full[:, :SEQ].reshape(batches * SEQ, width) for full in (outputs, inputs_grad)
        )
        dense = lax.psum_scatter(dense, both, scatter_dimension=0, tiled=True)
        dense = lax.all_gather(dense, "expert", axis=0, tiled=True).astype(F32)
        qkv_grad = dense[:, : 3 * width]
        proj_grad = dense[:, 3 * width : spot]
        vectors = [dense[:, spot + k] for k in range(4)]
        router_grad = dense[:, spot + 4 : spot + 4 + experts]
    grad_in = jnp.where(at_end, end_in[:width], sum_in[:width]).astype(F32)
    grad_bias = jnp.where(at_end, end_in[width], sum_in[width]).astype(F32)
    grad_out = jnp.where(at_end, end_out, sum_out).astype(F32)
    return (
        outputs,
        inputs_grad,
        vectors[0],
        vectors[1],
        qkv_grad,
        proj_grad,
        vectors[2],
        vectors[3],
        router_grad,
        grad_in[None],
        grad_bias[None],
        grad_out[None],
    )


def solution(mesh):
    token = P(("dp", "expert"), None)
    vector = P("dp")
    matrix = P("dp", None)
    return jax.shard_map(
        per_device,
        mesh=mesh,
        in_specs=(
            token,
            vector,
            vector,
            matrix,
            matrix,
            vector,
            vector,
            matrix,
            P("expert", None, "dp"),
            P("expert", "dp"),
            P("expert", "dp", None),
            token,
            token,
            token,
            P(("dp", "expert")),
        ),
        out_specs=(
            token,
            token,
            vector,
            vector,
            matrix,
            matrix,
            vector,
            vector,
            matrix,
            P("expert", None, "dp"),
            P("expert", "dp"),
            P("expert", "dp", None),
        ),
        check_vma=False,
    )
```
